32 devices in a mesh: ctx: 4 (over y, x), exp: 8 (over z, core).
Axes of the slice: x: 2, y: 2, z: 4, core: 2. Of those that a mesh axis runs over, the one named last changes fastest.
Arguments:
- inputs: bfloat16 [4, 6144, 768], P('ctx', 'exp'), may hold values from -6 to 6
- prev_logits: float32 [4, 6144, 12], P('ctx', 'exp'), may hold values from -4 to 4
- routes: int32 [4, 6144, 2], P('ctx', 'exp'), may hold values from 0 to 11, all different within a row; in each aligned block of 768 rows (0 to 767, 768 to 1535, ..., all dimensions but the last counted through in order) at most 144 rows name the same one
- attn_gain: float32 [768], replicated, may hold values from 0.25 to 1.75
- w_qkv: bfloat16 [768, 2304], replicated, may hold values from -0.21875 to 0.21875
- w_out: bfloat16 [768, 768], replicated, may hold values from -0.875 to 0.875
- moe_gain: float32 [768], replicated, may hold values from 0.25 to 1.75
- router: bfloat16 [768, 12], replicated, may hold values from -0.109375 to 0.109375
- const_gate: bfloat16 [2, 768, 2], replicated, may hold values from -0.21875 to 0.21875
- const_vec: float32 [2, 768], replicated, may hold values from -12 to 12
- w_gate: bfloat16 [8, 768, 2048], P('exp'), may hold values from -0.21875 to 0.21875
- w_up: bfloat16 [8, 768, 2048], P('exp'), may hold values from -0.21875 to 0.21875
- w_down: bfloat16 [8, 2048, 768], P('exp'), may hold values from -1.5 to 1.5
- out_grad: bfloat16 [4, 6144, 768], P('ctx', 'exp'), may hold values from -6 to 6
Outputs:
- mixed_out: bfloat16 [4, 6144, 768], P('ctx', 'exp')
- d_inputs: float32 [4, 6144, 768], P('ctx', 'exp')
- d_prev: float32 [4, 6144, 12], P('ctx', 'exp')
- d_attn_gain: float32 [768], replicated
- d_w_qkv: float32 [768, 2304], replicated
- d_w_out: float32 [768, 768], replicated
- d_moe_gain: float32 [768], replicated
- d_router: float32 [768, 12], replicated
- d_const_gate: float32 [2, 768, 2], replicated
- d_const_vec: float32 [2, 768], replicated
- d_w_gate: float32 [8, 768, 2048], P('exp', 'ctx')
- d_w_up: float32 [8, 768, 2048], P('exp', 'ctx')
- d_w_down: float32 [8, 2048, 768], P('exp', 'ctx')
The draws below stay inside these ranges and needn't reach their ends.
Inputs may be any that keep to these rules, and one draw needn't show every extreme that they name: `routes`: each row names two different experts. Among the 768 rows of one device no expert is named by more than 144 rows, and on some devices one is named by exactly 144.
All inputs are finite; a program needn't handle non-finite values.
Results may differ from the reference program's by a relative error of at most 0.015.
Values may be sent and summed in bfloat16 or wider, within the bound.
No kernel may reach another device: no remote copies, remote signals or barrier semaphores. Data moves between devices by JAX's collectives and lax.ppermute only.
A program may use at most 256 MiB of HBM per device.

```python
import math
import jax
import jax.numpy as jnp
import numpy as np
from jax import lax

D = 768
HEADS = 12
HEAD_DIM = 64
FF = 2048
FFN_EXPERTS = 8
ALL_EXPERTS = 12
CONT_LEN = 512
PROMPT = 1024
PROMPT_DEV = 256
TOK = 768
ROUTE_MOST = 144
SPLIT = 1
FF_PART = 2048
N_CTX = 4
N_EXP = 8


def level_of(key, extent, pieces, least, high):
    gain = 1.0
    for dim, parts in pieces:
        draws = jax.random.uniform(jax.random.fold_in(jax.random.fold_in(key, 6), dim), (parts,), jnp.float32, least / len(pieces), high / len(pieces))
        gain = gain * jnp.repeat(jnp.exp(draws), extent[dim] // parts).reshape((-1,) + (1,) * (len(extent) - 1 - dim))
    return gain


def deal_out(own_key, own, number, rows, number_of, top, limit, skew):
    sequence = jax.random.permutation(own_key, number_of)
    packed, usual = portions_of(number_of, rows * top, limit, skew, True), portions_of(number_of, rows * top, limit, skew, False)
    places = jnp.arange(number_of)

    def named(lengths, turn):
        used = int((lengths > 0).sum())
        fixed = max(1, used // 4)
        shifted = fixed + (places - fixed + turn * (used - fixed)) % max(1, number_of - fixed)
        return jnp.zeros((number_of,), jnp.int32).at[sequence[jnp.where(places < fixed, places, shifted)]].set(jnp.asarray(lengths, jnp.int32))

    lengths = jnp.where(number % 4 == 0, named(packed, number // 4), named(usual, number - number // 4 - 1))
    mixed = jax.random.permutation(jax.random.fold_in(own, 3), number_of)
    donor, receiver = mixed[0:number_of // 2 * 2:2], mixed[1:number_of // 2 * 2:2]
    margin = jnp.minimum(lengths[donor] - 1, limit - lengths[receiver]) // 2
    margin = jnp.where((donor == sequence[0]) | (receiver == sequence[0]) | (lengths[receiver] == 0), 0, jnp.maximum(margin, 0))
    shifted = jax.random.randint(jax.random.fold_in(own, 4), (number_of // 2,), 0, 1 << 20) % (margin + 1)
    lengths = lengths.at[donor].add(-shifted).at[receiver].add(shifted)
    items = jnp.searchsorted(jnp.cumsum(lengths), jnp.arange(rows * top), side="right").astype(jnp.int32)
    table = items.reshape(top, rows).T
    table = table[jax.random.permutation(jax.random.fold_in(own, 1), rows)]
    turn = jax.random.randint(jax.random.fold_in(own, 2), (rows, 1), 0, top)
    return jnp.take_along_axis(table, (jnp.arange(top)[None, :] + turn) % top, axis=1)


def portions_of(number_of, total, limit, lean, full):
    portions = [(1 << 20) // math.isqrt(grade ** lean) + 1 for grade in range(1, number_of + 1)]
    largest = limit if full else min(limit, max(-(-total // number_of), total * portions[0] // sum(portions)))
    least = 1 if total - largest >= number_of - 1 else 0
    counts, surplus = [largest] + [least] * (number_of - 1), total - largest - least * (number_of - 1)
    while surplus > 0:
        free = [i for i in range(1, number_of) if counts[i] < largest] or [i for i in range(1, number_of) if counts[i] < limit]
        whole, remaining = sum([portions[i] for i in free]), surplus
        for i in free:
            extra = min(limit - counts[i], max(1, remaining * portions[i] // whole), surplus)
            counts[i] = counts[i] + extra
            surplus = surplus - extra
    return np.array(counts)


def bell_draw(key, extent, scale, bound, pieces=(), held_as=jnp.bfloat16):
    values = scale * jax.random.normal(key, extent, jnp.float32)
    if pieces:
        values = values * level_of(key, extent, pieces, -0.22, 0.18)
    return jnp.clip(values, -bound, bound).astype(held_as)


def setup_inputs(seed: int = 0) -> dict:
    seeds = jax.random.split(jax.random.key(seed), 15)
    inputs = bell_draw(seeds[0], (N_CTX, N_EXP * TOK, D), 1.0, 6.0, ((0, 4), (1, 8)))
    prev_logits = bell_draw(seeds[1], (N_CTX, N_EXP * TOK, ALL_EXPERTS), 0.7, 4.0, ((0, 4), (1, 8)), jnp.float32)
    routes_keys = jax.random.split(jax.random.fold_in(seeds[2], 1), N_CTX * (N_EXP * TOK) // TOK)
    routes_turns = jax.random.permutation(jax.random.fold_in(seeds[2], 3), N_CTX * (N_EXP * TOK) // TOK)
    routes = jax.vmap(lambda own, number: deal_out(jax.random.fold_in(seeds[2], 2), own, number, TOK, ALL_EXPERTS, 2, ROUTE_MOST, 1))(routes_keys, routes_turns).reshape((N_CTX, N_EXP * TOK, 2))
    attn_gain = jnp.clip(1.0 + 0.15 * jax.random.normal(seeds[3], (D,), jnp.float32), 0.25, 1.75)
    w_qkv = bell_draw(seeds[4], (D, 3 * D), D ** -0.5, 0.21875)
    w_out = bell_draw(seeds[5], (D, D), (D // 16) ** -0.5, 0.875)
    moe_gain = jnp.clip(1.0 + 0.15 * jax.random.normal(seeds[6], (D,), jnp.float32), 0.25, 1.75)
    router = bell_draw(seeds[7], (D, ALL_EXPERTS), (4 * D) ** -0.5, 0.109375)
    const_gate = bell_draw(seeds[8], (2, D, 2), D ** -0.5, 0.21875)
    const_vec = bell_draw(seeds[9], (2, D), 2.0, 12.0, (), jnp.float32)
    w_gate = bell_draw(seeds[10], (N_EXP, D, FF_PART), D ** -0.5, 0.21875, ((0, 8),))
    w_up = bell_draw(seeds[11], (N_EXP, D, FF_PART), D ** -0.5, 0.21875, ((0, 8),))
    w_down = bell_draw(seeds[12], (N_EXP, FF_PART, D), (max(16, FF // 128)) ** -0.5, 1.5, ((0, 8),))
    out_grad = bell_draw(seeds[13], (N_CTX, N_EXP * TOK, D), 1.0, 6.0, ((0, 4), (1, 8)))
    return dict(inputs=inputs, prev_logits=prev_logits, routes=routes, attn_gain=attn_gain, w_qkv=w_qkv, w_out=w_out, moe_gain=moe_gain, router=router, const_gate=const_gate, const_vec=const_vec, w_gate=w_gate, w_up=w_up, w_down=w_down, out_grad=out_grad)


@jax.custom_vjp
def low(v):
    return lax.optimization_barrier(v.astype(jnp.bfloat16)).astype(jnp.float32)

@jax.custom_vjp
def low_back(v):
    return v

def low_keep(v):
    return (low(v), None)

def low_pass(kept, grad):
    return (grad,)

def back_keep(v):
    return (v, None)

def back_low(kept, grad):
    return (low(grad),)
low.defvjp(low_keep, low_pass)
low_back.defvjp(back_keep, back_low)
highest = lax.Precision.HIGHEST
epsilon = 1e-06
masked_value = -1e+30

def rms_scale(tensor, gain_vec):
    return tensor * lax.rsqrt(lax.optimization_barrier(jnp.mean(tensor * tensor, axis=-1, keepdims=True)) + epsilon) * gain_vec

def route_slots(route_rows):
    flat_ids = route_rows.reshape(-1)
    onehot = (flat_ids[:, None] == jnp.arange(ALL_EXPERTS, dtype=jnp.int32)[None, :]).astype(jnp.int32)
    before = jnp.cumsum(onehot, axis=0) - onehot
    return lax.optimization_barrier(jnp.sum(before * onehot, axis=1)).reshape(route_rows.shape).astype(jnp.int32)

def attend(queries, key_rows, value_rows, allowed):
    raw_scores = jnp.einsum('bqhd,bkhd->bhqk', queries, key_rows, precision=highest) * HEAD_DIM ** (-0.5)
    scores = jnp.where(allowed, low_back(raw_scores), masked_value)
    weights = low(jax.nn.softmax(scores, axis=-1))
    return jnp.einsum('bhqk,bkhd->bqhd', weights, value_rows, precision=highest)

def cycle_layer(params, cycle_inputs, cycle_prev, cycle_routes):
    attn_gain, w_qkv, w_out, moe_gain, router, const_gate, const_vec, w_gate, w_up, w_down = params
    model_width = cycle_inputs.shape[-1]
    act_low = low(rms_scale(cycle_inputs, attn_gain))
    projected = low_back(low(jnp.dot(act_low.reshape(-1, model_width), w_qkv, precision=highest)))
    projected = projected.reshape(N_CTX, TOK, 3, HEADS, HEAD_DIM)
    prompt_part = projected[:, :PROMPT_DEV].reshape(PROMPT, 3, HEADS, HEAD_DIM)
    cont_part = projected[:, PROMPT_DEV:]
    positions = jnp.arange(PROMPT, dtype=jnp.int32)
    causal = positions[None, :] <= positions[:, None]
    prompt_out = attend(prompt_part[None, :, 0], prompt_part[None, :, 1], prompt_part[None, :, 2], causal)
    shared_keys = jnp.broadcast_to(prompt_part[None, :, 1], (N_CTX, PROMPT, HEADS, HEAD_DIM))
    shared_values = jnp.broadcast_to(prompt_part[None, :, 2], (N_CTX, PROMPT, HEADS, HEAD_DIM))
    cont_keys = jnp.concatenate([shared_keys, cont_part[:, :, 1]], axis=1)
    cont_values = jnp.concatenate([shared_values, cont_part[:, :, 2]], axis=1)
    key_index = jnp.arange(PROMPT + CONT_LEN, dtype=jnp.int32)
    query_index = jnp.arange(CONT_LEN, dtype=jnp.int32)
    cont_allowed = (key_index[None, :] < PROMPT) | (key_index[None, :] - PROMPT <= query_index[:, None])
    cont_out = attend(cont_part[:, :, 0], cont_keys, cont_values, cont_allowed)
    prompt_out = prompt_out.reshape(N_CTX, PROMPT_DEV, model_width)
    mixed = jnp.concatenate([prompt_out, cont_out.reshape(N_CTX, CONT_LEN, model_width)], axis=1)
    mixed = low_back(low(mixed))
    attn_branch = low_back(jnp.dot(mixed.reshape(-1, model_width), w_out, precision=highest))
    hidden = cycle_inputs + attn_branch.reshape(N_CTX, TOK, model_width)
    normed = rms_scale(hidden, moe_gain)
    moe_low = low(normed)
    logits = jnp.einsum('ntd,de->nte', moe_low, router, precision=highest) + cycle_prev
    probs_all = jax.nn.softmax(logits, axis=-1)
    gate_values = jnp.take_along_axis(probs_all, cycle_routes, axis=-1)
    alphas = jax.nn.softmax(jnp.einsum('ntd,cda->ntca', moe_low, const_gate, precision=highest), axis=-1)
    const_out = alphas[..., 0:1] * normed[:, :, None, :] + alphas[..., 1:2] * const_vec[None, None]
    slot_index = jax.vmap(route_slots)(cycle_routes)
    is_ffn = cycle_routes < FFN_EXPERTS
    expert_ids = jnp.where(is_ffn, cycle_routes, FFN_EXPERTS)
    ctx_ids = jnp.broadcast_to(jnp.arange(N_CTX, dtype=jnp.int32)[:, None, None], cycle_routes.shape)
    token_ids = ctx_ids * TOK + jnp.arange(TOK, dtype=jnp.int32)[None, :, None]
    dispatch = jnp.full((FFN_EXPERTS, N_CTX, ROUTE_MOST), N_CTX * TOK, jnp.int32)
    dispatch = dispatch.at[expert_ids, ctx_ids, slot_index].set(token_ids, mode='drop')
    padded = jnp.concatenate([moe_low.reshape(-1, model_width), jnp.zeros((1, model_width), moe_low.dtype)], axis=0)
    row_block = padded[dispatch.reshape(FFN_EXPERTS, -1)]
    gate_pre = low_back(jnp.einsum('erd,esdf->esrf', row_block, w_gate, precision=highest))
    up_pre = low_back(jnp.einsum('erd,esdf->esrf', row_block, w_up, precision=highest))
    inner_act = low(jax.nn.silu(gate_pre) * up_pre)
    partial_out = low(jnp.einsum('esrf,esfd->esrd', inner_act, w_down, precision=highest))
    expert_out = low_back(lax.optimization_barrier(jnp.sum(partial_out, axis=1))).reshape(-1, model_width)
    position = expert_ids * (N_CTX * ROUTE_MOST) + ctx_ids * ROUTE_MOST + slot_index
    picked = jnp.where(is_ffn[..., None], expert_out[jnp.where(is_ffn, position, 0)], 0.0)
    selected = picked + jnp.where((cycle_routes == FFN_EXPERTS + 1)[..., None], normed[:, :, None, :], 0.0)
    selected = selected + jnp.where((cycle_routes == FFN_EXPERTS + 2)[..., None], const_out[:, :, 0:1], 0.0)
    selected = selected + jnp.where((cycle_routes == FFN_EXPERTS + 3)[..., None], const_out[:, :, 1:2], 0.0)
    return hidden + lax.optimization_barrier(jnp.sum(gate_values[..., None] * selected, axis=2))

def to_cycles(tensor):
    return jnp.swapaxes(tensor.reshape(N_CTX, N_EXP, TOK, tensor.shape[-1]), 0, 1)

def from_cycles(tensor):
    return jnp.swapaxes(tensor, 0, 1).reshape(N_CTX, N_EXP * TOK, tensor.shape[-1])

def reference(inputs, prev_logits, routes, attn_gain, w_qkv, w_out, moe_gain, router, const_gate, const_vec, w_gate, w_up, w_down, out_grad):
    listed = [attn_gain, w_qkv, w_out, moe_gain, router, const_gate, const_vec, w_gate.reshape(FFN_EXPERTS, SPLIT, D, FF_PART), w_up.reshape(FFN_EXPERTS, SPLIT, D, FF_PART), w_down.reshape(FFN_EXPERTS, SPLIT, FF_PART, D)]
    weights = tuple((tensor.astype(jnp.float32) for tensor in listed))

    def one_cycle(totals, cycle_data):
        cycle_inputs, cycle_prev, cycle_routes, cycle_grad = cycle_data

        def forward(inputs_cycle, prev_cycle, params):
            return cycle_layer(params, inputs_cycle, prev_cycle, cycle_routes)
        output, pullback = jax.vjp(forward, cycle_inputs, cycle_prev, weights)
        grad_inputs, grad_prev, grad_params = pullback(cycle_grad)
        totals = jax.tree.map(lambda earlier, addend: earlier + addend, totals, grad_params)
        return (totals, (output.astype(jnp.bfloat16), grad_inputs, grad_prev))
    initial = jax.tree.map(jnp.zeros_like, weights)
    stacked = (to_cycles(inputs.astype(jnp.float32)), to_cycles(prev_logits), to_cycles(routes), to_cycles(out_grad.astype(jnp.float32)))
    totals, cycle_outs = lax.scan(one_cycle, initial, stacked)
    mixed_out = from_cycles(cycle_outs[0])
    d_inputs = from_cycles(cycle_outs[1])
    d_prev = from_cycles(cycle_outs[2])
    return (mixed_out, d_inputs, d_prev, totals[0], totals[1], totals[2], totals[3], totals[4], totals[5], totals[6], totals[7].reshape(N_EXP, D, FF_PART), totals[8].reshape(N_EXP, D, FF_PART), totals[9].reshape(N_EXP, FF_PART, D))
```

```python
import functools, math
import jax, jax.numpy as jnp
from jax import lax
from jax.experimental import pallas as pl
from jax.experimental.pallas import tpu as pltpu

HEADS = 12
HEAD_DIM = 64
CONT_LEN = 512
LOG2E = 1.4426950408889634
SCALE = HEAD_DIM ** -0.5
bf16 = jnp.bfloat16
f32 = jnp.float32
NEG = -1e30


def dot_nt(a, b):
    return lax.dot_general(a, b, (((1,), (1,)), ((), ())), preferred_element_type=f32)


def dot_nn(a, b):
    return jnp.dot(a, b, preferred_element_type=f32)


def query_tiles(tok, plen):
    tiles = [(0, plen, True)]
    step = 256
    for start in range(plen, tok, step):
        tiles.append((start, step, False))
    return tiles


def attention_forward_kernel(plen, flags_ref, q_ref, k_ref, v_ref, kr_ref, vr_ref, o_ref, lse_ref):
    tok = q_ref.shape[0]
    remote = kr_ref.shape[0]
    lane = lax.broadcasted_iota(jnp.int32, (1, 128), 1)
    low_half = lane < HEAD_DIM
    c = SCALE * LOG2E
    one = jnp.ones((), bf16)
    zero = jnp.zeros((), bf16)
    for start, size, is_prompt in query_tiles(tok, plen):
        accs, peaks = [], []
        for head in range(2):
            mine = low_half if head == 0 else ~low_half
            qh = jnp.where(mine, q_ref[start : start + size, :], zero)
            pieces = []
            row = lax.broadcasted_iota(jnp.int32, (size, size), 0)
            col = lax.broadcasted_iota(jnp.int32, (size, size), 1)
            diag = dot_nt(qh, k_ref[start : start + size, :])
            pieces.append((jnp.where(col <= row, diag, NEG), v_ref, start, size))
            if is_prompt:
                for j in range(remote // plen):
                    s = dot_nt(qh, kr_ref[j * plen : (j + 1) * plen, :])
                    pieces.append((s + flags_ref[j], vr_ref, j * plen, plen))
            else:
                s = dot_nt(qh, k_ref[0:start, :])
                pieces.append((s, v_ref, 0, start))
                s = dot_nt(qh, kr_ref[...])
                pieces.append((s, vr_ref, 0, remote))
            peak = None
            for s, _, _, _ in pieces:
                m = jnp.max(s, axis=1, keepdims=True)
                peak = m if peak is None else jnp.maximum(peak, m)
            shift = peak * c
            acc = None
            for s, ref, at, n in pieces:
                p = jnp.exp2(s * c - shift).astype(bf16)
                vh = jnp.where(mine, ref[at : at + n, :], one)
                part = dot_nn(p, vh)
                acc = part if acc is None else acc + part
            accs.append(acc)
            peaks.append(shift)
        num = jnp.where(low_half, accs[0], accs[1])
        den = pltpu.roll(jnp.where(low_half, accs[1], accs[0]), HEAD_DIM, 1)
        o_ref[start : start + size, :] = (num / den).astype(bf16)
        logs = jnp.where(low_half, peaks[0], peaks[1]) + jnp.log2(den)
        turned = logs.T
        lse_ref[0, 0:8, start : start + size] = turned[0:8, :]
        lse_ref[0, 8:16, start : start + size] = turned[HEAD_DIM : HEAD_DIM + 8, :]


def attention_forward(flags, proj, kv_rem, plen):
    tok, width = proj.shape[0], proj.shape[1] // 3
    remote = kv_rem.shape[0]
    pairs = width // 128
    return pl.pallas_call(
        functools.partial(attention_forward_kernel, plen),
        grid=(pairs,),
        in_specs=[
            pl.BlockSpec(memory_space=pltpu.SMEM),
            pl.BlockSpec((tok, 128), lambda i: (0, i)),
            pl.BlockSpec((tok, 128), lambda i: (0, pairs + i)),
            pl.BlockSpec((tok, 128), lambda i: (0, 2 * pairs + i)),
            pl.BlockSpec((remote, 128), lambda i: (0, i)),
            pl.BlockSpec((remote, 128), lambda i: (0, pairs + i)),
        ],
        out_specs=[
            pl.BlockSpec((tok, 128), lambda i: (0, i)),
            pl.BlockSpec((1, 16, tok), lambda i: (i, 0, 0)),
        ],
        out_shape=[
            jax.ShapeDtypeStruct((tok, width), bf16),
            jax.ShapeDtypeStruct((pairs, 16, tok), f32),
        ],
        compiler_params=pltpu.CompilerParams(vmem_limit_bytes=48 * 2**20),
        cost_estimate=pl.CostEstimate(flops=4 * tok * (tok + remote) * width, bytes_accessed=2 * (tok * 4 + remote * 2) * width, transcendentals=tok * (tok + remote) * HEADS),
        name="attention_forward",
    )(flags, proj, proj, proj, kv_rem, kv_rem)


def attention_backward_kernel(plen, flags_ref, q_ref, k_ref, v_ref, kr_ref, vr_ref, o_ref, do_ref, lse_ref,
                              dq_ref, dk_ref, dv_ref, dkr_ref, dvr_ref, kt, krt, dka, dva, dkra, dvra):
    tok = q_ref.shape[0]
    remote = kr_ref.shape[0]
    lane = lax.broadcasted_iota(jnp.int32, (1, 128), 1)
    low_half = lane < HEAD_DIM
    c = SCALE * LOG2E
    zero = jnp.zeros((), bf16)
    kt[...] = k_ref[...].T
    krt[...] = kr_ref[...].T
    dka[...] = jnp.zeros_like(dka)
    dva[...] = jnp.zeros_like(dva)
    dkra[...] = jnp.zeros_like(dkra)
    dvra[...] = jnp.zeros_like(dvra)
    pick = lax.broadcasted_iota(jnp.int32, (16, 128), 0) // 8 == lax.broadcasted_iota(jnp.int32, (16, 128), 1) // HEAD_DIM
    pick = jnp.where(pick, 1.0, 0.0).astype(bf16)
    for start, size, is_prompt in query_tiles(tok, plen):
        rows = slice(start, start + size)
        product = do_ref[rows, :].astype(f32) * o_ref[rows, :].astype(f32)
        high = product.astype(bf16)
        rest = (product - high.astype(f32)).astype(bf16)
        delta = dot_nt(pick, high) + dot_nt(pick, rest)
        dqt = []
        for head in range(2):
            mine = low_half if head == 0 else ~low_half
            qh = jnp.where(mine, q_ref[rows, :], zero)
            doh = jnp.where(mine, do_ref[rows, :], zero)
            lse_row = lse_ref[0, 8 * head : 8 * head + 1, rows]
            delta_row = delta[8 * head : 8 * head + 1, :]
            segments = [(k_ref, v_ref, kt, dka, dva, start, size, "diag")]
            if is_prompt:
                for j in range(remote // plen):
                    segments.append((kr_ref, vr_ref, krt, dkra, dvra, j * plen, plen, j))
            else:
                segments.append((k_ref, v_ref, kt, dka, dva, 0, start, None))
                segments.append((kr_ref, vr_ref, krt, dkra, dvra, 0, remote, None))
            total = None
            for kk, vv, tt, dk_acc, dv_acc, at, n, mode in segments:
                keys = slice(at, at + n)
                st = dot_nt(kk[keys, :], qh) * c - lse_row
                if mode == "diag":
                    key = lax.broadcasted_iota(jnp.int32, (n, size), 0)
                    query = lax.broadcasted_iota(jnp.int32, (n, size), 1)
                    st = jnp.where(key <= query, st, NEG)
                elif mode is not None:
                    st = st + flags_ref[mode]
                pt = jnp.exp2(st)
                dpt = dot_nt(vv[keys, :], doh)
                dst = (pt * (dpt - delta_row)).astype(bf16)
                dv_acc[keys, :] += dot_nn(pt.astype(bf16), doh)
                dk_acc[keys, :] += dot_nn(dst, qh)
                part = dot_nn(tt[head * HEAD_DIM : (head + 1) * HEAD_DIM, keys], dst)
                total = part if total is None else total + part
            dqt.append(total)
        dq_ref[rows, :] = (jnp.concatenate(dqt, axis=0).T * SCALE).astype(bf16)
    dk_ref[...] = (dka[...] * SCALE).astype(bf16)
    dv_ref[...] = dva[...].astype(bf16)
    dkr_ref[...] = (dkra[...] * SCALE).astype(bf16)
    dvr_ref[...] = dvra[...].astype(bf16)


def attention_backward(flags, proj, kv_rem, mixed, d_mixed, lse, plen):
    tok, width = mixed.shape
    remote = kv_rem.shape[0]
    pairs = width // 128
    own = pl.BlockSpec((tok, 128), lambda i: (0, i))
    far = pl.BlockSpec((remote, 128), lambda i: (0, i))
    return pl.pallas_call(
        functools.partial(attention_backward_kernel, plen),
        grid=(pairs,),
        in_specs=[
            pl.BlockSpec(memory_space=pltpu.SMEM),
            own,
            pl.BlockSpec((tok, 128), lambda i: (0, pairs + i)),
            pl.BlockSpec((tok, 128), lambda i: (0, 2 * pairs + i)),
            far,
            pl.BlockSpec((remote, 128), lambda i: (0, pairs + i)),
            own,
            own,
            pl.BlockSpec((1, 16, tok), lambda i: (i, 0, 0)),
        ],
        out_specs=[own, own, own, far, far],
        out_shape=[jax.ShapeDtypeStruct((tok, width), bf16)] * 3 + [jax.ShapeDtypeStruct((remote, width), bf16)] * 2,
        scratch_shapes=[
            pltpu.VMEM((128, tok), bf16),
            pltpu.VMEM((128, remote), bf16),
            pltpu.VMEM((tok, 128), f32),
            pltpu.VMEM((tok, 128), f32),
            pltpu.VMEM((remote, 128), f32),
            pltpu.VMEM((remote, 128), f32),
        ],
        compiler_params=pltpu.CompilerParams(vmem_limit_bytes=48 * 2**20),
        cost_estimate=pl.CostEstimate(flops=10 * tok * (tok + remote) * width, bytes_accessed=2 * (tok * 8 + remote * 4) * width, transcendentals=tok * (tok + remote) * HEADS),
        name="attention_backward",
    )(flags, proj, proj, proj, kv_rem, kv_rem, mixed, d_mixed, lse)


FFN_EXPERTS = 8
ALL_EXPERTS = 12
EXTRA = 128
SMALL = 8
epsilon = 1e-06


def dot_tn(a, b):
    return lax.dot_general(a, b, (((0,), (0,)), ((), ())), preferred_element_type=f32)


def split_low(value, parts):
    pieces = []
    for _ in range(parts):
        piece = value.astype(bf16)
        pieces.append(piece)
        value = value - piece.astype(f32)
    return pieces


def route_kernel(groups, home_ref, ids_ref, grad_ref, prev_ref, *out_refs):
    tok, width = grad_ref.shape
    count = len(groups)
    turned_refs, chosen_refs, early_ref = out_refs[:count], out_refs[count : 2 * count], out_refs[2 * count]
    expert = lax.broadcasted_iota(jnp.int32, (16, tok), 0)
    names = [ids_ref[k : k + 1, :] == expert for k in range(2)]
    both = jnp.where(names[0] | names[1], 1.0, 0.0).astype(bf16)
    earlier = lax.broadcasted_iota(jnp.int32, (tok, tok), 0) < lax.broadcasted_iota(jnp.int32, (tok, tok), 1)
    before = dot_nn(both, jnp.where(earlier, 1.0, 0.0).astype(bf16))
    pieces = [piece.astype(f32) for piece in split_low(prev_ref[...], 3)]
    extra = (pieces[0] + pltpu.roll(pieces[1], 16, 1) + pltpu.roll(pieces[2], 32, 1)).astype(bf16)
    slot = [jnp.sum(jnp.where(n, before, 0.0), axis=0, keepdims=True).astype(jnp.int32) for n in names]
    for (first, size), turned_ref, chosen_ref in zip(groups, turned_refs, chosen_refs):
        spots = lax.broadcasted_iota(jnp.int32, (FFN_EXPERTS * size, tok), 0)
        hit = None
        for k in range(2):
            ids = ids_ref[k : k + 1, :]
            inside = (ids < FFN_EXPERTS) & (slot[k] >= first) & (slot[k] < first + size)
            place = jnp.where(inside, ids * size + slot[k] - first, -1)
            hit = spots == place if hit is None else hit | (spots == place)
        turned = jnp.where(hit, 1.0, 0.0).astype(bf16)
        turned_ref[...] = turned
        chosen_ref[...] = turned.T
        grads = dot_nn(turned, grad_ref[...]).astype(bf16)
        extras = dot_nn(turned, extra).astype(bf16)
        for e in range(FFN_EXPERTS):
            early_ref[e, first : first + size, 0:width] = grads[e * size : (e + 1) * size]
            early_ref[e, first : first + size, width : width + EXTRA] = extras[e * size : (e + 1) * size]


def route_plan(home, ids, grad, prev, groups):
    tok, width = grad.shape
    counts = [FFN_EXPERTS * size for _, size in groups]
    whole = pl.BlockSpec(memory_space=pltpu.VMEM)
    out = pl.pallas_call(
        functools.partial(route_kernel, groups),
        in_specs=[pl.BlockSpec(memory_space=pltpu.SMEM), whole, whole, whole],
        out_specs=[whole] * (2 * len(groups) + 1),
        out_shape=[jax.ShapeDtypeStruct((n, tok), bf16) for n in counts]
        + [jax.ShapeDtypeStruct((tok, n), bf16) for n in counts]
        + [jax.ShapeDtypeStruct((FFN_EXPERTS, sum(counts) // FFN_EXPERTS, width + EXTRA), bf16)],
        compiler_params=pltpu.CompilerParams(vmem_limit_bytes=48 * 2**20),
        cost_estimate=pl.CostEstimate(flops=2 * sum(counts) * tok * (width + EXTRA), bytes_accessed=4 * sum(counts) * width, transcendentals=0),
        name="route_plan",
    )(home, ids, grad, prev)
    return out[: len(groups)], out[len(groups) : -1], out[-1]


def expert_kernel(group, home_ref, rows_ref, early_ref, router_ref, wg_ref, wu_ref, wd_ref,
                  out_ref, drow_ref, dout_ref, inner_ref, dgate_ref, dup_ref, acc_out, acc_row, probs_ref):
    width = rows_ref.shape[1]
    step, steps = pl.program_id(0), pl.num_programs(0)
    home = home_ref[0]
    lane = lax.broadcasted_iota(jnp.int32, (1, EXTRA), 1)
    slots = slice(group[0], group[0] + group[1])

    @pl.when(step == 0)
    def _():
        extra = early_ref[:, slots, width : width + EXTRA].astype(f32).reshape(-1, EXTRA)
        logits = extra + pltpu.roll(extra, EXTRA - 16, 1) + pltpu.roll(extra, EXTRA - 32, 1)
        logits = logits + dot_nn(rows_ref[...], router_ref[...])
        logits = jnp.where(lane < ALL_EXPERTS, logits, NEG)
        unnormed = jnp.exp(logits - jnp.max(logits, axis=1, keepdims=True))
        probs = unnormed / jnp.sum(unnormed, axis=1, keepdims=True)
        probs_ref[...] = probs
        gate = jnp.sum(jnp.where(lane == home, probs, 0.0), axis=1, keepdims=True)
        dout_ref[...] = (gate * early_ref[:, slots, 0:width].astype(f32).reshape(-1, width)).astype(bf16)
        acc_out[...] = jnp.zeros_like(acc_out)
        acc_row[...] = jnp.zeros_like(acc_row)

    rows = rows_ref[...]
    gate_pre = dot_nn(rows, wg_ref[0])
    up_pre = dot_nn(rows, wu_ref[0])
    d_inner = dot_nt(dout_ref[...], wd_ref[0])
    sigmoid = jax.nn.sigmoid(gate_pre)
    silu = gate_pre * sigmoid
    inner = (silu * up_pre).astype(bf16)
    d_gate = (d_inner * up_pre * (sigmoid * (1.0 + gate_pre * (1.0 - sigmoid)))).astype(bf16)
    d_up = (d_inner * silu).astype(bf16)
    inner_ref[...] = inner
    dgate_ref[...] = d_gate
    dup_ref[...] = d_up
    acc_out[...] += dot_nn(inner, wd_ref[0])
    acc_row[...] += dot_nt(d_gate, wg_ref[0]) + dot_nt(d_up, wu_ref[0])

    @pl.when(step == steps - 1)
    def _():
        probs = probs_ref[...]
        gate = jnp.sum(jnp.where(lane == home, probs, 0.0), axis=1, keepdims=True)
        out = acc_out[...].astype(bf16).astype(f32)
        d_row_gate = jnp.sum(out * early_ref[:, slots, 0:width].astype(f32).reshape(-1, width), axis=1, keepdims=True)
        out_ref[:, 0:width] = (gate * out).astype(bf16)
        extra = jnp.zeros((out.shape[0], EXTRA), f32)
        for i, piece in enumerate(split_low(d_row_gate, 3)):
            extra = jnp.where(lane == home + 16 * i, piece.astype(f32), extra)
        out_ref[:, width : width + EXTRA] = extra.astype(bf16)
        term = d_row_gate * gate * (jnp.where(lane == home, 1.0, 0.0) - probs)
        high, rest = split_low(term, 2)
        drow_ref[...] = (acc_row[...] + dot_nt(high, router_ref[...]) + dot_nt(rest, router_ref[...])).astype(bf16)


def expert_pass(group, home, rows, early, router_pad, w_gate, w_up, w_down):
    count, width = rows.shape
    ff = w_gate.shape[2]
    tile = min(512, ff)
    full = pl.BlockSpec((count, width), lambda j: (0, 0))
    wide = pl.BlockSpec((count, width + EXTRA), lambda j: (0, 0))
    tall = pl.BlockSpec((1, width, tile), lambda j: (0, 0, j))
    piece = pl.BlockSpec((count, tile), lambda j: (0, j))
    return pl.pallas_call(
        functools.partial(expert_kernel, group),
        grid=(ff // tile,),
        in_specs=[
            pl.BlockSpec(memory_space=pltpu.SMEM),
            full,
            pl.BlockSpec(early.shape, lambda j: (0, 0, 0)),
            pl.BlockSpec((width, EXTRA), lambda j: (0, 0)),
            tall,
            tall,
            pl.BlockSpec((1, tile, width), lambda j: (0, j, 0)),
        ],
        out_specs=[wide, full, full, piece, piece, piece],
        out_shape=[
            jax.ShapeDtypeStruct((count, width + EXTRA), bf16),
            jax.ShapeDtypeStruct((count, width), bf16),
            jax.ShapeDtypeStruct((count, width), bf16),
        ]
        + [jax.ShapeDtypeStruct((count, ff), bf16)] * 3,
        scratch_shapes=[pltpu.VMEM((count, width), f32), pltpu.VMEM((count, width), f32), pltpu.VMEM((count, EXTRA), f32)],
        compiler_params=pltpu.CompilerParams(vmem_limit_bytes=48 * 2**20),
        cost_estimate=pl.CostEstimate(flops=12 * count * width * ff, bytes_accessed=6 * width * ff + 2 * count * (5 * width + 3 * ff), transcendentals=count * ff),
        name="expert_pass",
    )(home, rows, early, router_pad, w_gate, w_up, w_down)


def weight_kernel(count, *refs):
    rows, douts, inners, dgates, dups = (refs[i * count : (i + 1) * count] for i in range(5))
    gate_up_ref, down_ref = refs[5 * count : 5 * count + 2]
    turned = refs[5 * count + 2 :]

    @pl.when(pl.program_id(0) == 0)
    def _():
        for ref, scratch in zip(rows, turned):
            scratch[...] = ref[...].T

    gate_up_ref[0] = sum(dot_nn(t[...], d[...]) for t, d in zip(turned, dgates)).astype(bf16)
    gate_up_ref[1] = sum(dot_nn(t[...], d[...]) for t, d in zip(turned, dups)).astype(bf16)
    down_ref[...] = sum(dot_nn(i[...].T, d[...]) for i, d in zip(inners, douts)).astype(bf16)


def weight_gradients(rows, douts, inners, dgates, dups):
    count = len(rows)
    width, ff = rows[0].shape[1], inners[0].shape[1]
    tile = min(512, ff)
    total = sum(r.shape[0] for r in rows)
    full = [pl.BlockSpec(r.shape, lambda j: (0, 0)) for r in rows]
    piece = [pl.BlockSpec((r.shape[0], tile), lambda j: (0, j)) for r in rows]
    return pl.pallas_call(
        functools.partial(weight_kernel, count),
        grid=(ff // tile,),
        in_specs=full + full + piece * 3,
        out_specs=[pl.BlockSpec((2, width, tile), lambda j: (0, 0, j)), pl.BlockSpec((tile, width), lambda j: (j, 0))],
        out_shape=[jax.ShapeDtypeStruct((2, width, ff), bf16), jax.ShapeDtypeStruct((ff, width), bf16)],
        scratch_shapes=[pltpu.VMEM((width, r.shape[0]), bf16) for r in rows],
        compiler_params=pltpu.CompilerParams(vmem_limit_bytes=48 * 2**20),
        cost_estimate=pl.CostEstimate(flops=6 * total * width * ff, bytes_accessed=6 * width * ff + 2 * total * (2 * width + 3 * ff), transcendentals=0),
        name="weight_gradients",
    )(*rows, *douts, *inners, *dgates, *dups)


ANYWHERE = pl.BlockSpec(memory_space=pltpu.VMEM)
SCALARS = pl.BlockSpec(memory_space=pltpu.SMEM)


def inverse_rms(value):
    return lax.rsqrt(jnp.mean(value * value, axis=1, keepdims=True) + epsilon)


def after_attention_kernel(count, mixed_ref, x_ref, w_ref, gain_ref, *refs):
    turned, (hidden_ref, low_ref), sent = refs[:count], refs[count : count + 2], refs[count + 2 :]
    hidden = x_ref[...].astype(f32) + dot_nn(mixed_ref[...], w_ref[...])
    low = (hidden * inverse_rms(hidden) * gain_ref[...]).astype(bf16)
    hidden_ref[...] = hidden
    low_ref[...] = low
    for t, s in zip(turned, sent):
        s[...] = dot_nn(t[...], low).astype(bf16)


def after_attention(mixed, x, w_out, gain, turned):
    tok, width = x.shape
    rows = sum(t.shape[0] for t in turned)
    out = pl.pallas_call(
        functools.partial(after_attention_kernel, len(turned)),
        in_specs=[ANYWHERE] * (4 + len(turned)),
        out_specs=[ANYWHERE] * (2 + len(turned)),
        out_shape=[jax.ShapeDtypeStruct((tok, width), f32), jax.ShapeDtypeStruct((tok, width), bf16)]
        + [jax.ShapeDtypeStruct((t.shape[0], width), bf16) for t in turned],
        compiler_params=pltpu.CompilerParams(vmem_limit_bytes=40 * 2**20),
        cost_estimate=pl.CostEstimate(flops=2 * tok * width * (width + rows), bytes_accessed=2 * width * (6 * tok + 2 * rows), transcendentals=0),
        name="after_attention",
    )(mixed, x, w_out, gain, *turned)
    return out[0], out[1], out[2:]


def place(value, lane, at):
    return jnp.where(lane == at, value, 0.0)


def local_kernel(hidden_ref, low_ref, grad_ref, prev_ref, ids_ref, mix_ref, gain_ref, vec_ref, out_ref, dnormed_ref, probs_ref, dprobs_ref, small_ref):
    lane = lax.broadcasted_iota(jnp.int32, (1, EXTRA), 1)
    hidden = hidden_ref[...]
    normed = hidden * inverse_rms(hidden) * gain_ref[...]
    low = low_ref[...]
    grad = grad_ref[...].astype(f32)
    raw = dot_nn(low, mix_ref[...])
    logits = jnp.where(lane < ALL_EXPERTS, raw + prev_ref[...], NEG)
    unnormed = jnp.exp(logits - jnp.max(logits, axis=1, keepdims=True))
    probs = unnormed / jnp.sum(unnormed, axis=1, keepdims=True)
    named = (ids_ref[:, 0:1] == lane) | (ids_ref[:, 1:2] == lane)
    gates = jnp.where(named, probs, 0.0)
    copy_gate = gates[:, FFN_EXPERTS + 1 : FFN_EXPERTS + 2]
    dots = jnp.sum(grad * normed, axis=1, keepdims=True)
    out = hidden
    weight = copy_gate
    d_probs = place(dots, lane, FFN_EXPERTS + 1)
    logit_grads = jnp.zeros_like(probs)
    mixing_terms = jnp.zeros_like(probs)
    vec_terms = jnp.zeros_like(probs)
    for c in range(2):
        vec = vec_ref[c : c + 1, :]
        gate = gates[:, FFN_EXPERTS + 2 + c : FFN_EXPERTS + 3 + c]
        at = 16 + 2 * c
        a0 = jax.nn.sigmoid(raw[:, at : at + 1] - raw[:, at + 1 : at + 2])
        a1 = jax.nn.sigmoid(raw[:, at + 1 : at + 2] - raw[:, at : at + 1])
        vec_dots = jnp.sum(grad * vec, axis=1, keepdims=True)
        weight = weight + gate * a0
        out = out + (gate * a1) * vec
        d_probs = d_probs + place(a0 * dots + a1 * vec_dots, lane, FFN_EXPERTS + 2 + c)
        d0, d1 = gate * dots, gate * vec_dots
        mean = a0 * d0 + a1 * d1
        d0, d1 = a0 * (d0 - mean), a1 * (d1 - mean)
        logit_grads = logit_grads + place(d0, lane, at) + place(d1, lane, at + 1)
        mixing_terms = mixing_terms + place(d0, lane, 2 * c) + place(d1, lane, 2 * c + 1)
        vec_terms = vec_terms + place(gate * a1, lane, 4 + c)
    d_probs = jnp.where(named, d_probs, 0.0)
    logit_grads = logit_grads + probs * (d_probs - jnp.sum(probs * d_probs, axis=1, keepdims=True))
    high, rest = split_low(logit_grads, 2)
    out_ref[...] = out + weight * normed
    dnormed_ref[...] = weight * grad + dot_nt(high, mix_ref[...]) + dot_nt(rest, mix_ref[...])
    probs_ref[...] = probs
    dprobs_ref[...] = d_probs
    sums = None
    for terms, rows in ((mixing_terms, low), (vec_terms, grad_ref[...])):
        for piece in split_low(terms.T, 2):
            part = dot_nn(piece, rows)
            sums = part if sums is None else sums + part
    small_ref[...] = sums[0:SMALL, :]


def local_part(hidden, low, grad, prev, ids, mix, gain, vec):
    tok, width = hidden.shape
    shapes = [(tok, width), (tok, width), (tok, EXTRA), (tok, EXTRA), (SMALL, width)]
    return pl.pallas_call(
        local_kernel,
        in_specs=[ANYWHERE] * 8,
        out_specs=[ANYWHERE] * 5,
        out_shape=[jax.ShapeDtypeStruct(s, f32) for s in shapes],
        compiler_params=pltpu.CompilerParams(vmem_limit_bytes=48 * 2**20),
        cost_estimate=pl.CostEstimate(flops=14 * tok * width * EXTRA, bytes_accessed=16 * tok * width, transcendentals=tok * EXTRA),
        name="local_part",
    )(hidden, low, grad, prev, ids, mix, gain, vec)


def combine_kernel(count, parts, *refs):
    chosen, got = refs[:count], refs[count : count * (1 + parts)]
    local_ref, hidden_ref, gain_ref, grad_ref, w_ref, dhidden_ref, dlow_ref, dmixed_ref, small_ref = refs[count * (1 + parts) :]
    d_normed = local_ref[...]
    for g in range(count):
        for r in range(parts):
            d_normed = d_normed + dot_nn(chosen[g][...], got[g * parts + r][...])
    hidden = hidden_ref[...]
    inverse = inverse_rms(hidden)
    scaled = d_normed * gain_ref[...]
    mean = jnp.mean(scaled * hidden, axis=1, keepdims=True)
    d_hidden = grad_ref[...].astype(f32) + inverse * scaled - hidden * (inverse * inverse * inverse * mean)
    low = d_hidden.astype(bf16)
    dhidden_ref[...] = d_hidden
    dlow_ref[...] = low
    dmixed_ref[...] = dot_nt(low, w_ref[...]).astype(bf16)
    gain = jnp.sum(d_normed * hidden * inverse, axis=0, keepdims=True)
    row = lax.broadcasted_iota(jnp.int32, (SMALL, 1), 0)
    small_ref[...] = jnp.where(row == 0, gain, 0.0)


def combine(chosen, got, local, hidden, gain, grad, w_out):
    tok, width = hidden.shape
    rows = sum(c.shape[1] for c in chosen)
    arrays = [a for group in got for a in group]
    return pl.pallas_call(
        functools.partial(combine_kernel, len(chosen), len(got[0])),
        in_specs=[ANYWHERE] * (len(chosen) + len(arrays) + 5),
        out_specs=[ANYWHERE] * 4,
        out_shape=[jax.ShapeDtypeStruct((tok, width), f32)] + [jax.ShapeDtypeStruct((tok, width), bf16)] * 2 + [jax.ShapeDtypeStruct((SMALL, width), f32)],
        compiler_params=pltpu.CompilerParams(vmem_limit_bytes=48 * 2**20),
        cost_estimate=pl.CostEstimate(flops=2 * tok * width * (rows + width), bytes_accessed=2 * width * (9 * tok + 2 * rows), transcendentals=0),
        name="combine_gradients",
    )(*chosen, *arrays, local, hidden, gain, grad, w_out)


def flat_rows(value):
    if value.shape[1] % 16:
        return value.astype(f32).reshape(-1, value.shape[2]).astype(bf16)
    return value.reshape(-1, value.shape[2])


def finish_kernel(groups, parts, *refs):
    chosen, got = refs[: len(groups)], refs[len(groups) : len(groups) + parts]
    local_ref, probs_ref, dprobs_ref, low_ref, out_ref, dlogits_ref, small_ref = refs[len(groups) + parts :]
    width = local_ref.shape[1]
    lane = lax.broadcasted_iota(jnp.int32, (1, EXTRA), 1)
    picked = None
    for c, (at, size) in zip(chosen, groups):
        for r in range(parts):
            part = dot_nn(c[...], flat_rows(got[r][:, at : at + size, :]))
            picked = part if picked is None else picked + part
    out_ref[...] = (local_ref[...] + picked[:, 0:width]).astype(bf16)
    extra = picked[:, width : width + EXTRA]
    extra = extra + pltpu.roll(extra, EXTRA - 16, 1) + pltpu.roll(extra, EXTRA - 32, 1)
    d_probs = dprobs_ref[...] + jnp.where(lane < ALL_EXPERTS, extra, 0.0)
    probs = probs_ref[...]
    d_logits = probs * (d_probs - jnp.sum(probs * d_probs, axis=1, keepdims=True))
    dlogits_ref[...] = d_logits
    high, rest = split_low(d_logits.T, 2)
    sums = dot_nn(high, low_ref[...]) + dot_nn(rest, low_ref[...])
    small_ref[...] = sums[0 : 2 * SMALL, :]


def finish(chosen, got, groups, local, probs, d_probs, low):
    tok, width = local.shape
    return pl.pallas_call(
        functools.partial(finish_kernel, groups, len(got)),
        in_specs=[ANYWHERE] * (len(chosen) + len(got) + 4),
        out_specs=[ANYWHERE] * 3,
        out_shape=[jax.ShapeDtypeStruct((tok, width), bf16), jax.ShapeDtypeStruct((tok, EXTRA), f32), jax.ShapeDtypeStruct((2 * SMALL, width), f32)],
        compiler_params=pltpu.CompilerParams(vmem_limit_bytes=48 * 2**20),
        cost_estimate=pl.CostEstimate(flops=2 * tok * 1152 * (width + EXTRA), bytes_accessed=16 * tok * width, transcendentals=0),
        name="finish_outputs",
    )(*chosen, *got, local, probs, d_probs, low)


def xor_pairs(size, mask):
    return [(i, i ^ mask) for i in range(size)]


def pack_kernel(core_ref, mixed_ref, dlow_ref, act_ref, far_ref, dq_ref, dk_ref, dv_ref, dkf_ref, dvf_ref, local_ref, gain_ref, router_ref, mine_ref, theirs_ref, mixed_t, act_t, far_t):
    core = core_ref[0]
    width = mixed_ref.shape[1]
    half, piece = width // 2, width // 8

    @pl.when(pl.program_id(0) == 0)
    def _():
        mixed_t[...] = mixed_ref[...].T
        act_t[...] = act_ref[...].T
        far_t[...] = far_ref[...].T

    for out_ref, which in ((theirs_ref, 1 - core), (mine_ref, core)):
        rows = pl.ds(pl.multiple_of(which * half, half), half)
        parts = [
            dot_nn(mixed_t[rows, :], dlow_ref[...]),
            dot_nn(act_t[rows, :], dq_ref[...]),
            dot_nn(act_t[rows, :], dk_ref[...]) + dot_nn(far_t[rows, :], dkf_ref[...]),
            dot_nn(act_t[rows, :], dv_ref[...]) + dot_nn(far_t[rows, :], dvf_ref[...]),
        ]
        for j, part in enumerate(parts):
            for k in range(4):
                out_ref[j, k, 0:piece, :] = part[k * piece : (k + 1) * piece].astype(bf16)
                small = jnp.zeros((SMALL, part.shape[1]), f32)
                if j == 0:
                    small = (local_ref[...], gain_ref[...], router_ref[0:SMALL, :], router_ref[SMALL : 2 * SMALL, :])[k]
                    small = jnp.where(which == 0, small, 0.0)
                out_ref[j, k, piece : piece + SMALL, :] = small.astype(bf16)


def pack(core, mixed, dlow, act, far, dq, dk, dv, dkf, dvf, local, gain, router):
    tok, width = mixed.shape
    remote = far.shape[0]
    tile = 256
    whole = lambda n: pl.BlockSpec((n, width), lambda i: (0, 0))
    column = lambda n: pl.BlockSpec((n, tile), lambda i: (0, i))
    out = pl.BlockSpec((4, 4, width // 8 + SMALL, tile), lambda i: (0, 0, 0, i))
    return pl.pallas_call(
        pack_kernel,
        grid=(width // tile,),
        in_specs=[
            pl.BlockSpec(memory_space=pltpu.SMEM), whole(tok), column(tok), whole(tok), whole(remote),
            column(tok), column(tok), column(tok), column(remote), column(remote),
            column(SMALL), column(SMALL), column(2 * SMALL),
        ],
        out_specs=[out, out],
        out_shape=[jax.ShapeDtypeStruct((4, 4, width // 8 + SMALL, width), bf16)] * 2,
        scratch_shapes=[pltpu.VMEM((width, tok), bf16), pltpu.VMEM((width, tok), bf16), pltpu.VMEM((width, remote), bf16)],
        compiler_params=pltpu.CompilerParams(vmem_limit_bytes=48 * 2**20),
        cost_estimate=pl.CostEstimate(flops=2 * width * width * (4 * tok + 2 * remote), bytes_accessed=2 * width * (6 * tok + 3 * remote + 4 * width), transcendentals=0),
        name="pack_gradients",
    )(core, mixed, dlow, act, far, dq, dk, dv, dkf, dvf, local, gain, router)


def sum_kernel(terms, index_ref, *refs):
    count = (len(refs)) // (terms + 1)
    for k in range(count):
        total = None
        for t in range(terms):
            value = refs[t * count + k][...].astype(f32)
            total = value if total is None else total + value
        refs[terms * count + k][...] = total.astype(bf16)


def sum_pieces(index, arrays):
    n, shape = arrays[0].shape[0], arrays[0].shape[1:]
    zeros = (0,) * len(shape)
    views = [pl.BlockSpec((1,) + shape, functools.partial(lambda k, i, s: (s[0] ^ k,) + zeros, k)) for k in range(n)]
    return pl.pallas_call(
        functools.partial(sum_kernel, len(arrays)),
        grid_spec=pltpu.PrefetchScalarGridSpec(
            num_scalar_prefetch=1,
            grid=(1,),
            in_specs=views * len(arrays),
            out_specs=[pl.BlockSpec((1,) + shape, lambda i, s: (0,) + zeros)] * n,
        ),
        out_shape=[jax.ShapeDtypeStruct((1,) + shape, bf16)] * n,
        compiler_params=pltpu.CompilerParams(vmem_limit_bytes=48 * 2**20),
        cost_estimate=pl.CostEstimate(flops=0, bytes_accessed=2 * n * math.prod(shape) * (len(arrays) + 1), transcendentals=0),
        name="sum_pieces",
    )(index, *[a for a in arrays for _ in range(n)])


def unpack_kernel(index_ref, own_ref, other_ref, out_ref):
    piece = out_ref.shape[0] // 8
    for c in range(2):
        mine = index_ref[0] == c
        for k in range(4):
            at = k ^ index_ref[2]
            value = jnp.where(mine, own_ref[0, at, 0:piece, :].astype(f32), other_ref[0, at, 0:piece, :].astype(f32))
            out_ref[(c * 4 + k) * piece : (c * 4 + k + 1) * piece, :] = value


def unpack(index, own, other, first, count):
    width = own.shape[3]
    source = pl.BlockSpec((1,) + own.shape[1:], lambda j, s: ((j + first) ^ s[1], 0, 0, 0))
    return pl.pallas_call(
        unpack_kernel,
        grid_spec=pltpu.PrefetchScalarGridSpec(
            num_scalar_prefetch=1,
            grid=(count,),
            in_specs=[source, source],
            out_specs=pl.BlockSpec((width, width), lambda j, s: (0, j)),
        ),
        out_shape=jax.ShapeDtypeStruct((width, count * width), f32),
        compiler_params=pltpu.CompilerParams(vmem_limit_bytes=32 * 2**20),
        name="unpack_sums",
    )(index, own, other)


def sum_everywhere(mine, theirs):
    me_c, me_e = lax.axis_index("ctx"), lax.axis_index("exp")
    place = lambda v: v.reshape(1)
    got = lax.ppermute(theirs, "exp", xor_pairs(8, 1))
    parts = sum_pieces(place(me_c), [mine, got])
    parts = [parts[0]] + [lax.ppermute(parts[k], "ctx", xor_pairs(4, k)) for k in range(1, 4)]
    parts = sum_pieces(place(me_e >> 1), [p[0] for p in parts])
    parts = [parts[0]] + [lax.ppermute(parts[k], "exp", xor_pairs(8, 2 * k)) for k in range(1, 4)]
    [piece] = sum_pieces(place(me_e * 0), parts)
    column = jnp.concatenate([piece] + [lax.ppermute(piece, "exp", xor_pairs(8, 2 * k)) for k in range(1, 4)], axis=0)[None]
    own = jnp.concatenate([column] + [lax.ppermute(column, "ctx", xor_pairs(4, k)) for k in range(1, 4)], axis=0)
    other = lax.ppermute(own, "exp", xor_pairs(8, 1))
    return own, other

P = jax.sharding.PartitionSpec


def rms_inverse(tensor):
    return lax.rsqrt(jnp.mean(tensor * tensor, axis=-1, keepdims=True) + epsilon)


def body(inputs, prev_logits, routes, attn_gain, w_qkv, w_out, moe_gain, router, const_gate, const_vec, w_gate, w_up, w_down, out_grad):
    n_ctx, n_exp = lax.axis_size("ctx"), lax.axis_size("exp")
    me_c, me_e = lax.axis_index("ctx"), lax.axis_index("exp")
    tok, width = inputs.shape[1], inputs.shape[2]
    plen = tok - CONT_LEN
    split = n_exp // FFN_EXPERTS
    capacity = max(4, tok // 64 * 12)
    first = -(-capacity // 32) * 16
    groups = ((0, first), (first, capacity - first))
    home = (me_e // split).reshape(1)

    def deal(value):
        value = jnp.repeat(value, split, axis=0) if split > 1 else value
        return lax.all_to_all(value, "exp", 0, 0, tiled=True)

    def give_back(value):
        value = lax.all_to_all(value, "exp", 0, 0, tiled=True)
        return [value[r::split] if split > 1 else value for r in range(split)]

    x_low = inputs[0]
    far_rows = jnp.concatenate([lax.ppermute(x_low[:plen], "ctx", xor_pairs(n_ctx, k)) for k in range(1, n_ctx)], axis=0)
    flags = jnp.where((me_c ^ jnp.arange(1, n_ctx)) < me_c, 0.0, NEG).astype(f32)

    upstream_low = out_grad[0]
    prev = jnp.pad(prev_logits[0], ((0, 0), (0, EXTRA - ALL_EXPERTS)))
    mix = jnp.concatenate([router, jnp.zeros((width, 4), bf16), const_gate[0], const_gate[1], jnp.zeros((width, EXTRA - 20), bf16)], axis=1)
    router_pad = jnp.pad(router, ((0, 0), (0, EXTRA - ALL_EXPERTS)))
    turned, chosen, early_sent = route_plan(home, routes[0].T, upstream_low, prev, groups)

    tokens_in = x_low.astype(f32)
    inverse_attn = rms_inverse(tokens_in)
    act_low = (tokens_in * inverse_attn * attn_gain).astype(bf16)
    projected = dot_nn(act_low, w_qkv).astype(bf16)
    early = deal(early_sent)
    far_in = far_rows.astype(f32)
    act_far = (far_in * rms_inverse(far_in) * attn_gain).astype(bf16)
    kv_far = dot_nn(act_far, w_qkv[:, width:]).astype(bf16)

    mixed_low, lse = attention_forward(flags, projected, kv_far, plen)
    mixed_low, early = lax.optimization_barrier((mixed_low, early))
    hidden, moe_low, sent = after_attention(mixed_low, x_low, w_out, moe_gain[None], turned)
    got = [deal(part.reshape(FFN_EXPERTS, -1, width)) for part in sent]

    local_out, d_normed_local, probs, d_probs, small_local = local_part(hidden, moe_low, upstream_low, prev, routes[0], mix, moe_gain[None], const_vec)
    got[0], local_out, d_normed_local = lax.optimization_barrier((got[0], local_out, d_normed_local))

    got = [part.reshape(-1, width) for part in got]
    passes = [expert_pass(group, home, r, early, router_pad, w_gate, w_up, w_down) for group, r in zip(groups, got)]
    d_got = [give_back(p[1].reshape(n_exp, -1, width)) for p in passes]
    gate_up_low, down_low = weight_gradients(got, [p[2] for p in passes], [p[3] for p in passes], [p[4] for p in passes], [p[5] for p in passes])
    outs = jnp.concatenate([p[0].reshape(n_exp, -1, width + EXTRA) for p in passes], axis=1)
    d_got, gate_up_low, down_low, outs = lax.optimization_barrier((d_got, gate_up_low, down_low, outs))
    out_got = give_back(outs)

    d_got = [[part.reshape(-1, width) for part in group] for group in d_got]
    d_hidden, d_attn_low, d_mixed, small_gain = combine(chosen, d_got, d_normed_local, hidden, moe_gain[None], upstream_low, w_out)

    sum_gate_up = lax.psum_scatter(gate_up_low, "ctx", scatter_dimension=1, tiled=True).astype(f32)
    sum_down = lax.psum_scatter(down_low, "ctx", scatter_dimension=0, tiled=True).astype(f32)

    dq, dk, dv, dk_far, dv_far = attention_backward(flags, projected, kv_far, mixed_low, d_mixed, lse, plen)
    dq, out_got = lax.optimization_barrier((dq, out_got))
    mixed_out, d_logits, small_router = finish(chosen, out_got, groups, local_out, probs, d_probs, moe_low)

    wq, wk, wv = (w_qkv[:, i * width : (i + 1) * width] for i in range(3))
    d_act_far = (dot_nt(dk_far, wk) + dot_nt(dv_far, wv)).astype(bf16).reshape(n_ctx - 1, plen, width)
    far_back = [lax.ppermute(d_act_far[k - 1], "ctx", xor_pairs(n_ctx, k)) for k in range(1, n_ctx)]
    d_act = dot_nt(dq, wq) + dot_nt(dk, wk) + dot_nt(dv, wv)
    d_act = jnp.concatenate([d_act[:plen] + sum(part.astype(f32) for part in far_back), d_act[plen:]], axis=0)
    scaled = d_act * attn_gain
    d_inputs = d_hidden + inverse_attn * scaled - tokens_in * inverse_attn**3 * jnp.mean(scaled * tokens_in, axis=-1, keepdims=True)

    if n_ctx == 4 and n_exp == 8:
        core, z = me_e & 1, me_e >> 1
        mine, theirs = pack(core.reshape(1), mixed_low, d_attn_low, act_low, act_far, dq, dk, dv, dk_far, dv_far, small_local, small_gain, small_router)
        own, other = sum_everywhere(mine, theirs)
        index = jnp.stack([core, me_c, z])
        out_sum = unpack(index, own, other, 0, 1)
        qkv_sum = unpack(index, own, other, 1, 3)
        small = jnp.where(core == 0, own[:, :, -SMALL:], other[:, :, -SMALL:])
        small = [lax.dynamic_slice(small, (me_c, k ^ z, 0, 0), (1, 1, SMALL, width)).reshape(SMALL, width).astype(f32) for k in range(4)]
    else:
        d_w_k = dot_tn(act_low, dk) + dot_tn(act_far, dk_far)
        d_w_v = dot_tn(act_low, dv) + dot_tn(act_far, dv_far)
        parts = [dot_tn(mixed_low, d_attn_low), dot_tn(act_low, dq), d_w_k, d_w_v, small_local, small_gain, small_router]
        out_sum, q_sum, k_sum, v_sum, *small = [p.astype(f32) for p in lax.psum([p.astype(bf16) for p in parts], ("ctx", "exp"))]
        qkv_sum = jnp.concatenate([q_sum, k_sum, v_sum], axis=1)
        small = small[:2] + [small[2][:SMALL], small[2][SMALL:]]
    d_attn_gain = jnp.sum(qkv_sum * w_qkv.astype(f32), axis=1) / attn_gain
    d_const_gate = jnp.stack([small[0][0:2].T, small[0][2:4].T])
    return (
        mixed_out[None],
        d_inputs[None],
        d_logits[None, :, :ALL_EXPERTS],
        d_attn_gain,
        qkv_sum,
        out_sum,
        small[1][0],
        jnp.concatenate([small[2], small[3][: ALL_EXPERTS - SMALL]], axis=0).T,
        d_const_gate,
        small[0][4:6],
        sum_gate_up[0][None],
        sum_gate_up[1][None],
        sum_down[None],
    )


def solution(mesh):
    rows = P("ctx", "exp", None)
    expert = P("exp", None, None)
    summed = P("exp", "ctx", None)
    return jax.shard_map(
        body,
        mesh=mesh,
        in_specs=(rows, rows, rows, P(), P(), P(), P(), P(), P(), P(), expert, expert, expert, rows),
        out_specs=(rows, rows, rows, P(), P(), P(), P(), P(), P(), P(), summed, summed, summed),
        check_vma=False,
    )
```

```python
import functools, math
import jax, jax.numpy as jnp
from jax import lax
from jax.experimental import pallas as pl
from jax.experimental.pallas import tpu as pltpu

HEADS = 12
HEAD_DIM = 64
CONT_LEN = 512
LOG2E = 1.4426950408889634
SCALE = HEAD_DIM ** -0.5
bf16 = jnp.bfloat16
f32 = jnp.float32
NEG = -1e30


def dot_nt(a, b):
    return lax.dot_general(a, b, (((1,), (1,)), ((), ())), preferred_element_type=f32)


def dot_nn(a, b):
    return jnp.dot(a, b, preferred_element_type=f32)


def query_tiles(tok, plen):
    tiles = [(0, plen, True)]
    step = 256
    for start in range(plen, tok, step):
        tiles.append((start, step, False))
    return tiles


def attention_forward_kernel(plen, flags_ref, q_ref, k_ref, v_ref, kr_ref, vr_ref, o_ref, lse_ref):
    tok = q_ref.shape[0]
    remote = kr_ref.shape[0]
    lane = lax.broadcasted_iota(jnp.int32, (1, 128), 1)
    low_half = lane < HEAD_DIM
    c = SCALE * LOG2E
    one = jnp.ones((), bf16)
    zero = jnp.zeros((), bf16)
    for start, size, is_prompt in query_tiles(tok, plen):
        accs, peaks = [], []
        for head in range(2):
            mine = low_half if head == 0 else ~low_half
            qh = jnp.where(mine, q_ref[start : start + size, :], zero)
            pieces = []
            row = lax.broadcasted_iota(jnp.int32, (size, size), 0)
            col = lax.broadcasted_iota(jnp.int32, (size, size), 1)
            diag = dot_nt(qh, k_ref[start : start + size, :])
            pieces.append((jnp.where(col <= row, diag, NEG), v_ref, start, size))
            if is_prompt:
                for j in range(remote // plen):
                    s = dot_nt(qh, kr_ref[j * plen : (j + 1) * plen, :])
                    pieces.append((s + flags_ref[j], vr_ref, j * plen, plen))
            else:
                s = dot_nt(qh, k_ref[0:start, :])
                pieces.append((s, v_ref, 0, start))
                s = dot_nt(qh, kr_ref[...])
                pieces.append((s, vr_ref, 0, remote))
            peak = None
            for s, _, _, _ in pieces:
                m = jnp.max(s, axis=1, keepdims=True)
                peak = m if peak is None else jnp.maximum(peak, m)
            shift = peak * c
            acc = None
            for s, ref, at, n in pieces:
                p = jnp.exp2(s * c - shift).astype(bf16)
                vh = jnp.where(mine, ref[at : at + n, :], one)
                part = dot_nn(p, vh)
                acc = part if acc is None else acc + part
            accs.append(acc)
            peaks.append(shift)
        num = jnp.where(low_half, accs[0], accs[1])
        den = pltpu.roll(jnp.where(low_half, accs[1], accs[0]), HEAD_DIM, 1)
        o_ref[start : start + size, :] = (num / den).astype(bf16)
        logs = jnp.where(low_half, peaks[0], peaks[1]) + jnp.log2(den)
        turned = logs.T
        lse_ref[0, 0:8, start : start + size] = turned[0:8, :]
        lse_ref[0, 8:16, start : start + size] = turned[HEAD_DIM : HEAD_DIM + 8, :]


def attention_forward(flags, proj, kv_rem, plen):
    tok, width = proj.shape[0], proj.shape[1] // 3
    remote = kv_rem.shape[0]
    pairs = width // 128
    return pl.pallas_call(
        functools.partial(attention_forward_kernel, plen),
        grid=(pairs,),
        in_specs=[
            pl.BlockSpec(memory_space=pltpu.SMEM),
            pl.BlockSpec((tok, 128), lambda i: (0, i)),
            pl.BlockSpec((tok, 128), lambda i: (0, pairs + i)),
            pl.BlockSpec((tok, 128), lambda i: (0, 2 * pairs + i)),
            pl.BlockSpec((remote, 128), lambda i: (0, i)),
            pl.BlockSpec((remote, 128), lambda i: (0, pairs + i)),
        ],
        out_specs=[
            pl.BlockSpec((tok, 128), lambda i: (0, i)),
            pl.BlockSpec((1, 16, tok), lambda i: (i, 0, 0)),
        ],
        out_shape=[
            jax.ShapeDtypeStruct((tok, width), bf16),
            jax.ShapeDtypeStruct((pairs, 16, tok), f32),
        ],
        compiler_params=pltpu.CompilerParams(vmem_limit_bytes=60 * 2**20),
        cost_estimate=pl.CostEstimate(flops=4 * tok * (tok + remote) * width, bytes_accessed=2 * (tok * 4 + remote * 2) * width, transcendentals=tok * (tok + remote) * HEADS),
        name="attention_forward",
    )(flags, proj, proj, proj, kv_rem, kv_rem)


def attention_backward_kernel(plen, flags_ref, q_ref, k_ref, v_ref, kr_ref, vr_ref, o_ref, do_ref, lse_ref,
                              dq_ref, dk_ref, dv_ref, dkr_ref, dvr_ref, kt, krt, dka, dva, dkra, dvra):
    tok = q_ref.shape[0]
    remote = kr_ref.shape[0]
    lane = lax.broadcasted_iota(jnp.int32, (1, 128), 1)
    low_half = lane < HEAD_DIM
    c = SCALE * LOG2E
    zero = jnp.zeros((), bf16)
    kt[...] = k_ref[...].T
    krt[...] = kr_ref[...].T
    dka[...] = jnp.zeros_like(dka)
    dva[...] = jnp.zeros_like(dva)
    dkra[...] = jnp.zeros_like(dkra)
    dvra[...] = jnp.zeros_like(dvra)
    pick = lax.broadcasted_iota(jnp.int32, (16, 128), 0) // 8 == lax.broadcasted_iota(jnp.int32, (16, 128), 1) // HEAD_DIM
    pick = jnp.where(pick, 1.0, 0.0).astype(bf16)
    for start, size, is_prompt in query_tiles(tok, plen):
        rows = slice(start, start + size)
        product = do_ref[rows, :].astype(f32) * o_ref[rows, :].astype(f32)
        high = product.astype(bf16)
        rest = (product - high.astype(f32)).astype(bf16)
        delta = dot_nt(pick, high) + dot_nt(pick, rest)
        dqt = []
        for head in range(2):
            mine = low_half if head == 0 else ~low_half
            qh = jnp.where(mine, q_ref[rows, :], zero)
            doh = jnp.where(mine, do_ref[rows, :], zero)
            lse_row = lse_ref[0, 8 * head : 8 * head + 1, rows]
            delta_row = delta[8 * head : 8 * head + 1, :]
            segments = [(k_ref, v_ref, kt, dka, dva, start, size, "diag")]
            if is_prompt:
                for j in range(remote // plen):
                    segments.append((kr_ref, vr_ref, krt, dkra, dvra, j * plen, plen, j))
            else:
                segments.append((k_ref, v_ref, kt, dka, dva, 0, start, None))
                segments.append((kr_ref, vr_ref, krt, dkra, dvra, 0, remote, None))
            total = None
            for kk, vv, tt, dk_acc, dv_acc, at, n, mode in segments:
                keys = slice(at, at + n)
                st = dot_nt(kk[keys, :], qh) * c - lse_row
                if mode == "diag":
                    key = lax.broadcasted_iota(jnp.int32, (n, size), 0)
                    query = lax.broadcasted_iota(jnp.int32, (n, size), 1)
                    st = jnp.where(key <= query, st, NEG)
                elif mode is not None:
                    st = st + flags_ref[mode]
                pt = jnp.exp2(st)
                dpt = dot_nt(vv[keys, :], doh)
                dst = (pt * (dpt - delta_row)).astype(bf16)
                dv_acc[keys, :] += dot_nn(pt.astype(bf16), doh)
                dk_acc[keys, :] += dot_nn(dst, qh)
                part = dot_nn(tt[head * HEAD_DIM : (head + 1) * HEAD_DIM, keys], dst)
                total = part if total is None else total + part
            dqt.append(total)
        dq_ref[rows, :] = (jnp.concatenate(dqt, axis=0).T * SCALE).astype(bf16)
    dk_ref[...] = (dka[...] * SCALE).astype(bf16)
    dv_ref[...] = dva[...].astype(bf16)
    dkr_ref[...] = (dkra[...] * SCALE).astype(bf16)
    dvr_ref[...] = dvra[...].astype(bf16)


def attention_backward(flags, proj, kv_rem, mixed, d_mixed, lse, plen, begin, count):
    tok, width = mixed.shape
    remote = kv_rem.shape[0]
    pairs = width // 128
    own = lambda shift: pl.BlockSpec((tok, 128), lambda i: (0, shift + i))
    far = lambda shift: pl.BlockSpec((remote, 128), lambda i: (0, shift + i))
    return pl.pallas_call(
        functools.partial(attention_backward_kernel, plen),
        grid=(count,),
        in_specs=[
            pl.BlockSpec(memory_space=pltpu.SMEM),
            own(begin),
            own(pairs + begin),
            own(2 * pairs + begin),
            far(begin),
            far(pairs + begin),
            own(begin),
            own(begin),
            pl.BlockSpec((1, 16, tok), lambda i: (begin + i, 0, 0)),
        ],
        out_specs=[own(0), own(0), own(0), far(0), far(0)],
        out_shape=[jax.ShapeDtypeStruct((tok, count * 128), bf16)] * 3 + [jax.ShapeDtypeStruct((remote, count * 128), bf16)] * 2,
        scratch_shapes=[
            pltpu.VMEM((128, tok), bf16),
            pltpu.VMEM((128, remote), bf16),
            pltpu.VMEM((tok, 128), f32),
            pltpu.VMEM((tok, 128), f32),
            pltpu.VMEM((remote, 128), f32),
            pltpu.VMEM((remote, 128), f32),
        ],
        compiler_params=pltpu.CompilerParams(vmem_limit_bytes=60 * 2**20),
        cost_estimate=pl.CostEstimate(flops=10 * tok * (tok + remote) * count * 128, bytes_accessed=2 * (tok * 8 + remote * 4) * count * 128, transcendentals=tok * (tok + remote) * 2 * count),
        name="attention_backward",
    )(flags, proj, proj, proj, kv_rem, kv_rem, mixed, d_mixed, lse)


FFN_EXPERTS = 8
ALL_EXPERTS = 12
EXTRA = 128
SMALL = 8
epsilon = 1e-06


def dot_tn(a, b):
    return lax.dot_general(a, b, (((0,), (0,)), ((), ())), preferred_element_type=f32)


def split_low(value, parts):
    pieces = []
    for _ in range(parts):
        piece = value.astype(bf16)
        pieces.append(piece)
        value = value - piece.astype(f32)
    return pieces


def route_kernel(groups, home_ref, ids_ref, grad_ref, prev_ref, *out_refs):
    tok, width = grad_ref.shape
    count = len(groups)
    turned_refs, chosen_refs, early_ref = out_refs[:count], out_refs[count : 2 * count], out_refs[2 * count]
    expert = lax.broadcasted_iota(jnp.int32, (16, tok), 0)
    names = [ids_ref[k : k + 1, :] == expert for k in range(2)]
    both = jnp.where(names[0] | names[1], 1.0, 0.0).astype(bf16)
    earlier = lax.broadcasted_iota(jnp.int32, (tok, tok), 0) < lax.broadcasted_iota(jnp.int32, (tok, tok), 1)
    before = dot_nn(both, jnp.where(earlier, 1.0, 0.0).astype(bf16))
    pieces = [piece.astype(f32) for piece in split_low(prev_ref[...], 3)]
    extra = (pieces[0] + pltpu.roll(pieces[1], 16, 1) + pltpu.roll(pieces[2], 32, 1)).astype(bf16)
    slot = [jnp.sum(jnp.where(n, before, 0.0), axis=0, keepdims=True).astype(jnp.int32) for n in names]
    for (first, size), turned_ref, chosen_ref in zip(groups, turned_refs, chosen_refs):
        spots = lax.broadcasted_iota(jnp.int32, (FFN_EXPERTS * size, tok), 0)
        hit = None
        for k in range(2):
            ids = ids_ref[k : k + 1, :]
            inside = (ids < FFN_EXPERTS) & (slot[k] >= first) & (slot[k] < first + size)
            place = jnp.where(inside, ids * size + slot[k] - first, -1)
            hit = spots == place if hit is None else hit | (spots == place)
        turned = jnp.where(hit, 1.0, 0.0).astype(bf16)
        turned_ref[...] = turned
        chosen_ref[...] = turned.T
        grads = dot_nn(turned, grad_ref[...]).astype(bf16)
        extras = dot_nn(turned, extra).astype(bf16)
        for e in range(FFN_EXPERTS):
            early_ref[e, first : first + size, 0:width] = grads[e * size : (e + 1) * size]
            early_ref[e, first : first + size, width : width + EXTRA] = extras[e * size : (e + 1) * size]


def route_plan(home, ids, grad, prev, groups):
    tok, width = grad.shape
    counts = [FFN_EXPERTS * size for _, size in groups]
    whole = pl.BlockSpec(memory_space=pltpu.VMEM)
    out = pl.pallas_call(
        functools.partial(route_kernel, groups),
        in_specs=[pl.BlockSpec(memory_space=pltpu.SMEM), whole, whole, whole],
        out_specs=[whole] * (2 * len(groups) + 1),
        out_shape=[jax.ShapeDtypeStruct((n, tok), bf16) for n in counts]
        + [jax.ShapeDtypeStruct((tok, n), bf16) for n in counts]
        + [jax.ShapeDtypeStruct((FFN_EXPERTS, sum(counts) // FFN_EXPERTS, width + EXTRA), bf16)],
        compiler_params=pltpu.CompilerParams(vmem_limit_bytes=60 * 2**20),
        cost_estimate=pl.CostEstimate(flops=2 * sum(counts) * tok * (width + EXTRA), bytes_accessed=4 * sum(counts) * width, transcendentals=0),
        name="route_plan",
    )(home, ids, grad, prev)
    return out[: len(groups)], out[len(groups) : -1], out[-1]


def expert_kernel(group, home_ref, rows_ref, early_ref, router_ref, wg_ref, wu_ref, wd_ref,
                  out_ref, drow_ref, dout_ref, inner_ref, dgate_ref, dup_ref, acc_out, acc_row, probs_ref):
    width = rows_ref.shape[1]
    step, steps = pl.program_id(0), pl.num_programs(0)
    home = home_ref[0]
    lane = lax.broadcasted_iota(jnp.int32, (1, EXTRA), 1)
    slots = slice(group[0], group[0] + group[1])

    @pl.when(step == 0)
    def _():
        extra = early_ref[:, slots, width : width + EXTRA].astype(f32).reshape(-1, EXTRA)
        logits = extra + pltpu.roll(extra, EXTRA - 16, 1) + pltpu.roll(extra, EXTRA - 32, 1)
        logits = logits + dot_nn(rows_ref[...], router_ref[...])
        logits = jnp.where(lane < ALL_EXPERTS, logits, NEG)
        unnormed = jnp.exp(logits - jnp.max(logits, axis=1, keepdims=True))
        probs = unnormed / jnp.sum(unnormed, axis=1, keepdims=True)
        probs_ref[...] = probs
        gate = jnp.sum(jnp.where(lane == home, probs, 0.0), axis=1, keepdims=True)
        dout_ref[...] = (gate * early_ref[:, slots, 0:width].astype(f32).reshape(-1, width)).astype(bf16)
        acc_out[...] = jnp.zeros_like(acc_out)
        acc_row[...] = jnp.zeros_like(acc_row)

    rows = rows_ref[...]
    gate_pre = dot_nn(rows, wg_ref[0])
    up_pre = dot_nn(rows, wu_ref[0])
    d_inner = dot_nt(dout_ref[...], wd_ref[0])
    sigmoid = jax.nn.sigmoid(gate_pre)
    silu = gate_pre * sigmoid
    inner = (silu * up_pre).astype(bf16)
    d_gate = (d_inner * up_pre * (sigmoid * (1.0 + gate_pre * (1.0 - sigmoid)))).astype(bf16)
    d_up = (d_inner * silu).astype(bf16)
    inner_ref[...] = inner
    dgate_ref[...] = d_gate
    dup_ref[...] = d_up
    acc_out[...] += dot_nn(inner, wd_ref[0])
    acc_row[...] += dot_nt(d_gate, wg_ref[0]) + dot_nt(d_up, wu_ref[0])

    @pl.when(step == steps - 1)
    def _():
        probs = probs_ref[...]
        gate = jnp.sum(jnp.where(lane == home, probs, 0.0), axis=1, keepdims=True)
        out = acc_out[...].astype(bf16).astype(f32)
        d_row_gate = jnp.sum(out * early_ref[:, slots, 0:width].astype(f32).reshape(-1, width), axis=1, keepdims=True)
        out_ref[:, 0:width] = (gate * out).astype(bf16)
        extra = jnp.zeros((out.shape[0], EXTRA), f32)
        for i, piece in enumerate(split_low(d_row_gate, 3)):
            extra = jnp.where(lane == home + 16 * i, piece.astype(f32), extra)
        out_ref[:, width : width + EXTRA] = extra.astype(bf16)
        term = d_row_gate * gate * (jnp.where(lane == home, 1.0, 0.0) - probs)
        high, rest = split_low(term, 2)
        drow_ref[...] = (acc_row[...] + dot_nt(high, router_ref[...]) + dot_nt(rest, router_ref[...])).astype(bf16)


def expert_pass(group, home, rows, early, router_pad, w_gate, w_up, w_down):
    count, width = rows.shape
    ff = w_gate.shape[2]
    tile = min(512, ff)
    full = pl.BlockSpec((count, width), lambda j: (0, 0))
    wide = pl.BlockSpec((count, width + EXTRA), lambda j: (0, 0))
    tall = pl.BlockSpec((1, width, tile), lambda j: (0, 0, j))
    piece = pl.BlockSpec((count, tile), lambda j: (0, j))
    return pl.pallas_call(
        functools.partial(expert_kernel, group),
        grid=(ff // tile,),
        in_specs=[
            pl.BlockSpec(memory_space=pltpu.SMEM),
            full,
            pl.BlockSpec(early.shape, lambda j: (0, 0, 0)),
            pl.BlockSpec((width, EXTRA), lambda j: (0, 0)),
            tall,
            tall,
            pl.BlockSpec((1, tile, width), lambda j: (0, j, 0)),
        ],
        out_specs=[wide, full, full, piece, piece, piece],
        out_shape=[
            jax.ShapeDtypeStruct((count, width + EXTRA), bf16),
            jax.ShapeDtypeStruct((count, width), bf16),
            jax.ShapeDtypeStruct((count, width), bf16),
        ]
        + [jax.ShapeDtypeStruct((count, ff), bf16)] * 3,
        scratch_shapes=[pltpu.VMEM((count, width), f32), pltpu.VMEM((count, width), f32), pltpu.VMEM((count, EXTRA), f32)],
        compiler_params=pltpu.CompilerParams(vmem_limit_bytes=60 * 2**20),
        cost_estimate=pl.CostEstimate(flops=12 * count * width * ff, bytes_accessed=6 * width * ff + 2 * count * (5 * width + 3 * ff), transcendentals=count * ff),
        name="expert_pass",
    )(home, rows, early, router_pad, w_gate, w_up, w_down)


def weight_kernel(count, *refs):
    rows, douts, inners, dgates, dups = (refs[i * count : (i + 1) * count] for i in range(5))
    gate_up_ref, down_ref = refs[5 * count : 5 * count + 2]
    turned = refs[5 * count + 2 :]

    @pl.when(pl.program_id(0) == 0)
    def _():
        for ref, scratch in zip(rows, turned):
            scratch[...] = ref[...].T

    gate_up_ref[0] = sum(dot_nn(t[...], d[...]) for t, d in zip(turned, dgates)).astype(bf16)
    gate_up_ref[1] = sum(dot_nn(t[...], d[...]) for t, d in zip(turned, dups)).astype(bf16)
    down_ref[...] = sum(dot_nn(i[...].T, d[...]) for i, d in zip(inners, douts)).astype(bf16)


def weight_gradients(rows, douts, inners, dgates, dups):
    count = len(rows)
    width, ff = rows[0].shape[1], inners[0].shape[1]
    tile = min(512, ff)
    total = sum(r.shape[0] for r in rows)
    full = [pl.BlockSpec(r.shape, lambda j: (0, 0)) for r in rows]
    piece = [pl.BlockSpec((r.shape[0], tile), lambda j: (0, j)) for r in rows]
    return pl.pallas_call(
        functools.partial(weight_kernel, count),
        grid=(ff // tile,),
        in_specs=full + full + piece * 3,
        out_specs=[pl.BlockSpec((2, width, tile), lambda j: (0, 0, j)), pl.BlockSpec((tile, width), lambda j: (j, 0))],
        out_shape=[jax.ShapeDtypeStruct((2, width, ff), bf16), jax.ShapeDtypeStruct((ff, width), bf16)],
        scratch_shapes=[pltpu.VMEM((width, r.shape[0]), bf16) for r in rows],
        compiler_params=pltpu.CompilerParams(vmem_limit_bytes=60 * 2**20),
        cost_estimate=pl.CostEstimate(flops=6 * total * width * ff, bytes_accessed=6 * width * ff + 2 * total * (2 * width + 3 * ff), transcendentals=0),
        name="weight_gradients",
    )(*rows, *douts, *inners, *dgates, *dups)


ANYWHERE = pl.BlockSpec(memory_space=pltpu.VMEM)
SCALARS = pl.BlockSpec(memory_space=pltpu.SMEM)


def inverse_rms(value):
    return lax.rsqrt(jnp.mean(value * value, axis=1, keepdims=True) + epsilon)


def after_attention_kernel(count, mixed_ref, x_ref, w_ref, gain_ref, *refs):
    turned, (hidden_ref, low_ref), sent = refs[:count], refs[count : count + 2], refs[count + 2 :]
    hidden = x_ref[...].astype(f32) + dot_nn(mixed_ref[...], w_ref[...])
    low = (hidden * inverse_rms(hidden) * gain_ref[...]).astype(bf16)
    hidden_ref[...] = hidden
    low_ref[...] = low
    for t, s in zip(turned, sent):
        s[...] = dot_nn(t[...], low).astype(bf16)


def after_attention(mixed, x, w_out, gain, turned):
    tok, width = x.shape
    rows = sum(t.shape[0] for t in turned)
    out = pl.pallas_call(
        functools.partial(after_attention_kernel, len(turned)),
        in_specs=[ANYWHERE] * (4 + len(turned)),
        out_specs=[ANYWHERE] * (2 + len(turned)),
        out_shape=[jax.ShapeDtypeStruct((tok, width), f32), jax.ShapeDtypeStruct((tok, width), bf16)]
        + [jax.ShapeDtypeStruct((t.shape[0], width), bf16) for t in turned],
        compiler_params=pltpu.CompilerParams(vmem_limit_bytes=60 * 2**20),
        cost_estimate=pl.CostEstimate(flops=2 * tok * width * (width + rows), bytes_accessed=2 * width * (6 * tok + 2 * rows), transcendentals=0),
        name="after_attention",
    )(mixed, x, w_out, gain, *turned)
    return out[0], out[1], out[2:]


def place(value, lane, at):
    return jnp.where(lane == at, value, 0.0)


def local_kernel(hidden_ref, low_ref, grad_ref, prev_ref, ids_ref, mix_ref, gain_ref, vec_ref, out_ref, dnormed_ref, probs_ref, dprobs_ref, small_ref):
    lane = lax.broadcasted_iota(jnp.int32, (1, EXTRA), 1)
    hidden = hidden_ref[...]
    normed = hidden * inverse_rms(hidden) * gain_ref[...]
    low = low_ref[...]
    grad = grad_ref[...].astype(f32)
    raw = dot_nn(low, mix_ref[...])
    logits = jnp.where(lane < ALL_EXPERTS, raw + prev_ref[...], NEG)
    unnormed = jnp.exp(logits - jnp.max(logits, axis=1, keepdims=True))
    probs = unnormed / jnp.sum(unnormed, axis=1, keepdims=True)
    named = (ids_ref[:, 0:1] == lane) | (ids_ref[:, 1:2] == lane)
    gates = jnp.where(named, probs, 0.0)
    copy_gate = gates[:, FFN_EXPERTS + 1 : FFN_EXPERTS + 2]
    dots = jnp.sum(grad * normed, axis=1, keepdims=True)
    out = hidden
    weight = copy_gate
    d_probs = place(dots, lane, FFN_EXPERTS + 1)
    logit_grads = jnp.zeros_like(probs)
    mixing_terms = jnp.zeros_like(probs)
    vec_terms = jnp.zeros_like(probs)
    for c in range(2):
        vec = vec_ref[c : c + 1, :]
        gate = gates[:, FFN_EXPERTS + 2 + c : FFN_EXPERTS + 3 + c]
        at = 16 + 2 * c
        a0 = jax.nn.sigmoid(raw[:, at : at + 1] - raw[:, at + 1 : at + 2])
        a1 = jax.nn.sigmoid(raw[:, at + 1 : at + 2] - raw[:, at : at + 1])
        vec_dots = jnp.sum(grad * vec, axis=1, keepdims=True)
        weight = weight + gate * a0
        out = out + (gate * a1) * vec
        d_probs = d_probs + place(a0 * dots + a1 * vec_dots, lane, FFN_EXPERTS + 2 + c)
        d0, d1 = gate * dots, gate * vec_dots
        mean = a0 * d0 + a1 * d1
        d0, d1 = a0 * (d0 - mean), a1 * (d1 - mean)
        logit_grads = logit_grads + place(d0, lane, at) + place(d1, lane, at + 1)
        mixing_terms = mixing_terms + place(d0, lane, 2 * c) + place(d1, lane, 2 * c + 1)
        vec_terms = vec_terms + place(gate * a1, lane, 4 + c)
    d_probs = jnp.where(named, d_probs, 0.0)
    logit_grads = logit_grads + probs * (d_probs - jnp.sum(probs * d_probs, axis=1, keepdims=True))
    high, rest = split_low(logit_grads, 2)
    out_ref[...] = out + weight * normed
    dnormed_ref[...] = weight * grad + dot_nt(high, mix_ref[...]) + dot_nt(rest, mix_ref[...])
    probs_ref[...] = probs
    dprobs_ref[...] = d_probs
    sums = None
    for terms, rows in ((mixing_terms, low), (vec_terms, grad_ref[...])):
        for piece in split_low(terms.T, 2):
            part = dot_nn(piece, rows)
            sums = part if sums is None else sums + part
    sums = sums[0:SMALL, :]

    @pl.when(pl.program_id(0) == 0)
    def _():
        small_ref[...] = sums

    @pl.when(pl.program_id(0) > 0)
    def _():
        small_ref[...] += sums


def local_part(hidden, low, grad, prev, ids, mix, gain, vec):
    tok, width = hidden.shape
    block, tiles = row_tiles(tok)
    shapes = [(tok, width), (tok, width), (tok, EXTRA), (tok, EXTRA), (SMALL, width)]
    return pl.pallas_call(
        local_kernel,
        grid=(tok // block,),
        in_specs=[tiles(width), tiles(width), tiles(width), tiles(EXTRA), tiles(2), fixed(mix), fixed(gain), fixed(vec)],
        out_specs=[tiles(width), tiles(width), tiles(EXTRA), tiles(EXTRA), pl.BlockSpec((SMALL, width), lambda i: (0, 0))],
        out_shape=[jax.ShapeDtypeStruct(s, f32) for s in shapes],
        compiler_params=pltpu.CompilerParams(vmem_limit_bytes=60 * 2**20),
        cost_estimate=pl.CostEstimate(flops=14 * tok * width * EXTRA, bytes_accessed=16 * tok * width, transcendentals=tok * EXTRA),
        name="local_part",
    )(hidden, low, grad, prev, ids, mix, gain, vec)


def row_tiles(tok):
    block = 256 if tok % 256 == 0 else 128
    return block, lambda columns: pl.BlockSpec((block, columns), lambda i: (i, 0))


def fixed(value):
    return pl.BlockSpec(value.shape, lambda i: (0,) * value.ndim)


def combine_kernel(count, parts, *refs):
    chosen, got = refs[:count], refs[count : count * (1 + parts)]
    local_ref, hidden_ref, gain_ref, grad_ref, w_ref, dhidden_ref, dlow_ref, dmixed_ref, small_ref = refs[count * (1 + parts) :]
    d_normed = local_ref[...]
    for g in range(count):
        for r in range(parts):
            d_normed = d_normed + dot_nn(chosen[g][...], got[g * parts + r][...])
    hidden = hidden_ref[...]
    inverse = inverse_rms(hidden)
    scaled = d_normed * gain_ref[...]
    mean = jnp.mean(scaled * hidden, axis=1, keepdims=True)
    d_hidden = grad_ref[...].astype(f32) + inverse * scaled - hidden * (inverse * inverse * inverse * mean)
    low = d_hidden.astype(bf16)
    dhidden_ref[...] = d_hidden
    dlow_ref[...] = low
    dmixed_ref[...] = dot_nt(low, w_ref[...]).astype(bf16)
    gain = jnp.sum(d_normed * hidden * inverse, axis=0, keepdims=True)
    row = lax.broadcasted_iota(jnp.int32, (SMALL, 1), 0)
    gain = jnp.where(row == 0, gain, 0.0)

    @pl.when(pl.program_id(0) == 0)
    def _():
        small_ref[...] = gain

    @pl.when(pl.program_id(0) > 0)
    def _():
        small_ref[...] += gain


def combine(chosen, got, local, hidden, gain, grad, w_out):
    tok, width = hidden.shape
    rows = sum(c.shape[1] for c in chosen)
    arrays = [a for group in got for a in group]
    block, tiles = row_tiles(tok)
    return pl.pallas_call(
        functools.partial(combine_kernel, len(chosen), len(got[0])),
        grid=(tok // block,),
        in_specs=[tiles(c.shape[1]) for c in chosen] + [fixed(a) for a in arrays] + [tiles(width), tiles(width), fixed(gain), tiles(width), fixed(w_out)],
        out_specs=[tiles(width)] * 3 + [pl.BlockSpec((SMALL, width), lambda i: (0, 0))],
        out_shape=[jax.ShapeDtypeStruct((tok, width), f32)] + [jax.ShapeDtypeStruct((tok, width), bf16)] * 2 + [jax.ShapeDtypeStruct((SMALL, width), f32)],
        compiler_params=pltpu.CompilerParams(vmem_limit_bytes=60 * 2**20),
        cost_estimate=pl.CostEstimate(flops=2 * tok * width * (rows + width), bytes_accessed=2 * width * (9 * tok + 2 * rows), transcendentals=0),
        name="combine_gradients",
    )(*chosen, *arrays, local, hidden, gain, grad, w_out)


def flat_rows(value):
    if value.shape[1] % 16:
        return value.astype(f32).reshape(-1, value.shape[2]).astype(bf16)
    return value.reshape(-1, value.shape[2])


def finish_kernel(groups, parts, *refs):
    chosen, got = refs[: len(groups)], refs[len(groups) : len(groups) + parts]
    local_ref, probs_ref, dprobs_ref, low_ref, out_ref, dlogits_ref, small_ref = refs[len(groups) + parts :]
    width = local_ref.shape[1]
    lane = lax.broadcasted_iota(jnp.int32, (1, EXTRA), 1)
    picked = None
    for c, (at, size) in zip(chosen, groups):
        for r in range(parts):
            part = dot_nn(c[...], flat_rows(got[r][:, at : at + size, :]))
            picked = part if picked is None else picked + part
    out_ref[...] = (local_ref[...] + picked[:, 0:width]).astype(bf16)
    extra = picked[:, width : width + EXTRA]
    extra = extra + pltpu.roll(extra, EXTRA - 16, 1) + pltpu.roll(extra, EXTRA - 32, 1)
    d_probs = dprobs_ref[...] + jnp.where(lane < ALL_EXPERTS, extra, 0.0)
    probs = probs_ref[...]
    d_logits = probs * (d_probs - jnp.sum(probs * d_probs, axis=1, keepdims=True))
    dlogits_ref[...] = d_logits
    high, rest = split_low(d_logits.T, 2)
    sums = (dot_nn(high, low_ref[...]) + dot_nn(rest, low_ref[...]))[0 : 2 * SMALL, :]

    @pl.when(pl.program_id(0) == 0)
    def _():
        small_ref[...] = sums

    @pl.when(pl.program_id(0) > 0)
    def _():
        small_ref[...] += sums


def finish(chosen, got, groups, local, probs, d_probs, low):
    tok, width = local.shape
    block, tiles = row_tiles(tok)
    return pl.pallas_call(
        functools.partial(finish_kernel, groups, len(got)),
        grid=(tok // block,),
        in_specs=[tiles(c.shape[1]) for c in chosen] + [fixed(g) for g in got] + [tiles(width), tiles(EXTRA), tiles(EXTRA), tiles(width)],
        out_specs=[tiles(width), tiles(EXTRA), pl.BlockSpec((2 * SMALL, width), lambda i: (0, 0))],
        out_shape=[jax.ShapeDtypeStruct((tok, width), bf16), jax.ShapeDtypeStruct((tok, EXTRA), f32), jax.ShapeDtypeStruct((2 * SMALL, width), f32)],
        compiler_params=pltpu.CompilerParams(vmem_limit_bytes=60 * 2**20),
        cost_estimate=pl.CostEstimate(flops=2 * tok * 1152 * (width + EXTRA), bytes_accessed=16 * tok * width, transcendentals=0),
        name="finish_outputs",
    )(*chosen, *got, local, probs, d_probs, low)


def xor_pairs(size, mask):
    return [(i, i ^ mask) for i in range(size)]


def store_halves(core, turned_terms, at, mine_ref, theirs_ref):
    half = mine_ref.shape[0]
    columns = turned_terms[0][1].shape[1]
    for out_ref, which in ((theirs_ref, 1 - core), (mine_ref, core)):
        rows = pl.ds(pl.multiple_of(which * half, half), half)
        total = None
        for left, right in turned_terms:
            part = dot_nn(left[rows, :], right[...])
            total = part if total is None else total + part
        out_ref[:, at : at + columns] = total.astype(bf16)


def pack_first_kernel(core_ref, act_ref, far_ref, dq_ref, dk_ref, dv_ref, dkf_ref, dvf_ref, mixed_ref, dlow_ref, mine_ref, theirs_ref, act_t, far_t, mixed_t):
    core = core_ref[0]
    width, n = mixed_ref.shape[1], dq_ref.shape[1]
    mixed_t[...] = mixed_ref[...].T
    act_t[...] = act_ref[...].T
    far_t[...] = far_ref[...].T
    store_halves(core, [(mixed_t, dlow_ref)], 0, mine_ref, theirs_ref)
    store_halves(core, [(act_t, dq_ref)], width, mine_ref, theirs_ref)
    store_halves(core, [(act_t, dk_ref), (far_t, dkf_ref)], width + n, mine_ref, theirs_ref)
    store_halves(core, [(act_t, dv_ref), (far_t, dvf_ref)], width + 2 * n, mine_ref, theirs_ref)


def pack_second_kernel(core_ref, act_ref, far_ref, dq_ref, dk_ref, dv_ref, dkf_ref, dvf_ref, local_ref, gain_ref, router_ref, mine_ref, theirs_ref, act_t, far_t, small_t):
    core = core_ref[0]
    n = dq_ref.shape[1]
    half = mine_ref.shape[0]
    act_t[...] = act_ref[...].T
    far_t[...] = far_ref[...].T
    store_halves(core, [(act_t, dq_ref)], 0, mine_ref, theirs_ref)
    store_halves(core, [(act_t, dk_ref), (far_t, dkf_ref)], n, mine_ref, theirs_ref)
    store_halves(core, [(act_t, dv_ref), (far_t, dvf_ref)], 2 * n, mine_ref, theirs_ref)
    rows = [router_ref[...], local_ref[...], gain_ref[...]]
    rows.append(jnp.zeros((EXTRA - sum(r.shape[0] for r in rows), act_ref.shape[1]), f32))
    small_t[...] = jnp.concatenate(rows, axis=0).T
    for out_ref, which in ((theirs_ref, 1 - core), (mine_ref, core)):
        out_ref[:, 3 * n : 3 * n + EXTRA] = small_t[pl.ds(pl.multiple_of(which * half, half), half), :].astype(bf16)


def pack(core, act, far, grads, others, first):
    tok, width = act.shape
    n = grads[0].shape[1]
    columns = (width if first else EXTRA) + 3 * n
    arrays = [act, far, *grads, *others]
    extra = pltpu.VMEM((width, tok), bf16) if first else pltpu.VMEM((width, EXTRA), f32)
    return pl.pallas_call(
        pack_first_kernel if first else pack_second_kernel,
        in_specs=[SCALARS] + [ANYWHERE] * len(arrays),
        out_specs=[ANYWHERE] * 2,
        out_shape=[jax.ShapeDtypeStruct((width // 2, columns), bf16)] * 2,
        scratch_shapes=[pltpu.VMEM((width, tok), bf16), pltpu.VMEM((width, far.shape[0]), bf16), extra],
        compiler_params=pltpu.CompilerParams(vmem_limit_bytes=60 * 2**20),
        cost_estimate=pl.CostEstimate(flops=2 * width * columns * tok, bytes_accessed=2 * width * (5 * tok + columns), transcendentals=0),
        name="pack_first" if first else "pack_second",
    )(core, *arrays)


def sum_kernel(terms, index_ref, *refs):
    count = (len(refs)) // (terms + 1)
    for k in range(count):
        total = None
        for t in range(terms):
            value = refs[t * count + k][...].astype(f32)
            total = value if total is None else total + value
        refs[terms * count + k][...] = total.astype(bf16)


def sum_pieces(index, arrays):
    n, shape = arrays[0].shape[0], arrays[0].shape[1:]
    views = [pl.BlockSpec((1,) + shape, functools.partial(lambda k, i, s: (s[0] ^ k if n > 1 else 0, 0, 0), k)) for k in range(n)]
    return pl.pallas_call(
        functools.partial(sum_kernel, len(arrays)),
        grid_spec=pltpu.PrefetchScalarGridSpec(
            num_scalar_prefetch=1,
            grid=(1,),
            in_specs=views * len(arrays),
            out_specs=[pl.BlockSpec((1,) + shape, lambda i, s: (0, 0, 0))] * n,
        ),
        out_shape=[jax.ShapeDtypeStruct((1,) + shape, bf16)] * n,
        compiler_params=pltpu.CompilerParams(vmem_limit_bytes=60 * 2**20),
        cost_estimate=pl.CostEstimate(flops=0, bytes_accessed=2 * n * math.prod(shape) * (len(arrays) + 1), transcendentals=0),
        name="sum_pieces",
    )(index, *[a for a in arrays for _ in range(n)])


def quarters(value):
    return value.reshape(4, -1, value.shape[-1])


def swap(pieces, along):
    axis, size, unit = along
    return [pieces[0]] + [lax.ppermute(pieces[k], axis, xor_pairs(size, unit * k)) for k in range(1, 4)]


def spread(value, along):
    return swap([value] * 4, along)


def stack_kernel(*refs):
    n = len(refs) - 1
    size = refs[0].shape[0]
    for k in range(n):
        refs[n][k * size : (k + 1) * size] = refs[k][...]


def stack_pieces(pieces):
    shape = (len(pieces) * pieces[0].shape[0],) + pieces[0].shape[1:]
    return pl.pallas_call(
        stack_kernel,
        in_specs=[ANYWHERE] * len(pieces),
        out_specs=ANYWHERE,
        out_shape=jax.ShapeDtypeStruct(shape, bf16),
        compiler_params=pltpu.CompilerParams(vmem_limit_bytes=60 * 2**20),
        cost_estimate=pl.CostEstimate(flops=0, bytes_accessed=4 * math.prod(shape), transcendentals=0),
        name="stack_pieces",
    )(*pieces)


def unpack_kernel(index_ref, own1_ref, other1_ref, own2_ref, other2_ref, w_ref, out_ref, qkv_ref, small_ref):
    width = out_ref.shape[1]
    n = width // 2
    piece = own1_ref.shape[2]
    mine = pl.program_id(0) == index_ref[0]
    lane = lax.broadcasted_iota(jnp.int32, (1, EXTRA), 1)
    for k in range(4):
        rows = slice(k * piece, (k + 1) * piece)
        at_ctx, at_z = k ^ index_ref[1], k ^ index_ref[2]
        first = jnp.where(mine, own1_ref[at_ctx, 0, :, :], other1_ref[at_ctx, 0, :, :]).astype(f32)
        second = jnp.where(mine, own2_ref[0, at_z, :, :], other2_ref[0, at_z, :, :]).astype(f32)
        out_ref[rows, :] = first[:, 0:width]
        gain = None
        for p in range(3):
            for value, at in ((first[:, width + p * n : width + (p + 1) * n], 0), (second[:, p * n : (p + 1) * n], n)):
                columns = slice(p * width + at, p * width + at + n)
                qkv_ref[rows, columns] = value
                part = value * w_ref[rows, columns].astype(f32)
                gain = part if gain is None else gain + part
        gain = jnp.sum(gain, axis=1, keepdims=True)
        small_ref[rows, :] = second[:, 3 * n : 3 * n + EXTRA] + place(gain, lane, EXTRA - 1)


def unpack(index, first, second, w_qkv):
    width = w_qkv.shape[0]
    piece = width // 32
    block = 4 * piece
    shape = lambda value: value.reshape(4, 4, piece, -1)
    first, second = [shape(v) for v in first], [shape(v) for v in second]
    c1, c2 = first[0].shape[3], second[0].shape[3]
    row = lambda c, a, s: (c * 4 + a, 0)
    source1 = pl.BlockSpec((4, 1, piece, c1), lambda c, a, s: (0, a ^ s[2], 0, 0))
    source2 = pl.BlockSpec((1, 4, piece, c2), lambda c, a, s: (a ^ s[1], 0, 0, 0))
    return pl.pallas_call(
        unpack_kernel,
        grid_spec=pltpu.PrefetchScalarGridSpec(
            num_scalar_prefetch=1,
            grid=(2, 4),
            in_specs=[source1, source1, source2, source2, pl.BlockSpec((block, 3 * width), row)],
            out_specs=[pl.BlockSpec((block, width), row), pl.BlockSpec((block, 3 * width), row), pl.BlockSpec((block, EXTRA), row)],
        ),
        out_shape=[jax.ShapeDtypeStruct((width, width), f32), jax.ShapeDtypeStruct((width, 3 * width), f32), jax.ShapeDtypeStruct((width, EXTRA), f32)],
        compiler_params=pltpu.CompilerParams(vmem_limit_bytes=60 * 2**20),
        cost_estimate=pl.CostEstimate(flops=0, bytes_accessed=36 * width * width, transcendentals=0),
        name="unpack_sums",
    )(index, *first, *second, w_qkv)

P = jax.sharding.PartitionSpec


def rms_inverse(tensor):
    return lax.rsqrt(jnp.mean(tensor * tensor, axis=-1, keepdims=True) + epsilon)


def after(values, *others):
    return lax.optimization_barrier((values, others))[0]


def body(inputs, prev_logits, routes, attn_gain, w_qkv, w_out, moe_gain, router, const_gate, const_vec, w_gate, w_up, w_down, out_grad):
    n_ctx, n_exp = lax.axis_size("ctx"), lax.axis_size("exp")
    me_c, me_e = lax.axis_index("ctx"), lax.axis_index("exp")
    tok, width = inputs.shape[1], inputs.shape[2]
    plen = tok - CONT_LEN
    split = n_exp // FFN_EXPERTS
    capacity = max(4, tok // 64 * 12)
    first = -(-capacity // 32) * 16
    groups = ((0, first), (first, capacity - first))
    home = (me_e // split).reshape(1)

    def deal(value):
        value = jnp.repeat(value, split, axis=0) if split > 1 else value
        return lax.all_to_all(value, "exp", 0, 0, tiled=True)

    def give_back(value):
        value = lax.all_to_all(value, "exp", 0, 0, tiled=True)
        return [value[r::split] if split > 1 else value for r in range(split)]

    x_low = inputs[0]
    x_prompt, upstream_low = lax.optimization_barrier((x_low[:plen], out_grad[0]))
    far_rows = jnp.concatenate([lax.ppermute(x_prompt, "ctx", xor_pairs(n_ctx, k)) for k in range(1, n_ctx)], axis=0)
    flags = jnp.where((me_c ^ jnp.arange(1, n_ctx)) < me_c, 0.0, NEG).astype(f32)

    prev = jnp.pad(prev_logits[0], ((0, 0), (0, EXTRA - ALL_EXPERTS)))
    mix = jnp.concatenate([router, jnp.zeros((width, 4), bf16), const_gate[0], const_gate[1], jnp.zeros((width, EXTRA - 20), bf16)], axis=1)
    router_pad = jnp.pad(router, ((0, 0), (0, EXTRA - ALL_EXPERTS)))
    turned, chosen, early_sent = route_plan(home, routes[0].T, upstream_low, prev, groups)

    tokens_in = x_low.astype(f32)
    inverse_attn = rms_inverse(tokens_in)
    act_low = (tokens_in * inverse_attn * attn_gain).astype(bf16)
    projected = dot_nn(act_low, w_qkv).astype(bf16)
    early = deal(early_sent)
    far_in = after(far_rows, projected).astype(f32)
    act_far = (far_in * rms_inverse(far_in) * attn_gain).astype(bf16)
    kv_far = dot_nn(act_far, w_qkv[:, width:]).astype(bf16)

    mixed_low, lse = attention_forward(flags, projected, kv_far, plen)
    mixed_low, early = lax.optimization_barrier((mixed_low, early))
    hidden, moe_low, sent = after_attention(mixed_low, x_low, w_out, moe_gain[None], turned)
    local_out, d_normed_local, probs, d_probs, small_local = local_part(hidden, moe_low, upstream_low, prev, routes[0], mix, moe_gain[None], const_vec)
    sent = [after(sent[0], local_out, d_normed_local), sent[1]]
    got = [deal(part.reshape(FFN_EXPERTS, -1, width)) for part in sent]

    got = [part.reshape(-1, width) for part in got]
    passes = [expert_pass(group, home, r, early, router_pad, w_gate, w_up, w_down) for group, r in zip(groups, got)]
    d_got = [give_back(p[1].reshape(n_exp, -1, width)) for p in passes]
    gate_up_low, down_low = weight_gradients(got, [p[2] for p in passes], [p[3] for p in passes], [p[4] for p in passes], [p[5] for p in passes])
    outs = jnp.concatenate([p[0].reshape(n_exp, -1, width + EXTRA) for p in passes], axis=1)
    d_got, gate_up_low, down_low, outs = lax.optimization_barrier((d_got, gate_up_low, down_low, outs))
    out_got = give_back(outs)

    d_got = [[part.reshape(-1, width) for part in group] for group in d_got]
    d_hidden, d_attn_low, d_mixed, small_gain = combine(chosen, d_got, d_normed_local, hidden, moe_gain[None], upstream_low, w_out)

    sum_gate_up = lax.psum_scatter(gate_up_low, "ctx", scatter_dimension=1, tiled=True).astype(f32)
    sum_down = lax.psum_scatter(down_low, "ctx", scatter_dimension=0, tiled=True).astype(f32)

    pairs = width // 128
    cut = pairs // 2

    def attention(upstream, begin, count):
        return attention_backward(flags, projected, kv_far, mixed_low, upstream, lse, plen, begin, count)

    def weight_columns(part, group):
        at = part * width + group * cut * 128
        return w_qkv[:, at : at + grads_1[0].shape[1]]

    def far_gradient(both):
        total = sum(dot_nt(grads[p + 2], weight_columns(p, g)) for g, grads in enumerate(both) for p in (1, 2))
        total = total.astype(bf16).reshape(n_ctx - 1, plen, width)
        return total, [lax.ppermute(total[k - 1], "ctx", xor_pairs(n_ctx, k)) for k in range(1, n_ctx)]

    def own_gradient(both):
        return sum(dot_nt(grads[p], weight_columns(p, g)) for g, grads in enumerate(both) for p in range(3))

    grads_1 = attention(d_mixed, 0, cut)
    if n_ctx == 4 and n_exp == 8:
        core, z = me_e & 1, me_e >> 1
        at_core, at_ctx, at_z, at_none = (v.reshape(1) for v in (core, me_c, z, z * 0))
        along_ctx, along_z = ("ctx", 4, 1), ("exp", 8, 2)
        across = lambda value: lax.ppermute(value, "exp", xor_pairs(8, 1))
        mine_1, theirs_1 = pack(at_core, act_low, act_far, grads_1, [mixed_low, d_attn_low], True)
        got_1 = across(theirs_1)
        grads_2 = attention(after(d_mixed, mine_1), cut, pairs - cut)
        both = (grads_1, grads_2)
        sums_1 = sum_pieces(at_z, [quarters(mine_1), quarters(after(got_1, grads_2[0]))])
        parts_1 = swap(sums_1, along_z)
        mixed_out, d_logits, small_router = finish(chosen, out_got, groups, after(local_out, sums_1[0]), probs, d_probs, moe_low)
        mine_2, theirs_2 = pack(at_core, act_low, act_far, grads_2, [small_local, small_gain, small_router], False)
        got_2 = across(theirs_2)
        d_act_far, far_back = far_gradient(after(both, mine_2))
        sums_2 = sum_pieces(at_ctx, [quarters(mine_2), quarters(after(got_2, d_act_far))])
        parts_2 = swap(sums_2, along_ctx)
        d_act = own_gradient(after(both, sums_2[0]))
        sums_1 = sum_pieces(at_ctx, [quarters(p) for p in after(parts_1, d_act)])
        parts_1 = swap(sums_1, along_ctx)
        sums_2 = sum_pieces(at_z, [quarters(p) for p in after(parts_2, sums_1[0])])
        parts_2 = swap(sums_2, along_z)
        [piece_1] = sum_pieces(at_none, after(parts_1, sums_2[0]))
        spread_1 = spread(piece_1, along_z)
        [piece_2] = sum_pieces(at_none, after(parts_2, piece_1))
        spread_2 = spread(piece_2, along_z)
        column_1 = stack_pieces(after(spread_1, piece_2))
        spread_1 = spread(column_1, along_ctx)
        column_2 = stack_pieces(after(spread_2, column_1))
        spread_2 = spread(column_2, along_ctx)
        own_1 = stack_pieces(after(spread_1, column_2))
        other_1 = across(own_1)
        own_2 = stack_pieces(after(spread_2, own_1))
        other_2 = across(own_2)
    else:
        grads_2 = attention(d_mixed, cut, pairs - cut)
        both = (grads_1, grads_2)
        mixed_out, d_logits, small_router = finish(chosen, out_got, groups, local_out, probs, d_probs, moe_low)
        d_act_far, far_back = far_gradient(both)
        d_act = own_gradient(both)

    d_act = jnp.concatenate([d_act[:plen] + sum(part.astype(f32) for part in far_back), d_act[plen:]], axis=0)
    scaled = d_act * attn_gain
    d_inputs = d_hidden + inverse_attn * scaled - tokens_in * inverse_attn**3 * jnp.mean(scaled * tokens_in, axis=-1, keepdims=True)

    if n_ctx == 4 and n_exp == 8:
        weights = after(w_qkv, d_inputs, sum_gate_up, sum_down)
        out_sum, qkv_sum, small = unpack(jnp.stack([core, me_c, z]), (own_1, other_1), (own_2, other_2), weights)
        d_attn_gain = small[:, EXTRA - 1]
    else:
        dq, dk, dv, dk_far, dv_far = (jnp.concatenate(pair, axis=1) for pair in zip(grads_1, grads_2))
        d_w_k = dot_tn(act_low, dk) + dot_tn(act_far, dk_far)
        d_w_v = dot_tn(act_low, dv) + dot_tn(act_far, dv_far)
        parts = [dot_tn(mixed_low, d_attn_low), dot_tn(act_low, dq), d_w_k, d_w_v, small_router, small_local, small_gain]
        out_sum, q_sum, k_sum, v_sum, *small = [p.astype(f32) for p in lax.psum([p.astype(bf16) for p in parts], ("ctx", "exp"))]
        qkv_sum = jnp.concatenate([q_sum, k_sum, v_sum], axis=1)
        small = jnp.concatenate(small, axis=0).T
        d_attn_gain = jnp.sum(qkv_sum * w_qkv.astype(f32), axis=1)
    d_attn_gain = d_attn_gain / attn_gain
    at = 2 * SMALL
    d_const_gate = jnp.stack([small[:, at : at + 2], small[:, at + 2 : at + 4]])
    return (
        mixed_out[None],
        d_inputs[None],
        d_logits[None, :, :ALL_EXPERTS],
        d_attn_gain,
        qkv_sum,
        out_sum,
        small[:, at + SMALL],
        small[:, :ALL_EXPERTS],
        d_const_gate,
        small[:, at + 4 : at + 6].T,
        sum_gate_up[0][None],
        sum_gate_up[1][None],
        sum_down[None],
    )


def solution(mesh):
    rows = P("ctx", "exp", None)
    expert = P("exp", None, None)
    summed = P("exp", "ctx", None)
    return jax.shard_map(
        body,
        mesh=mesh,
        in_specs=(rows, rows, rows, P(), P(), P(), P(), P(), P(), P(), expert, expert, expert, rows),
        out_specs=(rows, rows, rows, P(), P(), P(), P(), P(), P(), P(), summed, summed, summed),
        check_vma=False,
    )
```

```python
import functools, math
import jax, jax.numpy as jnp
from jax import lax
from jax.experimental import pallas as pl
from jax.experimental.pallas import tpu as pltpu

HEADS = 12
HEAD_DIM = 64
CONT_LEN = 512
LOG2E = 1.4426950408889634
SCALE = HEAD_DIM ** -0.5
bf16 = jnp.bfloat16
f32 = jnp.float32
NEG = -1e30


def dot_nt(a, b):
    return lax.dot_general(a, b, (((1,), (1,)), ((), ())), preferred_element_type=f32)


def dot_nn(a, b):
    return jnp.dot(a, b, preferred_element_type=f32)


def query_tiles(tok, plen):
    tiles = [(0, plen, True)]
    step = 256
    for start in range(plen, tok, step):
        tiles.append((start, step, False))
    return tiles


def attention_forward_kernel(plen, flags_ref, q_ref, k_ref, v_ref, kr_ref, vr_ref, o_ref, lse_ref):
    tok = q_ref.shape[0]
    remote = kr_ref.shape[0]
    lane = lax.broadcasted_iota(jnp.int32, (1, 128), 1)
    low_half = lane < HEAD_DIM
    c = SCALE * LOG2E
    one = jnp.ones((), bf16)
    zero = jnp.zeros((), bf16)
    for start, size, is_prompt in query_tiles(tok, plen):
        accs, peaks = [], []
        for head in range(2):
            mine = low_half if head == 0 else ~low_half
            qh = jnp.where(mine, q_ref[start : start + size, :], zero)
            pieces = []
            row = lax.broadcasted_iota(jnp.int32, (size, size), 0)
            col = lax.broadcasted_iota(jnp.int32, (size, size), 1)
            diag = dot_nt(qh, k_ref[start : start + size, :])
            pieces.append((jnp.where(col <= row, diag, NEG), v_ref, start, size))
            if is_prompt:
                for j in range(remote // plen):
                    s = dot_nt(qh, kr_ref[j * plen : (j + 1) * plen, :])
                    pieces.append((s + flags_ref[j], vr_ref, j * plen, plen))
            else:
                s = dot_nt(qh, k_ref[0:start, :])
                pieces.append((s, v_ref, 0, start))
                s = dot_nt(qh, kr_ref[...])
                pieces.append((s, vr_ref, 0, remote))
            peak = None
            for s, _, _, _ in pieces:
                m = jnp.max(s, axis=1, keepdims=True)
                peak = m if peak is None else jnp.maximum(peak, m)
            shift = peak * c
            acc = None
            for s, ref, at, n in pieces:
                p = jnp.exp2(s * c - shift).astype(bf16)
                vh = jnp.where(mine, ref[at : at + n, :], one)
                part = dot_nn(p, vh)
                acc = part if acc is None else acc + part
            accs.append(acc)
            peaks.append(shift)
        num = jnp.where(low_half, accs[0], accs[1])
        den = pltpu.roll(jnp.where(low_half, accs[1], accs[0]), HEAD_DIM, 1)
        o_ref[start : start + size, :] = (num / den).astype(bf16)
        logs = jnp.where(low_half, peaks[0], peaks[1]) + jnp.log2(den)
        turned = logs.T
        lse_ref[0, 0:8, start : start + size] = turned[0:8, :]
        lse_ref[0, 8:16, start : start + size] = turned[HEAD_DIM : HEAD_DIM + 8, :]


def attention_forward(flags, proj, kv_rem, plen):
    tok, width = proj.shape[0], proj.shape[1] // 3
    remote = kv_rem.shape[0]
    pairs = width // 128
    return pl.pallas_call(
        functools.partial(attention_forward_kernel, plen),
        grid=(pairs,),
        in_specs=[
            pl.BlockSpec(memory_space=pltpu.SMEM),
            pl.BlockSpec((tok, 128), lambda i: (0, i)),
            pl.BlockSpec((tok, 128), lambda i: (0, pairs + i)),
            pl.BlockSpec((tok, 128), lambda i: (0, 2 * pairs + i)),
            pl.BlockSpec((remote, 128), lambda i: (0, i)),
            pl.BlockSpec((remote, 128), lambda i: (0, pairs + i)),
        ],
        out_specs=[
            pl.BlockSpec((tok, 128), lambda i: (0, i)),
            pl.BlockSpec((1, 16, tok), lambda i: (i, 0, 0)),
        ],
        out_shape=[
            jax.ShapeDtypeStruct((tok, width), bf16),
            jax.ShapeDtypeStruct((pairs, 16, tok), f32),
        ],
        compiler_params=pltpu.CompilerParams(vmem_limit_bytes=60 * 2**20),
        cost_estimate=pl.CostEstimate(flops=4 * tok * (tok + remote) * width, bytes_accessed=2 * (tok * 4 + remote * 2) * width, transcendentals=tok * (tok + remote) * HEADS),
        name="attention_forward",
    )(flags, proj, proj, proj, kv_rem, kv_rem)


def attention_backward_kernel(plen, started, last, skip, flags_ref, core_ref, q_ref, k_ref, v_ref, kr_ref, vr_ref, o_ref, do_ref, lse_ref, act_ref, far_ref, wq_ref, wk_ref, wv_ref, *refs):
    refs = refs[skip:]
    if started:
        start_act_ref, start_far_ref, *refs = refs
    mine_ref, theirs_ref, dact_ref, *refs = refs
    dfar_ref, *dfar_refs = (refs[-1:] + refs[:-9]) if last else refs[:1]
    kt, krt, dka, dva, dkra, dvra, own_grads, weights = refs[-9:-1] if last else refs[-8:]
    tok = q_ref.shape[0]
    remote = kr_ref.shape[0]
    lane = lax.broadcasted_iota(jnp.int32, (1, 128), 1)
    low_half = lane < HEAD_DIM
    c = SCALE * LOG2E
    zero = jnp.zeros((), bf16)
    kt[...] = k_ref[...].T
    krt[...] = kr_ref[...].T
    dka[...] = jnp.zeros_like(dka)
    dva[...] = jnp.zeros_like(dva)
    dkra[...] = jnp.zeros_like(dkra)
    dvra[...] = jnp.zeros_like(dvra)
    pick = lax.broadcasted_iota(jnp.int32, (16, 128), 0) // 8 == lax.broadcasted_iota(jnp.int32, (16, 128), 1) // HEAD_DIM
    pick = jnp.where(pick, 1.0, 0.0).astype(bf16)
    for start, size, is_prompt in query_tiles(tok, plen):
        rows = slice(start, start + size)
        product = do_ref[rows, :].astype(f32) * o_ref[rows, :].astype(f32)
        high = product.astype(bf16)
        rest = (product - high.astype(f32)).astype(bf16)
        delta = dot_nt(pick, high) + dot_nt(pick, rest)
        dqt = []
        for head in range(2):
            mine = low_half if head == 0 else ~low_half
            qh = jnp.where(mine, q_ref[rows, :], zero)
            doh = jnp.where(mine, do_ref[rows, :], zero)
            lse_row = lse_ref[0, 8 * head : 8 * head + 1, rows]
            delta_row = delta[8 * head : 8 * head + 1, :]
            segments = [(k_ref, v_ref, kt, dka, dva, start, size, "diag")]
            if is_prompt:
                for j in range(remote // plen):
                    segments.append((kr_ref, vr_ref, krt, dkra, dvra, j * plen, plen, j))
            else:
                segments.append((k_ref, v_ref, kt, dka, dva, 0, start, None))
                segments.append((kr_ref, vr_ref, krt, dkra, dvra, 0, remote, None))
            total = None
            for kk, vv, tt, dk_acc, dv_acc, at, n, mode in segments:
                keys = slice(at, at + n)
                st = dot_nt(kk[keys, :], qh) * c - lse_row
                if mode == "diag":
                    key = lax.broadcasted_iota(jnp.int32, (n, size), 0)
                    query = lax.broadcasted_iota(jnp.int32, (n, size), 1)
                    st = jnp.where(key <= query, st, NEG)
                elif mode is not None:
                    st = st + flags_ref[mode]
                pt = jnp.exp2(st)
                dpt = dot_nt(vv[keys, :], doh)
                dst = (pt * (dpt - delta_row)).astype(bf16)
                dv_acc[keys, :] += dot_nn(pt.astype(bf16), doh)
                dk_acc[keys, :] += dot_nn(dst, qh)
                part = dot_nn(tt[head * HEAD_DIM : (head + 1) * HEAD_DIM, keys], dst)
                total = part if total is None else total + part
            dqt.append(total)
        own_grads[rows, 0:128] = (jnp.concatenate(dqt, axis=0).T * SCALE).astype(bf16)
    own_grads[:, 128:256] = (dka[...] * SCALE).astype(bf16)
    own_grads[:, 256:384] = dva[...].astype(bf16)
    far_grads = jnp.concatenate([(dkra[...] * SCALE).astype(bf16), dvra[...].astype(bf16)], axis=1)
    weights[:, 0:128] = wq_ref[...]
    weights[:, 128:256] = wk_ref[...]
    weights[:, 256:384] = wv_ref[...]
    half = mine_ref.shape[0]
    for out_ref, which in ((theirs_ref, 1 - core_ref[0]), (mine_ref, core_ref[0])):
        rows = pl.ds(pl.multiple_of(which * half, half), half)
        total = dot_nn(act_ref[rows, :], own_grads[...])
        out_ref[:, 0:128] = total[:, 0:128].astype(bf16)
        out_ref[:, 128:384] = (total[:, 128:384] + dot_nn(far_ref[rows, :], far_grads)).astype(bf16)
    d_act = dot_nt(own_grads[...], weights[...])
    d_far = dot_nt(far_grads, weights[:, 128:384])
    step = pl.program_id(0)

    @pl.when(step == 0)
    def _():
        dact_ref[...] = d_act + start_act_ref[...] if started else d_act
        dfar_ref[...] = d_far + start_far_ref[...] if started else d_far

    @pl.when(step > 0)
    def _():
        dact_ref[...] += d_act
        dfar_ref[...] += d_far

    if last:

        @pl.when(step == pl.num_programs(0) - 1)
        def _():
            for k, ref in enumerate(dfar_refs):
                ref[...] = dfar_ref[k * plen : (k + 1) * plen, :].astype(bf16)


def attention_backward(flags, core, proj, kv_rem, mixed, d_mixed, lse, act_t, far_t, w_qkv, plen, begin, count, buffers, at, starts, last):
    tok, width = mixed.shape
    remote = kv_rem.shape[0]
    pairs = width // 128
    own = lambda shift: pl.BlockSpec((tok, 128), lambda i: (0, shift + i))
    far = lambda shift: pl.BlockSpec((remote, 128), lambda i: (0, shift + i))
    weight = lambda shift: pl.BlockSpec((width, 128), lambda i: (0, shift + i))
    still = lambda shape: pl.BlockSpec(shape, lambda i: (0, 0))
    half = pl.BlockSpec((width // 2, 384), lambda i: (0, at + i))
    in_specs = [
        pl.BlockSpec(memory_space=pltpu.SMEM),
        pl.BlockSpec(memory_space=pltpu.SMEM),
        own(begin),
        own(pairs + begin),
        own(2 * pairs + begin),
        far(begin),
        far(pairs + begin),
        own(begin),
        own(begin),
        pl.BlockSpec((1, 16, tok), lambda i: (begin + i, 0, 0)),
        still((width, tok)),
        still((width, remote)),
        weight(begin),
        weight(pairs + begin),
        weight(2 * pairs + begin),
    ]
    arrays = [flags, core, proj, proj, proj, kv_rem, kv_rem, mixed, d_mixed, lse, act_t, far_t, w_qkv, w_qkv, w_qkv]
    scratch = [
        pltpu.VMEM((128, tok), bf16),
        pltpu.VMEM((128, remote), bf16),
        pltpu.VMEM((tok, 128), f32),
        pltpu.VMEM((tok, 128), f32),
        pltpu.VMEM((remote, 128), f32),
        pltpu.VMEM((remote, 128), f32),
        pltpu.VMEM((tok, 384), bf16),
        pltpu.VMEM((width, 384), bf16),
    ]
    sums = [jax.ShapeDtypeStruct((tok, width), f32), jax.ShapeDtypeStruct((remote, width), f32)]
    aliases = {}
    skip = 0
    if not isinstance(buffers, int):
        aliases = {len(arrays): 0, len(arrays) + 1: 1}
        in_specs += [pl.BlockSpec(memory_space=pl.ANY)] * 2
        arrays += list(buffers)
        skip = 2
        buffers = buffers[0].shape[1]
    if starts:
        in_specs += [still((tok, width)), still((remote, width))]
        arrays += list(starts)
    out_specs = [half, half, still((tok, width))]
    out_shape = [jax.ShapeDtypeStruct((width // 2, buffers), bf16)] * 2 + sums[:1]
    if last:
        out_specs += [still((plen, width))] * (remote // plen)
        out_shape += [jax.ShapeDtypeStruct((plen, width), bf16)] * (remote // plen)
        scratch = scratch + [pltpu.VMEM((remote, width), f32)]
    else:
        out_specs += [still((remote, width))]
        out_shape += sums[1:]
    return pl.pallas_call(
        functools.partial(attention_backward_kernel, plen, bool(starts), last, skip),
        grid=(count,),
        in_specs=in_specs,
        out_specs=out_specs,
        out_shape=out_shape,
        scratch_shapes=scratch,
        input_output_aliases=aliases,
        compiler_params=pltpu.CompilerParams(vmem_limit_bytes=60 * 2**20),
        cost_estimate=pl.CostEstimate(flops=10 * tok * (tok + remote) * count * 128 + 20 * tok * width * count * 128, bytes_accessed=2 * (tok * 8 + remote * 4) * count * 128 + 16 * tok * width, transcendentals=tok * (tok + remote) * 2 * count),
        name="attention_backward",
    )(*arrays)


FFN_EXPERTS = 8
ALL_EXPERTS = 12
EXTRA = 128
SMALL = 8
epsilon = 1e-06


def dot_tn(a, b):
    return lax.dot_general(a, b, (((0,), (0,)), ((), ())), preferred_element_type=f32)


def split_low(value, parts):
    pieces = []
    for _ in range(parts):
        piece = value.astype(bf16)
        pieces.append(piece)
        value = value - piece.astype(f32)
    return pieces


def route_kernel(groups, home_ref, ids_ref, grad_ref, prev_ref, *out_refs):
    tok, width = grad_ref.shape
    count = len(groups)
    turned_refs, chosen_refs, early_ref = out_refs[:count], out_refs[count : 2 * count], out_refs[2 * count]
    expert = lax.broadcasted_iota(jnp.int32, (16, tok), 0)
    names = [ids_ref[k : k + 1, :] == expert for k in range(2)]
    both = jnp.where(names[0] | names[1], 1.0, 0.0).astype(bf16)
    earlier = lax.broadcasted_iota(jnp.int32, (tok, tok), 0) < lax.broadcasted_iota(jnp.int32, (tok, tok), 1)
    before = dot_nn(both, jnp.where(earlier, 1.0, 0.0).astype(bf16))
    pieces = [piece.astype(f32) for piece in split_low(prev_ref[...], 3)]
    extra = (pieces[0] + pltpu.roll(pieces[1], 16, 1) + pltpu.roll(pieces[2], 32, 1)).astype(bf16)
    slot = [jnp.sum(jnp.where(n, before, 0.0), axis=0, keepdims=True).astype(jnp.int32) for n in names]
    for (first, size), turned_ref, chosen_ref in zip(groups, turned_refs, chosen_refs):
        spots = lax.broadcasted_iota(jnp.int32, (FFN_EXPERTS * size, tok), 0)
        hit = None
        for k in range(2):
            ids = ids_ref[k : k + 1, :]
            inside = (ids < FFN_EXPERTS) & (slot[k] >= first) & (slot[k] < first + size)
            place = jnp.where(inside, ids * size + slot[k] - first, -1)
            hit = spots == place if hit is None else hit | (spots == place)
        turned = jnp.where(hit, 1.0, 0.0).astype(bf16)
        turned_ref[...] = turned
        chosen_ref[...] = turned.T
        grads = dot_nn(turned, grad_ref[...]).astype(bf16)
        extras = dot_nn(turned, extra).astype(bf16)
        for e in range(FFN_EXPERTS):
            early_ref[e, first : first + size, 0:width] = grads[e * size : (e + 1) * size]
            early_ref[e, first : first + size, width : width + EXTRA] = extras[e * size : (e + 1) * size]


def route_plan(home, ids, grad, prev, groups):
    tok, width = grad.shape
    counts = [FFN_EXPERTS * size for _, size in groups]
    whole = pl.BlockSpec(memory_space=pltpu.VMEM)
    out = pl.pallas_call(
        functools.partial(route_kernel, groups),
        in_specs=[pl.BlockSpec(memory_space=pltpu.SMEM), whole, whole, whole],
        out_specs=[whole] * (2 * len(groups) + 1),
        out_shape=[jax.ShapeDtypeStruct((n, tok), bf16) for n in counts]
        + [jax.ShapeDtypeStruct((tok, n), bf16) for n in counts]
        + [jax.ShapeDtypeStruct((FFN_EXPERTS, sum(counts) // FFN_EXPERTS, width + EXTRA), bf16)],
        compiler_params=pltpu.CompilerParams(vmem_limit_bytes=60 * 2**20),
        cost_estimate=pl.CostEstimate(flops=2 * sum(counts) * tok * (width + EXTRA), bytes_accessed=4 * sum(counts) * width, transcendentals=0),
        name="route_plan",
    )(home, ids, grad, prev)
    return out[: len(groups)], out[len(groups) : -1], out[-1]


def expert_kernel(group, home_ref, rows_ref, early_ref, router_ref, wg_ref, wu_ref, wd_ref,
                  out_ref, drow_ref, dout_ref, inner_ref, dgate_ref, dup_ref, small_ref, acc_out, acc_row, probs_ref):
    width = rows_ref.shape[1]
    step, steps = pl.program_id(0), pl.num_programs(0)
    home = home_ref[0]
    lane = lax.broadcasted_iota(jnp.int32, (1, EXTRA), 1)
    slots = slice(group[0], group[0] + group[1])

    @pl.when(step == 0)
    def _():
        extra = early_ref[:, slots, width : width + EXTRA].astype(f32).reshape(-1, EXTRA)
        logits = extra + pltpu.roll(extra, EXTRA - 16, 1) + pltpu.roll(extra, EXTRA - 32, 1)
        logits = logits + dot_nn(rows_ref[...], router_ref[...])
        logits = jnp.where(lane < ALL_EXPERTS, logits, NEG)
        unnormed = jnp.exp(logits - jnp.max(logits, axis=1, keepdims=True))
        probs = unnormed / jnp.sum(unnormed, axis=1, keepdims=True)
        probs_ref[...] = probs
        gate = jnp.sum(jnp.where(lane == home, probs, 0.0), axis=1, keepdims=True)
        dout_ref[...] = (gate * early_ref[:, slots, 0:width].astype(f32).reshape(-1, width)).astype(bf16)
        acc_out[...] = jnp.zeros_like(acc_out)
        acc_row[...] = jnp.zeros_like(acc_row)

    rows = rows_ref[...]
    gate_pre = dot_nn(rows, wg_ref[0])
    up_pre = dot_nn(rows, wu_ref[0])
    d_inner = dot_nt(dout_ref[...], wd_ref[0])
    sigmoid = jax.nn.sigmoid(gate_pre)
    silu = gate_pre * sigmoid
    inner = (silu * up_pre).astype(bf16)
    d_gate = (d_inner * up_pre * (sigmoid * (1.0 + gate_pre * (1.0 - sigmoid)))).astype(bf16)
    d_up = (d_inner * silu).astype(bf16)
    inner_ref[...] = inner
    dgate_ref[...] = d_gate
    dup_ref[...] = d_up
    acc_out[...] += dot_nn(inner, wd_ref[0])
    acc_row[...] += dot_nt(d_gate, wg_ref[0]) + dot_nt(d_up, wu_ref[0])

    @pl.when(step == steps - 1)
    def _():
        probs = probs_ref[...]
        gate = jnp.sum(jnp.where(lane == home, probs, 0.0), axis=1, keepdims=True)
        out = acc_out[...].astype(bf16).astype(f32)
        d_row_gate = jnp.sum(out * early_ref[:, slots, 0:width].astype(f32).reshape(-1, width), axis=1, keepdims=True)
        out_ref[:, 0:width] = (gate * out).astype(bf16)
        extra = jnp.zeros((out.shape[0], EXTRA), f32)
        for i, piece in enumerate(split_low(d_row_gate, 3)):
            extra = jnp.where(lane == home + 16 * i, piece.astype(f32), extra)
        out_ref[:, width : width + EXTRA] = extra.astype(bf16)
        term = d_row_gate * gate * (jnp.where(lane == home, 1.0, 0.0) - probs)
        high, rest = split_low(term, 2)
        turned = [piece.T for piece in (high, rest)]
        small_ref[...] = (dot_nn(turned[0], rows) + dot_nn(turned[1], rows))[0 : 2 * SMALL, :]
        drow_ref[...] = (acc_row[...] + dot_nt(high, router_ref[...]) + dot_nt(rest, router_ref[...])).astype(bf16)


def expert_pass(group, home, rows, early, router_pad, w_gate, w_up, w_down):
    count, width = rows.shape
    ff = w_gate.shape[2]
    tile = min(512, ff)
    full = pl.BlockSpec((count, width), lambda j: (0, 0))
    wide = pl.BlockSpec((count, width + EXTRA), lambda j: (0, 0))
    tall = pl.BlockSpec((1, width, tile), lambda j: (0, 0, j))
    piece = pl.BlockSpec((count, tile), lambda j: (0, j))
    return pl.pallas_call(
        functools.partial(expert_kernel, group),
        grid=(ff // tile,),
        in_specs=[
            pl.BlockSpec(memory_space=pltpu.SMEM),
            full,
            pl.BlockSpec(early.shape, lambda j: (0, 0, 0)),
            pl.BlockSpec((width, EXTRA), lambda j: (0, 0)),
            tall,
            tall,
            pl.BlockSpec((1, tile, width), lambda j: (0, j, 0)),
        ],
        out_specs=[wide, full, full, piece, piece, piece, pl.BlockSpec((2 * SMALL, width), lambda j: (0, 0))],
        out_shape=[
            jax.ShapeDtypeStruct((count, width + EXTRA), bf16),
            jax.ShapeDtypeStruct((count, width), bf16),
            jax.ShapeDtypeStruct((count, width), bf16),
        ]
        + [jax.ShapeDtypeStruct((count, ff), bf16)] * 3
        + [jax.ShapeDtypeStruct((2 * SMALL, width), f32)],
        scratch_shapes=[pltpu.VMEM((count, width), f32), pltpu.VMEM((count, width), f32), pltpu.VMEM((count, EXTRA), f32)],
        compiler_params=pltpu.CompilerParams(vmem_limit_bytes=60 * 2**20),
        cost_estimate=pl.CostEstimate(flops=12 * count * width * ff, bytes_accessed=6 * width * ff + 2 * count * (5 * width + 3 * ff), transcendentals=count * ff),
        name="expert_pass",
    )(home, rows, early, router_pad, w_gate, w_up, w_down)


def weight_kernel(count, *refs):
    rows, douts, inners, dgates, dups = (refs[i * count : (i + 1) * count] for i in range(5))
    gate_up_ref, down_ref = refs[5 * count : 5 * count + 2]
    turned = refs[5 * count + 2 :]

    @pl.when(pl.program_id(0) == 0)
    def _():
        for ref, scratch in zip(rows, turned):
            scratch[...] = ref[...].T

    gate_up_ref[0] = sum(dot_nn(t[...], d[...]) for t, d in zip(turned, dgates)).astype(bf16)
    gate_up_ref[1] = sum(dot_nn(t[...], d[...]) for t, d in zip(turned, dups)).astype(bf16)
    down_ref[...] = sum(dot_nn(i[...].T, d[...]) for i, d in zip(inners, douts)).astype(bf16)


def weight_gradients(rows, douts, inners, dgates, dups):
    count = len(rows)
    width, ff = rows[0].shape[1], inners[0].shape[1]
    tile = min(512, ff)
    total = sum(r.shape[0] for r in rows)
    full = [pl.BlockSpec(r.shape, lambda j: (0, 0)) for r in rows]
    piece = [pl.BlockSpec((r.shape[0], tile), lambda j: (0, j)) for r in rows]
    return pl.pallas_call(
        functools.partial(weight_kernel, count),
        grid=(ff // tile,),
        in_specs=full + full + piece * 3,
        out_specs=[pl.BlockSpec((2, width, tile), lambda j: (0, 0, j)), pl.BlockSpec((tile, width), lambda j: (j, 0))],
        out_shape=[jax.ShapeDtypeStruct((2, width, ff), bf16), jax.ShapeDtypeStruct((ff, width), bf16)],
        scratch_shapes=[pltpu.VMEM((width, r.shape[0]), bf16) for r in rows],
        compiler_params=pltpu.CompilerParams(vmem_limit_bytes=60 * 2**20),
        cost_estimate=pl.CostEstimate(flops=6 * total * width * ff, bytes_accessed=6 * width * ff + 2 * total * (2 * width + 3 * ff), transcendentals=0),
        name="weight_gradients",
    )(*rows, *douts, *inners, *dgates, *dups)


ANYWHERE = pl.BlockSpec(memory_space=pltpu.VMEM)
SCALARS = pl.BlockSpec(memory_space=pltpu.SMEM)


def inverse_rms(value):
    return lax.rsqrt(jnp.mean(value * value, axis=1, keepdims=True) + epsilon)


def after_attention_kernel(count, mixed_ref, x_ref, w_ref, gain_ref, *refs):
    turned, (hidden_ref, low_ref), sent = refs[:count], refs[count : count + 2], refs[count + 2 :]
    hidden = x_ref[...].astype(f32) + dot_nn(mixed_ref[...], w_ref[...])
    low = (hidden * inverse_rms(hidden) * gain_ref[...]).astype(bf16)
    hidden_ref[...] = hidden
    low_ref[...] = low
    for t, s in zip(turned, sent):
        s[...] = dot_nn(t[...], low).astype(bf16)


def after_attention(mixed, x, w_out, gain, turned):
    tok, width = x.shape
    rows = sum(t.shape[0] for t in turned)
    out = pl.pallas_call(
        functools.partial(after_attention_kernel, len(turned)),
        in_specs=[ANYWHERE] * (4 + len(turned)),
        out_specs=[ANYWHERE] * (2 + len(turned)),
        out_shape=[jax.ShapeDtypeStruct((tok, width), f32), jax.ShapeDtypeStruct((tok, width), bf16)]
        + [jax.ShapeDtypeStruct((t.shape[0], width), bf16) for t in turned],
        compiler_params=pltpu.CompilerParams(vmem_limit_bytes=60 * 2**20),
        cost_estimate=pl.CostEstimate(flops=2 * tok * width * (width + rows), bytes_accessed=2 * width * (6 * tok + 2 * rows), transcendentals=0),
        name="after_attention",
    )(mixed, x, w_out, gain, *turned)
    return out[0], out[1], out[2:]


def place(value, lane, at):
    return jnp.where(lane == at, value, 0.0)


def local_kernel(hidden_ref, low_ref, grad_ref, prev_ref, ids_ref, mix_ref, gain_ref, vec_ref, out_ref, dnormed_ref, probs_ref, dprobs_ref, small_ref):
    lane = lax.broadcasted_iota(jnp.int32, (1, EXTRA), 1)
    hidden = hidden_ref[...]
    normed = hidden * inverse_rms(hidden) * gain_ref[...]
    low = low_ref[...]
    grad = grad_ref[...].astype(f32)
    raw = dot_nn(low, mix_ref[...])
    logits = jnp.where(lane < ALL_EXPERTS, raw + prev_ref[...], NEG)
    unnormed = jnp.exp(logits - jnp.max(logits, axis=1, keepdims=True))
    probs = unnormed / jnp.sum(unnormed, axis=1, keepdims=True)
    named = (ids_ref[:, 0:1] == lane) | (ids_ref[:, 1:2] == lane)
    gates = jnp.where(named, probs, 0.0)
    copy_gate = gates[:, FFN_EXPERTS + 1 : FFN_EXPERTS + 2]
    dots = jnp.sum(grad * normed, axis=1, keepdims=True)
    out = hidden
    weight = copy_gate
    d_probs = place(dots, lane, FFN_EXPERTS + 1)
    logit_grads = jnp.zeros_like(probs)
    vec_terms = jnp.zeros_like(probs)
    for c in range(2):
        vec = vec_ref[c : c + 1, :]
        gate = gates[:, FFN_EXPERTS + 2 + c : FFN_EXPERTS + 3 + c]
        at = 16 + 2 * c
        a0 = jax.nn.sigmoid(raw[:, at : at + 1] - raw[:, at + 1 : at + 2])
        a1 = jax.nn.sigmoid(raw[:, at + 1 : at + 2] - raw[:, at : at + 1])
        vec_dots = jnp.sum(grad * vec, axis=1, keepdims=True)
        weight = weight + gate * a0
        out = out + (gate * a1) * vec
        d_probs = d_probs + place(a0 * dots + a1 * vec_dots, lane, FFN_EXPERTS + 2 + c)
        d0, d1 = gate * dots, gate * vec_dots
        mean = a0 * d0 + a1 * d1
        d0, d1 = a0 * (d0 - mean), a1 * (d1 - mean)
        logit_grads = logit_grads + place(d0, lane, at) + place(d1, lane, at + 1)
        vec_terms = vec_terms + place(gate * a1, lane, 20 + c)
    d_probs = jnp.where(named, d_probs, 0.0)
    logit_grads = logit_grads + probs * (d_probs - jnp.sum(probs * d_probs, axis=1, keepdims=True))
    high, rest = split_low(logit_grads, 2)
    out_ref[...] = out + weight * normed
    dnormed_ref[...] = weight * grad + dot_nt(high, mix_ref[...]) + dot_nt(rest, mix_ref[...])
    probs_ref[...] = probs
    dprobs_ref[...] = d_probs
    sums = None
    for terms, rows in ((logit_grads, low), (vec_terms, grad_ref[...])):
        for piece in split_low(terms.T, 2):
            part = dot_nn(piece, rows)
            sums = part if sums is None else sums + part
    sums = sums[0 : 3 * SMALL, :]

    @pl.when(pl.program_id(0) == 0)
    def _():
        small_ref[...] = sums

    @pl.when(pl.program_id(0) > 0)
    def _():
        small_ref[...] += sums


def local_part(hidden, low, grad, prev, ids, mix, gain, vec):
    tok, width = hidden.shape
    block, tiles = row_tiles(tok)
    shapes = [(tok, width), (tok, width), (tok, EXTRA), (tok, EXTRA), (3 * SMALL, width)]
    return pl.pallas_call(
        local_kernel,
        grid=(tok // block,),
        in_specs=[tiles(width), tiles(width), tiles(width), tiles(EXTRA), tiles(2), fixed(mix), fixed(gain), fixed(vec)],
        out_specs=[tiles(width), tiles(width), tiles(EXTRA), tiles(EXTRA), pl.BlockSpec((3 * SMALL, width), lambda i: (0, 0))],
        out_shape=[jax.ShapeDtypeStruct(s, f32) for s in shapes],
        compiler_params=pltpu.CompilerParams(vmem_limit_bytes=60 * 2**20),
        cost_estimate=pl.CostEstimate(flops=14 * tok * width * EXTRA, bytes_accessed=16 * tok * width, transcendentals=tok * EXTRA),
        name="local_part",
    )(hidden, low, grad, prev, ids, mix, gain, vec)


def row_tiles(tok):
    block = 256 if tok % 256 == 0 else 128
    return block, lambda columns: pl.BlockSpec((block, columns), lambda i: (i, 0))


def fixed(value):
    return pl.BlockSpec(value.shape, lambda i: (0,) * value.ndim)


def combine_kernel(count, parts, core_ref, *refs):
    chosen, got, refs = refs[:count], refs[count : count * (1 + parts)], refs[count * (1 + parts) :]
    smalls, refs = refs[: count + 1], refs[count + 1 :]
    local_ref, hidden_ref, gain_ref, grad_ref, mixed_ref, w_ref, dhidden_ref, dmixed_ref, mine_ref, theirs_ref, total_w, total_gain, small_t = refs
    step = pl.program_id(0)

    @pl.when(step == 0)
    def _():
        total_w[...] = jnp.zeros_like(total_w)
        total_gain[...] = jnp.zeros_like(total_gain)

    d_normed = local_ref[...]
    for g in range(count):
        for r in range(parts):
            d_normed = d_normed + dot_nn(chosen[g][...], got[g * parts + r][...])
    hidden = hidden_ref[...]
    inverse = inverse_rms(hidden)
    scaled = d_normed * gain_ref[...]
    mean = jnp.mean(scaled * hidden, axis=1, keepdims=True)
    d_hidden = grad_ref[...].astype(f32) + inverse * scaled - hidden * (inverse * inverse * inverse * mean)
    low = d_hidden.astype(bf16)
    dhidden_ref[...] = d_hidden
    dmixed_ref[...] = dot_nt(low, w_ref[...]).astype(bf16)
    total_w[...] += dot_nn(mixed_ref[...].T, low)
    total_gain[...] += jnp.sum(d_normed * hidden * inverse, axis=0, keepdims=True)

    @pl.when(step == pl.num_programs(0) - 1)
    def _():
        width = w_ref.shape[0]
        half = width // 2
        row = lax.broadcasted_iota(jnp.int32, (SMALL, 1), 0)
        top = smalls[0][0 : 2 * SMALL, :]
        for small in smalls[1:]:
            top = top + small[...]
        rest = jnp.zeros((EXTRA - 4 * SMALL, width), f32)
        rows = [top, smalls[0][2 * SMALL : 3 * SMALL, :], jnp.where(row == 0, total_gain[...], 0.0), rest]
        small_t[...] = jnp.concatenate(rows, axis=0).T
        at = mine_ref.shape[1] - width - EXTRA
        for out_ref, which in ((theirs_ref, 1 - core_ref[0]), (mine_ref, core_ref[0])):
            place_rows = pl.ds(pl.multiple_of(which * half, half), half)
            out_ref[:, at : at + width] = total_w[place_rows, :].astype(bf16)
            out_ref[:, at + width : at + width + EXTRA] = small_t[place_rows, :].astype(bf16)


def combine(core, chosen, got, smalls, local, hidden, gain, grad, mixed, w_out, columns):
    tok, width = hidden.shape
    rows = sum(c.shape[1] for c in chosen)
    arrays = [a for group in got for a in group]
    block, tiles = row_tiles(tok)
    half = (width // 2, columns + width + EXTRA)
    return pl.pallas_call(
        functools.partial(combine_kernel, len(chosen), len(got[0])),
        grid=(tok // block,),
        in_specs=[SCALARS] + [tiles(c.shape[1]) for c in chosen] + [fixed(a) for a in arrays + smalls]
        + [tiles(width), tiles(width), fixed(gain), tiles(width), tiles(width), fixed(w_out)],
        out_specs=[tiles(width)] * 2 + [pl.BlockSpec(half, lambda i: (0, 0))] * 2,
        out_shape=[jax.ShapeDtypeStruct((tok, width), f32), jax.ShapeDtypeStruct((tok, width), bf16)] + [jax.ShapeDtypeStruct(half, bf16)] * 2,
        scratch_shapes=[pltpu.VMEM((width, width), f32), pltpu.VMEM((1, width), f32), pltpu.VMEM((width, EXTRA), f32)],
        compiler_params=pltpu.CompilerParams(vmem_limit_bytes=60 * 2**20),
        cost_estimate=pl.CostEstimate(flops=2 * tok * width * (rows + 2 * width), bytes_accessed=2 * width * (10 * tok + 2 * rows), transcendentals=0),
        name="combine_gradients",
    )(core, *chosen, *arrays, *smalls, local, hidden, gain, grad, mixed, w_out)


def flat_rows(value):
    if value.shape[1] % 16:
        return value.astype(f32).reshape(-1, value.shape[2]).astype(bf16)
    return value.reshape(-1, value.shape[2])


def finish_kernel(groups, parts, *refs):
    chosen, got = refs[: len(groups)], refs[len(groups) : len(groups) + parts]
    local_ref, probs_ref, dprobs_ref, out_ref, dlogits_ref = refs[len(groups) + parts :]
    width = local_ref.shape[1]
    lane = lax.broadcasted_iota(jnp.int32, (1, EXTRA), 1)
    picked = None
    for c, (at, size) in zip(chosen, groups):
        for r in range(parts):
            part = dot_nn(c[...], flat_rows(got[r][:, at : at + size, :]))
            picked = part if picked is None else picked + part
    out_ref[...] = (local_ref[...] + picked[:, 0:width]).astype(bf16)
    extra = picked[:, width : width + EXTRA]
    extra = extra + pltpu.roll(extra, EXTRA - 16, 1) + pltpu.roll(extra, EXTRA - 32, 1)
    d_probs = dprobs_ref[...] + jnp.where(lane < ALL_EXPERTS, extra, 0.0)
    probs = probs_ref[...]
    d_logits = probs * (d_probs - jnp.sum(probs * d_probs, axis=1, keepdims=True))
    dlogits_ref[...] = d_logits.T


def finish(chosen, got, groups, local, probs, d_probs):
    tok, width = local.shape
    block, tiles = row_tiles(tok)
    return pl.pallas_call(
        functools.partial(finish_kernel, groups, len(got)),
        grid=(tok // block,),
        in_specs=[tiles(c.shape[1]) for c in chosen] + [fixed(g) for g in got] + [tiles(width), tiles(EXTRA), tiles(EXTRA)],
        out_specs=[tiles(width), pl.BlockSpec((EXTRA, block), lambda i: (0, i))],
        out_shape=[jax.ShapeDtypeStruct((tok, width), bf16), jax.ShapeDtypeStruct((EXTRA, tok), f32)],
        compiler_params=pltpu.CompilerParams(vmem_limit_bytes=60 * 2**20),
        cost_estimate=pl.CostEstimate(flops=2 * tok * 1152 * (width + EXTRA), bytes_accessed=16 * tok * width, transcendentals=0),
        name="finish_outputs",
    )(*chosen, *got, local, probs, d_probs)


def input_kernel(dact_ref, x_ref, gain_ref, dhidden_ref, *refs):
    out_ref = refs[-1]
    far = refs[0][...].astype(f32)
    for ref in refs[1:-1]:
        far = far + ref[...].astype(f32)
    x = x_ref[...].astype(f32)
    inverse = inverse_rms(x)
    scaled = (dact_ref[...] + jnp.where(pl.program_id(0) == 0, far, 0.0)) * gain_ref[...]
    mean = jnp.mean(scaled * x, axis=1, keepdims=True)
    out_ref[...] = dhidden_ref[...] + inverse * scaled - x * (inverse * inverse * inverse * mean)


def input_gradient(d_act, x, gain, d_hidden, far):
    tok, width = x.shape
    block = far[0].shape[0]
    tiles = pl.BlockSpec((block, width), lambda i: (i, 0))
    return pl.pallas_call(
        input_kernel,
        grid=(tok // block,),
        in_specs=[tiles, tiles, fixed(gain), tiles] + [fixed(f) for f in far],
        out_specs=tiles,
        out_shape=jax.ShapeDtypeStruct((tok, width), f32),
        compiler_params=pltpu.CompilerParams(vmem_limit_bytes=60 * 2**20),
        cost_estimate=pl.CostEstimate(flops=12 * tok * width, bytes_accessed=16 * tok * width, transcendentals=0),
        name="input_gradient",
    )(d_act, x, gain, d_hidden, *far)


def xor_pairs(size, mask):
    return [(i, i ^ mask) for i in range(size)]


def sum_kernel(terms, index_ref, *refs):
    count = len(refs) // (sum(terms) + 1)
    outs = refs[-count:]
    for k, out_ref in enumerate(outs):
        at = 0
        first = 0
        for number in terms:
            total = None
            for t in range(first, first + number):
                value = refs[t * count + k][0].astype(f32)
                total = value if total is None else total + value
            out_ref[0, :, at : at + total.shape[1]] = total.astype(bf16)
            at += total.shape[1]
            first += number


def sum_pieces(index, groups):
    arrays = [a for group in groups for a in group]
    n, rows = arrays[0].shape[:2]
    columns = sum(group[0].shape[2] for group in groups)
    view = lambda a, k: pl.BlockSpec((1, rows, a.shape[2]), lambda i, s: (s[0] ^ k if n > 1 else 0, 0, 0))
    return pl.pallas_call(
        functools.partial(sum_kernel, [len(g) for g in groups]),
        grid_spec=pltpu.PrefetchScalarGridSpec(
            num_scalar_prefetch=1,
            grid=(1,),
            in_specs=[view(a, k) for a in arrays for k in range(n)],
            out_specs=[pl.BlockSpec((1, rows, columns), lambda i, s: (0, 0, 0))] * n,
        ),
        out_shape=[jax.ShapeDtypeStruct((1, rows, columns), bf16)] * n,
        compiler_params=pltpu.CompilerParams(vmem_limit_bytes=60 * 2**20),
        cost_estimate=pl.CostEstimate(flops=0, bytes_accessed=2 * n * rows * columns * 5, transcendentals=0),
        name="sum_pieces",
    )(index, *[a for a in arrays for _ in range(n)])


def quarters(value):
    return value.reshape(4, -1, value.shape[-1])


def swap(pieces, along):
    axis, size, unit = along
    return [pieces[0]] + [lax.ppermute(pieces[k], axis, xor_pairs(size, unit * k)) for k in range(1, 4)]


def spread(value, along):
    return swap([value] * 4, along)


def stack_kernel(*refs):
    n = len(refs) - 1
    size = refs[0].shape[0]
    for k in range(n):
        refs[n][k * size : (k + 1) * size] = refs[k][...]


def stack_pieces(pieces):
    shape = (len(pieces) * pieces[0].shape[0],) + pieces[0].shape[1:]
    return pl.pallas_call(
        stack_kernel,
        in_specs=[ANYWHERE] * len(pieces),
        out_specs=ANYWHERE,
        out_shape=jax.ShapeDtypeStruct(shape, bf16),
        compiler_params=pltpu.CompilerParams(vmem_limit_bytes=60 * 2**20),
        cost_estimate=pl.CostEstimate(flops=0, bytes_accessed=4 * math.prod(shape), transcendentals=0),
        name="stack_pieces",
    )(*pieces)


def unpack_kernel(left, index_ref, own_ref, other_ref, w_ref, out_ref, qkv_ref, turned_ref, small):
    width = out_ref.shape[1]
    piece = own_ref.shape[2]
    mine = pl.program_id(0) == index_ref[0]
    lane = lax.broadcasted_iota(jnp.int32, (1, EXTRA), 1)
    block = pl.program_id(0) * 4 + pl.program_id(1)
    for k in range(4):
        rows = slice(k * piece, (k + 1) * piece)
        at_ctx = k ^ index_ref[1]
        total = jnp.where(mine, own_ref[at_ctx, 0, :, :], other_ref[at_ctx, 0, :, :]).astype(f32)
        out_ref[rows, :] = total[:, left : left + width]
        gain = None
        for p in range(3):
            for i in range(width // 128):
                at = i * 384 + p * 128 + (0 if i * 384 < left else width + EXTRA)
                value = total[:, at : at + 128]
                columns = slice(p * width + i * 128, p * width + (i + 1) * 128)
                qkv_ref[rows, columns] = value
                part = value * w_ref[rows, columns].astype(f32)
                gain = part if gain is None else gain + part
        gain = jnp.sum(gain, axis=1, keepdims=True)
        small[pl.ds(block * 4 * piece + k * piece, piece), :] = total[:, left + width : left + width + EXTRA] + place(gain, lane, EXTRA - 1)

    @pl.when(block == 7)
    def _():
        turned_ref[...] = small[...].T


def unpack(index, own, other, w_qkv, left):
    width = w_qkv.shape[0]
    piece = width // 32
    block = 4 * piece
    own, other = own.reshape(4, 4, piece, -1), other.reshape(4, 4, piece, -1)
    row = lambda c, a, s: (c * 4 + a, 0)
    source = pl.BlockSpec((4, 1, piece, own.shape[3]), lambda c, a, s: (0, a ^ s[2], 0, 0))
    return pl.pallas_call(
        functools.partial(unpack_kernel, left),
        grid_spec=pltpu.PrefetchScalarGridSpec(
            num_scalar_prefetch=1,
            grid=(2, 4),
            in_specs=[source, source, pl.BlockSpec((block, 3 * width), row)],
            out_specs=[pl.BlockSpec((block, width), row), pl.BlockSpec((block, 3 * width), row), pl.BlockSpec((EXTRA, width), lambda c, a, s: (0, 0))],
            scratch_shapes=[pltpu.VMEM((width, EXTRA), f32)],
        ),
        out_shape=[jax.ShapeDtypeStruct((width, width), f32), jax.ShapeDtypeStruct((width, 3 * width), f32), jax.ShapeDtypeStruct((EXTRA, width), f32)],
        compiler_params=pltpu.CompilerParams(vmem_limit_bytes=60 * 2**20),
        cost_estimate=pl.CostEstimate(flops=0, bytes_accessed=36 * width * width, transcendentals=0),
        name="unpack_sums",
    )(index, own, other, w_qkv)

P = jax.sharding.PartitionSpec


def rms_inverse(tensor):
    return lax.rsqrt(jnp.mean(tensor * tensor, axis=-1, keepdims=True) + epsilon)


def after(values, *others):
    return lax.optimization_barrier((values, others))[0]


def body(inputs, prev_logits, routes, attn_gain, w_qkv, w_out, moe_gain, router, const_gate, const_vec, w_gate, w_up, w_down, out_grad):
    n_ctx, n_exp = lax.axis_size("ctx"), lax.axis_size("exp")
    me_c, me_e = lax.axis_index("ctx"), lax.axis_index("exp")
    tok, width = inputs.shape[1], inputs.shape[2]
    plen = tok - CONT_LEN
    split = n_exp // FFN_EXPERTS
    capacity = max(4, tok // 64 * 12)
    first = -(-capacity // 32) * 16
    groups = ((0, first), (first, capacity - first))
    home = (me_e // split).reshape(1)

    def deal(value):
        value = jnp.repeat(value, split, axis=0) if split > 1 else value
        return lax.all_to_all(value, "exp", 0, 0, tiled=True)

    def give_back(value):
        value = lax.all_to_all(value, "exp", 0, 0, tiled=True)
        return [value[r::split] if split > 1 else value for r in range(split)]

    x_low = inputs[0]
    x_prompt, upstream_low = lax.optimization_barrier((x_low[:plen], out_grad[0]))
    far_rows = jnp.concatenate([lax.ppermute(x_prompt, "ctx", xor_pairs(n_ctx, k)) for k in range(1, n_ctx)], axis=0)
    flags = jnp.where((me_c ^ jnp.arange(1, n_ctx)) < me_c, 0.0, NEG).astype(f32)

    prev = jnp.pad(prev_logits[0], ((0, 0), (0, EXTRA - ALL_EXPERTS)))
    mix = jnp.concatenate([router, jnp.zeros((width, 4), bf16), const_gate[0], const_gate[1], jnp.zeros((width, EXTRA - 20), bf16)], axis=1)
    router_pad = jnp.pad(router, ((0, 0), (0, EXTRA - ALL_EXPERTS)))
    turned, chosen, early_sent = route_plan(home, routes[0].T, upstream_low, prev, groups)

    tokens_in = x_low.astype(f32)
    inverse_attn = rms_inverse(tokens_in)
    act_low = (tokens_in * inverse_attn * attn_gain).astype(bf16)
    projected = dot_nn(act_low, w_qkv).astype(bf16)
    early = deal(early_sent)
    far_in = after(far_rows, projected).astype(f32)
    act_far = (far_in * rms_inverse(far_in) * attn_gain).astype(bf16)
    kv_far = dot_nn(act_far, w_qkv[:, width:]).astype(bf16)

    mixed_low, lse = attention_forward(flags, projected, kv_far, plen)
    mixed_low, early = lax.optimization_barrier((mixed_low, early))
    hidden, moe_low, sent = after_attention(mixed_low, x_low, w_out, moe_gain[None], turned)
    local_out, d_normed_local, probs, d_probs, small_local = local_part(hidden, moe_low, upstream_low, prev, routes[0], mix, moe_gain[None], const_vec)
    act_t, far_t = act_low.T, act_far.T
    sent = [after(sent[0], local_out, d_normed_local, act_t, far_t), sent[1]]
    got = [deal(part.reshape(FFN_EXPERTS, -1, width)) for part in sent]

    got = [part.reshape(-1, width) for part in got]
    passes = [expert_pass(group, home, r, early, router_pad, w_gate, w_up, w_down) for group, r in zip(groups, got)]
    d_got = [give_back(p[1].reshape(n_exp, -1, width)) for p in passes]
    gate_up_low, down_low = weight_gradients(got, [p[2] for p in passes], [p[3] for p in passes], [p[4] for p in passes], [p[5] for p in passes])
    outs = jnp.concatenate([p[0].reshape(n_exp, -1, width + EXTRA) for p in passes], axis=1)
    d_got, gate_up_low, down_low, outs = lax.optimization_barrier((d_got, gate_up_low, down_low, outs))
    out_got = give_back(outs)

    d_got = [[part.reshape(-1, width) for part in group] for group in d_got]
    pairs = width // 128
    cut = pairs // 3
    core = (me_e & 1).reshape(1)
    smalls = [small_local] + [p[6] for p in passes]
    d_hidden, d_mixed, *buffers = combine(core, chosen, d_got, smalls, d_normed_local, hidden, moe_gain[None], upstream_low, mixed_low, w_out, cut * 384)

    sum_gate_up = lax.psum_scatter(gate_up_low, "ctx", scatter_dimension=1, tiled=True).astype(f32)
    sum_down = lax.psum_scatter(down_low, "ctx", scatter_dimension=0, tiled=True).astype(f32)

    def attention(upstream, begin, count, buffers, at, starts, last):
        return attention_backward(flags, core, projected, kv_far, mixed_low, upstream, lse, act_t, far_t, w_qkv, plen, begin, count, buffers, at, starts, last)

    dense = n_ctx == 4 and n_exp == 8
    left, right = cut * 384, (pairs - cut) * 384
    z = me_e >> 1
    at_ctx, at_z = me_c.reshape(1), z.reshape(1)
    along_ctx, along_z = ("ctx", 4, 1), ("exp", 8, 2)
    across = lambda value: lax.ppermute(value, "exp", xor_pairs(n_exp, 1))
    mine_1, theirs_1, *starts = attention(d_mixed, 0, cut, buffers, 0, None, False)
    if dense:
        got_1 = across(theirs_1)
    mine_2, theirs_2, *starts = attention(d_mixed, cut, 1, right, 0, starts, False)
    if dense:
        mine_2, theirs_2, starts, got_1 = lax.optimization_barrier((mine_2, theirs_2, starts, got_1))
        sums_1 = sum_pieces(at_z, [[quarters(mine_1), quarters(got_1)]])
        parts_1 = swap(sums_1, along_z)
        mine_2 = after(mine_2, sums_1[0])
    mine_2, theirs_2, d_act, *d_far = attention(d_mixed, cut + 1, pairs - cut - 1, (mine_2, theirs_2), 1, starts, True)
    if dense:
        mine_2, theirs_2, d_act, d_far, parts_1 = lax.optimization_barrier((mine_2, theirs_2, d_act, d_far, parts_1))
    far_back = [lax.ppermute(d_far[k - 1], "ctx", xor_pairs(n_ctx, k)) for k in range(1, n_ctx)]
    if dense:
        got_2 = across(theirs_2)
        mixed_out, d_logits = finish(chosen, out_got, groups, after(local_out, d_act), probs, d_probs)
        mixed_out, d_logits, got_2 = lax.optimization_barrier((mixed_out, d_logits, got_2))
        sums_2 = sum_pieces(at_z, [[quarters(mine_2), quarters(got_2)]])
        parts_2 = swap(sums_2, along_z)
    else:
        mixed_out, d_logits = finish(chosen, out_got, groups, local_out, probs, d_probs)
    d_inputs = input_gradient(d_act, x_low, attn_gain[None], d_hidden, far_back)

    total_gate, total_up, total_down = sum_gate_up[0][None], sum_gate_up[1][None], sum_down[None]
    if dense:
        parts_1, parts_2 = ([quarters(p) for p in parts] for parts in (parts_1, after(parts_2, d_inputs)))
        parts = swap(sum_pieces(at_ctx, [parts_1, parts_2]), along_ctx)
        [piece] = sum_pieces(at_ctx, [parts])
        column = stack_pieces(spread(piece, along_z))
        own = stack_pieces(after(spread(column, along_ctx), total_gate, total_up, total_down))
        other = across(own)
        out_sum, qkv_sum, small = unpack(jnp.stack([core[0], me_c, z]), own, other, w_qkv, left)
        d_attn_gain = small[EXTRA - 1]
    else:
        whole = lambda mine, theirs: jnp.where(core == 0, jnp.concatenate([mine, theirs], axis=0), jnp.concatenate([theirs, mine], axis=0))
        total_1, total_2 = [v.astype(f32) for v in lax.psum((whole(mine_1, theirs_1), whole(mine_2, theirs_2)), ("ctx", "exp"))]
        columns = jnp.concatenate([total_1[:, :left], total_2], axis=1).reshape(width, pairs, 3, 128)
        qkv_sum = columns.transpose(0, 2, 1, 3).reshape(width, 3 * width)
        out_sum, small = total_1[:, left : left + width], total_1[:, left + width :].T
        d_attn_gain = jnp.sum(qkv_sum * w_qkv.astype(f32), axis=1)
    d_attn_gain = d_attn_gain / attn_gain
    at = 2 * SMALL
    d_const_gate = jnp.stack([small[at : at + 2].T, small[at + 2 : at + 4].T])
    return (
        mixed_out[None],
        d_inputs[None],
        d_logits[:ALL_EXPERTS].T[None],
        d_attn_gain,
        qkv_sum,
        out_sum,
        small[at + SMALL],
        small[:ALL_EXPERTS].T,
        d_const_gate,
        small[at + 4 : at + 6],
        total_gate,
        total_up,
        total_down,
    )


def solution(mesh):
    rows = P("ctx", "exp", None)
    expert = P("exp", None, None)
    summed = P("exp", "ctx", None)
    return jax.shard_map(
        body,
        mesh=mesh,
        in_specs=(rows, rows, rows, P(), P(), P(), P(), P(), P(), P(), expert, expert, expert, rows),
        out_specs=(rows, rows, rows, P(), P(), P(), P(), P(), P(), P(), summed, summed, summed),
        check_vma=False,
    )
```

```python
import functools, math
import jax, jax.numpy as jnp
from jax import lax
from jax.experimental import pallas as pl
from jax.experimental.pallas import tpu as pltpu

HEADS = 12
HEAD_DIM = 64
CONT_LEN = 512
LOG2E = 1.4426950408889634
SCALE = HEAD_DIM ** -0.5
bf16 = jnp.bfloat16
f32 = jnp.float32
NEG = -1e30


def dot_nt(a, b):
    return lax.dot_general(a, b, (((1,), (1,)), ((), ())), preferred_element_type=f32)


def dot_nn(a, b):
    return jnp.dot(a, b, preferred_element_type=f32)


def query_tiles(tok, plen):
    tiles = [(0, plen, True)]
    step = 256
    for start in range(plen, tok, step):
        tiles.append((start, step, False))
    return tiles


def split_high(value):
    high = value.astype(bf16)
    return high, (value - high.astype(f32)).astype(bf16)


def both_halves(value, head, low_half):
    turned = pltpu.roll(value, HEAD_DIM, 1)
    return jnp.where(low_half, value, turned) if head == 0 else jnp.where(low_half, turned, value)


def scaled_queries(value, head, low_half):
    high, rest = split_high(value.astype(f32) * (SCALE * LOG2E))
    rest = pltpu.roll(rest, HEAD_DIM, 1)
    return jnp.where(low_half, high, rest) if head == 0 else jnp.where(low_half, rest, high)


def attention_forward_kernel(plen, flags_ref, q_ref, k_ref, v_ref, kr_ref, vr_ref, o_ref, lse_ref, kd, krd, vd, vrd):
    tok = q_ref.shape[0]
    remote = kr_ref.shape[0]
    low_half = lax.broadcasted_iota(jnp.int32, (1, 128), 1) < HEAD_DIM
    one = jnp.ones((), bf16)
    for head in range(2):
        mine = low_half if head == 0 else ~low_half
        kd[head] = both_halves(k_ref[...], head, low_half)
        krd[head] = both_halves(kr_ref[...], head, low_half)
        vd[head] = jnp.where(mine, v_ref[...], one)
        vrd[head] = jnp.where(mine, vr_ref[...], one)
    for start, size, is_prompt in query_tiles(tok, plen):
        row = lax.broadcasted_iota(jnp.int32, (size, size), 0)
        col = lax.broadcasted_iota(jnp.int32, (size, size), 1)
        queries = q_ref[start : start + size, :]
        units = []
        for head in range(2):
            qh = scaled_queries(queries, head, low_half)
            pieces = []
            diag = dot_nt(qh, kd[head, start : start + size, :])
            pieces.append((jnp.where(col <= row, diag, NEG), vd, start, size))
            if is_prompt:
                for j in range(remote // plen):
                    s = dot_nt(qh, krd[head, j * plen : (j + 1) * plen, :])
                    pieces.append((s + flags_ref[j], vrd, j * plen, plen))
            else:
                s = dot_nt(qh, kd[head, 0:start, :])
                pieces.append((s, vd, 0, start))
                s = dot_nt(qh, krd[head])
                pieces.append((s, vrd, 0, remote))
            units.append(pieces)
        accs, peaks = [], []
        for head, pieces in enumerate(units):
            peak = None
            for s, _, _, _ in pieces:
                m = jnp.max(s, axis=1, keepdims=True)
                peak = m if peak is None else jnp.maximum(peak, m)
            acc = None
            for s, ref, at, n in pieces:
                p = jnp.exp2(s - peak).astype(bf16)
                part = dot_nn(p, ref[head, at : at + n, :])
                acc = part if acc is None else acc + part
            accs.append(acc)
            peaks.append(peak)
        num = jnp.where(low_half, accs[0], accs[1])
        den = pltpu.roll(jnp.where(low_half, accs[1], accs[0]), HEAD_DIM, 1)
        o_ref[start : start + size, :] = (num / den).astype(bf16)
        turned = (jnp.where(low_half, peaks[0], peaks[1]) + jnp.log2(den)).T
        lse_ref[0, 0:8, start : start + size] = turned[0:8, :]
        lse_ref[0, 8:16, start : start + size] = turned[HEAD_DIM : HEAD_DIM + 8, :]


def attention_forward(flags, proj, kv_rem, plen):
    tok, width = proj.shape[0], proj.shape[1] // 3
    remote = kv_rem.shape[0]
    pairs = width // 128
    return pl.pallas_call(
        functools.partial(attention_forward_kernel, plen),
        grid=(pairs,),
        in_specs=[
            pl.BlockSpec(memory_space=pltpu.SMEM),
            pl.BlockSpec((tok, 128), lambda i: (0, i)),
            pl.BlockSpec((tok, 128), lambda i: (0, pairs + i)),
            pl.BlockSpec((tok, 128), lambda i: (0, 2 * pairs + i)),
            pl.BlockSpec((remote, 128), lambda i: (0, i)),
            pl.BlockSpec((remote, 128), lambda i: (0, pairs + i)),
        ],
        out_specs=[
            pl.BlockSpec((tok, 128), lambda i: (0, i)),
            pl.BlockSpec((1, 16, tok), lambda i: (i, 0, 0)),
        ],
        out_shape=[
            jax.ShapeDtypeStruct((tok, width), bf16),
            jax.ShapeDtypeStruct((pairs, 16, tok), f32),
        ],
        scratch_shapes=[pltpu.VMEM((2, n, 128), bf16) for n in (tok, remote, tok, remote)],
        compiler_params=pltpu.CompilerParams(vmem_limit_bytes=60 * 2**20),
        cost_estimate=pl.CostEstimate(flops=4 * tok * (tok + remote) * width, bytes_accessed=2 * (tok * 4 + remote * 2) * width, transcendentals=tok * (tok + remote) * HEADS),
        name="attention_forward",
    )(flags, proj, proj, proj, kv_rem, kv_rem)


def attention_backward_kernel(plen, started, last, skip, flags_ref, core_ref, q_ref, k_ref, v_ref, kr_ref, vr_ref, o_ref, do_ref, lse_ref, act_ref, far_ref, wq_ref, wk_ref, wv_ref, *refs):
    refs = refs[skip:]
    if started:
        start_act_ref, start_far_ref, *refs = refs
    mine_ref, theirs_ref, dact_ref, *refs = refs
    dfar_ref, *dfar_refs = (refs[-1:] + refs[:-11]) if last else refs[:1]
    kt, krt, dka, dva, dkra, dvra, own_grads, weights, kd, krd = refs[-11:-1] if last else refs[-10:]
    tok = q_ref.shape[0]
    remote = kr_ref.shape[0]
    lane = lax.broadcasted_iota(jnp.int32, (1, 128), 1)
    low_half = lane < HEAD_DIM
    c = SCALE * LOG2E
    zero = jnp.zeros((), bf16)
    for head in range(2):
        kd[head] = both_halves(k_ref[...], head, low_half)
        krd[head] = both_halves(kr_ref[...], head, low_half)
    kt[...] = k_ref[...].T
    krt[...] = kr_ref[...].T
    dka[...] = jnp.zeros_like(dka)
    dva[...] = jnp.zeros_like(dva)
    dkra[...] = jnp.zeros_like(dkra)
    dvra[...] = jnp.zeros_like(dvra)
    pick = lax.broadcasted_iota(jnp.int32, (16, 128), 0) // 8 == lax.broadcasted_iota(jnp.int32, (16, 128), 1) // HEAD_DIM
    pick = jnp.where(pick, 1.0, 0.0).astype(bf16)
    for start, size, is_prompt in query_tiles(tok, plen):
        rows = slice(start, start + size)
        product = do_ref[rows, :].astype(f32) * o_ref[rows, :].astype(f32)
        high = product.astype(bf16)
        rest = (product - high.astype(f32)).astype(bf16)
        delta = dot_nt(pick, high) + dot_nt(pick, rest)
        totals = [None, None]
        masks = [low_half, ~low_half]
        qh = [jnp.where(m, q_ref[rows, :], zero) for m in masks]
        qs = [scaled_queries(q_ref[rows, :], head, low_half) for head in range(2)]
        doh = [jnp.where(m, do_ref[rows, :], zero) for m in masks]
        segments = [(kd, v_ref, kt, dka, dva, start, size, "diag")]
        if is_prompt:
            for j in range(remote // plen):
                segments.append((krd, vr_ref, krt, dkra, dvra, j * plen, plen, j))
        else:
            segments.append((kd, v_ref, kt, dka, dva, 0, start, None))
            segments.append((krd, vr_ref, krt, dkra, dvra, 0, remote, None))
        for kk, vv, tt, dk_acc, dv_acc, at, n, mode in segments:
            keys = slice(at, at + n)
            scores = [dot_nt(kk[head, keys, :], qs[head]) for head in range(2)]
            d_probs = [dot_nt(vv[keys, :], doh[head]) for head in range(2)]
            low_p, low_d = [], []
            for head in range(2):
                st = scores[head] - lse_ref[0, 8 * head : 8 * head + 1, rows]
                if mode == "diag":
                    key = lax.broadcasted_iota(jnp.int32, (n, size), 0)
                    query = lax.broadcasted_iota(jnp.int32, (n, size), 1)
                    st = jnp.where(key <= query, st, NEG)
                elif mode is not None:
                    st = st + flags_ref[mode]
                pt = jnp.exp2(st)
                low_p.append(pt.astype(bf16))
                low_d.append((pt * (d_probs[head] - delta[8 * head : 8 * head + 1, :])).astype(bf16))
            dv_acc[keys, :] += dot_nn(low_p[0], doh[0]) + dot_nn(low_p[1], doh[1])
            dk_acc[keys, :] += dot_nn(low_d[0], qh[0]) + dot_nn(low_d[1], qh[1])
            for head in range(2):
                part = dot_nn(tt[head * HEAD_DIM : (head + 1) * HEAD_DIM, keys], low_d[head])
                totals[head] = part if totals[head] is None else totals[head] + part
        dqt = totals
        own_grads[rows, 0:128] = (jnp.concatenate(dqt, axis=0).T * SCALE).astype(bf16)
    own_grads[:, 128:256] = (dka[...] * SCALE).astype(bf16)
    own_grads[:, 256:384] = dva[...].astype(bf16)
    far_grads = jnp.concatenate([(dkra[...] * SCALE).astype(bf16), dvra[...].astype(bf16)], axis=1)
    weights[:, 0:128] = wq_ref[...]
    weights[:, 128:256] = wk_ref[...]
    weights[:, 256:384] = wv_ref[...]
    half = mine_ref.shape[0]
    for out_ref, which in ((theirs_ref, 1 - core_ref[0]), (mine_ref, core_ref[0])):
        rows = pl.ds(pl.multiple_of(which * half, half), half)
        total = dot_nn(act_ref[rows, :], own_grads[...])
        out_ref[:, 0:128] = total[:, 0:128].astype(bf16)
        out_ref[:, 128:384] = (total[:, 128:384] + dot_nn(far_ref[rows, :], far_grads)).astype(bf16)
    d_act = dot_nt(own_grads[...], weights[...])
    d_far = dot_nt(far_grads, weights[:, 128:384])
    step = pl.program_id(0)

    @pl.when(step == 0)
    def _():
        dact_ref[...] = d_act + start_act_ref[...] if started else d_act
        dfar_ref[...] = d_far + start_far_ref[...] if started else d_far

    @pl.when(step > 0)
    def _():
        dact_ref[...] += d_act
        dfar_ref[...] += d_far

    if last:

        @pl.when(step == pl.num_programs(0) - 1)
        def _():
            for k, ref in enumerate(dfar_refs):
                ref[...] = dfar_ref[k * plen : (k + 1) * plen, :].astype(bf16)


def attention_backward(flags, core, proj, kv_rem, mixed, d_mixed, lse, act_t, far_t, w_qkv, plen, begin, count, buffers, at, starts, last):
    tok, width = mixed.shape
    remote = kv_rem.shape[0]
    pairs = width // 128
    own = lambda shift: pl.BlockSpec((tok, 128), lambda i: (0, shift + i))
    far = lambda shift: pl.BlockSpec((remote, 128), lambda i: (0, shift + i))
    weight = lambda shift: pl.BlockSpec((width, 128), lambda i: (0, shift + i))
    still = lambda shape: pl.BlockSpec(shape, lambda i: (0, 0))
    half = pl.BlockSpec((width // 2, 384), lambda i: (0, at + i))
    in_specs = [
        pl.BlockSpec(memory_space=pltpu.SMEM),
        pl.BlockSpec(memory_space=pltpu.SMEM),
        own(begin),
        own(pairs + begin),
        own(2 * pairs + begin),
        far(begin),
        far(pairs + begin),
        own(begin),
        own(begin),
        pl.BlockSpec((1, 16, tok), lambda i: (begin + i, 0, 0)),
        still((width, tok)),
        still((width, remote)),
        weight(begin),
        weight(pairs + begin),
        weight(2 * pairs + begin),
    ]
    arrays = [flags, core, proj, proj, proj, kv_rem, kv_rem, mixed, d_mixed, lse, act_t, far_t, w_qkv, w_qkv, w_qkv]
    scratch = [
        pltpu.VMEM((128, tok), bf16),
        pltpu.VMEM((128, remote), bf16),
        pltpu.VMEM((tok, 128), f32),
        pltpu.VMEM((tok, 128), f32),
        pltpu.VMEM((remote, 128), f32),
        pltpu.VMEM((remote, 128), f32),
        pltpu.VMEM((tok, 384), bf16),
        pltpu.VMEM((width, 384), bf16),
        pltpu.VMEM((2, tok, 128), bf16),
        pltpu.VMEM((2, remote, 128), bf16),
    ]
    sums = [jax.ShapeDtypeStruct((tok, width), f32), jax.ShapeDtypeStruct((remote, width), f32)]
    aliases = {}
    skip = 0
    if not isinstance(buffers, int):
        aliases = {len(arrays): 0, len(arrays) + 1: 1}
        in_specs += [pl.BlockSpec(memory_space=pl.ANY)] * 2
        arrays += list(buffers)
        skip = 2
        buffers = buffers[0].shape[1]
    if starts:
        in_specs += [still((tok, width)), still((remote, width))]
        arrays += list(starts)
    out_specs = [half, half, still((tok, width))]
    out_shape = [jax.ShapeDtypeStruct((width // 2, buffers), bf16)] * 2 + sums[:1]
    if last:
        out_specs += [still((plen, width))] * (remote // plen)
        out_shape += [jax.ShapeDtypeStruct((plen, width), bf16)] * (remote // plen)
        scratch = scratch + [pltpu.VMEM((remote, width), f32)]
    else:
        out_specs += [still((remote, width))]
        out_shape += sums[1:]
    return pl.pallas_call(
        functools.partial(attention_backward_kernel, plen, bool(starts), last, skip),
        grid=(count,),
        in_specs=in_specs,
        out_specs=out_specs,
        out_shape=out_shape,
        scratch_shapes=scratch,
        input_output_aliases=aliases,
        compiler_params=pltpu.CompilerParams(vmem_limit_bytes=60 * 2**20),
        cost_estimate=pl.CostEstimate(flops=10 * tok * (tok + remote) * count * 128 + 20 * tok * width * count * 128, bytes_accessed=2 * (tok * 8 + remote * 4) * count * 128 + 16 * tok * width, transcendentals=tok * (tok + remote) * 2 * count),
        name="attention_backward",
    )(*arrays)


FFN_EXPERTS = 8
ALL_EXPERTS = 12
EXTRA = 128
SMALL = 8
epsilon = 1e-06


def dot_tn(a, b):
    return lax.dot_general(a, b, (((0,), (0,)), ((), ())), preferred_element_type=f32)


def split_low(value, parts):
    pieces = []
    for _ in range(parts):
        piece = value.astype(bf16)
        pieces.append(piece)
        value = value - piece.astype(f32)
    return pieces


def route_kernel(groups, home_ref, ids_ref, grad_ref, prev_ref, *out_refs):
    tok, width = grad_ref.shape
    count = len(groups)
    turned_refs, chosen_refs, early_ref = out_refs[:count], out_refs[count : 2 * count], out_refs[2 * count]
    expert = lax.broadcasted_iota(jnp.int32, (16, tok), 0)
    ids = jnp.concatenate([ids_ref[...].astype(f32), jnp.zeros((tok, EXTRA - 2), f32)], axis=1).T.astype(jnp.int32)
    ids = [ids[k : k + 1, :] for k in range(2)]
    names = [row == expert for row in ids]
    both = jnp.where(names[0] | names[1], 1.0, 0.0).astype(bf16)
    earlier = lax.broadcasted_iota(jnp.int32, (tok, tok), 0) < lax.broadcasted_iota(jnp.int32, (tok, tok), 1)
    before = dot_nn(both, jnp.where(earlier, 1.0, 0.0).astype(bf16))
    pieces = [piece.astype(f32) for piece in split_low(jnp.concatenate([prev_ref[...], jnp.zeros((tok, EXTRA - ALL_EXPERTS), f32)], axis=1), 3)]
    extra = (pieces[0] + pltpu.roll(pieces[1], 16, 1) + pltpu.roll(pieces[2], 32, 1)).astype(bf16)
    slot = [jnp.sum(jnp.where(n, before, 0.0), axis=0, keepdims=True).astype(jnp.int32) for n in names]
    for (first, size), turned_ref, chosen_ref in zip(groups, turned_refs, chosen_refs):
        spots = lax.broadcasted_iota(jnp.int32, (FFN_EXPERTS * size, tok), 0)
        hit = None
        for k in range(2):
            inside = (ids[k] < FFN_EXPERTS) & (slot[k] >= first) & (slot[k] < first + size)
            place = jnp.where(inside, ids[k] * size + slot[k] - first, -1)
            hit = spots == place if hit is None else hit | (spots == place)
        turned = jnp.where(hit, 1.0, 0.0).astype(bf16)
        turned_ref[...] = turned
        chosen_ref[...] = turned.T
        grads = dot_nn(turned, grad_ref[...]).astype(bf16)
        extras = dot_nn(turned, extra).astype(bf16)
        for e in range(FFN_EXPERTS):
            early_ref[e, first : first + size, 0:width] = grads[e * size : (e + 1) * size]
            early_ref[e, first : first + size, width : width + EXTRA] = extras[e * size : (e + 1) * size]


def route_plan(home, ids, grad, prev, groups):
    tok, width = grad.shape
    counts = [FFN_EXPERTS * size for _, size in groups]
    whole = pl.BlockSpec(memory_space=pltpu.VMEM)
    out = pl.pallas_call(
        functools.partial(route_kernel, groups),
        in_specs=[pl.BlockSpec(memory_space=pltpu.SMEM), whole, whole, whole],
        out_specs=[whole] * (2 * len(groups) + 1),
        out_shape=[jax.ShapeDtypeStruct((n, tok), bf16) for n in counts]
        + [jax.ShapeDtypeStruct((tok, n), bf16) for n in counts]
        + [jax.ShapeDtypeStruct((FFN_EXPERTS, sum(counts) // FFN_EXPERTS, width + EXTRA), bf16)],
        compiler_params=pltpu.CompilerParams(vmem_limit_bytes=60 * 2**20),
        cost_estimate=pl.CostEstimate(flops=2 * sum(counts) * tok * (width + EXTRA), bytes_accessed=4 * sum(counts) * width, transcendentals=0),
        name="route_plan",
    )(home, ids, grad, prev)
    return out[: len(groups)], out[len(groups) : -1], out[-1]


def expert_kernel(group, home_ref, rows_ref, early_ref, router_ref, wg_ref, wu_ref, wd_ref,
                  out_ref, drow_ref, dout_ref, inner_ref, dgate_ref, dup_ref, small_ref, acc_out, acc_row, probs_ref):
    width = rows_ref.shape[1]
    step, steps = pl.program_id(0), pl.num_programs(0)
    home = home_ref[0]
    lane = lax.broadcasted_iota(jnp.int32, (1, EXTRA), 1)
    slots = slice(group[0], group[0] + group[1])

    @pl.when(step == 0)
    def _():
        extra = early_ref[:, slots, width : width + EXTRA].astype(f32).reshape(-1, EXTRA)
        logits = extra + pltpu.roll(extra, EXTRA - 16, 1) + pltpu.roll(extra, EXTRA - 32, 1)
        logits = logits + dot_nn(rows_ref[...], router_ref[...])
        logits = jnp.where(lane < ALL_EXPERTS, logits, NEG)
        unnormed = jnp.exp(logits - jnp.max(logits, axis=1, keepdims=True))
        probs = unnormed / jnp.sum(unnormed, axis=1, keepdims=True)
        probs_ref[...] = probs
        gate = jnp.sum(jnp.where(lane == home, probs, 0.0), axis=1, keepdims=True)
        dout_ref[...] = (gate * early_ref[:, slots, 0:width].astype(f32).reshape(-1, width)).astype(bf16)
        acc_out[...] = jnp.zeros_like(acc_out)
        acc_row[...] = jnp.zeros_like(acc_row)

    rows = rows_ref[...]
    gate_pre = dot_nn(rows, wg_ref[0])
    up_pre = dot_nn(rows, wu_ref[0])
    d_inner = dot_nt(dout_ref[...], wd_ref[0])
    sigmoid = jax.nn.sigmoid(gate_pre)
    silu = gate_pre * sigmoid
    inner = (silu * up_pre).astype(bf16)
    d_gate = (d_inner * up_pre * (sigmoid * (1.0 + gate_pre * (1.0 - sigmoid)))).astype(bf16)
    d_up = (d_inner * silu).astype(bf16)
    inner_ref[...] = inner
    dgate_ref[...] = d_gate
    dup_ref[...] = d_up
    acc_out[...] += dot_nn(inner, wd_ref[0])
    acc_row[...] += dot_nt(d_gate, wg_ref[0]) + dot_nt(d_up, wu_ref[0])

    @pl.when(step == steps - 1)
    def _():
        probs = probs_ref[...]
        gate = jnp.sum(jnp.where(lane == home, probs, 0.0), axis=1, keepdims=True)
        out = acc_out[...].astype(bf16).astype(f32)
        d_row_gate = jnp.sum(out * early_ref[:, slots, 0:width].astype(f32).reshape(-1, width), axis=1, keepdims=True)
        out_ref[:, 0:width] = (gate * out).astype(bf16)
        extra = jnp.zeros((out.shape[0], EXTRA), f32)
        for i, piece in enumerate(split_low(d_row_gate, 3)):
            extra = jnp.where(lane == home + 16 * i, piece.astype(f32), extra)
        out_ref[:, width : width + EXTRA] = extra.astype(bf16)
        term = d_row_gate * gate * (jnp.where(lane == home, 1.0, 0.0) - probs)
        high, rest = split_low(term, 2)
        turned = [piece.T for piece in (high, rest)]
        small_ref[...] = (dot_nn(turned[0], rows) + dot_nn(turned[1], rows))[0 : 2 * SMALL, :]
        drow_ref[...] = (acc_row[...] + dot_nt(high, router_ref[...]) + dot_nt(rest, router_ref[...])).astype(bf16)


def expert_pass(group, home, rows, early, router_pad, w_gate, w_up, w_down):
    count, width = rows.shape
    ff = w_gate.shape[2]
    tile = min(512, ff)
    full = pl.BlockSpec((count, width), lambda j: (0, 0))
    wide = pl.BlockSpec((count, width + EXTRA), lambda j: (0, 0))
    tall = pl.BlockSpec((1, width, tile), lambda j: (0, 0, j))
    piece = pl.BlockSpec((count, tile), lambda j: (0, j))
    return pl.pallas_call(
        functools.partial(expert_kernel, group),
        grid=(ff // tile,),
        in_specs=[
            pl.BlockSpec(memory_space=pltpu.SMEM),
            full,
            pl.BlockSpec(early.shape, lambda j: (0, 0, 0)),
            pl.BlockSpec((width, EXTRA), lambda j: (0, 0)),
            tall,
            tall,
            pl.BlockSpec((1, tile, width), lambda j: (0, j, 0)),
        ],
        out_specs=[wide, full, full, piece, piece, piece, pl.BlockSpec((2 * SMALL, width), lambda j: (0, 0))],
        out_shape=[
            jax.ShapeDtypeStruct((count, width + EXTRA), bf16),
            jax.ShapeDtypeStruct((count, width), bf16),
            jax.ShapeDtypeStruct((count, width), bf16),
        ]
        + [jax.ShapeDtypeStruct((count, ff), bf16)] * 3
        + [jax.ShapeDtypeStruct((2 * SMALL, width), f32)],
        scratch_shapes=[pltpu.VMEM((count, width), f32), pltpu.VMEM((count, width), f32), pltpu.VMEM((count, EXTRA), f32)],
        compiler_params=pltpu.CompilerParams(vmem_limit_bytes=60 * 2**20),
        cost_estimate=pl.CostEstimate(flops=12 * count * width * ff, bytes_accessed=6 * width * ff + 2 * count * (5 * width + 3 * ff), transcendentals=count * ff),
        name="expert_pass",
    )(home, rows, early, router_pad, w_gate, w_up, w_down)


def weight_kernel(count, *refs):
    rows, douts, inners, dgates, dups = (refs[i * count : (i + 1) * count] for i in range(5))
    gate_up_ref, down_ref = refs[5 * count : 5 * count + 2]
    turned = refs[5 * count + 2 :]

    @pl.when(pl.program_id(0) == 0)
    def _():
        for ref, scratch in zip(rows, turned):
            scratch[...] = ref[...].T

    gate_up_ref[0] = sum(dot_nn(t[...], d[...]) for t, d in zip(turned, dgates)).astype(bf16)
    gate_up_ref[1] = sum(dot_nn(t[...], d[...]) for t, d in zip(turned, dups)).astype(bf16)
    down_ref[...] = sum(dot_nn(i[...].T, d[...]) for i, d in zip(inners, douts)).astype(bf16)


def weight_gradients(rows, douts, inners, dgates, dups):
    count = len(rows)
    width, ff = rows[0].shape[1], inners[0].shape[1]
    tile = min(512, ff)
    total = sum(r.shape[0] for r in rows)
    full = [pl.BlockSpec(r.shape, lambda j: (0, 0)) for r in rows]
    piece = [pl.BlockSpec((r.shape[0], tile), lambda j: (0, j)) for r in rows]
    return pl.pallas_call(
        functools.partial(weight_kernel, count),
        grid=(ff // tile,),
        in_specs=full + full + piece * 3,
        out_specs=[pl.BlockSpec((2, width, tile), lambda j: (0, 0, j)), pl.BlockSpec((tile, width), lambda j: (j, 0))],
        out_shape=[jax.ShapeDtypeStruct((2, width, ff), bf16), jax.ShapeDtypeStruct((ff, width), bf16)],
        scratch_shapes=[pltpu.VMEM((width, r.shape[0]), bf16) for r in rows],
        compiler_params=pltpu.CompilerParams(vmem_limit_bytes=60 * 2**20),
        cost_estimate=pl.CostEstimate(flops=6 * total * width * ff, bytes_accessed=6 * width * ff + 2 * total * (2 * width + 3 * ff), transcendentals=0),
        name="weight_gradients",
    )(*rows, *douts, *inners, *dgates, *dups)


ANYWHERE = pl.BlockSpec(memory_space=pltpu.VMEM)
SCALARS = pl.BlockSpec(memory_space=pltpu.SMEM)


def inverse_rms(value):
    return lax.rsqrt(jnp.mean(value * value, axis=1, keepdims=True) + epsilon)


def after_attention_kernel(count, mixed_ref, x_ref, w_ref, gain_ref, *refs):
    turned, (hidden_ref, low_ref), sent = refs[:count], refs[count : count + 2], refs[count + 2 : 2 * count + 2]
    kept, local, sems = refs[2 * count + 2], refs[2 * count + 3 : 3 * count + 3], refs[-1]
    step = pl.program_id(0)
    copies = [pltpu.make_async_copy(t, s, sems.at[g]) for g, (t, s) in enumerate(zip(turned, local))]

    @pl.when(step == 0)
    def _():
        for copy in copies:
            copy.start()

    hidden = x_ref[...].astype(f32) + dot_nn(mixed_ref[...], w_ref[...])
    low = (hidden * inverse_rms(hidden) * gain_ref[...]).astype(bf16)
    hidden_ref[...] = hidden
    low_ref[...] = low
    block = low.shape[0]
    kept[pl.ds(pl.multiple_of(step * block, block), block), :] = low

    @pl.when(step == pl.num_programs(0) - 1)
    def _():
        for copy, t, s in zip(copies, local, sent):
            copy.wait()
            s[...] = dot_nn(t[...], kept[...]).astype(bf16)


def after_attention(mixed, x, w_out, gain, turned):
    tok, width = x.shape
    rows = sum(t.shape[0] for t in turned)
    block, tiles = row_tiles(tok)
    out = pl.pallas_call(
        functools.partial(after_attention_kernel, len(turned)),
        grid=(tok // block,),
        in_specs=[tiles(width), tiles(width), fixed(w_out), fixed(gain)] + [pl.BlockSpec(memory_space=pl.ANY)] * len(turned),
        out_specs=[tiles(width)] * 2 + [pl.BlockSpec((t.shape[0], width), lambda i: (0, 0)) for t in turned],
        out_shape=[jax.ShapeDtypeStruct((tok, width), f32), jax.ShapeDtypeStruct((tok, width), bf16)]
        + [jax.ShapeDtypeStruct((t.shape[0], width), bf16) for t in turned],
        scratch_shapes=[pltpu.VMEM((tok, width), bf16)] + [pltpu.VMEM(t.shape, bf16) for t in turned] + [pltpu.SemaphoreType.DMA((len(turned),))],
        compiler_params=pltpu.CompilerParams(vmem_limit_bytes=60 * 2**20),
        cost_estimate=pl.CostEstimate(flops=2 * tok * width * (width + rows), bytes_accessed=2 * width * (6 * tok + 2 * rows), transcendentals=0),
        name="after_attention",
    )(mixed, x, w_out, gain, *turned)
    return out[0], out[1], out[2:]


def turn_kernel(in_ref, out_ref):
    out_ref[...] = in_ref[...].T


def turn(value):
    rows, columns = value.shape
    block = 256 if rows % 256 == 0 else 128
    return pl.pallas_call(
        turn_kernel,
        grid=(rows // block,),
        in_specs=[pl.BlockSpec((block, columns), lambda i: (i, 0))],
        out_specs=pl.BlockSpec((columns, block), lambda i: (0, i)),
        out_shape=jax.ShapeDtypeStruct((columns, rows), value.dtype),
        compiler_params=pltpu.CompilerParams(vmem_limit_bytes=60 * 2**20),
        cost_estimate=pl.CostEstimate(flops=0, bytes_accessed=4 * rows * columns, transcendentals=0),
        name="turn",
    )(value)


def place(value, lane, at):
    return jnp.where(lane == at, value, 0.0)


def local_kernel(hidden_ref, low_ref, grad_ref, prev_ref, ids_ref, mix_ref, gain_ref, vec_ref, out_ref, dnormed_ref, probs_ref, dprobs_ref, small_ref):
    lane = lax.broadcasted_iota(jnp.int32, (1, EXTRA), 1)
    hidden = hidden_ref[...]
    normed = hidden * inverse_rms(hidden) * gain_ref[...]
    low = low_ref[...]
    grad = grad_ref[...].astype(f32)
    raw = dot_nn(low, mix_ref[...])
    prev = jnp.concatenate([prev_ref[...], jnp.zeros((raw.shape[0], EXTRA - ALL_EXPERTS), f32)], axis=1)
    logits = jnp.where(lane < ALL_EXPERTS, raw + prev, NEG)
    unnormed = jnp.exp(logits - jnp.max(logits, axis=1, keepdims=True))
    probs = unnormed / jnp.sum(unnormed, axis=1, keepdims=True)
    named = (ids_ref[:, 0:1] == lane) | (ids_ref[:, 1:2] == lane)
    gates = jnp.where(named, probs, 0.0)
    copy_gate = gates[:, FFN_EXPERTS + 1 : FFN_EXPERTS + 2]
    dots = jnp.sum(grad * normed, axis=1, keepdims=True)
    out = hidden
    weight = copy_gate
    d_probs = place(dots, lane, FFN_EXPERTS + 1)
    logit_grads = jnp.zeros_like(probs)
    vec_terms = jnp.zeros_like(probs)
    for c in range(2):
        vec = vec_ref[c : c + 1, :]
        gate = gates[:, FFN_EXPERTS + 2 + c : FFN_EXPERTS + 3 + c]
        at = 16 + 2 * c
        a0 = jax.nn.sigmoid(raw[:, at : at + 1] - raw[:, at + 1 : at + 2])
        a1 = jax.nn.sigmoid(raw[:, at + 1 : at + 2] - raw[:, at : at + 1])
        vec_dots = jnp.sum(grad * vec, axis=1, keepdims=True)
        weight = weight + gate * a0
        out = out + (gate * a1) * vec
        d_probs = d_probs + place(a0 * dots + a1 * vec_dots, lane, FFN_EXPERTS + 2 + c)
        d0, d1 = gate * dots, gate * vec_dots
        mean = a0 * d0 + a1 * d1
        d0, d1 = a0 * (d0 - mean), a1 * (d1 - mean)
        logit_grads = logit_grads + place(d0, lane, at) + place(d1, lane, at + 1)
        vec_terms = vec_terms + place(gate * a1, lane, 20 + c)
    d_probs = jnp.where(named, d_probs, 0.0)
    logit_grads = logit_grads + probs * (d_probs - jnp.sum(probs * d_probs, axis=1, keepdims=True))
    high, rest = split_low(logit_grads, 2)
    out_ref[...] = out + weight * normed
    dnormed_ref[...] = weight * grad + dot_nt(high, mix_ref[...]) + dot_nt(rest, mix_ref[...])
    probs_ref[...] = probs
    dprobs_ref[...] = d_probs
    sums = None
    for terms, rows in ((logit_grads, low), (vec_terms, grad_ref[...])):
        for piece in split_low(terms.T, 2):
            part = dot_nn(piece, rows)
            sums = part if sums is None else sums + part
    sums = sums[0 : 3 * SMALL, :]

    @pl.when(pl.program_id(0) == 0)
    def _():
        small_ref[...] = sums

    @pl.when(pl.program_id(0) > 0)
    def _():
        small_ref[...] += sums


def local_part(hidden, low, grad, prev, ids, mix, gain, vec):
    tok, width = hidden.shape
    block, tiles = row_tiles(tok)
    shapes = [(tok, width), (tok, width), (tok, EXTRA), (tok, EXTRA), (3 * SMALL, width)]
    return pl.pallas_call(
        local_kernel,
        grid=(tok // block,),
        in_specs=[tiles(width), tiles(width), tiles(width), tiles(ALL_EXPERTS), tiles(2), fixed(mix), fixed(gain), fixed(vec)],
        out_specs=[tiles(width), tiles(width), tiles(EXTRA), tiles(EXTRA), pl.BlockSpec((3 * SMALL, width), lambda i: (0, 0))],
        out_shape=[jax.ShapeDtypeStruct(s, f32) for s in shapes],
        compiler_params=pltpu.CompilerParams(vmem_limit_bytes=60 * 2**20),
        cost_estimate=pl.CostEstimate(flops=14 * tok * width * EXTRA, bytes_accessed=16 * tok * width, transcendentals=tok * EXTRA),
        name="local_part",
    )(hidden, low, grad, prev, ids, mix, gain, vec)


def row_tiles(tok):
    block = 256 if tok % 256 == 0 else 128
    return block, lambda columns: pl.BlockSpec((block, columns), lambda i: (i, 0))


def fixed(value):
    return pl.BlockSpec(value.shape, lambda i: (0,) * value.ndim)


def combine_kernel(count, parts, core_ref, *refs):
    chosen, got, refs = refs[:count], refs[count : count * (1 + parts)], refs[count * (1 + parts) :]
    smalls, refs = refs[: count + 1], refs[count + 1 :]
    local_ref, hidden_ref, gain_ref, grad_ref, mixed_ref, w_ref, dhidden_ref, dmixed_ref, mine_ref, theirs_ref, total_w, total_gain, small_t = refs
    step = pl.program_id(0)

    @pl.when(step == 0)
    def _():
        total_w[...] = jnp.zeros_like(total_w)
        total_gain[...] = jnp.zeros_like(total_gain)

    d_normed = local_ref[...]
    for g in range(count):
        for r in range(parts):
            d_normed = d_normed + dot_nn(chosen[g][...], got[g * parts + r][...])
    hidden = hidden_ref[...]
    inverse = inverse_rms(hidden)
    scaled = d_normed * gain_ref[...]
    mean = jnp.mean(scaled * hidden, axis=1, keepdims=True)
    d_hidden = grad_ref[...].astype(f32) + inverse * scaled - hidden * (inverse * inverse * inverse * mean)
    low = d_hidden.astype(bf16)
    dhidden_ref[...] = d_hidden
    dmixed_ref[...] = dot_nt(low, w_ref[...]).astype(bf16)
    total_w[...] += dot_nn(mixed_ref[...].T, low)
    total_gain[...] += jnp.sum(d_normed * hidden * inverse, axis=0, keepdims=True)

    @pl.when(step == pl.num_programs(0) - 1)
    def _():
        width = w_ref.shape[0]
        half = width // 2
        row = lax.broadcasted_iota(jnp.int32, (SMALL, 1), 0)
        top = smalls[0][0 : 2 * SMALL, :]
        for small in smalls[1:]:
            top = top + small[...]
        rest = jnp.zeros((EXTRA - 4 * SMALL, width), f32)
        rows = [top, smalls[0][2 * SMALL : 3 * SMALL, :], jnp.where(row == 0, total_gain[...], 0.0), rest]
        small_t[...] = jnp.concatenate(rows, axis=0).T
        at = mine_ref.shape[1] - width - EXTRA
        for out_ref, which in ((theirs_ref, 1 - core_ref[0]), (mine_ref, core_ref[0])):
            place_rows = pl.ds(pl.multiple_of(which * half, half), half)
            out_ref[:, at : at + width] = total_w[place_rows, :].astype(bf16)
            out_ref[:, at + width : at + width + EXTRA] = small_t[place_rows, :].astype(bf16)


def combine(core, chosen, got, smalls, local, hidden, gain, grad, mixed, w_out, columns):
    tok, width = hidden.shape
    rows = sum(c.shape[1] for c in chosen)
    arrays = [a for group in got for a in group]
    block, tiles = 128, lambda columns: pl.BlockSpec((128, columns), lambda i: (i, 0))
    half = (width // 2, columns + width + EXTRA)
    return pl.pallas_call(
        functools.partial(combine_kernel, len(chosen), len(got[0])),
        grid=(tok // block,),
        in_specs=[SCALARS] + [tiles(c.shape[1]) for c in chosen] + [fixed(a) for a in arrays + smalls]
        + [tiles(width), tiles(width), fixed(gain), tiles(width), tiles(width), fixed(w_out)],
        out_specs=[tiles(width)] * 2 + [pl.BlockSpec(half, lambda i: (0, 0))] * 2,
        out_shape=[jax.ShapeDtypeStruct((tok, width), f32), jax.ShapeDtypeStruct((tok, width), bf16)] + [jax.ShapeDtypeStruct(half, bf16)] * 2,
        scratch_shapes=[pltpu.VMEM((width, width), f32), pltpu.VMEM((1, width), f32), pltpu.VMEM((width, EXTRA), f32)],
        compiler_params=pltpu.CompilerParams(vmem_limit_bytes=60 * 2**20),
        cost_estimate=pl.CostEstimate(flops=2 * tok * width * (rows + 2 * width), bytes_accessed=2 * width * (10 * tok + 2 * rows), transcendentals=0),
        name="combine_gradients",
    )(core, *chosen, *arrays, *smalls, local, hidden, gain, grad, mixed, w_out)


def flat_rows(value):
    if value.shape[1] % 16:
        return value.astype(f32).reshape(-1, value.shape[2]).astype(bf16)
    return value.reshape(-1, value.shape[2])


def finish_kernel(groups, parts, *refs):
    chosen, got = refs[: len(groups)], refs[len(groups) : len(groups) + parts]
    local_ref, probs_ref, dprobs_ref, out_ref, dlogits_ref = refs[len(groups) + parts :]
    width = local_ref.shape[1]
    lane = lax.broadcasted_iota(jnp.int32, (1, EXTRA), 1)
    picked = None
    for c, (at, size) in zip(chosen, groups):
        for r in range(parts):
            part = dot_nn(c[...], flat_rows(got[r][:, at : at + size, :]))
            picked = part if picked is None else picked + part
    out_ref[...] = (local_ref[...] + picked[:, 0:width]).astype(bf16)
    extra = picked[:, width : width + EXTRA]
    extra = extra + pltpu.roll(extra, EXTRA - 16, 1) + pltpu.roll(extra, EXTRA - 32, 1)
    d_probs = dprobs_ref[...] + jnp.where(lane < ALL_EXPERTS, extra, 0.0)
    probs = probs_ref[...]
    d_logits = probs * (d_probs - jnp.sum(probs * d_probs, axis=1, keepdims=True))
    dlogits_ref[...] = d_logits.T


def finish(chosen, got, groups, local, probs, d_probs):
    tok, width = local.shape
    block, tiles = row_tiles(tok)
    return pl.pallas_call(
        functools.partial(finish_kernel, groups, len(got)),
        grid=(tok // block,),
        in_specs=[tiles(c.shape[1]) for c in chosen] + [fixed(g) for g in got] + [tiles(width), tiles(EXTRA), tiles(EXTRA)],
        out_specs=[tiles(width), pl.BlockSpec((EXTRA, block), lambda i: (0, i))],
        out_shape=[jax.ShapeDtypeStruct((tok, width), bf16), jax.ShapeDtypeStruct((EXTRA, tok), f32)],
        compiler_params=pltpu.CompilerParams(vmem_limit_bytes=60 * 2**20),
        cost_estimate=pl.CostEstimate(flops=2 * tok * 1152 * (width + EXTRA), bytes_accessed=16 * tok * width, transcendentals=0),
        name="finish_outputs",
    )(*chosen, *got, local, probs, d_probs)


def input_kernel(dact_ref, x_ref, gain_ref, dhidden_ref, *refs):
    out_ref = refs[-1]
    far = refs[0][...].astype(f32)
    for ref in refs[1:-1]:
        far = far + ref[...].astype(f32)
    x = x_ref[...].astype(f32)
    inverse = inverse_rms(x)
    scaled = (dact_ref[...] + jnp.where(pl.program_id(0) == 0, far, 0.0)) * gain_ref[...]
    mean = jnp.mean(scaled * x, axis=1, keepdims=True)
    out_ref[...] = dhidden_ref[...] + inverse * scaled - x * (inverse * inverse * inverse * mean)


def input_gradient(d_act, x, gain, d_hidden, far):
    tok, width = x.shape
    block = far[0].shape[0]
    tiles = pl.BlockSpec((block, width), lambda i: (i, 0))
    return pl.pallas_call(
        input_kernel,
        grid=(tok // block,),
        in_specs=[tiles, tiles, fixed(gain), tiles] + [fixed(f) for f in far],
        out_specs=tiles,
        out_shape=jax.ShapeDtypeStruct((tok, width), f32),
        compiler_params=pltpu.CompilerParams(vmem_limit_bytes=60 * 2**20),
        cost_estimate=pl.CostEstimate(flops=12 * tok * width, bytes_accessed=16 * tok * width, transcendentals=0),
        name="input_gradient",
    )(d_act, x, gain, d_hidden, *far)


def xor_pairs(size, mask):
    return [(i, i ^ mask) for i in range(size)]


def sum_kernel(terms, index_ref, *refs):
    count = len(refs) // (sum(terms) + 1)
    outs = refs[-count:]
    for k, out_ref in enumerate(outs):
        at = 0
        first = 0
        for number in terms:
            total = None
            for t in range(first, first + number):
                value = refs[t * count + k][0].astype(f32)
                total = value if total is None else total + value
            out_ref[0, :, at : at + total.shape[1]] = total.astype(bf16)
            at += total.shape[1]
            first += number


def sum_pieces(index, groups):
    arrays = [a for group in groups for a in group]
    n, rows = arrays[0].shape[:2]
    columns = sum(group[0].shape[2] for group in groups)
    view = lambda a, k: pl.BlockSpec((1, rows, a.shape[2]), lambda i, s: (s[0] ^ k if n > 1 else 0, 0, 0))
    return pl.pallas_call(
        functools.partial(sum_kernel, [len(g) for g in groups]),
        grid_spec=pltpu.PrefetchScalarGridSpec(
            num_scalar_prefetch=1,
            grid=(1,),
            in_specs=[view(a, k) for a in arrays for k in range(n)],
            out_specs=[pl.BlockSpec((1, rows, columns), lambda i, s: (0, 0, 0))] * n,
        ),
        out_shape=[jax.ShapeDtypeStruct((1, rows, columns), bf16)] * n,
        compiler_params=pltpu.CompilerParams(vmem_limit_bytes=60 * 2**20),
        cost_estimate=pl.CostEstimate(flops=0, bytes_accessed=2 * n * rows * columns * 5, transcendentals=0),
        name="sum_pieces",
    )(index, *[a for a in arrays for _ in range(n)])


def quarters(value):
    return value.reshape(4, -1, value.shape[-1])


def swap(pieces, along):
    axis, size, unit = along
    return [pieces[0]] + [lax.ppermute(pieces[k], axis, xor_pairs(size, unit * k)) for k in range(1, 4)]


def spread(value, along):
    return swap([value] * 4, along)


def stack_kernel(*refs):
    n = len(refs) - 1
    size = refs[0].shape[0]
    for k in range(n):
        refs[n][k * size : (k + 1) * size] = refs[k][...]


def stack_pieces(pieces):
    shape = (len(pieces) * pieces[0].shape[0],) + pieces[0].shape[1:]
    return pl.pallas_call(
        stack_kernel,
        in_specs=[ANYWHERE] * len(pieces),
        out_specs=ANYWHERE,
        out_shape=jax.ShapeDtypeStruct(shape, bf16),
        compiler_params=pltpu.CompilerParams(vmem_limit_bytes=60 * 2**20),
        cost_estimate=pl.CostEstimate(flops=0, bytes_accessed=4 * math.prod(shape), transcendentals=0),
        name="stack_pieces",
    )(*pieces)


def unpack_kernel(left, index_ref, own_ref, other_ref, w_ref, scale_ref, out_ref, qkv_ref, router_ref, mixing_ref, vec_ref, gain_ref, attn_ref, small):
    width = out_ref.shape[1]
    piece = own_ref.shape[2]
    mine = pl.program_id(0) == index_ref[0]
    lane = lax.broadcasted_iota(jnp.int32, (1, EXTRA), 1)
    block = pl.program_id(0) * 4 + pl.program_id(1)
    for k in range(4):
        rows = slice(k * piece, (k + 1) * piece)
        at_ctx = k ^ index_ref[1]
        total = jnp.where(mine, own_ref[at_ctx, 0, :, :], other_ref[at_ctx, 0, :, :]).astype(f32)
        out_ref[rows, :] = total[:, left : left + width]
        gain = None
        for p in range(3):
            for i in range(width // 128):
                at = i * 384 + p * 128 + (0 if i * 384 < left else width + EXTRA)
                value = total[:, at : at + 128]
                columns = slice(p * width + i * 128, p * width + (i + 1) * 128)
                qkv_ref[rows, columns] = value
                part = value * w_ref[rows, columns].astype(f32)
                gain = part if gain is None else gain + part
        gain = jnp.sum(gain, axis=1, keepdims=True)
        small[pl.ds(block * 4 * piece + k * piece, piece), :] = total[:, left + width : left + width + EXTRA] + place(gain, lane, EXTRA - 1)

    @pl.when(block == 7)
    def _():
        turned = small[...].T
        router_ref[...] = turned[0:ALL_EXPERTS]
        mixing_ref[...] = turned[16:20]
        vec_ref[...] = turned[20:22]
        gain_ref[...] = turned[24:25]
        attn_ref[...] = turned[EXTRA - 1 : EXTRA] / scale_ref[...]


def unpack(index, own, other, w_qkv, scale, left):
    width = w_qkv.shape[0]
    piece = width // 32
    block = 4 * piece
    own, other = own.reshape(4, 4, piece, -1), other.reshape(4, 4, piece, -1)
    row = lambda c, a, s: (c * 4 + a, 0)

    def source(core_of):
        def at(c, a, s):
            core = core_of(s[0])
            return 0, jnp.where(c == core, a, jnp.where(c < core, 0, 3)) ^ s[2], 0, 0

        return pl.BlockSpec((4, 1, piece, own.shape[3]), at)

    whole = lambda n: pl.BlockSpec((n, width), lambda c, a, s: (0, 0))
    counts = (ALL_EXPERTS, 4, 2, 1, 1)
    return pl.pallas_call(
        functools.partial(unpack_kernel, left),
        grid_spec=pltpu.PrefetchScalarGridSpec(
            num_scalar_prefetch=1,
            grid=(2, 4),
            in_specs=[source(lambda core: core), source(lambda core: 1 - core), pl.BlockSpec((block, 3 * width), row), whole(1)],
            out_specs=[pl.BlockSpec((block, width), row), pl.BlockSpec((block, 3 * width), row), *[whole(n) for n in counts]],
            scratch_shapes=[pltpu.VMEM((width, EXTRA), f32)],
        ),
        out_shape=[jax.ShapeDtypeStruct((width, width), f32), jax.ShapeDtypeStruct((width, 3 * width), f32), *[jax.ShapeDtypeStruct((n, width), f32) for n in counts]],
        compiler_params=pltpu.CompilerParams(vmem_limit_bytes=60 * 2**20),
        cost_estimate=pl.CostEstimate(flops=0, bytes_accessed=36 * width * width, transcendentals=0),
        name="unpack_sums",
    )(index, own, other, w_qkv, scale)

P = jax.sharding.PartitionSpec


def rms_inverse(tensor):
    return lax.rsqrt(jnp.mean(tensor * tensor, axis=-1, keepdims=True) + epsilon)


def after(values, *others):
    return lax.optimization_barrier((values, others))[0]


def body(inputs, prev_logits, routes, attn_gain, w_qkv, w_out, moe_gain, router, const_gate, const_vec, w_gate, w_up, w_down, out_grad):
    n_ctx, n_exp = lax.axis_size("ctx"), lax.axis_size("exp")
    me_c, me_e = lax.axis_index("ctx"), lax.axis_index("exp")
    tok, width = inputs.shape[1], inputs.shape[2]
    plen = tok - CONT_LEN
    split = n_exp // FFN_EXPERTS
    capacity = max(4, tok // 64 * 12)
    first = -(-capacity // 32) * 16
    groups = ((0, first), (first, capacity - first))
    home = (me_e // split).reshape(1)

    def deal(value):
        value = jnp.repeat(value, split, axis=0) if split > 1 else value
        return lax.all_to_all(value, "exp", 0, 0, tiled=True)

    def give_back(value):
        value = lax.all_to_all(value, "exp", 0, 0, tiled=True)
        return [value[r::split] if split > 1 else value for r in range(split)]

    x_low = inputs[0]
    upstream_low = out_grad[0]
    far_rows = jnp.concatenate([lax.ppermute(x_low[:plen], "ctx", xor_pairs(n_ctx, k)) for k in range(1, n_ctx)], axis=0)
    flags = jnp.where((me_c ^ jnp.arange(1, n_ctx)) < me_c, 0.0, NEG).astype(f32)

    prev = prev_logits[0]
    mix = jnp.concatenate([router, jnp.zeros((width, 4), bf16), const_gate[0], const_gate[1], jnp.zeros((width, EXTRA - 20), bf16)], axis=1)
    router_pad = jnp.pad(router, ((0, 0), (0, EXTRA - ALL_EXPERTS)))
    turned, chosen, early_sent = route_plan(home, routes[0], upstream_low, prev, groups)

    tokens_in = x_low.astype(f32)
    inverse_attn = rms_inverse(tokens_in)
    act_low = (tokens_in * inverse_attn * attn_gain).astype(bf16)
    projected = dot_nn(act_low, w_qkv).astype(bf16)
    early = deal(early_sent)
    far_in = after(far_rows, projected).astype(f32)
    act_far = (far_in * rms_inverse(far_in) * attn_gain).astype(bf16)
    kv_far = dot_nn(act_far, w_qkv[:, width:]).astype(bf16)

    mixed_low, lse = attention_forward(flags, projected, kv_far, plen)
    mixed_low, early = lax.optimization_barrier((mixed_low, early))
    hidden, moe_low, sent = after_attention(mixed_low, x_low, w_out, moe_gain[None], turned)
    local_out, d_normed_local, probs, d_probs, small_local = local_part(hidden, moe_low, upstream_low, prev, routes[0], mix, moe_gain[None], const_vec)
    act_t, far_t = turn(act_low), turn(act_far)
    sent = [after(sent[0], local_out, d_normed_local, act_t, far_t), sent[1]]
    got = [deal(part.reshape(FFN_EXPERTS, -1, width)) for part in sent]

    got = [part.reshape(-1, width) for part in got]
    passes = [expert_pass(group, home, r, early, router_pad, w_gate, w_up, w_down) for group, r in zip(groups, got)]
    d_got = [give_back(p[1].reshape(n_exp, -1, width)) for p in passes]
    gate_up_low, down_low = weight_gradients(got, [p[2] for p in passes], [p[3] for p in passes], [p[4] for p in passes], [p[5] for p in passes])
    outs = jnp.concatenate([p[0].reshape(n_exp, -1, width + EXTRA) for p in passes], axis=1)
    d_got, gate_up_low, down_low, outs = lax.optimization_barrier((d_got, gate_up_low, down_low, outs))
    out_got = give_back(outs)

    d_got = [[part.reshape(-1, width) for part in group] for group in d_got]
    pairs = width // 128
    cut = pairs // 3
    core = (me_e & 1).reshape(1)
    smalls = [small_local] + [p[6] for p in passes]
    d_hidden, d_mixed, *buffers = combine(core, chosen, d_got, smalls, d_normed_local, hidden, moe_gain[None], upstream_low, mixed_low, w_out, cut * 384)

    sum_gate_up = lax.psum_scatter(gate_up_low, "ctx", scatter_dimension=1, tiled=True).astype(f32)
    sum_down = lax.psum_scatter(down_low, "ctx", scatter_dimension=0, tiled=True).astype(f32)

    def attention(upstream, begin, count, buffers, at, starts, last):
        return attention_backward(flags, core, projected, kv_far, mixed_low, upstream, lse, act_t, far_t, w_qkv, plen, begin, count, buffers, at, starts, last)

    dense = n_ctx == 4 and n_exp == 8
    left, right = cut * 384, (pairs - cut) * 384
    z = me_e >> 1
    at_ctx, at_z = me_c.reshape(1), z.reshape(1)
    along_ctx, along_z = ("ctx", 4, 1), ("exp", 8, 2)
    across = lambda value: lax.ppermute(value, "exp", xor_pairs(n_exp, 1))
    mine_1, theirs_1, *starts = attention(d_mixed, 0, cut, buffers, 0, None, False)
    if dense:
        got_1 = across(theirs_1)
    mine_2, theirs_2, *starts = attention(d_mixed, cut, 1, right, 0, starts, False)
    if dense:
        mine_2, theirs_2, starts, got_1 = lax.optimization_barrier((mine_2, theirs_2, starts, got_1))
        sums_1 = sum_pieces(at_z, [[quarters(mine_1), quarters(got_1)]])
        parts_1 = swap(sums_1, along_z)
        mine_2 = after(mine_2, sums_1[0])
    mine_2, theirs_2, d_act, *d_far = attention(d_mixed, cut + 1, pairs - cut - 1, (mine_2, theirs_2), 1, starts, True)
    if dense:
        mine_2, theirs_2, d_act, d_far, parts_1 = lax.optimization_barrier((mine_2, theirs_2, d_act, d_far, parts_1))
    far_back = [lax.ppermute(d_far[k - 1], "ctx", xor_pairs(n_ctx, k)) for k in range(1, n_ctx)]
    if dense:
        sums_2 = sum_pieces(at_z, [[quarters(mine_2), quarters(across(theirs_2))]])
        parts_2 = swap(sums_2, along_z)
        mixed_out, d_logits = finish(chosen, out_got, groups, after(local_out, sums_2[0]), probs, d_probs)
        mixed_out, d_logits, far_back = lax.optimization_barrier((mixed_out, d_logits, far_back))
    else:
        mixed_out, d_logits = finish(chosen, out_got, groups, local_out, probs, d_probs)
    d_inputs = input_gradient(d_act, x_low, attn_gain[None], d_hidden, far_back)

    total_gate, total_up, total_down = sum_gate_up[0][None], sum_gate_up[1][None], sum_down[None]
    if dense:
        parts_1, parts_2 = ([quarters(p) for p in parts] for parts in (parts_1, after(parts_2, d_inputs)))
        parts = swap(sum_pieces(at_ctx, [parts_1, parts_2]), along_ctx)
        [piece] = sum_pieces(at_ctx, [parts])
        column = stack_pieces(spread(piece, along_z))
        own = stack_pieces(after(spread(column, along_ctx), total_gate, total_up, total_down))
        other = across(own)
        out_sum, qkv_sum, d_router, d_mixing, d_const_vec, d_moe_gain, d_attn_gain = unpack(
            jnp.stack([core[0], me_c, z]), own, other, w_qkv, attn_gain[None], left
        )
    else:
        whole = lambda mine, theirs: jnp.where(core == 0, jnp.concatenate([mine, theirs], axis=0), jnp.concatenate([theirs, mine], axis=0))
        total_1, total_2 = [v.astype(f32) for v in lax.psum((whole(mine_1, theirs_1), whole(mine_2, theirs_2)), ("ctx", "exp"))]
        columns = jnp.concatenate([total_1[:, :left], total_2], axis=1).reshape(width, pairs, 3, 128)
        qkv_sum = columns.transpose(0, 2, 1, 3).reshape(width, 3 * width)
        out_sum, small = total_1[:, left : left + width], total_1[:, left + width :].T
        d_attn_gain = (jnp.sum(qkv_sum * w_qkv.astype(f32), axis=1) / attn_gain)[None]
        d_router, d_mixing, d_const_vec, d_moe_gain = small[:ALL_EXPERTS], small[16:20], small[20:22], small[24:25]
    return (
        mixed_out[None],
        d_inputs[None],
        d_logits[:ALL_EXPERTS].T[None],
        d_attn_gain[0],
        qkv_sum,
        out_sum,
        d_moe_gain[0],
        d_router.T,
        d_mixing.reshape(2, 2, width).transpose(0, 2, 1),
        d_const_vec,
        total_gate,
        total_up,
        total_down,
    )


def solution(mesh):
    rows = P("ctx", "exp", None)
    expert = P("exp", None, None)
    summed = P("exp", "ctx", None)
    return jax.shard_map(
        body,
        mesh=mesh,
        in_specs=(rows, rows, rows, P(), P(), P(), P(), P(), P(), P(), expert, expert, expert, rows),
        out_specs=(rows, rows, rows, P(), P(), P(), P(), P(), P(), P(), summed, summed, summed),
        check_vma=False,
    )
```

```python
import functools, math
import jax, jax.numpy as jnp
from jax import lax
from jax.experimental import pallas as pl
from jax.experimental.pallas import tpu as pltpu

HEADS = 12
HEAD_DIM = 64
CONT_LEN = 512
LOG2E = 1.4426950408889634
SCALE = HEAD_DIM ** -0.5
bf16 = jnp.bfloat16
f32 = jnp.float32
NEG = -1e30


def dot_nt(a, b):
    return lax.dot_general(a, b, (((1,), (1,)), ((), ())), preferred_element_type=f32)


def dot_nn(a, b):
    return jnp.dot(a, b, preferred_element_type=f32)


def query_tiles(tok, plen):
    tiles = [(0, plen, True)]
    step = 256
    for start in range(plen, tok, step):
        tiles.append((start, step, False))
    return tiles


def split_high(value):
    high = value.astype(bf16)
    return high, (value - high.astype(f32)).astype(bf16)


def both_halves(value, head, low_half):
    turned = pltpu.roll(value, HEAD_DIM, 1)
    return jnp.where(low_half, value, turned) if head == 0 else jnp.where(low_half, turned, value)


def scaled_queries(value, head, low_half):
    high, rest = split_high(value.astype(f32) * (SCALE * LOG2E))
    rest = pltpu.roll(rest, HEAD_DIM, 1)
    return jnp.where(low_half, high, rest) if head == 0 else jnp.where(low_half, rest, high)


def attention_forward_kernel(plen, flags_ref, q_ref, k_ref, v_ref, kr_ref, vr_ref, o_ref, lse_ref, kd, krd, vd, vrd):
    tok = q_ref.shape[0]
    remote = kr_ref.shape[0]
    low_half = lax.broadcasted_iota(jnp.int32, (1, 128), 1) < HEAD_DIM
    one = jnp.ones((), bf16)
    for head in range(2):
        mine = low_half if head == 0 else ~low_half
        kd[head] = both_halves(k_ref[...], head, low_half)
        krd[head] = both_halves(kr_ref[...], head, low_half)
        vd[head] = jnp.where(mine, v_ref[...], one)
        vrd[head] = jnp.where(mine, vr_ref[...], one)
    for start, size, is_prompt in query_tiles(tok, plen):
        row = lax.broadcasted_iota(jnp.int32, (size, size), 0)
        col = lax.broadcasted_iota(jnp.int32, (size, size), 1)
        queries = q_ref[start : start + size, :]
        units = []
        for head in range(2):
            qh = scaled_queries(queries, head, low_half)
            pieces = []
            diag = dot_nt(qh, kd[head, start : start + size, :])
            pieces.append((jnp.where(col <= row, diag, NEG), vd, start, size))
            if is_prompt:
                for j in range(remote // plen):
                    s = dot_nt(qh, krd[head, j * plen : (j + 1) * plen, :])
                    pieces.append((s + flags_ref[j], vrd, j * plen, plen))
            else:
                s = dot_nt(qh, kd[head, 0:start, :])
                pieces.append((s, vd, 0, start))
                s = dot_nt(qh, krd[head])
                pieces.append((s, vrd, 0, remote))
            units.append(pieces)
        accs, peaks = [], []
        for head, pieces in enumerate(units):
            peak = None
            for s, _, _, _ in pieces:
                m = jnp.max(s, axis=1, keepdims=True)
                peak = m if peak is None else jnp.maximum(peak, m)
            acc = None
            for s, ref, at, n in pieces:
                p = jnp.exp2(s - peak).astype(bf16)
                part = dot_nn(p, ref[head, at : at + n, :])
                acc = part if acc is None else acc + part
            accs.append(acc)
            peaks.append(peak)
        num = jnp.where(low_half, accs[0], accs[1])
        den = pltpu.roll(jnp.where(low_half, accs[1], accs[0]), HEAD_DIM, 1)
        o_ref[start : start + size, :] = (num / den).astype(bf16)
        turned = (jnp.where(low_half, peaks[0], peaks[1]) + jnp.log2(den)).T
        lse_ref[0, 0:8, start : start + size] = turned[0:8, :]
        lse_ref[0, 8:16, start : start + size] = turned[HEAD_DIM : HEAD_DIM + 8, :]


def attention_forward(flags, proj, kv_rem, plen):
    tok, width = proj.shape[0], proj.shape[1] // 3
    remote = kv_rem.shape[0]
    pairs = width // 128
    return pl.pallas_call(
        functools.partial(attention_forward_kernel, plen),
        grid=(pairs,),
        in_specs=[
            pl.BlockSpec(memory_space=pltpu.SMEM),
            pl.BlockSpec((tok, 128), lambda i: (0, i)),
            pl.BlockSpec((tok, 128), lambda i: (0, pairs + i)),
            pl.BlockSpec((tok, 128), lambda i: (0, 2 * pairs + i)),
            pl.BlockSpec((remote, 128), lambda i: (0, i)),
            pl.BlockSpec((remote, 128), lambda i: (0, pairs + i)),
        ],
        out_specs=[
            pl.BlockSpec((tok, 128), lambda i: (0, i)),
            pl.BlockSpec((1, 16, tok), lambda i: (i, 0, 0)),
        ],
        out_shape=[
            jax.ShapeDtypeStruct((tok, width), bf16),
            jax.ShapeDtypeStruct((pairs, 16, tok), f32),
        ],
        scratch_shapes=[pltpu.VMEM((2, n, 128), bf16) for n in (tok, remote, tok, remote)],
        compiler_params=pltpu.CompilerParams(vmem_limit_bytes=60 * 2**20),
        cost_estimate=pl.CostEstimate(flops=4 * tok * (tok + remote) * width, bytes_accessed=2 * (tok * 4 + remote * 2) * width, transcendentals=tok * (tok + remote) * HEADS),
        name="attention_forward",
    )(flags, proj, proj, proj, kv_rem, kv_rem)


def attention_backward_kernel(plen, started, last, skip, flags_ref, core_ref, q_ref, k_ref, v_ref, kr_ref, vr_ref, o_ref, do_ref, lse_ref, act_ref, far_ref, wk_ref, wv_ref, *refs):
    refs = refs[skip:]
    if started:
        start_far_ref, *refs = refs
    mine_ref, theirs_ref, own_grads, *refs = refs
    dfar_ref, *dfar_refs = (refs[-1:] + refs[:-10]) if last else refs[:1]
    kt, krt, dka, dva, dkra, dvra, weights, kd, krd = refs[-10:-1] if last else refs[-9:]
    tok = q_ref.shape[0]
    remote = kr_ref.shape[0]
    lane = lax.broadcasted_iota(jnp.int32, (1, 128), 1)
    low_half = lane < HEAD_DIM
    c = SCALE * LOG2E
    zero = jnp.zeros((), bf16)
    for head in range(2):
        kd[head] = both_halves(k_ref[...], head, low_half)
        krd[head] = both_halves(kr_ref[...], head, low_half)
    kt[...] = k_ref[...].T
    krt[...] = kr_ref[...].T
    dka[...] = jnp.zeros_like(dka)
    dva[...] = jnp.zeros_like(dva)
    dkra[...] = jnp.zeros_like(dkra)
    dvra[...] = jnp.zeros_like(dvra)
    pick = lax.broadcasted_iota(jnp.int32, (16, 128), 0) // 8 == lax.broadcasted_iota(jnp.int32, (16, 128), 1) // HEAD_DIM
    pick = jnp.where(pick, 1.0, 0.0).astype(bf16)
    for start, size, is_prompt in query_tiles(tok, plen):
        rows = slice(start, start + size)
        product = do_ref[rows, :].astype(f32) * o_ref[rows, :].astype(f32)
        high = product.astype(bf16)
        rest = (product - high.astype(f32)).astype(bf16)
        delta = dot_nt(pick, high) + dot_nt(pick, rest)
        totals = [None, None]
        masks = [low_half, ~low_half]
        qh = [jnp.where(m, q_ref[rows, :], zero) for m in masks]
        qs = [scaled_queries(q_ref[rows, :], head, low_half) for head in range(2)]
        doh = [jnp.where(m, do_ref[rows, :], zero) for m in masks]
        segments = [(kd, v_ref, kt, dka, dva, start, size, "diag")]
        if is_prompt:
            for j in range(remote // plen):
                segments.append((krd, vr_ref, krt, dkra, dvra, j * plen, plen, j))
        else:
            segments.append((kd, v_ref, kt, dka, dva, 0, start, None))
            segments.append((krd, vr_ref, krt, dkra, dvra, 0, remote, None))
        for kk, vv, tt, dk_acc, dv_acc, at, n, mode in segments:
            keys = slice(at, at + n)
            scores = [dot_nt(kk[head, keys, :], qs[head]) for head in range(2)]
            d_probs = [dot_nt(vv[keys, :], doh[head]) for head in range(2)]
            low_p, low_d = [], []
            for head in range(2):
                st = scores[head] - lse_ref[0, 8 * head : 8 * head + 1, rows]
                if mode == "diag":
                    key = lax.broadcasted_iota(jnp.int32, (n, size), 0)
                    query = lax.broadcasted_iota(jnp.int32, (n, size), 1)
                    st = jnp.where(key <= query, st, NEG)
                elif mode is not None:
                    st = st + flags_ref[mode]
                pt = jnp.exp2(st)
                low_p.append(pt.astype(bf16))
                low_d.append((pt * (d_probs[head] - delta[8 * head : 8 * head + 1, :])).astype(bf16))
            dv_acc[keys, :] += dot_nn(low_p[0], doh[0]) + dot_nn(low_p[1], doh[1])
            dk_acc[keys, :] += dot_nn(low_d[0], qh[0]) + dot_nn(low_d[1], qh[1])
            for head in range(2):
                part = dot_nn(tt[head * HEAD_DIM : (head + 1) * HEAD_DIM, keys], low_d[head])
                totals[head] = part if totals[head] is None else totals[head] + part
        dqt = totals
        own_grads[rows, 0:128] = (jnp.concatenate(dqt, axis=0).T * SCALE).astype(bf16)
    own_grads[:, 128:256] = (dka[...] * SCALE).astype(bf16)
    own_grads[:, 256:384] = dva[...].astype(bf16)
    far_grads = jnp.concatenate([(dkra[...] * SCALE).astype(bf16), dvra[...].astype(bf16)], axis=1)
    weights[:, 0:128] = wk_ref[...]
    weights[:, 128:256] = wv_ref[...]
    half = mine_ref.shape[0]
    for out_ref, which in ((theirs_ref, 1 - core_ref[0]), (mine_ref, core_ref[0])):
        rows = pl.ds(pl.multiple_of(which * half, half), half)
        total = dot_nn(act_ref[rows, :], own_grads[...])
        out_ref[:, 0:128] = total[:, 0:128].astype(bf16)
        out_ref[:, 128:384] = (total[:, 128:384] + dot_nn(far_ref[rows, :], far_grads)).astype(bf16)
    d_far = dot_nt(far_grads, weights[...])
    step = pl.program_id(0)

    @pl.when(step == 0)
    def _():
        dfar_ref[...] = d_far + start_far_ref[...] if started else d_far

    @pl.when(step > 0)
    def _():
        dfar_ref[...] += d_far

    if last:

        @pl.when(step == pl.num_programs(0) - 1)
        def _():
            for k, ref in enumerate(dfar_refs):
                ref[...] = dfar_ref[k * plen : (k + 1) * plen, :].astype(bf16)


def attention_backward(flags, core, proj, kv_rem, mixed, d_mixed, lse, act_t, far_t, w_qkv, plen, begin, count, buffers, at, starts, last):
    tok, width = mixed.shape
    remote = kv_rem.shape[0]
    pairs = width // 128
    own = lambda shift: pl.BlockSpec((tok, 128), lambda i: (0, shift + i))
    far = lambda shift: pl.BlockSpec((remote, 128), lambda i: (0, shift + i))
    weight = lambda shift: pl.BlockSpec((width, 128), lambda i: (0, shift + i))
    still = lambda shape: pl.BlockSpec(shape, lambda i: (0, 0))
    half = pl.BlockSpec((width // 2, 384), lambda i: (0, at + i))
    in_specs = [
        pl.BlockSpec(memory_space=pltpu.SMEM),
        pl.BlockSpec(memory_space=pltpu.SMEM),
        own(begin),
        own(pairs + begin),
        own(2 * pairs + begin),
        far(begin),
        far(pairs + begin),
        own(begin),
        own(begin),
        pl.BlockSpec((1, 16, tok), lambda i: (begin + i, 0, 0)),
        still((width, tok)),
        still((width, remote)),
        weight(pairs + begin),
        weight(2 * pairs + begin),
    ]
    arrays = [flags, core, proj, proj, proj, kv_rem, kv_rem, mixed, d_mixed, lse, act_t, far_t, w_qkv, w_qkv]
    scratch = [
        pltpu.VMEM((128, tok), bf16),
        pltpu.VMEM((128, remote), bf16),
        pltpu.VMEM((tok, 128), f32),
        pltpu.VMEM((tok, 128), f32),
        pltpu.VMEM((remote, 128), f32),
        pltpu.VMEM((remote, 128), f32),
        pltpu.VMEM((width, 256), bf16),
        pltpu.VMEM((2, tok, 128), bf16),
        pltpu.VMEM((2, remote, 128), bf16),
    ]
    aliases = {}
    skip = 0
    if not isinstance(buffers, int):
        aliases = {len(arrays): 0, len(arrays) + 1: 1}
        in_specs += [pl.BlockSpec(memory_space=pl.ANY)] * 2
        arrays += list(buffers)
        skip = 2
        buffers = buffers[0].shape[1]
    if starts:
        in_specs += [still((remote, width))]
        arrays += list(starts)
    out_specs = [half, half, pl.BlockSpec((tok, 384), lambda i: (0, i))]
    out_shape = [jax.ShapeDtypeStruct((width // 2, buffers), bf16)] * 2 + [jax.ShapeDtypeStruct((tok, count * 384), bf16)]
    if last:
        out_specs += [still((plen, width))] * (remote // plen)
        out_shape += [jax.ShapeDtypeStruct((plen, width), bf16)] * (remote // plen)
        scratch = scratch + [pltpu.VMEM((remote, width), f32)]
    else:
        out_specs += [still((remote, width))]
        out_shape += [jax.ShapeDtypeStruct((remote, width), f32)]
    return pl.pallas_call(
        functools.partial(attention_backward_kernel, plen, bool(starts), last, skip),
        grid=(count,),
        in_specs=in_specs,
        out_specs=out_specs,
        out_shape=out_shape,
        scratch_shapes=scratch,
        input_output_aliases=aliases,
        compiler_params=pltpu.CompilerParams(vmem_limit_bytes=60 * 2**20),
        cost_estimate=pl.CostEstimate(flops=10 * tok * (tok + remote) * count * 128 + 20 * tok * width * count * 128, bytes_accessed=2 * (tok * 8 + remote * 4) * count * 128 + 16 * tok * width, transcendentals=tok * (tok + remote) * 2 * count),
        name="attention_backward",
    )(*arrays)


FFN_EXPERTS = 8
ALL_EXPERTS = 12
EXTRA = 128
SMALL = 8
epsilon = 1e-06


def dot_tn(a, b):
    return lax.dot_general(a, b, (((0,), (0,)), ((), ())), preferred_element_type=f32)


def split_low(value, parts):
    pieces = []
    for _ in range(parts):
        piece = value.astype(bf16)
        pieces.append(piece)
        value = value - piece.astype(f32)
    return pieces


def route_kernel(groups, home_ref, ids_ref, grad_ref, prev_ref, *out_refs):
    tok, width = grad_ref.shape
    count = len(groups)
    turned_refs, chosen_refs, early_ref = out_refs[:count], out_refs[count : 2 * count], out_refs[2 * count]
    expert = lax.broadcasted_iota(jnp.int32, (16, tok), 0)
    ids = jnp.concatenate([ids_ref[...].astype(f32), jnp.zeros((tok, EXTRA - 2), f32)], axis=1).T.astype(jnp.int32)
    ids = [ids[k : k + 1, :] for k in range(2)]
    names = [row == expert for row in ids]
    both = jnp.where(names[0] | names[1], 1.0, 0.0).astype(bf16)
    earlier = lax.broadcasted_iota(jnp.int32, (tok, tok), 0) < lax.broadcasted_iota(jnp.int32, (tok, tok), 1)
    before = dot_nn(both, jnp.where(earlier, 1.0, 0.0).astype(bf16))
    pieces = [piece.astype(f32) for piece in split_low(jnp.concatenate([prev_ref[...], jnp.zeros((tok, EXTRA - ALL_EXPERTS), f32)], axis=1), 3)]
    extra = (pieces[0] + pltpu.roll(pieces[1], 16, 1) + pltpu.roll(pieces[2], 32, 1)).astype(bf16)
    slot = [jnp.sum(jnp.where(n, before, 0.0), axis=0, keepdims=True).astype(jnp.int32) for n in names]
    for (first, size), turned_ref, chosen_ref in zip(groups, turned_refs, chosen_refs):
        spots = lax.broadcasted_iota(jnp.int32, (FFN_EXPERTS * size, tok), 0)
        hit = None
        for k in range(2):
            inside = (ids[k] < FFN_EXPERTS) & (slot[k] >= first) & (slot[k] < first + size)
            place = jnp.where(inside, ids[k] * size + slot[k] - first, -1)
            hit = spots == place if hit is None else hit | (spots == place)
        turned = jnp.where(hit, 1.0, 0.0).astype(bf16)
        turned_ref[...] = turned
        chosen_ref[...] = turned.T
        grads = dot_nn(turned, grad_ref[...]).astype(bf16)
        extras = dot_nn(turned, extra).astype(bf16)
        for e in range(FFN_EXPERTS):
            early_ref[e, first : first + size, 0:width] = grads[e * size : (e + 1) * size]
            early_ref[e, first : first + size, width : width + EXTRA] = extras[e * size : (e + 1) * size]


def route_plan(home, ids, grad, prev, groups):
    tok, width = grad.shape
    counts = [FFN_EXPERTS * size for _, size in groups]
    whole = pl.BlockSpec(memory_space=pltpu.VMEM)
    out = pl.pallas_call(
        functools.partial(route_kernel, groups),
        in_specs=[pl.BlockSpec(memory_space=pltpu.SMEM), whole, whole, whole],
        out_specs=[whole] * (2 * len(groups) + 1),
        out_shape=[jax.ShapeDtypeStruct((n, tok), bf16) for n in counts]
        + [jax.ShapeDtypeStruct((tok, n), bf16) for n in counts]
        + [jax.ShapeDtypeStruct((FFN_EXPERTS, sum(counts) // FFN_EXPERTS, width + EXTRA), bf16)],
        compiler_params=pltpu.CompilerParams(vmem_limit_bytes=60 * 2**20),
        cost_estimate=pl.CostEstimate(flops=2 * sum(counts) * tok * (width + EXTRA), bytes_accessed=4 * sum(counts) * width, transcendentals=0),
        name="route_plan",
    )(home, ids, grad, prev)
    return out[: len(groups)], out[len(groups) : -1], out[-1]


def expert_kernel(group, home_ref, rows_ref, early_ref, router_ref, wg_ref, wu_ref, wd_ref,
                  out_ref, drow_ref, dout_ref, inner_ref, dgate_ref, dup_ref, small_ref, acc_out, acc_row, probs_ref):
    width = rows_ref.shape[1]
    step, steps = pl.program_id(0), pl.num_programs(0)
    home = home_ref[0]
    lane = lax.broadcasted_iota(jnp.int32, (1, EXTRA), 1)
    slots = slice(group[0], group[0] + group[1])

    @pl.when(step == 0)
    def _():
        extra = early_ref[:, slots, width : width + EXTRA].astype(f32).reshape(-1, EXTRA)
        logits = extra + pltpu.roll(extra, EXTRA - 16, 1) + pltpu.roll(extra, EXTRA - 32, 1)
        logits = logits + dot_nn(rows_ref[...], router_ref[...])
        logits = jnp.where(lane < ALL_EXPERTS, logits, NEG)
        unnormed = jnp.exp(logits - jnp.max(logits, axis=1, keepdims=True))
        probs = unnormed / jnp.sum(unnormed, axis=1, keepdims=True)
        probs_ref[...] = probs
        gate = jnp.sum(jnp.where(lane == home, probs, 0.0), axis=1, keepdims=True)
        dout_ref[...] = (gate * early_ref[:, slots, 0:width].astype(f32).reshape(-1, width)).astype(bf16)
        acc_out[...] = jnp.zeros_like(acc_out)
        acc_row[...] = jnp.zeros_like(acc_row)

    rows = rows_ref[...]
    gate_pre = dot_nn(rows, wg_ref[0])
    up_pre = dot_nn(rows, wu_ref[0])
    d_inner = dot_nt(dout_ref[...], wd_ref[0])
    sigmoid = jax.nn.sigmoid(gate_pre)
    silu = gate_pre * sigmoid
    inner = (silu * up_pre).astype(bf16)
    d_gate = (d_inner * up_pre * (sigmoid * (1.0 + gate_pre * (1.0 - sigmoid)))).astype(bf16)
    d_up = (d_inner * silu).astype(bf16)
    inner_ref[...] = inner
    dgate_ref[...] = d_gate
    dup_ref[...] = d_up
    acc_out[...] += dot_nn(inner, wd_ref[0])
    acc_row[...] += dot_nt(d_gate, wg_ref[0]) + dot_nt(d_up, wu_ref[0])

    @pl.when(step == steps - 1)
    def _():
        probs = probs_ref[...]
        gate = jnp.sum(jnp.where(lane == home, probs, 0.0), axis=1, keepdims=True)
        out = acc_out[...].astype(bf16).astype(f32)
        d_row_gate = jnp.sum(out * early_ref[:, slots, 0:width].astype(f32).reshape(-1, width), axis=1, keepdims=True)
        out_ref[:, 0:width] = (gate * out).astype(bf16)
        extra = jnp.zeros((out.shape[0], EXTRA), f32)
        for i, piece in enumerate(split_low(d_row_gate, 3)):
            extra = jnp.where(lane == home + 16 * i, piece.astype(f32), extra)
        out_ref[:, width : width + EXTRA] = extra.astype(bf16)
        term = d_row_gate * gate * (jnp.where(lane == home, 1.0, 0.0) - probs)
        high, rest = split_low(term, 2)
        turned = [piece.T for piece in (high, rest)]
        small_ref[...] = (dot_nn(turned[0], rows) + dot_nn(turned[1], rows))[0 : 2 * SMALL, :]
        drow_ref[...] = (acc_row[...] + dot_nt(high, router_ref[...]) + dot_nt(rest, router_ref[...])).astype(bf16)


def expert_pass(group, home, rows, early, router_pad, w_gate, w_up, w_down):
    count, width = rows.shape
    ff = w_gate.shape[2]
    tile = min(512, ff)
    full = pl.BlockSpec((count, width), lambda j: (0, 0))
    wide = pl.BlockSpec((count, width + EXTRA), lambda j: (0, 0))
    tall = pl.BlockSpec((1, width, tile), lambda j: (0, 0, j))
    piece = pl.BlockSpec((count, tile), lambda j: (0, j))
    return pl.pallas_call(
        functools.partial(expert_kernel, group),
        grid=(ff // tile,),
        in_specs=[
            pl.BlockSpec(memory_space=pltpu.SMEM),
            full,
            pl.BlockSpec(early.shape, lambda j: (0, 0, 0)),
            pl.BlockSpec((width, EXTRA), lambda j: (0, 0)),
            tall,
            tall,
            pl.BlockSpec((1, tile, width), lambda j: (0, j, 0)),
        ],
        out_specs=[wide, full, full, piece, piece, piece, pl.BlockSpec((2 * SMALL, width), lambda j: (0, 0))],
        out_shape=[
            jax.ShapeDtypeStruct((count, width + EXTRA), bf16),
            jax.ShapeDtypeStruct((count, width), bf16),
            jax.ShapeDtypeStruct((count, width), bf16),
        ]
        + [jax.ShapeDtypeStruct((count, ff), bf16)] * 3
        + [jax.ShapeDtypeStruct((2 * SMALL, width), f32)],
        scratch_shapes=[pltpu.VMEM((count, width), f32), pltpu.VMEM((count, width), f32), pltpu.VMEM((count, EXTRA), f32)],
        compiler_params=pltpu.CompilerParams(vmem_limit_bytes=60 * 2**20),
        cost_estimate=pl.CostEstimate(flops=12 * count * width * ff, bytes_accessed=6 * width * ff + 2 * count * (5 * width + 3 * ff), transcendentals=count * ff),
        name="expert_pass",
    )(home, rows, early, router_pad, w_gate, w_up, w_down)


def weight_kernel(count, *refs):
    rows, douts, inners, dgates, dups = (refs[i * count : (i + 1) * count] for i in range(5))
    gate_up_ref, down_ref = refs[5 * count : 5 * count + 2]
    turned = refs[5 * count + 2 :]

    @pl.when(pl.program_id(0) == 0)
    def _():
        for ref, scratch in zip(rows, turned):
            scratch[...] = ref[...].T

    gate_up_ref[0] = sum(dot_nn(t[...], d[...]) for t, d in zip(turned, dgates)).astype(bf16)
    gate_up_ref[1] = sum(dot_nn(t[...], d[...]) for t, d in zip(turned, dups)).astype(bf16)
    down_ref[...] = sum(dot_nn(i[...].T, d[...]) for i, d in zip(inners, douts)).astype(bf16)


def weight_gradients(rows, douts, inners, dgates, dups):
    count = len(rows)
    width, ff = rows[0].shape[1], inners[0].shape[1]
    tile = min(512, ff)
    total = sum(r.shape[0] for r in rows)
    full = [pl.BlockSpec(r.shape, lambda j: (0, 0)) for r in rows]
    piece = [pl.BlockSpec((r.shape[0], tile), lambda j: (0, j)) for r in rows]
    return pl.pallas_call(
        functools.partial(weight_kernel, count),
        grid=(ff // tile,),
        in_specs=full + full + piece * 3,
        out_specs=[pl.BlockSpec((2, width, tile), lambda j: (0, 0, j)), pl.BlockSpec((tile, width), lambda j: (j, 0))],
        out_shape=[jax.ShapeDtypeStruct((2, width, ff), bf16), jax.ShapeDtypeStruct((ff, width), bf16)],
        scratch_shapes=[pltpu.VMEM((width, r.shape[0]), bf16) for r in rows],
        compiler_params=pltpu.CompilerParams(vmem_limit_bytes=60 * 2**20),
        cost_estimate=pl.CostEstimate(flops=6 * total * width * ff, bytes_accessed=6 * width * ff + 2 * total * (2 * width + 3 * ff), transcendentals=0),
        name="weight_gradients",
    )(*rows, *douts, *inners, *dgates, *dups)


ANYWHERE = pl.BlockSpec(memory_space=pltpu.VMEM)
SCALARS = pl.BlockSpec(memory_space=pltpu.SMEM)


def inverse_rms(value):
    return lax.rsqrt(jnp.mean(value * value, axis=1, keepdims=True) + epsilon)


def after_attention_kernel(count, mixed_ref, x_ref, w_ref, gain_ref, *refs):
    turned, (hidden_ref, low_ref), sent = refs[:count], refs[count : count + 2], refs[count + 2 :]
    hidden = x_ref[...].astype(f32) + dot_nn(mixed_ref[...], w_ref[...])
    low = (hidden * inverse_rms(hidden) * gain_ref[...]).astype(bf16)
    hidden_ref[...] = hidden
    low_ref[...] = low
    for t, s in zip(turned, sent):
        s[...] = dot_nn(t[...], low).astype(bf16)


def after_attention(mixed, x, w_out, gain, turned):
    tok, width = x.shape
    rows = sum(t.shape[0] for t in turned)
    out = pl.pallas_call(
        functools.partial(after_attention_kernel, len(turned)),
        in_specs=[ANYWHERE] * (4 + len(turned)),
        out_specs=[ANYWHERE] * (2 + len(turned)),
        out_shape=[jax.ShapeDtypeStruct((tok, width), f32), jax.ShapeDtypeStruct((tok, width), bf16)]
        + [jax.ShapeDtypeStruct((t.shape[0], width), bf16) for t in turned],
        compiler_params=pltpu.CompilerParams(vmem_limit_bytes=60 * 2**20),
        cost_estimate=pl.CostEstimate(flops=2 * tok * width * (width + rows), bytes_accessed=2 * width * (6 * tok + 2 * rows), transcendentals=0),
        name="after_attention",
    )(mixed, x, w_out, gain, *turned)
    return out[0], out[1], out[2:]


def turn_kernel(in_ref, out_ref):
    out_ref[...] = in_ref[...].T


def turn(value):
    rows, columns = value.shape
    block = 256 if rows % 256 == 0 else 128
    return pl.pallas_call(
        turn_kernel,
        grid=(rows // block,),
        in_specs=[pl.BlockSpec((block, columns), lambda i: (i, 0))],
        out_specs=pl.BlockSpec((columns, block), lambda i: (0, i)),
        out_shape=jax.ShapeDtypeStruct((columns, rows), value.dtype),
        compiler_params=pltpu.CompilerParams(vmem_limit_bytes=60 * 2**20),
        cost_estimate=pl.CostEstimate(flops=0, bytes_accessed=4 * rows * columns, transcendentals=0),
        name="turn",
    )(value)


def place(value, lane, at):
    return jnp.where(lane == at, value, 0.0)


def local_kernel(hidden_ref, low_ref, grad_ref, prev_ref, ids_ref, mix_ref, gain_ref, vec_ref, out_ref, dnormed_ref, probs_ref, dprobs_ref, small_ref):
    lane = lax.broadcasted_iota(jnp.int32, (1, EXTRA), 1)
    hidden = hidden_ref[...]
    normed = hidden * inverse_rms(hidden) * gain_ref[...]
    low = low_ref[...]
    grad = grad_ref[...].astype(f32)
    raw = dot_nn(low, mix_ref[...])
    prev = jnp.concatenate([prev_ref[...], jnp.zeros((raw.shape[0], EXTRA - ALL_EXPERTS), f32)], axis=1)
    logits = jnp.where(lane < ALL_EXPERTS, raw + prev, NEG)
    unnormed = jnp.exp(logits - jnp.max(logits, axis=1, keepdims=True))
    probs = unnormed / jnp.sum(unnormed, axis=1, keepdims=True)
    named = (ids_ref[:, 0:1] == lane) | (ids_ref[:, 1:2] == lane)
    gates = jnp.where(named, probs, 0.0)
    copy_gate = gates[:, FFN_EXPERTS + 1 : FFN_EXPERTS + 2]
    dots = jnp.sum(grad * normed, axis=1, keepdims=True)
    out = hidden
    weight = copy_gate
    d_probs = place(dots, lane, FFN_EXPERTS + 1)
    logit_grads = jnp.zeros_like(probs)
    vec_terms = jnp.zeros_like(probs)
    for c in range(2):
        vec = vec_ref[c : c + 1, :]
        gate = gates[:, FFN_EXPERTS + 2 + c : FFN_EXPERTS + 3 + c]
        at = 16 + 2 * c
        a0 = jax.nn.sigmoid(raw[:, at : at + 1] - raw[:, at + 1 : at + 2])
        a1 = jax.nn.sigmoid(raw[:, at + 1 : at + 2] - raw[:, at : at + 1])
        vec_dots = jnp.sum(grad * vec, axis=1, keepdims=True)
        weight = weight + gate * a0
        out = out + (gate * a1) * vec
        d_probs = d_probs + place(a0 * dots + a1 * vec_dots, lane, FFN_EXPERTS + 2 + c)
        d0, d1 = gate * dots, gate * vec_dots
        mean = a0 * d0 + a1 * d1
        d0, d1 = a0 * (d0 - mean), a1 * (d1 - mean)
        logit_grads = logit_grads + place(d0, lane, at) + place(d1, lane, at + 1)
        vec_terms = vec_terms + place(gate * a1, lane, 20 + c)
    d_probs = jnp.where(named, d_probs, 0.0)
    logit_grads = logit_grads + probs * (d_probs - jnp.sum(probs * d_probs, axis=1, keepdims=True))
    high, rest = split_low(logit_grads, 2)
    out_ref[...] = out + weight * normed
    dnormed_ref[...] = weight * grad + dot_nt(high, mix_ref[...]) + dot_nt(rest, mix_ref[...])
    probs_ref[...] = probs
    dprobs_ref[...] = d_probs
    sums = None
    for terms, rows in ((logit_grads, low), (vec_terms, grad_ref[...])):
        for piece in split_low(terms.T, 2):
            part = dot_nn(piece, rows)
            sums = part if sums is None else sums + part
    sums = sums[0 : 3 * SMALL, :]

    @pl.when(pl.program_id(0) == 0)
    def _():
        small_ref[...] = sums

    @pl.when(pl.program_id(0) > 0)
    def _():
        small_ref[...] += sums


def local_part(hidden, low, grad, prev, ids, mix, gain, vec):
    tok, width = hidden.shape
    block, tiles = row_tiles(tok)
    shapes = [(tok, width), (tok, width), (tok, EXTRA), (tok, EXTRA), (3 * SMALL, width)]
    return pl.pallas_call(
        local_kernel,
        grid=(tok // block,),
        in_specs=[tiles(width), tiles(width), tiles(width), tiles(ALL_EXPERTS), tiles(2), fixed(mix), fixed(gain), fixed(vec)],
        out_specs=[tiles(width), tiles(width), tiles(EXTRA), tiles(EXTRA), pl.BlockSpec((3 * SMALL, width), lambda i: (0, 0))],
        out_shape=[jax.ShapeDtypeStruct(s, f32) for s in shapes],
        compiler_params=pltpu.CompilerParams(vmem_limit_bytes=60 * 2**20),
        cost_estimate=pl.CostEstimate(flops=14 * tok * width * EXTRA, bytes_accessed=16 * tok * width, transcendentals=tok * EXTRA),
        name="local_part",
    )(hidden, low, grad, prev, ids, mix, gain, vec)


def row_tiles(tok):
    block = 256 if tok % 256 == 0 else 128
    return block, lambda columns: pl.BlockSpec((block, columns), lambda i: (i, 0))


def fixed(value):
    return pl.BlockSpec(value.shape, lambda i: (0,) * value.ndim)


def combine_kernel(count, parts, core_ref, *refs):
    chosen, got, refs = refs[:count], refs[count : count * (1 + parts)], refs[count * (1 + parts) :]
    smalls, refs = refs[: count + 1], refs[count + 1 :]
    local_ref, hidden_ref, gain_ref, grad_ref, mixed_ref, w_ref, dhidden_ref, dmixed_ref, mine_ref, theirs_ref, total_w, total_gain, small_t = refs
    step = pl.program_id(0)

    @pl.when(step == 0)
    def _():
        total_w[...] = jnp.zeros_like(total_w)
        total_gain[...] = jnp.zeros_like(total_gain)

    d_normed = local_ref[...]
    for g in range(count):
        for r in range(parts):
            d_normed = d_normed + dot_nn(chosen[g][...], got[g * parts + r][...])
    hidden = hidden_ref[...]
    inverse = inverse_rms(hidden)
    scaled = d_normed * gain_ref[...]
    mean = jnp.mean(scaled * hidden, axis=1, keepdims=True)
    d_hidden = grad_ref[...].astype(f32) + inverse * scaled - hidden * (inverse * inverse * inverse * mean)
    low = d_hidden.astype(bf16)
    dhidden_ref[...] = d_hidden
    dmixed_ref[...] = dot_nt(low, w_ref[...]).astype(bf16)
    total_w[...] += dot_nn(mixed_ref[...].T, low)
    total_gain[...] += jnp.sum(d_normed * hidden * inverse, axis=0, keepdims=True)

    @pl.when(step == pl.num_programs(0) - 1)
    def _():
        width = w_ref.shape[0]
        half = width // 2
        row = lax.broadcasted_iota(jnp.int32, (SMALL, 1), 0)
        top = smalls[0][0 : 2 * SMALL, :]
        for small in smalls[1:]:
            top = top + small[...]
        rest = jnp.zeros((EXTRA - 4 * SMALL, width), f32)
        rows = [top, smalls[0][2 * SMALL : 3 * SMALL, :], jnp.where(row == 0, total_gain[...], 0.0), rest]
        small_t[...] = jnp.concatenate(rows, axis=0).T
        at = mine_ref.shape[1] - width - EXTRA
        for out_ref, which in ((theirs_ref, 1 - core_ref[0]), (mine_ref, core_ref[0])):
            place_rows = pl.ds(pl.multiple_of(which * half, half), half)
            out_ref[:, at : at + width] = total_w[place_rows, :].astype(bf16)
            out_ref[:, at + width : at + width + EXTRA] = small_t[place_rows, :].astype(bf16)


def combine(core, chosen, got, smalls, local, hidden, gain, grad, mixed, w_out, columns):
    tok, width = hidden.shape
    rows = sum(c.shape[1] for c in chosen)
    arrays = [a for group in got for a in group]
    block, tiles = row_tiles(tok)
    half = (width // 2, columns + width + EXTRA)
    return pl.pallas_call(
        functools.partial(combine_kernel, len(chosen), len(got[0])),
        grid=(tok // block,),
        in_specs=[SCALARS] + [tiles(c.shape[1]) for c in chosen] + [fixed(a) for a in arrays + smalls]
        + [tiles(width), tiles(width), fixed(gain), tiles(width), tiles(width), fixed(w_out)],
        out_specs=[tiles(width)] * 2 + [pl.BlockSpec(half, lambda i: (0, 0))] * 2,
        out_shape=[jax.ShapeDtypeStruct((tok, width), f32), jax.ShapeDtypeStruct((tok, width), bf16)] + [jax.ShapeDtypeStruct(half, bf16)] * 2,
        scratch_shapes=[pltpu.VMEM((width, width), f32), pltpu.VMEM((1, width), f32), pltpu.VMEM((width, EXTRA), f32)],
        compiler_params=pltpu.CompilerParams(vmem_limit_bytes=60 * 2**20),
        cost_estimate=pl.CostEstimate(flops=2 * tok * width * (rows + 2 * width), bytes_accessed=2 * width * (10 * tok + 2 * rows), transcendentals=0),
        name="combine_gradients",
    )(core, *chosen, *arrays, *smalls, local, hidden, gain, grad, mixed, w_out)


def flat_rows(value):
    if value.shape[1] % 16:
        return value.astype(f32).reshape(-1, value.shape[2]).astype(bf16)
    return value.reshape(-1, value.shape[2])


def finish_kernel(groups, parts, *refs):
    chosen, got = refs[: len(groups)], refs[len(groups) : len(groups) + parts]
    local_ref, probs_ref, dprobs_ref, out_ref, dlogits_ref = refs[len(groups) + parts :]
    width = local_ref.shape[1]
    lane = lax.broadcasted_iota(jnp.int32, (1, EXTRA), 1)
    picked = None
    for c, (at, size) in zip(chosen, groups):
        for r in range(parts):
            part = dot_nn(c[...], flat_rows(got[r][:, at : at + size, :]))
            picked = part if picked is None else picked + part
    out_ref[...] = (local_ref[...] + picked[:, 0:width]).astype(bf16)
    extra = picked[:, width : width + EXTRA]
    extra = extra + pltpu.roll(extra, EXTRA - 16, 1) + pltpu.roll(extra, EXTRA - 32, 1)
    d_probs = dprobs_ref[...] + jnp.where(lane < ALL_EXPERTS, extra, 0.0)
    probs = probs_ref[...]
    d_logits = probs * (d_probs - jnp.sum(probs * d_probs, axis=1, keepdims=True))
    dlogits_ref[...] = d_logits.T


def finish(chosen, got, groups, local, probs, d_probs):
    tok, width = local.shape
    block, tiles = row_tiles(tok)
    return pl.pallas_call(
        functools.partial(finish_kernel, groups, len(got)),
        grid=(tok // block,),
        in_specs=[tiles(c.shape[1]) for c in chosen] + [fixed(g) for g in got] + [tiles(width), tiles(EXTRA), tiles(EXTRA)],
        out_specs=[tiles(width), pl.BlockSpec((EXTRA, block), lambda i: (0, i))],
        out_shape=[jax.ShapeDtypeStruct((tok, width), bf16), jax.ShapeDtypeStruct((EXTRA, tok), f32)],
        compiler_params=pltpu.CompilerParams(vmem_limit_bytes=60 * 2**20),
        cost_estimate=pl.CostEstimate(flops=2 * tok * 1152 * (width + EXTRA), bytes_accessed=16 * tok * width, transcendentals=0),
        name="finish_outputs",
    )(*chosen, *got, local, probs, d_probs)


def input_kernel(count, x_ref, gain_ref, dhidden_ref, w_ref, *refs):
    grads, far, (out_ref, weights) = refs[:count], refs[count:-2], refs[-2:]
    width = x_ref.shape[1]

    @pl.when(pl.program_id(0) == 0)
    def _():
        for i in range(width // 128):
            for p in range(3):
                weights[:, i * 384 + p * 128 : i * 384 + (p + 1) * 128] = w_ref[:, p * width + i * 128 : p * width + (i + 1) * 128]

    total = None
    for ref in far:
        total = ref[...].astype(f32) if total is None else total + ref[...].astype(f32)
    d_act = jnp.where(pl.program_id(0) == 0, total, 0.0)
    at = 0
    for ref in grads:
        columns = ref.shape[1]
        d_act = d_act + dot_nt(ref[...], weights[:, at : at + columns])
        at += columns
    x = x_ref[...].astype(f32)
    inverse = inverse_rms(x)
    scaled = d_act * gain_ref[...]
    mean = jnp.mean(scaled * x, axis=1, keepdims=True)
    out_ref[...] = dhidden_ref[...] + inverse * scaled - x * (inverse * inverse * inverse * mean)


def input_gradient(grads, x, gain, d_hidden, w_qkv, far):
    tok, width = x.shape
    block = far[0].shape[0]
    tiles = lambda columns: pl.BlockSpec((block, columns), lambda i: (i, 0))
    return pl.pallas_call(
        functools.partial(input_kernel, len(grads)),
        grid=(tok // block,),
        in_specs=[tiles(width), fixed(gain), tiles(width), fixed(w_qkv)] + [tiles(g.shape[1]) for g in grads] + [fixed(f) for f in far],
        out_specs=tiles(width),
        out_shape=jax.ShapeDtypeStruct((tok, width), f32),
        scratch_shapes=[pltpu.VMEM((width, 3 * width), bf16)],
        compiler_params=pltpu.CompilerParams(vmem_limit_bytes=60 * 2**20),
        cost_estimate=pl.CostEstimate(flops=6 * tok * width * width, bytes_accessed=22 * tok * width, transcendentals=0),
        name="input_gradient",
    )(x, gain, d_hidden, w_qkv, *grads, *far)


def xor_pairs(size, mask):
    return [(i, i ^ mask) for i in range(size)]


def sum_kernel(terms, index_ref, *refs):
    count = len(refs) // (sum(terms) + 1)
    outs = refs[-count:]
    for k, out_ref in enumerate(outs):
        at = 0
        first = 0
        for number in terms:
            total = None
            for t in range(first, first + number):
                value = refs[t * count + k][0].astype(f32)
                total = value if total is None else total + value
            out_ref[0, :, at : at + total.shape[1]] = total.astype(bf16)
            at += total.shape[1]
            first += number


def sum_pieces(index, groups):
    arrays = [a for group in groups for a in group]
    n, rows = arrays[0].shape[:2]
    columns = sum(group[0].shape[2] for group in groups)
    view = lambda a, k: pl.BlockSpec((1, rows, a.shape[2]), lambda i, s: (s[0] ^ k if n > 1 else 0, 0, 0))
    return pl.pallas_call(
        functools.partial(sum_kernel, [len(g) for g in groups]),
        grid_spec=pltpu.PrefetchScalarGridSpec(
            num_scalar_prefetch=1,
            grid=(1,),
            in_specs=[view(a, k) for a in arrays for k in range(n)],
            out_specs=[pl.BlockSpec((1, rows, columns), lambda i, s: (0, 0, 0))] * n,
        ),
        out_shape=[jax.ShapeDtypeStruct((1, rows, columns), bf16)] * n,
        compiler_params=pltpu.CompilerParams(vmem_limit_bytes=60 * 2**20),
        cost_estimate=pl.CostEstimate(flops=0, bytes_accessed=2 * n * rows * columns * 5, transcendentals=0),
        name="sum_pieces",
    )(index, *[a for a in arrays for _ in range(n)])


def quarters(value):
    return value.reshape(4, -1, value.shape[-1])


def swap(pieces, along):
    axis, size, unit = along
    return [pieces[0]] + [lax.ppermute(pieces[k], axis, xor_pairs(size, unit * k)) for k in range(1, 4)]


def spread(value, along):
    return swap([value] * 4, along)


def stack_kernel(*refs):
    n = len(refs) - 1
    size = refs[0].shape[0]
    for k in range(n):
        refs[n][k * size : (k + 1) * size] = refs[k][...]


def stack_pieces(pieces):
    shape = (len(pieces) * pieces[0].shape[0],) + pieces[0].shape[1:]
    return pl.pallas_call(
        stack_kernel,
        in_specs=[ANYWHERE] * len(pieces),
        out_specs=ANYWHERE,
        out_shape=jax.ShapeDtypeStruct(shape, bf16),
        compiler_params=pltpu.CompilerParams(vmem_limit_bytes=60 * 2**20),
        cost_estimate=pl.CostEstimate(flops=0, bytes_accessed=4 * math.prod(shape), transcendentals=0),
        name="stack_pieces",
    )(*pieces)


def unpack_kernel(left, index_ref, own_ref, other_ref, w_ref, scale_ref, out_ref, qkv_ref, router_ref, mixing_ref, vec_ref, gain_ref, attn_ref, small):
    width = out_ref.shape[1]
    piece = own_ref.shape[2]
    mine = pl.program_id(0) == index_ref[0]
    lane = lax.broadcasted_iota(jnp.int32, (1, EXTRA), 1)
    block = pl.program_id(0) * 4 + pl.program_id(1)
    for k in range(4):
        rows = slice(k * piece, (k + 1) * piece)
        at_ctx = k ^ index_ref[1]
        total = jnp.where(mine, own_ref[at_ctx, 0, :, :], other_ref[at_ctx, 0, :, :]).astype(f32)
        out_ref[rows, :] = total[:, left : left + width]
        gain = None
        for p in range(3):
            for i in range(width // 128):
                at = i * 384 + p * 128 + (0 if i * 384 < left else width + EXTRA)
                value = total[:, at : at + 128]
                columns = slice(p * width + i * 128, p * width + (i + 1) * 128)
                qkv_ref[rows, columns] = value
                part = value * w_ref[rows, columns].astype(f32)
                gain = part if gain is None else gain + part
        gain = jnp.sum(gain, axis=1, keepdims=True)
        small[pl.ds(block * 4 * piece + k * piece, piece), :] = total[:, left + width : left + width + EXTRA] + place(gain, lane, EXTRA - 1)

    @pl.when(block == 7)
    def _():
        turned = small[...].T
        router_ref[...] = turned[0:ALL_EXPERTS]
        mixing_ref[0] = turned[16:18]
        mixing_ref[1] = turned[18:20]
        vec_ref[...] = turned[20:22]
        gain_ref[...] = turned[24]
        attn_ref[...] = (turned[EXTRA - 1 : EXTRA] / scale_ref[...])[0]


def unpack(index, own, other, w_qkv, scale, left):
    width = w_qkv.shape[0]
    piece = width // 32
    block = 4 * piece
    own, other = own.reshape(4, 4, piece, -1), other.reshape(4, 4, piece, -1)
    row = lambda c, a, s: (c * 4 + a, 0)

    def source(core_of):
        def at(c, a, s):
            core = core_of(s[0])
            return 0, jnp.where(c == core, a, jnp.where(c < core, 0, 3)) ^ s[2], 0, 0

        return pl.BlockSpec((4, 1, piece, own.shape[3]), at)

    whole = lambda shape: pl.BlockSpec(shape, lambda c, a, s: (0,) * len(shape))
    shapes = ((ALL_EXPERTS, width), (2, 2, width), (2, width), (width,), (width,))
    return pl.pallas_call(
        functools.partial(unpack_kernel, left),
        grid_spec=pltpu.PrefetchScalarGridSpec(
            num_scalar_prefetch=1,
            grid=(2, 4),
            in_specs=[source(lambda core: core), source(lambda core: 1 - core), pl.BlockSpec((block, 3 * width), row), whole((1, width))],
            out_specs=[pl.BlockSpec((block, width), row), pl.BlockSpec((block, 3 * width), row), *[whole(s) for s in shapes]],
            scratch_shapes=[pltpu.VMEM((width, EXTRA), f32)],
        ),
        out_shape=[jax.ShapeDtypeStruct((width, width), f32), jax.ShapeDtypeStruct((width, 3 * width), f32), *[jax.ShapeDtypeStruct(s, f32) for s in shapes]],
        compiler_params=pltpu.CompilerParams(vmem_limit_bytes=60 * 2**20),
        cost_estimate=pl.CostEstimate(flops=0, bytes_accessed=36 * width * width, transcendentals=0),
        name="unpack_sums",
    )(index, own, other, w_qkv, scale)

P = jax.sharding.PartitionSpec


def rms_inverse(tensor):
    return lax.rsqrt(jnp.mean(tensor * tensor, axis=-1, keepdims=True) + epsilon)


def after(values, *others):
    return lax.optimization_barrier((values, others))[0]


def body(inputs, prev_logits, routes, attn_gain, w_qkv, w_out, moe_gain, router, const_gate, const_vec, w_gate, w_up, w_down, out_grad):
    n_ctx, n_exp = lax.axis_size("ctx"), lax.axis_size("exp")
    me_c, me_e = lax.axis_index("ctx"), lax.axis_index("exp")
    tok, width = inputs.shape[1], inputs.shape[2]
    plen = tok - CONT_LEN
    split = n_exp // FFN_EXPERTS
    capacity = max(4, tok // 64 * 12)
    first = -(-capacity // 32) * 16
    groups = ((0, first), (first, capacity - first))
    home = (me_e // split).reshape(1)

    def deal(value):
        value = jnp.repeat(value, split, axis=0) if split > 1 else value
        return lax.all_to_all(value, "exp", 0, 0, tiled=True)

    def give_back(value):
        value = lax.all_to_all(value, "exp", 0, 0, tiled=True)
        return [value[r::split] if split > 1 else value for r in range(split)]

    x_low = inputs[0]
    upstream_low = out_grad[0]
    far_rows = jnp.concatenate([lax.ppermute(x_low[:plen], "ctx", xor_pairs(n_ctx, k)) for k in range(1, n_ctx)], axis=0)
    flags = jnp.where((me_c ^ jnp.arange(1, n_ctx)) < me_c, 0.0, NEG).astype(f32)

    prev = prev_logits[0]
    mix = jnp.concatenate([router, jnp.zeros((width, 4), bf16), const_gate[0], const_gate[1], jnp.zeros((width, EXTRA - 20), bf16)], axis=1)
    router_pad = jnp.pad(router, ((0, 0), (0, EXTRA - ALL_EXPERTS)))
    turned, chosen, early_sent = route_plan(home, routes[0], upstream_low, prev, groups)

    tokens_in = x_low.astype(f32)
    inverse_attn = rms_inverse(tokens_in)
    act_low = (tokens_in * inverse_attn * attn_gain).astype(bf16)
    projected = dot_nn(act_low, w_qkv).astype(bf16)
    early = deal(early_sent)
    far_in = after(far_rows, projected).astype(f32)
    act_far = (far_in * rms_inverse(far_in) * attn_gain).astype(bf16)
    kv_far = dot_nn(act_far, w_qkv[:, width:]).astype(bf16)

    mixed_low, lse = attention_forward(flags, projected, kv_far, plen)
    mixed_low, early = lax.optimization_barrier((mixed_low, early))
    hidden, moe_low, sent = after_attention(mixed_low, x_low, w_out, moe_gain[None], turned)
    local_out, d_normed_local, probs, d_probs, small_local = local_part(hidden, moe_low, upstream_low, prev, routes[0], mix, moe_gain[None], const_vec)
    act_t, far_t = turn(act_low), turn(act_far)
    sent = [after(sent[0], local_out, d_normed_local, act_t, far_t), sent[1]]
    got = [deal(part.reshape(FFN_EXPERTS, -1, width)) for part in sent]

    got = [part.reshape(-1, width) for part in got]
    passes = [expert_pass(group, home, r, early, router_pad, w_gate, w_up, w_down) for group, r in zip(groups, got)]
    d_got = [give_back(p[1].reshape(n_exp, -1, width)) for p in passes]
    gate_up_low, down_low = weight_gradients(got, [p[2] for p in passes], [p[3] for p in passes], [p[4] for p in passes], [p[5] for p in passes])
    outs = jnp.concatenate([p[0].reshape(n_exp, -1, width + EXTRA) for p in passes], axis=1)
    d_got, gate_up_low, down_low, outs = lax.optimization_barrier((d_got, gate_up_low, down_low, outs))
    out_got = give_back(outs)

    d_got = [[part.reshape(-1, width) for part in group] for group in d_got]
    pairs = width // 128
    cut = pairs // 3
    core = (me_e & 1).reshape(1)
    smalls = [small_local] + [p[6] for p in passes]
    d_hidden, d_mixed, *buffers = combine(core, chosen, d_got, smalls, d_normed_local, hidden, moe_gain[None], upstream_low, mixed_low, w_out, cut * 384)

    sum_gate_up = lax.psum_scatter(gate_up_low, "ctx", scatter_dimension=1, tiled=True).astype(f32)
    sum_down = lax.psum_scatter(down_low, "ctx", scatter_dimension=0, tiled=True).astype(f32)

    def attention(upstream, begin, count, buffers, at, starts, last):
        return attention_backward(flags, core, projected, kv_far, mixed_low, upstream, lse, act_t, far_t, w_qkv, plen, begin, count, buffers, at, starts, last)

    dense = n_ctx == 4 and n_exp == 8
    left, right = cut * 384, (pairs - cut) * 384
    z = me_e >> 1
    at_ctx, at_z = me_c.reshape(1), z.reshape(1)
    along_ctx, along_z = ("ctx", 4, 1), ("exp", 8, 2)
    across = lambda value: lax.ppermute(value, "exp", xor_pairs(n_exp, 1))
    mine_1, theirs_1, grads_1, *starts = attention(d_mixed, 0, cut, buffers, 0, None, False)
    if dense:
        got_1 = across(theirs_1)
    mine_2, theirs_2, grads_2, *starts = attention(d_mixed, cut, 1, right, 0, starts, False)
    if dense:
        mine_2, theirs_2, starts, got_1 = lax.optimization_barrier((mine_2, theirs_2, starts, got_1))
        sums_1 = sum_pieces(at_z, [[quarters(mine_1), quarters(got_1)]])
        parts_1 = swap(sums_1, along_z)
        mine_2 = after(mine_2, sums_1[0])
    mine_2, theirs_2, grads_3, *d_far = attention(d_mixed, cut + 1, pairs - cut - 1, (mine_2, theirs_2), 1, starts, True)
    if dense:
        mine_2, theirs_2, grads_3, d_far, parts_1 = lax.optimization_barrier((mine_2, theirs_2, grads_3, d_far, parts_1))
    send_far = lambda k: lax.ppermute(d_far[k - 1], "ctx", xor_pairs(n_ctx, k))
    far_back = [send_far(k) for k in range(1, n_ctx - 1)]
    if dense:
        sums_2 = sum_pieces(at_z, [[quarters(mine_2), quarters(across(theirs_2))]])
        parts_2 = swap(sums_2, along_z)
        mixed_out, d_logits = finish(chosen, out_got, groups, after(local_out, sums_2[0]), probs, d_probs)
        mixed_out, d_logits, far_back, d_far = lax.optimization_barrier((mixed_out, d_logits, far_back, d_far))
        far_back = far_back + [send_far(n_ctx - 1)]
        mixed_out, parts_2 = lax.optimization_barrier((mixed_out, parts_2))
        parts_1, parts_2 = ([quarters(p) for p in parts] for parts in (parts_1, parts_2))
        parts = swap(sum_pieces(at_ctx, [parts_1, parts_2]), along_ctx)
        [piece] = sum_pieces(at_ctx, [parts])
        spread_z = spread(piece, along_z)
    else:
        mixed_out, d_logits = finish(chosen, out_got, groups, local_out, probs, d_probs)
        far_back = far_back + [send_far(n_ctx - 1)]
    d_inputs = input_gradient([grads_1, grads_2, grads_3], x_low, attn_gain[None], d_hidden, w_qkv, far_back)

    total_gate, total_up, total_down = sum_gate_up[0][None], sum_gate_up[1][None], sum_down[None]
    if dense:
        d_inputs, spread_z = lax.optimization_barrier((d_inputs, spread_z))
        column = stack_pieces(spread_z)
        own = stack_pieces(after(spread(column, along_ctx), total_gate, total_up, total_down))
        other = across(own)
        out_sum, qkv_sum, d_router, d_mixing, d_const_vec, d_moe_gain, d_attn_gain = unpack(
            jnp.stack([core[0], me_c, z]), own, other, w_qkv, attn_gain[None], left
        )
    else:
        whole = lambda mine, theirs: jnp.where(core == 0, jnp.concatenate([mine, theirs], axis=0), jnp.concatenate([theirs, mine], axis=0))
        total_1, total_2 = [v.astype(f32) for v in lax.psum((whole(mine_1, theirs_1), whole(mine_2, theirs_2)), ("ctx", "exp"))]
        columns = jnp.concatenate([total_1[:, :left], total_2], axis=1).reshape(width, pairs, 3, 128)
        qkv_sum = columns.transpose(0, 2, 1, 3).reshape(width, 3 * width)
        out_sum, small = total_1[:, left : left + width], total_1[:, left + width :].T
        d_attn_gain = (jnp.sum(qkv_sum * w_qkv.astype(f32), axis=1) / attn_gain)
        d_router, d_mixing, d_const_vec, d_moe_gain = small[:ALL_EXPERTS], small[16:20].reshape(2, 2, width), small[20:22], small[24]
    return (
        mixed_out[None],
        d_inputs[None],
        d_logits[:ALL_EXPERTS].T[None],
        d_attn_gain,
        qkv_sum,
        out_sum,
        d_moe_gain,
        d_router.T,
        d_mixing.transpose(0, 2, 1),
        d_const_vec,
        total_gate,
        total_up,
        total_down,
    )


def solution(mesh):
    rows = P("ctx", "exp", None)
    expert = P("exp", None, None)
    summed = P("exp", "ctx", None)
    return jax.shard_map(
        body,
        mesh=mesh,
        in_specs=(rows, rows, rows, P(), P(), P(), P(), P(), P(), P(), expert, expert, expert, rows),
        out_specs=(rows, rows, rows, P(), P(), P(), P(), P(), P(), P(), summed, summed, summed),
        check_vma=False,
    )
```

```python
import functools, math
import jax, jax.numpy as jnp
from jax import lax
from jax.experimental import pallas as pl
from jax.experimental.pallas import tpu as pltpu

HEADS = 12
HEAD_DIM = 64
CONT_LEN = 512
LOG2E = 1.4426950408889634
SCALE = HEAD_DIM ** -0.5
bf16 = jnp.bfloat16
f32 = jnp.float32
NEG = -1e30


def dot_nt(a, b):
    return lax.dot_general(a, b, (((1,), (1,)), ((), ())), preferred_element_type=f32)


def dot_nn(a, b):
    return jnp.dot(a, b, preferred_element_type=f32)


def query_tiles(tok, plen):
    tiles = [(0, plen, True)]
    step = 256
    for start in range(plen, tok, step):
        tiles.append((start, step, False))
    return tiles


def split_high(value):
    high = value.astype(bf16)
    return high, (value - high.astype(f32)).astype(bf16)


def both_halves(value, head, low_half):
    turned = pltpu.roll(value, HEAD_DIM, 1)
    return jnp.where(low_half, value, turned) if head == 0 else jnp.where(low_half, turned, value)


def scaled_queries(value, head, low_half):
    high, rest = split_high(value.astype(f32) * (SCALE * LOG2E))
    rest = pltpu.roll(rest, HEAD_DIM, 1)
    return jnp.where(low_half, high, rest) if head == 0 else jnp.where(low_half, rest, high)


def attention_forward_kernel(plen, flags_ref, q_ref, k_ref, v_ref, kr_ref, vr_ref, o_ref, lse_ref, kd, krd, vd, vrd):
    tok = q_ref.shape[0]
    remote = kr_ref.shape[0]
    low_half = lax.broadcasted_iota(jnp.int32, (1, 128), 1) < HEAD_DIM
    one = jnp.ones((), bf16)
    for head in range(2):
        mine = low_half if head == 0 else ~low_half
        kd[head] = both_halves(k_ref[...], head, low_half)
        krd[head] = both_halves(kr_ref[...], head, low_half)
        vd[head] = jnp.where(mine, v_ref[...], one)
        vrd[head] = jnp.where(mine, vr_ref[...], one)
    for start, size, is_prompt in query_tiles(tok, plen):
        row = lax.broadcasted_iota(jnp.int32, (size, size), 0)
        col = lax.broadcasted_iota(jnp.int32, (size, size), 1)
        queries = q_ref[start : start + size, :]
        units = []
        for head in range(2):
            qh = scaled_queries(queries, head, low_half)
            pieces = []
            diag = dot_nt(qh, kd[head, start : start + size, :])
            pieces.append((jnp.where(col <= row, diag, NEG), vd, start, size))
            if is_prompt:
                for j in range(remote // plen):
                    s = dot_nt(qh, krd[head, j * plen : (j + 1) * plen, :])
                    pieces.append((s + flags_ref[j], vrd, j * plen, plen))
            else:
                s = dot_nt(qh, kd[head, 0:start, :])
                pieces.append((s, vd, 0, start))
                s = dot_nt(qh, krd[head])
                pieces.append((s, vrd, 0, remote))
            units.append(pieces)
        accs, peaks = [], []
        for head, pieces in enumerate(units):
            peak = None
            for s, _, _, _ in pieces:
                m = jnp.max(s, axis=1, keepdims=True)
                peak = m if peak is None else jnp.maximum(peak, m)
            acc = None
            for s, ref, at, n in pieces:
                p = jnp.exp2(s - peak).astype(bf16)
                part = dot_nn(p, ref[head, at : at + n, :])
                acc = part if acc is None else acc + part
            accs.append(acc)
            peaks.append(peak)
        num = jnp.where(low_half, accs[0], accs[1])
        den = pltpu.roll(jnp.where(low_half, accs[1], accs[0]), HEAD_DIM, 1)
        o_ref[start : start + size, :] = (num / den).astype(bf16)
        turned = (jnp.where(low_half, peaks[0], peaks[1]) + jnp.log2(den)).T
        lse_ref[0, 0:8, start : start + size] = turned[0:8, :]
        lse_ref[0, 8:16, start : start + size] = turned[HEAD_DIM : HEAD_DIM + 8, :]


def attention_forward(flags, proj, kv_rem, plen):
    tok, width = proj.shape[0], proj.shape[1] // 3
    remote = kv_rem.shape[0]
    pairs = width // 128
    return pl.pallas_call(
        functools.partial(attention_forward_kernel, plen),
        grid=(pairs,),
        in_specs=[
            pl.BlockSpec(memory_space=pltpu.SMEM),
            pl.BlockSpec((tok, 128), lambda i: (0, i)),
            pl.BlockSpec((tok, 128), lambda i: (0, pairs + i)),
            pl.BlockSpec((tok, 128), lambda i: (0, 2 * pairs + i)),
            pl.BlockSpec((remote, 128), lambda i: (0, i)),
            pl.BlockSpec((remote, 128), lambda i: (0, pairs + i)),
        ],
        out_specs=[
            pl.BlockSpec((tok, 128), lambda i: (0, i)),
            pl.BlockSpec((1, 16, tok), lambda i: (i, 0, 0)),
        ],
        out_shape=[
            jax.ShapeDtypeStruct((tok, width), bf16),
            jax.ShapeDtypeStruct((pairs, 16, tok), f32),
        ],
        scratch_shapes=[pltpu.VMEM((2, n, 128), bf16) for n in (tok, remote, tok, remote)],
        compiler_params=pltpu.CompilerParams(vmem_limit_bytes=60 * 2**20),
        cost_estimate=pl.CostEstimate(flops=4 * tok * (tok + remote) * width, bytes_accessed=2 * (tok * 4 + remote * 2) * width, transcendentals=tok * (tok + remote) * HEADS),
        name="attention_forward",
    )(flags, proj, proj, proj, kv_rem, kv_rem)


def attention_backward_kernel(plen, started, last, skip, flags_ref, core_ref, q_ref, k_ref, v_ref, kr_ref, vr_ref, o_ref, do_ref, lse_ref, act_ref, far_ref, wk_ref, wv_ref, *refs):
    refs = refs[skip:]
    if started:
        start_far_ref, *refs = refs
    mine_ref, theirs_ref, own_grads, *refs = refs
    dfar_ref, *dfar_refs = (refs[-1:] + refs[:-10]) if last else refs[:1]
    kt, krt, dka, dva, dkra, dvra, weights, kd, krd = refs[-10:-1] if last else refs[-9:]
    tok = q_ref.shape[0]
    remote = kr_ref.shape[0]
    lane = lax.broadcasted_iota(jnp.int32, (1, 128), 1)
    low_half = lane < HEAD_DIM
    c = SCALE * LOG2E
    zero = jnp.zeros((), bf16)
    for head in range(2):
        kd[head] = both_halves(k_ref[...], head, low_half)
        krd[head] = both_halves(kr_ref[...], head, low_half)
    kt[...] = k_ref[...].T
    krt[...] = kr_ref[...].T
    dka[...] = jnp.zeros_like(dka)
    dva[...] = jnp.zeros_like(dva)
    dkra[...] = jnp.zeros_like(dkra)
    dvra[...] = jnp.zeros_like(dvra)
    pick = lax.broadcasted_iota(jnp.int32, (16, 128), 0) // 8 == lax.broadcasted_iota(jnp.int32, (16, 128), 1) // HEAD_DIM
    pick = jnp.where(pick, 1.0, 0.0).astype(bf16)
    for start, size, is_prompt in query_tiles(tok, plen):
        rows = slice(start, start + size)
        product = do_ref[rows, :].astype(f32) * o_ref[rows, :].astype(f32)
        high = product.astype(bf16)
        rest = (product - high.astype(f32)).astype(bf16)
        delta = dot_nt(pick, high) + dot_nt(pick, rest)
        totals = [None, None]
        masks = [low_half, ~low_half]
        qh = [jnp.where(m, q_ref[rows, :], zero) for m in masks]
        qs = [scaled_queries(q_ref[rows, :], head, low_half) for head in range(2)]
        doh = [jnp.where(m, do_ref[rows, :], zero) for m in masks]
        segments = [(kd, v_ref, kt, dka, dva, start, size, "diag")]
        if is_prompt:
            for j in range(remote // plen):
                segments.append((krd, vr_ref, krt, dkra, dvra, j * plen, plen, j))
        else:
            segments.append((kd, v_ref, kt, dka, dva, 0, start, None))
            segments.append((krd, vr_ref, krt, dkra, dvra, 0, remote, None))
        for kk, vv, tt, dk_acc, dv_acc, at, n, mode in segments:
            keys = slice(at, at + n)
            scores = [dot_nt(kk[head, keys, :], qs[head]) for head in range(2)]
            d_probs = [dot_nt(vv[keys, :], doh[head]) for head in range(2)]
            low_p, low_d = [], []
            for head in range(2):
                st = scores[head] - lse_ref[0, 8 * head : 8 * head + 1, rows]
                if mode == "diag":
                    key = lax.broadcasted_iota(jnp.int32, (n, size), 0)
                    query = lax.broadcasted_iota(jnp.int32, (n, size), 1)
                    st = jnp.where(key <= query, st, NEG)
                elif mode is not None:
                    st = st + flags_ref[mode]
                pt = jnp.exp2(st)
                low_p.append(pt.astype(bf16))
                low_d.append((pt * (d_probs[head] - delta[8 * head : 8 * head + 1, :])).astype(bf16))
            dv_acc[keys, :] += dot_nn(low_p[0], doh[0]) + dot_nn(low_p[1], doh[1])
            dk_acc[keys, :] += dot_nn(low_d[0], qh[0]) + dot_nn(low_d[1], qh[1])
            for head in range(2):
                part = dot_nn(tt[head * HEAD_DIM : (head + 1) * HEAD_DIM, keys], low_d[head])
                totals[head] = part if totals[head] is None else totals[head] + part
        dqt = totals
        own_grads[rows, 0:128] = (jnp.concatenate(dqt, axis=0).T * SCALE).astype(bf16)
    own_grads[:, 128:256] = (dka[...] * SCALE).astype(bf16)
    own_grads[:, 256:384] = dva[...].astype(bf16)
    far_grads = jnp.concatenate([(dkra[...] * SCALE).astype(bf16), dvra[...].astype(bf16)], axis=1)
    weights[:, 0:128] = wk_ref[...]
    weights[:, 128:256] = wv_ref[...]
    half = mine_ref.shape[0]
    for out_ref, which in ((theirs_ref, 1 - core_ref[0]), (mine_ref, core_ref[0])):
        rows = pl.ds(pl.multiple_of(which * half, half), half)
        total = dot_nn(act_ref[rows, :], own_grads[...])
        out_ref[:, 0:128] = total[:, 0:128].astype(bf16)
        out_ref[:, 128:384] = (total[:, 128:384] + dot_nn(far_ref[rows, :], far_grads)).astype(bf16)
    d_far = dot_nt(far_grads, weights[...])
    step = pl.program_id(0)

    @pl.when(step == 0)
    def _():
        dfar_ref[...] = d_far + start_far_ref[...] if started else d_far

    @pl.when(step > 0)
    def _():
        dfar_ref[...] += d_far

    if last:

        @pl.when(step == pl.num_programs(0) - 1)
        def _():
            for k, ref in enumerate(dfar_refs):
                ref[...] = dfar_ref[k * plen : (k + 1) * plen, :].astype(bf16)


def attention_backward(flags, core, proj, kv_rem, mixed, d_mixed, lse, act_t, far_t, w_qkv, plen, begin, count, buffers, at, starts, last):
    tok, width = mixed.shape
    remote = kv_rem.shape[0]
    pairs = width // 128
    own = lambda shift: pl.BlockSpec((tok, 128), lambda i: (0, shift + i))
    far = lambda shift: pl.BlockSpec((remote, 128), lambda i: (0, shift + i))
    weight = lambda shift: pl.BlockSpec((width, 128), lambda i: (0, shift + i))
    still = lambda shape: pl.BlockSpec(shape, lambda i: (0, 0))
    half = pl.BlockSpec((width // 2, 384), lambda i: (0, at + i))
    in_specs = [
        pl.BlockSpec(memory_space=pltpu.SMEM),
        pl.BlockSpec(memory_space=pltpu.SMEM),
        own(begin),
        own(pairs + begin),
        own(2 * pairs + begin),
        far(begin),
        far(pairs + begin),
        own(begin),
        own(begin),
        pl.BlockSpec((1, 16, tok), lambda i: (begin + i, 0, 0)),
        still((width, tok)),
        still((width, remote)),
        weight(pairs + begin),
        weight(2 * pairs + begin),
    ]
    arrays = [flags, core, proj, proj, proj, kv_rem, kv_rem, mixed, d_mixed, lse, act_t, far_t, w_qkv, w_qkv]
    scratch = [
        pltpu.VMEM((128, tok), bf16),
        pltpu.VMEM((128, remote), bf16),
        pltpu.VMEM((tok, 128), f32),
        pltpu.VMEM((tok, 128), f32),
        pltpu.VMEM((remote, 128), f32),
        pltpu.VMEM((remote, 128), f32),
        pltpu.VMEM((width, 256), bf16),
        pltpu.VMEM((2, tok, 128), bf16),
        pltpu.VMEM((2, remote, 128), bf16),
    ]
    aliases = {}
    skip = 0
    if not isinstance(buffers, int):
        aliases = {len(arrays): 0, len(arrays) + 1: 1}
        in_specs += [pl.BlockSpec(memory_space=pl.ANY)] * 2
        arrays += list(buffers)
        skip = 2
        buffers = buffers[0].shape[1]
    if starts:
        in_specs += [still((remote, width))]
        arrays += list(starts)
    out_specs = [half, half, pl.BlockSpec((tok, 384), lambda i: (0, i))]
    out_shape = [jax.ShapeDtypeStruct((width // 2, buffers), bf16)] * 2 + [jax.ShapeDtypeStruct((tok, count * 384), bf16)]
    if last:
        out_specs += [still((plen, width))] * (remote // plen)
        out_shape += [jax.ShapeDtypeStruct((plen, width), bf16)] * (remote // plen)
        scratch = scratch + [pltpu.VMEM((remote, width), f32)]
    else:
        out_specs += [still((remote, width))]
        out_shape += [jax.ShapeDtypeStruct((remote, width), f32)]
    return pl.pallas_call(
        functools.partial(attention_backward_kernel, plen, bool(starts), last, skip),
        grid=(count,),
        in_specs=in_specs,
        out_specs=out_specs,
        out_shape=out_shape,
        scratch_shapes=scratch,
        input_output_aliases=aliases,
        compiler_params=pltpu.CompilerParams(vmem_limit_bytes=60 * 2**20),
        cost_estimate=pl.CostEstimate(flops=10 * tok * (tok + remote) * count * 128 + 20 * tok * width * count * 128, bytes_accessed=2 * (tok * 8 + remote * 4) * count * 128 + 16 * tok * width, transcendentals=tok * (tok + remote) * 2 * count),
        name="attention_backward",
    )(*arrays)


FFN_EXPERTS = 8
ALL_EXPERTS = 12
EXTRA = 128
SMALL = 8
epsilon = 1e-06


def dot_tn(a, b):
    return lax.dot_general(a, b, (((0,), (0,)), ((), ())), preferred_element_type=f32)


def split_low(value, parts):
    pieces = []
    for _ in range(parts):
        piece = value.astype(bf16)
        pieces.append(piece)
        value = value - piece.astype(f32)
    return pieces


def route_kernel(groups, home_ref, ids_ref, grad_ref, prev_ref, *out_refs):
    tok, width = grad_ref.shape
    count = len(groups)
    turned_refs, chosen_refs, early_ref = out_refs[:count], out_refs[count : 2 * count], out_refs[2 * count]
    capacity = early_ref.shape[1] - SMALL
    expert = lax.broadcasted_iota(jnp.int32, (16, tok), 0)
    ids = [ids_ref[k : k + 1, :] for k in range(2)]
    names = [row == expert for row in ids]
    both = jnp.where(names[0] | names[1], 1.0, 0.0).astype(bf16)
    earlier = lax.broadcasted_iota(jnp.int32, (tok, tok), 0) < lax.broadcasted_iota(jnp.int32, (tok, tok), 1)
    before = dot_nn(both, jnp.where(earlier, 1.0, 0.0).astype(bf16))
    pieces = [piece.astype(f32) for piece in split_low(prev_ref[...], 3)]
    extra = jnp.concatenate(pieces + [jnp.zeros((EXTRA - 3 * ALL_EXPERTS, tok), f32)], axis=0).T.astype(bf16)
    slot = [jnp.sum(jnp.where(n, before, 0.0), axis=0, keepdims=True).astype(jnp.int32) for n in names]
    extras = []
    for (first, size), turned_ref, chosen_ref in zip(groups, turned_refs, chosen_refs):
        spots = lax.broadcasted_iota(jnp.int32, (FFN_EXPERTS * size, tok), 0)
        hit = None
        for k in range(2):
            inside = (ids[k] < FFN_EXPERTS) & (slot[k] >= first) & (slot[k] < first + size)
            place = jnp.where(inside, ids[k] * size + slot[k] - first, -1)
            hit = spots == place if hit is None else hit | (spots == place)
        turned = jnp.where(hit, 1.0, 0.0).astype(bf16)
        turned_ref[...] = turned
        chosen_ref[...] = turned.T
        grads = dot_nn(turned, grad_ref[...]).astype(bf16)
        extras.append(dot_nn(turned, extra))
        for e in range(FFN_EXPERTS):
            early_ref[e, first : first + size, :] = grads[e * size : (e + 1) * size]
    third = capacity // 3
    for e in range(FFN_EXPERTS):
        rows = jnp.concatenate([x[e * size : (e + 1) * size] for x, (_, size) in zip(extras, groups)], axis=0)
        rows = rows[0:third] + pltpu.roll(rows[third : 2 * third], 40, 1) + pltpu.roll(rows[2 * third : capacity], 80, 1)
        early_ref[e, capacity : capacity + SMALL, :] = jnp.zeros((SMALL, width), bf16)
        for g in range(third // SMALL):
            early_ref[e, capacity : capacity + SMALL, g * EXTRA : (g + 1) * EXTRA] = rows[g * SMALL : (g + 1) * SMALL].astype(bf16)


def route_plan(home, ids, grad, prev, groups):
    tok, width = grad.shape
    counts = [FFN_EXPERTS * size for _, size in groups]
    whole = pl.BlockSpec(memory_space=pltpu.VMEM)
    early = (FFN_EXPERTS, sum(counts) // FFN_EXPERTS + SMALL, width)
    out = pl.pallas_call(
        functools.partial(route_kernel, groups),
        in_specs=[pl.BlockSpec(memory_space=pltpu.SMEM), whole, whole, whole],
        out_specs=[whole] * (2 * len(groups) + 1),
        out_shape=[jax.ShapeDtypeStruct((n, tok), bf16) for n in counts]
        + [jax.ShapeDtypeStruct((tok, n), bf16) for n in counts]
        + [jax.ShapeDtypeStruct(early, bf16)],
        compiler_params=pltpu.CompilerParams(vmem_limit_bytes=60 * 2**20),
        cost_estimate=pl.CostEstimate(flops=2 * sum(counts) * tok * (width + EXTRA), bytes_accessed=4 * sum(counts) * width, transcendentals=0),
        name="route_plan",
    )(home, ids, grad, prev)
    return out[: len(groups)], out[len(groups) : -1], out[-1]


def router_inputs(early_ref, slots):
    capacity = early_ref.shape[1] - SMALL
    groups = capacity // 3 // SMALL
    rows = []
    for sender in range(early_ref.shape[0]):
        packed = early_ref[sender, capacity : capacity + SMALL, :].astype(f32)
        third = jnp.concatenate([packed[:, g * EXTRA : (g + 1) * EXTRA] for g in range(groups)], axis=0)
        every = jnp.concatenate([third, pltpu.roll(third, EXTRA - 40, 1), pltpu.roll(third, EXTRA - 80, 1)], axis=0)
        rows.append(every[slots])
    rows = jnp.concatenate(rows, axis=0)
    return rows + pltpu.roll(rows, EXTRA - ALL_EXPERTS, 1) + pltpu.roll(rows, EXTRA - 2 * ALL_EXPERTS, 1)


def expert_kernel(group, home_ref, rows_ref, early_ref, router_ref, wg_ref, wu_ref, wd_ref,
                  out_ref, drow_ref, dout_ref, inner_ref, dgate_ref, dup_ref, small_ref, acc_out, acc_row, probs_ref):
    width = rows_ref.shape[1]
    step, steps = pl.program_id(0), pl.num_programs(0)
    home = home_ref[0]
    lane = lax.broadcasted_iota(jnp.int32, (1, EXTRA), 1)
    slots = slice(group[0], group[0] + group[1])

    @pl.when(step == 0)
    def _():
        logits = router_inputs(early_ref, slots) + dot_nn(rows_ref[...], router_ref[...])
        logits = jnp.where(lane < ALL_EXPERTS, logits, NEG)
        unnormed = jnp.exp(logits - jnp.max(logits, axis=1, keepdims=True))
        probs = unnormed / jnp.sum(unnormed, axis=1, keepdims=True)
        probs_ref[...] = probs
        gate = jnp.sum(jnp.where(lane == home, probs, 0.0), axis=1, keepdims=True)
        dout_ref[...] = (gate * early_ref[:, slots, 0:width].astype(f32).reshape(-1, width)).astype(bf16)
        acc_out[...] = jnp.zeros_like(acc_out)
        acc_row[...] = jnp.zeros_like(acc_row)

    rows = rows_ref[...]
    gate_pre = dot_nn(rows, wg_ref[0])
    up_pre = dot_nn(rows, wu_ref[0])
    d_inner = dot_nt(dout_ref[...], wd_ref[0])
    sigmoid = jax.nn.sigmoid(gate_pre)
    silu = gate_pre * sigmoid
    inner = (silu * up_pre).astype(bf16)
    d_gate = (d_inner * up_pre * (sigmoid * (1.0 + gate_pre * (1.0 - sigmoid)))).astype(bf16)
    d_up = (d_inner * silu).astype(bf16)
    inner_ref[...] = inner
    dgate_ref[...] = d_gate
    dup_ref[...] = d_up
    acc_out[...] += dot_nn(inner, wd_ref[0])
    acc_row[...] += dot_nt(d_gate, wg_ref[0]) + dot_nt(d_up, wu_ref[0])

    @pl.when(step == steps - 1)
    def _():
        probs = probs_ref[...]
        gate = jnp.sum(jnp.where(lane == home, probs, 0.0), axis=1, keepdims=True)
        out = acc_out[...].astype(bf16).astype(f32)
        d_row_gate = jnp.sum(out * early_ref[:, slots, 0:width].astype(f32).reshape(-1, width), axis=1, keepdims=True)
        out_ref[:, 0:width] = (gate * out).astype(bf16)
        extra = jnp.zeros((out.shape[0], EXTRA), f32)
        for i, piece in enumerate(split_low(d_row_gate, 3)):
            extra = jnp.where(lane == home + 16 * i, piece.astype(f32), extra)
        out_ref[:, width : width + EXTRA] = extra.astype(bf16)
        term = d_row_gate * gate * (jnp.where(lane == home, 1.0, 0.0) - probs)
        high, rest = split_low(term, 2)
        turned = [piece.T for piece in (high, rest)]
        small_ref[...] = (dot_nn(turned[0], rows) + dot_nn(turned[1], rows))[0 : 2 * SMALL, :]
        drow_ref[...] = (acc_row[...] + dot_nt(high, router_ref[...]) + dot_nt(rest, router_ref[...])).astype(bf16)


def expert_pass(group, home, rows, early, router_pad, w_gate, w_up, w_down):
    count, width = rows.shape
    ff = w_gate.shape[2]
    tile = min(512, ff)
    full = pl.BlockSpec((count, width), lambda j: (0, 0))
    wide = pl.BlockSpec((count, width + EXTRA), lambda j: (0, 0))
    tall = pl.BlockSpec((1, width, tile), lambda j: (0, 0, j))
    piece = pl.BlockSpec((count, tile), lambda j: (0, j))
    return pl.pallas_call(
        functools.partial(expert_kernel, group),
        grid=(ff // tile,),
        in_specs=[
            pl.BlockSpec(memory_space=pltpu.SMEM),
            full,
            pl.BlockSpec(early.shape, lambda j: (0, 0, 0)),
            pl.BlockSpec((width, EXTRA), lambda j: (0, 0)),
            tall,
            tall,
            pl.BlockSpec((1, tile, width), lambda j: (0, j, 0)),
        ],
        out_specs=[wide, full, full, piece, piece, piece, pl.BlockSpec((2 * SMALL, width), lambda j: (0, 0))],
        out_shape=[
            jax.ShapeDtypeStruct((count, width + EXTRA), bf16),
            jax.ShapeDtypeStruct((count, width), bf16),
            jax.ShapeDtypeStruct((count, width), bf16),
        ]
        + [jax.ShapeDtypeStruct((count, ff), bf16)] * 3
        + [jax.ShapeDtypeStruct((2 * SMALL, width), f32)],
        scratch_shapes=[pltpu.VMEM((count, width), f32), pltpu.VMEM((count, width), f32), pltpu.VMEM((count, EXTRA), f32)],
        compiler_params=pltpu.CompilerParams(vmem_limit_bytes=60 * 2**20),
        cost_estimate=pl.CostEstimate(flops=12 * count * width * ff, bytes_accessed=6 * width * ff + 2 * count * (5 * width + 3 * ff), transcendentals=count * ff),
        name="expert_pass",
    )(home, rows, early, router_pad, w_gate, w_up, w_down)


def weight_kernel(count, *refs):
    rows, douts, inners, dgates, dups = (refs[i * count : (i + 1) * count] for i in range(5))
    gate_up_ref, down_ref = refs[5 * count : 5 * count + 2]
    turned = refs[5 * count + 2 :]

    @pl.when(pl.program_id(0) == 0)
    def _():
        for ref, scratch in zip(rows, turned):
            scratch[...] = ref[...].T

    gate_up_ref[0] = sum(dot_nn(t[...], d[...]) for t, d in zip(turned, dgates)).astype(bf16)
    gate_up_ref[1] = sum(dot_nn(t[...], d[...]) for t, d in zip(turned, dups)).astype(bf16)
    down_ref[...] = sum(dot_nn(i[...].T, d[...]) for i, d in zip(inners, douts)).astype(bf16)


def weight_gradients(rows, douts, inners, dgates, dups):
    count = len(rows)
    width, ff = rows[0].shape[1], inners[0].shape[1]
    tile = min(512, ff)
    total = sum(r.shape[0] for r in rows)
    full = [pl.BlockSpec(r.shape, lambda j: (0, 0)) for r in rows]
    piece = [pl.BlockSpec((r.shape[0], tile), lambda j: (0, j)) for r in rows]
    return pl.pallas_call(
        functools.partial(weight_kernel, count),
        grid=(ff // tile,),
        in_specs=full + full + piece * 3,
        out_specs=[pl.BlockSpec((2, width, tile), lambda j: (0, 0, j)), pl.BlockSpec((tile, width), lambda j: (j, 0))],
        out_shape=[jax.ShapeDtypeStruct((2, width, ff), bf16), jax.ShapeDtypeStruct((ff, width), bf16)],
        scratch_shapes=[pltpu.VMEM((width, r.shape[0]), bf16) for r in rows],
        compiler_params=pltpu.CompilerParams(vmem_limit_bytes=60 * 2**20),
        cost_estimate=pl.CostEstimate(flops=6 * total * width * ff, bytes_accessed=6 * width * ff + 2 * total * (2 * width + 3 * ff), transcendentals=0),
        name="weight_gradients",
    )(*rows, *douts, *inners, *dgates, *dups)


ANYWHERE = pl.BlockSpec(memory_space=pltpu.VMEM)
SCALARS = pl.BlockSpec(memory_space=pltpu.SMEM)


def inverse_rms(value):
    return lax.rsqrt(jnp.mean(value * value, axis=1, keepdims=True) + epsilon)


def after_attention_kernel(count, mixed_ref, x_ref, w_ref, gain_ref, *refs):
    turned, (hidden_ref, low_ref), sent = refs[:count], refs[count : count + 2], refs[count + 2 :]
    hidden = x_ref[...].astype(f32) + dot_nn(mixed_ref[...], w_ref[...])
    low = (hidden * inverse_rms(hidden) * gain_ref[...]).astype(bf16)
    hidden_ref[...] = hidden
    low_ref[...] = low
    for t, s in zip(turned, sent):
        s[...] = dot_nn(t[...], low).astype(bf16)


def after_attention(mixed, x, w_out, gain, turned):
    tok, width = x.shape
    rows = sum(t.shape[0] for t in turned)
    out = pl.pallas_call(
        functools.partial(after_attention_kernel, len(turned)),
        in_specs=[ANYWHERE] * (4 + len(turned)),
        out_specs=[ANYWHERE] * (2 + len(turned)),
        out_shape=[jax.ShapeDtypeStruct((tok, width), f32), jax.ShapeDtypeStruct((tok, width), bf16)]
        + [jax.ShapeDtypeStruct((t.shape[0], width), bf16) for t in turned],
        compiler_params=pltpu.CompilerParams(vmem_limit_bytes=60 * 2**20),
        cost_estimate=pl.CostEstimate(flops=2 * tok * width * (width + rows), bytes_accessed=2 * width * (6 * tok + 2 * rows), transcendentals=0),
        name="after_attention",
    )(mixed, x, w_out, gain, *turned)
    return out[0], out[1], out[2:]


def turn_kernel(in_ref, out_ref):
    out_ref[...] = in_ref[...].T


def turn(value):
    rows, columns = value.shape
    block = 256 if rows % 256 == 0 else 128
    return pl.pallas_call(
        turn_kernel,
        grid=(rows // block,),
        in_specs=[pl.BlockSpec((block, columns), lambda i: (i, 0))],
        out_specs=pl.BlockSpec((columns, block), lambda i: (0, i)),
        out_shape=jax.ShapeDtypeStruct((columns, rows), value.dtype),
        compiler_params=pltpu.CompilerParams(vmem_limit_bytes=60 * 2**20),
        cost_estimate=pl.CostEstimate(flops=0, bytes_accessed=4 * rows * columns, transcendentals=0),
        name="turn",
    )(value)


def place(value, lane, at):
    return jnp.where(lane == at, value, 0.0)


def local_kernel(hidden_ref, low_ref, grad_ref, prev_ref, ids_ref, mix_ref, gain_ref, vec_ref, out_ref, dnormed_ref, probs_ref, dprobs_ref, small_ref):
    lane = lax.broadcasted_iota(jnp.int32, (1, EXTRA), 1)
    hidden = hidden_ref[...]
    normed = hidden * inverse_rms(hidden) * gain_ref[...]
    low = low_ref[...]
    grad = grad_ref[...].astype(f32)
    raw = dot_nn(low, mix_ref[...])
    prev = jnp.concatenate([prev_ref[...], jnp.zeros((raw.shape[0], EXTRA - ALL_EXPERTS), f32)], axis=1)
    logits = jnp.where(lane < ALL_EXPERTS, raw + prev, NEG)
    unnormed = jnp.exp(logits - jnp.max(logits, axis=1, keepdims=True))
    probs = unnormed / jnp.sum(unnormed, axis=1, keepdims=True)
    named = (ids_ref[:, 0:1] == lane) | (ids_ref[:, 1:2] == lane)
    gates = jnp.where(named, probs, 0.0)
    copy_gate = gates[:, FFN_EXPERTS + 1 : FFN_EXPERTS + 2]
    dots = jnp.sum(grad * normed, axis=1, keepdims=True)
    out = hidden
    weight = copy_gate
    d_probs = place(dots, lane, FFN_EXPERTS + 1)
    logit_grads = jnp.zeros_like(probs)
    vec_terms = jnp.zeros_like(probs)
    for c in range(2):
        vec = vec_ref[c : c + 1, :]
        gate = gates[:, FFN_EXPERTS + 2 + c : FFN_EXPERTS + 3 + c]
        at = 16 + 2 * c
        a0 = jax.nn.sigmoid(raw[:, at : at + 1] - raw[:, at + 1 : at + 2])
        a1 = jax.nn.sigmoid(raw[:, at + 1 : at + 2] - raw[:, at : at + 1])
        vec_dots = jnp.sum(grad * vec, axis=1, keepdims=True)
        weight = weight + gate * a0
        out = out + (gate * a1) * vec
        d_probs = d_probs + place(a0 * dots + a1 * vec_dots, lane, FFN_EXPERTS + 2 + c)
        d0, d1 = gate * dots, gate * vec_dots
        mean = a0 * d0 + a1 * d1
        d0, d1 = a0 * (d0 - mean), a1 * (d1 - mean)
        logit_grads = logit_grads + place(d0, lane, at) + place(d1, lane, at + 1)
        vec_terms = vec_terms + place(gate * a1, lane, 20 + c)
    d_probs = jnp.where(named, d_probs, 0.0)
    logit_grads = logit_grads + probs * (d_probs - jnp.sum(probs * d_probs, axis=1, keepdims=True))
    high, rest = split_low(logit_grads, 2)
    out_ref[...] = out + weight * normed
    dnormed_ref[...] = weight * grad + dot_nt(high, mix_ref[...]) + dot_nt(rest, mix_ref[...])
    probs_ref[...] = probs
    dprobs_ref[...] = d_probs
    sums = None
    for terms, rows in ((logit_grads, low), (vec_terms, grad_ref[...])):
        for piece in split_low(terms.T, 2):
            part = dot_nn(piece, rows)
            sums = part if sums is None else sums + part
    sums = sums[0 : 3 * SMALL, :]

    @pl.when(pl.program_id(0) == 0)
    def _():
        small_ref[...] = sums

    @pl.when(pl.program_id(0) > 0)
    def _():
        small_ref[...] += sums


def local_part(hidden, low, grad, prev, ids, mix, gain, vec):
    tok, width = hidden.shape
    block, tiles = row_tiles(tok)
    shapes = [(tok, width), (tok, width), (tok, EXTRA), (tok, EXTRA), (3 * SMALL, width)]
    return pl.pallas_call(
        local_kernel,
        grid=(tok // block,),
        in_specs=[tiles(width), tiles(width), tiles(width), tiles(ALL_EXPERTS), tiles(2), fixed(mix), fixed(gain), fixed(vec)],
        out_specs=[tiles(width), tiles(width), tiles(EXTRA), tiles(EXTRA), pl.BlockSpec((3 * SMALL, width), lambda i: (0, 0))],
        out_shape=[jax.ShapeDtypeStruct(s, f32) for s in shapes],
        compiler_params=pltpu.CompilerParams(vmem_limit_bytes=60 * 2**20),
        cost_estimate=pl.CostEstimate(flops=14 * tok * width * EXTRA, bytes_accessed=16 * tok * width, transcendentals=tok * EXTRA),
        name="local_part",
    )(hidden, low, grad, prev, ids, mix, gain, vec)


def row_tiles(tok):
    block = 256 if tok % 256 == 0 else 128
    return block, lambda columns: pl.BlockSpec((block, columns), lambda i: (i, 0))


def fixed(value):
    return pl.BlockSpec(value.shape, lambda i: (0,) * value.ndim)


def combine_kernel(count, parts, core_ref, *refs):
    chosen, got, refs = refs[:count], refs[count : count * (1 + parts)], refs[count * (1 + parts) :]
    smalls, refs = refs[: count + 1], refs[count + 1 :]
    local_ref, hidden_ref, gain_ref, grad_ref, mixed_ref, w_ref, dhidden_ref, dmixed_ref, mine_ref, theirs_ref, total_w, total_gain, small_t = refs
    step = pl.program_id(0)

    @pl.when(step == 0)
    def _():
        total_w[...] = jnp.zeros_like(total_w)
        total_gain[...] = jnp.zeros_like(total_gain)

    d_normed = local_ref[...]
    for g in range(count):
        for r in range(parts):
            d_normed = d_normed + dot_nn(chosen[g][...], got[g * parts + r][...])
    hidden = hidden_ref[...]
    inverse = inverse_rms(hidden)
    scaled = d_normed * gain_ref[...]
    mean = jnp.mean(scaled * hidden, axis=1, keepdims=True)
    d_hidden = grad_ref[...].astype(f32) + inverse * scaled - hidden * (inverse * inverse * inverse * mean)
    low = d_hidden.astype(bf16)
    dhidden_ref[...] = d_hidden
    dmixed_ref[...] = dot_nt(low, w_ref[...]).astype(bf16)
    total_w[...] += dot_nn(mixed_ref[...].T, low)
    total_gain[...] += jnp.sum(d_normed * hidden * inverse, axis=0, keepdims=True)

    @pl.when(step == pl.num_programs(0) - 1)
    def _():
        width = w_ref.shape[0]
        half = width // 2
        row = lax.broadcasted_iota(jnp.int32, (SMALL, 1), 0)
        top = smalls[0][0 : 2 * SMALL, :]
        for small in smalls[1:]:
            top = top + small[...]
        rest = jnp.zeros((EXTRA - 4 * SMALL, width), f32)
        rows = [top, smalls[0][2 * SMALL : 3 * SMALL, :], jnp.where(row == 0, total_gain[...], 0.0), rest]
        small_t[...] = jnp.concatenate(rows, axis=0).T
        at = mine_ref.shape[1] - width - EXTRA
        for out_ref, which in ((theirs_ref, 1 - core_ref[0]), (mine_ref, core_ref[0])):
            place_rows = pl.ds(pl.multiple_of(which * half, half), half)
            out_ref[:, at : at + width] = total_w[place_rows, :].astype(bf16)
            out_ref[:, at + width : at + width + EXTRA] = small_t[place_rows, :].astype(bf16)


def combine(core, chosen, got, smalls, local, hidden, gain, grad, mixed, w_out, columns):
    tok, width = hidden.shape
    rows = sum(c.shape[1] for c in chosen)
    arrays = [a for group in got for a in group]
    block, tiles = row_tiles(tok)
    half = (width // 2, columns + width + EXTRA)
    return pl.pallas_call(
        functools.partial(combine_kernel, len(chosen), len(got[0])),
        grid=(tok // block,),
        in_specs=[SCALARS] + [tiles(c.shape[1]) for c in chosen] + [fixed(a) for a in arrays + smalls]
        + [tiles(width), tiles(width), fixed(gain), tiles(width), tiles(width), fixed(w_out)],
        out_specs=[tiles(width)] * 2 + [pl.BlockSpec(half, lambda i: (0, 0))] * 2,
        out_shape=[jax.ShapeDtypeStruct((tok, width), f32), jax.ShapeDtypeStruct((tok, width), bf16)] + [jax.ShapeDtypeStruct(half, bf16)] * 2,
        scratch_shapes=[pltpu.VMEM((width, width), f32), pltpu.VMEM((1, width), f32), pltpu.VMEM((width, EXTRA), f32)],
        compiler_params=pltpu.CompilerParams(vmem_limit_bytes=60 * 2**20),
        cost_estimate=pl.CostEstimate(flops=2 * tok * width * (rows + 2 * width), bytes_accessed=2 * width * (10 * tok + 2 * rows), transcendentals=0),
        name="combine_gradients",
    )(core, *chosen, *arrays, *smalls, local, hidden, gain, grad, mixed, w_out)


def flat_rows(value):
    if value.shape[1] % 16:
        return value.astype(f32).reshape(-1, value.shape[2]).astype(bf16)
    return value.reshape(-1, value.shape[2])


def finish_kernel(groups, parts, *refs):
    chosen, got = refs[: len(groups)], refs[len(groups) : len(groups) + parts]
    local_ref, probs_ref, dprobs_ref, out_ref, dlogits_ref = refs[len(groups) + parts :]
    width = local_ref.shape[1]
    lane = lax.broadcasted_iota(jnp.int32, (1, EXTRA), 1)
    picked = None
    for c, (at, size) in zip(chosen, groups):
        for r in range(parts):
            part = dot_nn(c[...], flat_rows(got[r][:, at : at + size, :]))
            picked = part if picked is None else picked + part
    out_ref[...] = (local_ref[...] + picked[:, 0:width]).astype(bf16)
    extra = picked[:, width : width + EXTRA]
    extra = extra + pltpu.roll(extra, EXTRA - 16, 1) + pltpu.roll(extra, EXTRA - 32, 1)
    d_probs = dprobs_ref[...] + jnp.where(lane < ALL_EXPERTS, extra, 0.0)
    probs = probs_ref[...]
    d_logits = probs * (d_probs - jnp.sum(probs * d_probs, axis=1, keepdims=True))
    dlogits_ref[...] = d_logits.T


def finish(chosen, got, groups, local, probs, d_probs):
    tok, width = local.shape
    block, tiles = row_tiles(tok)
    return pl.pallas_call(
        functools.partial(finish_kernel, groups, len(got)),
        grid=(tok // block,),
        in_specs=[tiles(c.shape[1]) for c in chosen] + [fixed(g) for g in got] + [tiles(width), tiles(EXTRA), tiles(EXTRA)],
        out_specs=[tiles(width), pl.BlockSpec((EXTRA, block), lambda i: (0, i))],
        out_shape=[jax.ShapeDtypeStruct((tok, width), bf16), jax.ShapeDtypeStruct((EXTRA, tok), f32)],
        compiler_params=pltpu.CompilerParams(vmem_limit_bytes=60 * 2**20),
        cost_estimate=pl.CostEstimate(flops=2 * tok * 1152 * (width + EXTRA), bytes_accessed=16 * tok * width, transcendentals=0),
        name="finish_outputs",
    )(*chosen, *got, local, probs, d_probs)


def input_kernel(count, x_ref, gain_ref, dhidden_ref, w_ref, *refs):
    grads, far, (out_ref, weights) = refs[:count], refs[count:-2], refs[-2:]
    width = x_ref.shape[1]

    @pl.when(pl.program_id(0) == 0)
    def _():
        for i in range(width // 128):
            for p in range(3):
                weights[:, i * 384 + p * 128 : i * 384 + (p + 1) * 128] = w_ref[:, p * width + i * 128 : p * width + (i + 1) * 128]

    total = None
    for ref in far:
        total = ref[...].astype(f32) if total is None else total + ref[...].astype(f32)
    d_act = jnp.where(pl.program_id(0) == 0, total, 0.0)
    at = 0
    for ref in grads:
        columns = ref.shape[1]
        d_act = d_act + dot_nt(ref[...], weights[:, at : at + columns])
        at += columns
    x = x_ref[...].astype(f32)
    inverse = inverse_rms(x)
    scaled = d_act * gain_ref[...]
    mean = jnp.mean(scaled * x, axis=1, keepdims=True)
    out_ref[...] = dhidden_ref[...] + inverse * scaled - x * (inverse * inverse * inverse * mean)


def input_gradient(grads, x, gain, d_hidden, w_qkv, far):
    tok, width = x.shape
    block = far[0].shape[0]
    tiles = lambda columns: pl.BlockSpec((block, columns), lambda i: (i, 0))
    return pl.pallas_call(
        functools.partial(input_kernel, len(grads)),
        grid=(tok // block,),
        in_specs=[tiles(width), fixed(gain), tiles(width), fixed(w_qkv)] + [tiles(g.shape[1]) for g in grads] + [fixed(f) for f in far],
        out_specs=tiles(width),
        out_shape=jax.ShapeDtypeStruct((tok, width), f32),
        scratch_shapes=[pltpu.VMEM((width, 3 * width), bf16)],
        compiler_params=pltpu.CompilerParams(vmem_limit_bytes=60 * 2**20),
        cost_estimate=pl.CostEstimate(flops=6 * tok * width * width, bytes_accessed=22 * tok * width, transcendentals=0),
        name="input_gradient",
    )(x, gain, d_hidden, w_qkv, *grads, *far)


def far_kernel(count, gain_ref, wk_ref, wv_ref, *refs):
    far, (act_ref, kv_ref) = refs[:count], refs[count:]
    width = wk_ref.shape[0]
    for k, ref in enumerate(far):

        @pl.when(pl.program_id(0) == k)
        def _():
            x = ref[...].astype(f32)
            act = (x * inverse_rms(x) * gain_ref[...]).astype(bf16)
            act_ref[...] = act
            kv_ref[:, 0:width] = dot_nn(act, wk_ref[...]).astype(bf16)
            kv_ref[:, width : 2 * width] = dot_nn(act, wv_ref[...]).astype(bf16)


def far_projection(far, gain, w_qkv):
    rows, width = far[0].shape
    count = len(far)
    return pl.pallas_call(
        functools.partial(far_kernel, count),
        grid=(count,),
        in_specs=[fixed(gain), pl.BlockSpec((width, width), lambda i: (0, 1)), pl.BlockSpec((width, width), lambda i: (0, 2))] + [fixed(f) for f in far],
        out_specs=[pl.BlockSpec((rows, width), lambda i: (i, 0)), pl.BlockSpec((rows, 2 * width), lambda i: (i, 0))],
        out_shape=[jax.ShapeDtypeStruct((count * rows, width), bf16), jax.ShapeDtypeStruct((count * rows, 2 * width), bf16)],
        compiler_params=pltpu.CompilerParams(vmem_limit_bytes=60 * 2**20),
        cost_estimate=pl.CostEstimate(flops=4 * count * rows * width * width, bytes_accessed=2 * width * (4 * count * rows + 2 * width), transcendentals=0),
        name="far_projection",
    )(gain, w_qkv, w_qkv, *far)


def xor_pairs(size, mask):
    return [(i, i ^ mask) for i in range(size)]


def sum_kernel(terms, index_ref, *refs):
    count = len(refs) // (sum(terms) + 1)
    outs = refs[-count:]
    for k, out_ref in enumerate(outs):
        at = 0
        first = 0
        for number in terms:
            total = None
            for t in range(first, first + number):
                value = refs[t * count + k][0].astype(f32)
                total = value if total is None else total + value
            out_ref[0, :, at : at + total.shape[1]] = total.astype(bf16)
            at += total.shape[1]
            first += number


def sum_pieces(index, groups):
    arrays = [a for group in groups for a in group]
    n, rows = arrays[0].shape[:2]
    columns = sum(group[0].shape[2] for group in groups)
    view = lambda a, k: pl.BlockSpec((1, rows, a.shape[2]), lambda i, s: (s[0] ^ k if n > 1 else 0, 0, 0))
    return pl.pallas_call(
        functools.partial(sum_kernel, [len(g) for g in groups]),
        grid_spec=pltpu.PrefetchScalarGridSpec(
            num_scalar_prefetch=1,
            grid=(1,),
            in_specs=[view(a, k) for a in arrays for k in range(n)],
            out_specs=[pl.BlockSpec((1, rows, columns), lambda i, s: (0, 0, 0))] * n,
        ),
        out_shape=[jax.ShapeDtypeStruct((1, rows, columns), bf16)] * n,
        compiler_params=pltpu.CompilerParams(vmem_limit_bytes=60 * 2**20),
        cost_estimate=pl.CostEstimate(flops=0, bytes_accessed=2 * n * rows * columns * 5, transcendentals=0),
        name="sum_pieces",
    )(index, *[a for a in arrays for _ in range(n)])


def quarters(value):
    return value.reshape(4, -1, value.shape[-1])


def swap(pieces, along):
    axis, size, unit = along
    return [pieces[0]] + [lax.ppermute(pieces[k], axis, xor_pairs(size, unit * k)) for k in range(1, 4)]


def spread(value, along):
    return swap([value] * 4, along)


def stack_kernel(*refs):
    n = len(refs) - 1
    size = refs[0].shape[0]
    for k in range(n):
        refs[n][k * size : (k + 1) * size] = refs[k][...]


def stack_pieces(pieces):
    shape = (len(pieces) * pieces[0].shape[0],) + pieces[0].shape[1:]
    return pl.pallas_call(
        stack_kernel,
        in_specs=[ANYWHERE] * len(pieces),
        out_specs=ANYWHERE,
        out_shape=jax.ShapeDtypeStruct(shape, bf16),
        compiler_params=pltpu.CompilerParams(vmem_limit_bytes=60 * 2**20),
        cost_estimate=pl.CostEstimate(flops=0, bytes_accessed=4 * math.prod(shape), transcendentals=0),
        name="stack_pieces",
    )(*pieces)


def unpack_kernel(left, last, index_ref, *refs):
    pieces, (w_ref, *refs) = refs[:4], refs[4:]
    if last:
        scale_ref, first_ref, _, _, out_ref, qkv_ref, router_ref, mixing_ref, vec_ref, gain_ref, attn_ref, small = refs
    else:
        out_ref, qkv_ref, small = refs
    width = out_ref.shape[1]
    size = pieces[0].shape[1]
    lane = lax.broadcasted_iota(jnp.int32, (1, EXTRA), 1)
    step = pl.program_id(0)
    half = index_ref[0]
    base = (half * width // 2 if last else 0) + step * 4 * size
    for k in range(4):
        at_ctx = pl.multiple_of((k ^ index_ref[1]) * size, size)
        rows = pl.ds(at_ctx, size)
        total = pieces[k][0].astype(f32)
        out_ref[rows, :] = total[:, left : left + width]
        gain = None
        for p in range(3):
            for i in range(width // 128):
                at = i * 384 + p * 128 + (0 if i * 384 < left else width + EXTRA)
                value = total[:, at : at + 128]
                columns = slice(p * width + i * 128, p * width + (i + 1) * 128)
                qkv_ref[rows, columns] = value
                part = value * w_ref[rows, columns].astype(f32)
                gain = part if gain is None else gain + part
        gain = jnp.sum(gain, axis=1, keepdims=True)
        small[pl.ds(pl.multiple_of(base + at_ctx, size), size), :] = total[:, left + width : left + width + EXTRA] + place(gain, lane, EXTRA - 1)
    if last:

        @pl.when(step == 3)
        def _():
            small[pl.ds(pl.multiple_of((1 - half) * (width // 2), width // 2), width // 2), :] = first_ref[...]
            turned = small[...].T
            router_ref[...] = turned[0:ALL_EXPERTS]
            mixing_ref[0] = turned[16:18]
            mixing_ref[1] = turned[18:20]
            vec_ref[...] = turned[20:22]
            gain_ref[...] = turned[24]
            attn_ref[...] = (turned[EXTRA - 1 : EXTRA] / scale_ref[...])[0]


def unpack_half(index, pieces, w_qkv, left, scale, before):
    width = w_qkv.shape[0]
    size = width // 32
    last = before is not None
    row = lambda a, s: (s[0] * 4 + a, 0)
    source = pl.BlockSpec((1, size, pieces[0].shape[2]), lambda a, s: (a ^ s[2], 0, 0))
    whole = lambda shape: pl.BlockSpec(shape, lambda a, s: (0,) * len(shape))
    in_specs = [source] * 4 + [pl.BlockSpec((4 * size, 3 * width), row)]
    out_specs = [pl.BlockSpec((4 * size, width), row), pl.BlockSpec((4 * size, 3 * width), row)]
    out_shape = [jax.ShapeDtypeStruct((width, width), f32), jax.ShapeDtypeStruct((width, 3 * width), f32)]
    arrays = [*pieces, w_qkv]
    if last:
        shapes = ((ALL_EXPERTS, width), (2, 2, width), (2, width), (width,), (width,))
        in_specs += [whole((1, width)), whole((width // 2, EXTRA))] + [pl.BlockSpec(memory_space=pl.ANY)] * 2
        arrays += [scale, before[2], before[0], before[1]]
        scratch = [pltpu.VMEM((width, EXTRA), f32)]
        aliases = {len(arrays) - 1: 0, len(arrays): 1}
    else:
        shapes = ((width // 2, EXTRA),)
        scratch = []
        aliases = {}
    return pl.pallas_call(
        functools.partial(unpack_kernel, left, last),
        grid_spec=pltpu.PrefetchScalarGridSpec(
            num_scalar_prefetch=1,
            grid=(4,),
            in_specs=in_specs,
            out_specs=out_specs + [whole(s) for s in shapes],
            scratch_shapes=scratch,
        ),
        out_shape=out_shape + [jax.ShapeDtypeStruct(s, f32) for s in shapes],
        input_output_aliases=aliases,
        compiler_params=pltpu.CompilerParams(vmem_limit_bytes=60 * 2**20),
        cost_estimate=pl.CostEstimate(flops=0, bytes_accessed=14 * width * width, transcendentals=0),
        name="unpack_half",
    )(index, *arrays)

P = jax.sharding.PartitionSpec


def rms_inverse(tensor):
    return lax.rsqrt(jnp.mean(tensor * tensor, axis=-1, keepdims=True) + epsilon)


def after(values, *others):
    return lax.optimization_barrier((values, others))[0]


def body(inputs, prev_logits, routes, attn_gain, w_qkv, w_out, moe_gain, router, const_gate, const_vec, w_gate, w_up, w_down, out_grad):
    n_ctx, n_exp = lax.axis_size("ctx"), lax.axis_size("exp")
    me_c, me_e = lax.axis_index("ctx"), lax.axis_index("exp")
    tok, width = inputs.shape[1], inputs.shape[2]
    plen = tok - CONT_LEN
    split = n_exp // FFN_EXPERTS
    capacity = max(4, tok // 64 * 12)
    first = -(-capacity // 32) * 16
    groups = ((0, first), (first, capacity - first))
    home = (me_e // split).reshape(1)

    def deal(value):
        value = jnp.repeat(value, split, axis=0) if split > 1 else value
        return lax.all_to_all(value, "exp", 0, 0, tiled=True)

    def give_back(value):
        value = lax.all_to_all(value, "exp", 0, 0, tiled=True)
        return [value[r::split] if split > 1 else value for r in range(split)]

    x_low = inputs[0]
    upstream_low = out_grad[0]
    flags = jnp.where((me_c ^ jnp.arange(1, n_ctx)) < me_c, 0.0, NEG).astype(f32)

    prev = prev_logits[0]
    mix = jnp.concatenate([router, jnp.zeros((width, 4), bf16), const_gate[0], const_gate[1], jnp.zeros((width, EXTRA - 20), bf16)], axis=1)
    router_pad = jnp.pad(router, ((0, 0), (0, EXTRA - ALL_EXPERTS)))
    turned, chosen, early_sent = route_plan(home, routes[0].T, upstream_low, prev.T, groups)
    far = [lax.ppermute(x_low[:plen], "ctx", xor_pairs(n_ctx, k)) for k in range(1, n_ctx)]

    tokens_in = x_low.astype(f32)
    inverse_attn = rms_inverse(tokens_in)
    act_low = (tokens_in * inverse_attn * attn_gain).astype(bf16)
    projected = dot_nn(act_low, w_qkv).astype(bf16)
    early = deal(early_sent)
    act_t = turn(act_low)
    act_far, kv_far = far_projection(after(far, projected, act_t), attn_gain[None], w_qkv)

    mixed_low, lse = attention_forward(flags, projected, kv_far, plen)
    mixed_low, early = lax.optimization_barrier((mixed_low, early))
    hidden, moe_low, sent = after_attention(mixed_low, x_low, w_out, moe_gain[None], turned)
    local_out, d_normed_local, probs, d_probs, small_local = local_part(hidden, moe_low, upstream_low, prev, routes[0], mix, moe_gain[None], const_vec)
    far_t = turn(act_far)
    sent = [after(sent[0], local_out, d_normed_local, far_t), sent[1]]
    got = [deal(part.reshape(FFN_EXPERTS, -1, width)) for part in sent]

    got = [part.reshape(-1, width) for part in got]
    passes = [expert_pass(group, home, r, early, router_pad, w_gate, w_up, w_down) for group, r in zip(groups, got)]
    d_got = [give_back(p[1].reshape(n_exp, -1, width)) for p in passes]
    gate_up_low, down_low = weight_gradients(got, [p[2] for p in passes], [p[3] for p in passes], [p[4] for p in passes], [p[5] for p in passes])
    outs = jnp.concatenate([p[0].reshape(n_exp, -1, width + EXTRA) for p in passes], axis=1)
    d_got, gate_up_low, down_low, outs = lax.optimization_barrier((d_got, gate_up_low, down_low, outs))
    out_got = give_back(outs)

    d_got = [[part.reshape(-1, width) for part in group] for group in d_got]
    pairs = width // 128
    cut = pairs // 3
    core = (me_e & 1).reshape(1)
    smalls = [small_local] + [p[6] for p in passes]
    d_hidden, d_mixed, *buffers = combine(core, chosen, d_got, smalls, d_normed_local, hidden, moe_gain[None], upstream_low, mixed_low, w_out, cut * 384)

    sum_gate_up = lax.psum_scatter(gate_up_low, "ctx", scatter_dimension=1, tiled=True).astype(f32)
    sum_down = lax.psum_scatter(down_low, "ctx", scatter_dimension=0, tiled=True).astype(f32)

    def attention(upstream, begin, count, buffers, at, starts, last):
        return attention_backward(flags, core, projected, kv_far, mixed_low, upstream, lse, act_t, far_t, w_qkv, plen, begin, count, buffers, at, starts, last)

    dense = n_ctx == 4 and n_exp == 8
    left, right = cut * 384, (pairs - cut) * 384
    z = me_e >> 1
    at_ctx, at_z = me_c.reshape(1), z.reshape(1)
    along_ctx, along_z = ("ctx", 4, 1), ("exp", 8, 2)
    across = lambda value: lax.ppermute(value, "exp", xor_pairs(n_exp, 1))
    mine_1, theirs_1, grads_1, *starts = attention(d_mixed, 0, cut, buffers, 0, None, False)
    if dense:
        got_1 = across(theirs_1)
    mine_2, theirs_2, grads_2, *starts = attention(d_mixed, cut, 1, right, 0, starts, False)
    if dense:
        mine_2, theirs_2, starts, got_1 = lax.optimization_barrier((mine_2, theirs_2, starts, got_1))
        sums_1 = sum_pieces(at_z, [[quarters(mine_1), quarters(got_1)]])
        parts_1 = swap(sums_1, along_z)
        mine_2 = after(mine_2, sums_1[0])
    mine_2, theirs_2, grads_3, *d_far = attention(d_mixed, cut + 1, pairs - cut - 1, (mine_2, theirs_2), 1, starts, True)
    if dense:
        mine_2, theirs_2, grads_3, d_far, parts_1 = lax.optimization_barrier((mine_2, theirs_2, grads_3, d_far, parts_1))
    send_far = lambda k: lax.ppermute(d_far[k - 1], "ctx", xor_pairs(n_ctx, k))
    far_back = [send_far(k) for k in range(1, n_ctx - 1)]
    if dense:
        sums_2 = sum_pieces(at_z, [[quarters(mine_2), quarters(across(theirs_2))]])
        parts_2 = swap(sums_2, along_z)
        mixed_out, d_logits = finish(chosen, out_got, groups, after(local_out, sums_2[0]), probs, d_probs)
        mixed_out, d_logits, far_back, d_far = lax.optimization_barrier((mixed_out, d_logits, far_back, d_far))
        far_back = far_back + [send_far(n_ctx - 1)]
        mixed_out, parts_2 = lax.optimization_barrier((mixed_out, parts_2))
        parts_1, parts_2 = ([quarters(p) for p in parts] for parts in (parts_1, parts_2))
        parts = swap(sum_pieces(at_ctx, [parts_1, parts_2]), along_ctx)
        [piece] = sum_pieces(at_ctx, [parts])
        spread_z = spread(piece, along_z)
    else:
        mixed_out, d_logits = finish(chosen, out_got, groups, local_out, probs, d_probs)
        far_back = far_back + [send_far(n_ctx - 1)]
    d_inputs = input_gradient([grads_1, grads_2, grads_3], x_low, attn_gain[None], d_hidden, w_qkv, far_back)

    d_prev = d_logits[:ALL_EXPERTS].T[None]
    total_gate, total_up, total_down = sum_gate_up[0][None], sum_gate_up[1][None], sum_down[None]
    if dense:
        d_inputs, spread_z = lax.optimization_barrier((d_inputs, spread_z))
        column = stack_pieces(spread_z)
        own = after(spread(column, along_ctx), total_gate, total_up, total_down, d_prev)
        other = [across(piece) for piece in own]
        place_of = lambda half: jnp.stack([half, me_c, z])
        first = unpack_half(place_of(core[0]), own, w_qkv, left, None, None)
        first, other = lax.optimization_barrier((first, other))
        out_sum, qkv_sum, d_router, d_mixing, d_const_vec, d_moe_gain, d_attn_gain = unpack_half(place_of(1 - core[0]), other, w_qkv, left, attn_gain[None], first)
    else:
        whole = lambda mine, theirs: jnp.where(core == 0, jnp.concatenate([mine, theirs], axis=0), jnp.concatenate([theirs, mine], axis=0))
        total_1, total_2 = [v.astype(f32) for v in lax.psum((whole(mine_1, theirs_1), whole(mine_2, theirs_2)), ("ctx", "exp"))]
        columns = jnp.concatenate([total_1[:, :left], total_2], axis=1).reshape(width, pairs, 3, 128)
        qkv_sum = columns.transpose(0, 2, 1, 3).reshape(width, 3 * width)
        out_sum, small = total_1[:, left : left + width], total_1[:, left + width :].T
        d_attn_gain = (jnp.sum(qkv_sum * w_qkv.astype(f32), axis=1) / attn_gain)
        d_router, d_mixing, d_const_vec, d_moe_gain = small[:ALL_EXPERTS], small[16:20].reshape(2, 2, width), small[20:22], small[24]
    return (
        mixed_out[None],
        d_inputs[None],
        d_prev,
        d_attn_gain,
        qkv_sum,
        out_sum,
        d_moe_gain,
        d_router.T,
        d_mixing.transpose(0, 2, 1),
        d_const_vec,
        total_gate,
        total_up,
        total_down,
    )


def solution(mesh):
    rows = P("ctx", "exp", None)
    expert = P("exp", None, None)
    summed = P("exp", "ctx", None)
    return jax.shard_map(
        body,
        mesh=mesh,
        in_specs=(rows, rows, rows, P(), P(), P(), P(), P(), P(), P(), expert, expert, expert, rows),
        out_specs=(rows, rows, rows, P(), P(), P(), P(), P(), P(), P(), summed, summed, summed),
        check_vma=False,
    )
```

```python
import functools, math
import jax, jax.numpy as jnp
from jax import lax
from jax.experimental import pallas as pl
from jax.experimental.pallas import tpu as pltpu

HEADS = 12
HEAD_DIM = 64
CONT_LEN = 512
LOG2E = 1.4426950408889634
SCALE = HEAD_DIM ** -0.5
bf16 = jnp.bfloat16
f32 = jnp.float32
NEG = -1e30
epsilon = 1e-06


def dot_nt(a, b):
    return lax.dot_general(a, b, (((1,), (1,)), ((), ())), preferred_element_type=f32)


def dot_nn(a, b):
    return jnp.dot(a, b, preferred_element_type=f32)


def query_tiles(tok, plen):
    tiles = [(0, plen, True)]
    step = 256
    for start in range(plen, tok, step):
        tiles.append((start, step, False))
    return tiles


def split_high(value):
    high = value.astype(bf16)
    return high, (value - high.astype(f32)).astype(bf16)


def both_halves(value, head, low_half):
    turned = pltpu.roll(value, HEAD_DIM, 1)
    return jnp.where(low_half, value, turned) if head == 0 else jnp.where(low_half, turned, value)


def scaled_queries(value, head, low_half):
    high, rest = split_high(value.astype(f32) * (SCALE * LOG2E))
    rest = pltpu.roll(rest, HEAD_DIM, 1)
    return jnp.where(low_half, high, rest) if head == 0 else jnp.where(low_half, rest, high)


def attention_forward_kernel(plen, count, flags_ref, q_ref, k_ref, v_ref, kr_ref, vr_ref, gain_ref, x_any, w_any, *refs):
    turned_any, (o_ref, lse_ref, hidden_ref, low_ref), sent = refs[:count], refs[count : count + 4], refs[count + 4 : 2 * count + 4]
    kd, krd, vd, vrd, mixed, x_ref, w_ref, *select, sems = refs[2 * count + 4 :]
    step = pl.program_id(0)
    copies = [pltpu.make_async_copy(a, r, sems.at[i]) for i, (a, r) in enumerate(zip((x_any, w_any, *turned_any), (x_ref, w_ref, *select)))]

    @pl.when(step == 0)
    def _():
        for copy in copies:
            copy.start()

    tok = q_ref.shape[0]
    remote = kr_ref.shape[0]
    low_half = lax.broadcasted_iota(jnp.int32, (1, 128), 1) < HEAD_DIM
    one = jnp.ones((), bf16)
    for head in range(2):
        mine = low_half if head == 0 else ~low_half
        kd[head] = both_halves(k_ref[...], head, low_half)
        krd[head] = both_halves(kr_ref[...], head, low_half)
        vd[head] = jnp.where(mine, v_ref[...], one)
        vrd[head] = jnp.where(mine, vr_ref[...], one)
    for start, size, is_prompt in query_tiles(tok, plen):
        row = lax.broadcasted_iota(jnp.int32, (size, size), 0)
        col = lax.broadcasted_iota(jnp.int32, (size, size), 1)
        queries = q_ref[start : start + size, :]
        units = []
        for head in range(2):
            qh = scaled_queries(queries, head, low_half)
            pieces = []
            diag = dot_nt(qh, kd[head, start : start + size, :])
            pieces.append((jnp.where(col <= row, diag, NEG), vd, start, size))
            if is_prompt:
                for j in range(remote // plen):
                    s = dot_nt(qh, krd[head, j * plen : (j + 1) * plen, :])
                    pieces.append((s + flags_ref[j], vrd, j * plen, plen))
            else:
                s = dot_nt(qh, kd[head, 0:start, :])
                pieces.append((s, vd, 0, start))
                s = dot_nt(qh, krd[head])
                pieces.append((s, vrd, 0, remote))
            units.append(pieces)
        accs, peaks = [], []
        for head, pieces in enumerate(units):
            peak = None
            for s, _, _, _ in pieces:
                m = jnp.max(s, axis=1, keepdims=True)
                peak = m if peak is None else jnp.maximum(peak, m)
            acc = None
            for s, ref, at, n in pieces:
                p = jnp.exp2(s - peak).astype(bf16)
                part = dot_nn(p, ref[head, at : at + n, :])
                acc = part if acc is None else acc + part
            accs.append(acc)
            peaks.append(peak)
        num = jnp.where(low_half, accs[0], accs[1])
        den = pltpu.roll(jnp.where(low_half, accs[1], accs[0]), HEAD_DIM, 1)
        value = (num / den).astype(bf16)
        o_ref[start : start + size, :] = value
        mixed[step, start : start + size, :] = value
        turned = (jnp.where(low_half, peaks[0], peaks[1]) + jnp.log2(den)).T
        lse_ref[0, 0:8, start : start + size] = turned[0:8, :]
        lse_ref[0, 8:16, start : start + size] = turned[HEAD_DIM : HEAD_DIM + 8, :]


    @pl.when(step == pl.num_programs(0) - 1)
    def _():
        for copy in copies:
            copy.wait()
        joined = jnp.concatenate([mixed[i] for i in range(mixed.shape[0])], axis=1)
        hidden = x_ref[...].astype(f32) + dot_nn(joined, w_ref[...])
        inverse = lax.rsqrt(jnp.mean(hidden * hidden, axis=1, keepdims=True) + epsilon)
        low = (hidden * inverse * gain_ref[...]).astype(bf16)
        hidden_ref[...] = hidden
        low_ref[...] = low
        for rows_ref, s in zip(select, sent):
            s[...] = dot_nn(rows_ref[...], low).astype(bf16)


def attention_forward(flags, proj, kv_rem, plen, x, w_out, gain, turned):
    tok, width = proj.shape[0], proj.shape[1] // 3
    remote = kv_rem.shape[0]
    pairs = width // 128
    still = lambda shape: pl.BlockSpec(shape, lambda i: (0, 0))
    sent = [(r.shape[0], width) for r in turned]
    out = pl.pallas_call(
        functools.partial(attention_forward_kernel, plen, len(turned)),
        grid=(pairs,),
        in_specs=[
            pl.BlockSpec(memory_space=pltpu.SMEM),
            pl.BlockSpec((tok, 128), lambda i: (0, i)),
            pl.BlockSpec((tok, 128), lambda i: (0, pairs + i)),
            pl.BlockSpec((tok, 128), lambda i: (0, 2 * pairs + i)),
            pl.BlockSpec((remote, 128), lambda i: (0, i)),
            pl.BlockSpec((remote, 128), lambda i: (0, pairs + i)),
            still((1, width)),
        ]
        + [pl.BlockSpec(memory_space=pl.ANY)] * (2 + len(turned)),
        out_specs=[
            pl.BlockSpec((tok, 128), lambda i: (0, i)),
            pl.BlockSpec((1, 16, tok), lambda i: (i, 0, 0)),
            still((tok, width)),
            still((tok, width)),
        ]
        + [still(s) for s in sent],
        out_shape=[
            jax.ShapeDtypeStruct((tok, width), bf16),
            jax.ShapeDtypeStruct((pairs, 16, tok), f32),
            jax.ShapeDtypeStruct((tok, width), f32),
            jax.ShapeDtypeStruct((tok, width), bf16),
        ]
        + [jax.ShapeDtypeStruct(s, bf16) for s in sent],
        scratch_shapes=[pltpu.VMEM((2, n, 128), bf16) for n in (tok, remote, tok, remote)]
        + [pltpu.VMEM((pairs, tok, 128), bf16)]
        + [pltpu.VMEM(a.shape, bf16) for a in (x, w_out, *turned)]
        + [pltpu.SemaphoreType.DMA((2 + len(turned),))],
        compiler_params=pltpu.CompilerParams(vmem_limit_bytes=60 * 2**20),
        cost_estimate=pl.CostEstimate(flops=4 * tok * (tok + remote) * width + 4 * tok * width * width, bytes_accessed=2 * (tok * 10 + remote * 2) * width, transcendentals=tok * (tok + remote) * HEADS),
        name="attention_forward",
    )(flags, proj, proj, proj, kv_rem, kv_rem, gain, x, w_out, *turned)
    return out[0], out[1], out[2], out[3], out[4:]


def attention_backward_kernel(plen, started, last, skip, flags_ref, core_ref, q_ref, k_ref, v_ref, kr_ref, vr_ref, o_ref, do_ref, lse_ref, act_ref, far_ref, wk_ref, wv_ref, *refs):
    refs = refs[skip:]
    if started:
        start_far_ref, *refs = refs
    mine_ref, theirs_ref, own_grads, *refs = refs
    dfar_ref, *dfar_refs = (refs[-1:] + refs[:-10]) if last else refs[:1]
    kt, krt, dka, dva, dkra, dvra, weights, kd, krd = refs[-10:-1] if last else refs[-9:]
    tok = q_ref.shape[0]
    remote = kr_ref.shape[0]
    lane = lax.broadcasted_iota(jnp.int32, (1, 128), 1)
    low_half = lane < HEAD_DIM
    c = SCALE * LOG2E
    zero = jnp.zeros((), bf16)
    for head in range(2):
        kd[head] = both_halves(k_ref[...], head, low_half)
        krd[head] = both_halves(kr_ref[...], head, low_half)
    kt[...] = k_ref[...].T
    krt[...] = kr_ref[...].T
    dka[...] = jnp.zeros_like(dka)
    dva[...] = jnp.zeros_like(dva)
    dkra[...] = jnp.zeros_like(dkra)
    dvra[...] = jnp.zeros_like(dvra)
    pick = lax.broadcasted_iota(jnp.int32, (16, 128), 0) // 8 == lax.broadcasted_iota(jnp.int32, (16, 128), 1) // HEAD_DIM
    pick = jnp.where(pick, 1.0, 0.0).astype(bf16)
    for start, size, is_prompt in query_tiles(tok, plen):
        rows = slice(start, start + size)
        product = do_ref[rows, :].astype(f32) * o_ref[rows, :].astype(f32)
        high = product.astype(bf16)
        rest = (product - high.astype(f32)).astype(bf16)
        delta = dot_nt(pick, high) + dot_nt(pick, rest)
        totals = [None, None]
        masks = [low_half, ~low_half]
        qh = [jnp.where(m, q_ref[rows, :], zero) for m in masks]
        qs = [scaled_queries(q_ref[rows, :], head, low_half) for head in range(2)]
        doh = [jnp.where(m, do_ref[rows, :], zero) for m in masks]
        segments = [(kd, v_ref, kt, dka, dva, start, size, "diag")]
        if is_prompt:
            for j in range(remote // plen):
                segments.append((krd, vr_ref, krt, dkra, dvra, j * plen, plen, j))
        else:
            segments.append((kd, v_ref, kt, dka, dva, 0, start, None))
            segments.append((krd, vr_ref, krt, dkra, dvra, 0, remote, None))
        for kk, vv, tt, dk_acc, dv_acc, at, n, mode in segments:
            keys = slice(at, at + n)
            scores = [dot_nt(kk[head, keys, :], qs[head]) for head in range(2)]
            d_probs = [dot_nt(vv[keys, :], doh[head]) for head in range(2)]
            low_p, low_d = [], []
            for head in range(2):
                st = scores[head] - lse_ref[0, 8 * head : 8 * head + 1, rows]
                if mode == "diag":
                    key = lax.broadcasted_iota(jnp.int32, (n, size), 0)
                    query = lax.broadcasted_iota(jnp.int32, (n, size), 1)
                    st = jnp.where(key <= query, st, NEG)
                elif mode is not None:
                    st = st + flags_ref[mode]
                pt = jnp.exp2(st)
                low_p.append(pt.astype(bf16))
                low_d.append((pt * (d_probs[head] - delta[8 * head : 8 * head + 1, :])).astype(bf16))
            dv_acc[keys, :] += dot_nn(low_p[0], doh[0]) + dot_nn(low_p[1], doh[1])
            dk_acc[keys, :] += dot_nn(low_d[0], qh[0]) + dot_nn(low_d[1], qh[1])
            for head in range(2):
                part = dot_nn(tt[head * HEAD_DIM : (head + 1) * HEAD_DIM, keys], low_d[head])
                totals[head] = part if totals[head] is None else totals[head] + part
        dqt = totals
        own_grads[rows, 0:128] = (jnp.concatenate(dqt, axis=0).T * SCALE).astype(bf16)
    own_grads[:, 128:256] = (dka[...] * SCALE).astype(bf16)
    own_grads[:, 256:384] = dva[...].astype(bf16)
    far_grads = jnp.concatenate([(dkra[...] * SCALE).astype(bf16), dvra[...].astype(bf16)], axis=1)
    weights[:, 0:128] = wk_ref[...]
    weights[:, 128:256] = wv_ref[...]
    half = mine_ref.shape[0]
    for out_ref, which in ((theirs_ref, 1 - core_ref[0]), (mine_ref, core_ref[0])):
        rows = pl.ds(pl.multiple_of(which * half, half), half)
        total = dot_nn(act_ref[rows, :], own_grads[...])
        out_ref[:, 0:128] = total[:, 0:128].astype(bf16)
        out_ref[:, 128:384] = (total[:, 128:384] + dot_nn(far_ref[rows, :], far_grads)).astype(bf16)
    d_far = dot_nt(far_grads, weights[...])
    step = pl.program_id(0)

    @pl.when(step == 0)
    def _():
        dfar_ref[...] = d_far + start_far_ref[...] if started else d_far

    @pl.when(step > 0)
    def _():
        dfar_ref[...] += d_far

    if last:

        @pl.when(step == pl.num_programs(0) - 1)
        def _():
            for k, ref in enumerate(dfar_refs):
                ref[...] = dfar_ref[k * plen : (k + 1) * plen, :].astype(bf16)


def attention_backward(flags, core, proj, kv_rem, mixed, d_mixed, lse, act_t, far_t, w_qkv, plen, begin, count, buffers, at, starts, last):
    tok, width = mixed.shape
    remote = kv_rem.shape[0]
    pairs = width // 128
    own = lambda shift: pl.BlockSpec((tok, 128), lambda i: (0, shift + i))
    far = lambda shift: pl.BlockSpec((remote, 128), lambda i: (0, shift + i))
    weight = lambda shift: pl.BlockSpec((width, 128), lambda i: (0, shift + i))
    still = lambda shape: pl.BlockSpec(shape, lambda i: (0, 0))
    half = pl.BlockSpec((width // 2, 384), lambda i: (0, at + i))
    in_specs = [
        pl.BlockSpec(memory_space=pltpu.SMEM),
        pl.BlockSpec(memory_space=pltpu.SMEM),
        own(begin),
        own(pairs + begin),
        own(2 * pairs + begin),
        far(begin),
        far(pairs + begin),
        own(begin),
        own(begin),
        pl.BlockSpec((1, 16, tok), lambda i: (begin + i, 0, 0)),
        still((width, tok)),
        still((width, remote)),
        weight(pairs + begin),
        weight(2 * pairs + begin),
    ]
    arrays = [flags, core, proj, proj, proj, kv_rem, kv_rem, mixed, d_mixed, lse, act_t, far_t, w_qkv, w_qkv]
    scratch = [
        pltpu.VMEM((128, tok), bf16),
        pltpu.VMEM((128, remote), bf16),
        pltpu.VMEM((tok, 128), f32),
        pltpu.VMEM((tok, 128), f32),
        pltpu.VMEM((remote, 128), f32),
        pltpu.VMEM((remote, 128), f32),
        pltpu.VMEM((width, 256), bf16),
        pltpu.VMEM((2, tok, 128), bf16),
        pltpu.VMEM((2, remote, 128), bf16),
    ]
    aliases = {}
    skip = 0
    if not isinstance(buffers, int):
        aliases = {len(arrays): 0, len(arrays) + 1: 1}
        in_specs += [pl.BlockSpec(memory_space=pl.ANY)] * 2
        arrays += list(buffers)
        skip = 2
        buffers = buffers[0].shape[1]
    if starts:
        in_specs += [still((remote, width))]
        arrays += list(starts)
    out_specs = [half, half, pl.BlockSpec((tok, 384), lambda i: (0, i))]
    out_shape = [jax.ShapeDtypeStruct((width // 2, buffers), bf16)] * 2 + [jax.ShapeDtypeStruct((tok, count * 384), bf16)]
    if last:
        out_specs += [still((plen, width))] * (remote // plen)
        out_shape += [jax.ShapeDtypeStruct((plen, width), bf16)] * (remote // plen)
        scratch = scratch + [pltpu.VMEM((remote, width), f32)]
    else:
        out_specs += [still((remote, width))]
        out_shape += [jax.ShapeDtypeStruct((remote, width), f32)]
    return pl.pallas_call(
        functools.partial(attention_backward_kernel, plen, bool(starts), last, skip),
        grid=(count,),
        in_specs=in_specs,
        out_specs=out_specs,
        out_shape=out_shape,
        scratch_shapes=scratch,
        input_output_aliases=aliases,
        compiler_params=pltpu.CompilerParams(vmem_limit_bytes=60 * 2**20),
        cost_estimate=pl.CostEstimate(flops=10 * tok * (tok + remote) * count * 128 + 20 * tok * width * count * 128, bytes_accessed=2 * (tok * 8 + remote * 4) * count * 128 + 16 * tok * width, transcendentals=tok * (tok + remote) * 2 * count),
        name="attention_backward",
    )(*arrays)


FFN_EXPERTS = 8
ALL_EXPERTS = 12
EXTRA = 128
SMALL = 8


def dot_tn(a, b):
    return lax.dot_general(a, b, (((0,), (0,)), ((), ())), preferred_element_type=f32)


def split_low(value, parts):
    pieces = []
    for _ in range(parts):
        piece = value.astype(bf16)
        pieces.append(piece)
        value = value - piece.astype(f32)
    return pieces


def route_kernel(groups, home_ref, ids_ref, grad_ref, prev_ref, x_ref, *out_refs):
    tok, width = grad_ref.shape
    count = len(groups)
    turned_refs, chosen_refs, (early_ref, prompt_ref) = out_refs[:count], out_refs[count : 2 * count], out_refs[2 * count :]
    prompt_ref[...] = x_ref[0 : prompt_ref.shape[0], :]
    capacity = early_ref.shape[1] - SMALL
    expert = lax.broadcasted_iota(jnp.int32, (16, tok), 0)
    ids = [ids_ref[k : k + 1, :] for k in range(2)]
    names = [row == expert for row in ids]
    both = jnp.where(names[0] | names[1], 1.0, 0.0).astype(bf16)
    earlier = lax.broadcasted_iota(jnp.int32, (tok, tok), 0) < lax.broadcasted_iota(jnp.int32, (tok, tok), 1)
    before = dot_nn(both, jnp.where(earlier, 1.0, 0.0).astype(bf16))
    pieces = [piece.astype(f32) for piece in split_low(prev_ref[...], 3)]
    extra = jnp.concatenate(pieces + [jnp.zeros((EXTRA - 3 * ALL_EXPERTS, tok), f32)], axis=0).T.astype(bf16)
    slot = [jnp.sum(jnp.where(n, before, 0.0), axis=0, keepdims=True).astype(jnp.int32) for n in names]
    extras = []
    for (first, size), turned_ref, chosen_ref in zip(groups, turned_refs, chosen_refs):
        spots = lax.broadcasted_iota(jnp.int32, (FFN_EXPERTS * size, tok), 0)
        hit = None
        for k in range(2):
            inside = (ids[k] < FFN_EXPERTS) & (slot[k] >= first) & (slot[k] < first + size)
            place = jnp.where(inside, ids[k] * size + slot[k] - first, -1)
            hit = spots == place if hit is None else hit | (spots == place)
        turned = jnp.where(hit, 1.0, 0.0).astype(bf16)
        turned_ref[...] = turned
        chosen_ref[...] = turned.T
        grads = dot_nn(turned, grad_ref[...]).astype(bf16)
        extras.append(dot_nn(turned, extra))
        for e in range(FFN_EXPERTS):
            early_ref[e, first : first + size, :] = grads[e * size : (e + 1) * size]
    third = capacity // 3
    for e in range(FFN_EXPERTS):
        rows = jnp.concatenate([x[e * size : (e + 1) * size] for x, (_, size) in zip(extras, groups)], axis=0)
        rows = rows[0:third] + pltpu.roll(rows[third : 2 * third], 40, 1) + pltpu.roll(rows[2 * third : capacity], 80, 1)
        early_ref[e, capacity : capacity + SMALL, :] = jnp.zeros((SMALL, width), bf16)
        for g in range(third // SMALL):
            early_ref[e, capacity : capacity + SMALL, g * EXTRA : (g + 1) * EXTRA] = rows[g * SMALL : (g + 1) * SMALL].astype(bf16)


def route_plan(home, ids, grad, prev, x, plen, groups):
    tok, width = grad.shape
    counts = [FFN_EXPERTS * size for _, size in groups]
    whole = pl.BlockSpec(memory_space=pltpu.VMEM)
    early = (FFN_EXPERTS, sum(counts) // FFN_EXPERTS + SMALL, width)
    out = pl.pallas_call(
        functools.partial(route_kernel, groups),
        in_specs=[pl.BlockSpec(memory_space=pltpu.SMEM), whole, whole, whole, whole],
        out_specs=[whole] * (2 * len(groups) + 2),
        out_shape=[jax.ShapeDtypeStruct((n, tok), bf16) for n in counts]
        + [jax.ShapeDtypeStruct((tok, n), bf16) for n in counts]
        + [jax.ShapeDtypeStruct(early, bf16), jax.ShapeDtypeStruct((plen, width), bf16)],
        compiler_params=pltpu.CompilerParams(vmem_limit_bytes=60 * 2**20),
        cost_estimate=pl.CostEstimate(flops=2 * sum(counts) * tok * (width + EXTRA), bytes_accessed=4 * sum(counts) * width, transcendentals=0),
        name="route_plan",
    )(home, ids, grad, prev, x)
    return out[: len(groups)], out[len(groups) : -2], out[-2], out[-1]


def router_inputs(early_ref, slots):
    capacity = early_ref.shape[1] - SMALL
    groups = capacity // 3 // SMALL
    rows = []
    for sender in range(early_ref.shape[0]):
        packed = early_ref[sender, capacity : capacity + SMALL, :].astype(f32)
        third = jnp.concatenate([packed[:, g * EXTRA : (g + 1) * EXTRA] for g in range(groups)], axis=0)
        every = jnp.concatenate([third, pltpu.roll(third, EXTRA - 40, 1), pltpu.roll(third, EXTRA - 80, 1)], axis=0)
        rows.append(every[slots])
    rows = jnp.concatenate(rows, axis=0)
    return rows + pltpu.roll(rows, EXTRA - ALL_EXPERTS, 1) + pltpu.roll(rows, EXTRA - 2 * ALL_EXPERTS, 1)


def expert_kernel(group, home_ref, rows_ref, early_ref, router_ref, wg_ref, wu_ref, wd_ref,
                  out_ref, drow_ref, dout_ref, inner_ref, dgate_ref, dup_ref, small_ref, acc_out, acc_row, probs_ref):
    width = rows_ref.shape[1]
    step, steps = pl.program_id(0), pl.num_programs(0)
    home = home_ref[0]
    lane = lax.broadcasted_iota(jnp.int32, (1, EXTRA), 1)
    slots = slice(group[0], group[0] + group[1])

    @pl.when(step == 0)
    def _():
        logits = router_inputs(early_ref, slots) + dot_nn(rows_ref[...], router_ref[...])
        logits = jnp.where(lane < ALL_EXPERTS, logits, NEG)
        unnormed = jnp.exp(logits - jnp.max(logits, axis=1, keepdims=True))
        probs = unnormed / jnp.sum(unnormed, axis=1, keepdims=True)
        probs_ref[...] = probs
        gate = jnp.sum(jnp.where(lane == home, probs, 0.0), axis=1, keepdims=True)
        dout_ref[...] = (gate * early_ref[:, slots, 0:width].astype(f32).reshape(-1, width)).astype(bf16)
        acc_out[...] = jnp.zeros_like(acc_out)
        acc_row[...] = jnp.zeros_like(acc_row)

    rows = rows_ref[...]
    gate_pre = dot_nn(rows, wg_ref[0])
    up_pre = dot_nn(rows, wu_ref[0])
    d_inner = dot_nt(dout_ref[...], wd_ref[0])
    sigmoid = jax.nn.sigmoid(gate_pre)
    silu = gate_pre * sigmoid
    inner = (silu * up_pre).astype(bf16)
    d_gate = (d_inner * up_pre * (sigmoid * (1.0 + gate_pre * (1.0 - sigmoid)))).astype(bf16)
    d_up = (d_inner * silu).astype(bf16)
    inner_ref[...] = inner
    dgate_ref[...] = d_gate
    dup_ref[...] = d_up
    acc_out[...] += dot_nn(inner, wd_ref[0])
    acc_row[...] += dot_nt(d_gate, wg_ref[0]) + dot_nt(d_up, wu_ref[0])

    @pl.when(step == steps - 1)
    def _():
        probs = probs_ref[...]
        gate = jnp.sum(jnp.where(lane == home, probs, 0.0), axis=1, keepdims=True)
        out = acc_out[...].astype(bf16).astype(f32)
        d_row_gate = jnp.sum(out * early_ref[:, slots, 0:width].astype(f32).reshape(-1, width), axis=1, keepdims=True)
        out_ref[:, 0:width] = (gate * out).astype(bf16)
        extra = jnp.zeros((out.shape[0], EXTRA), f32)
        for i, piece in enumerate(split_low(d_row_gate, 3)):
            extra = jnp.where(lane == home + 16 * i, piece.astype(f32), extra)
        out_ref[:, width : width + EXTRA] = extra.astype(bf16)
        term = d_row_gate * gate * (jnp.where(lane == home, 1.0, 0.0) - probs)
        high, rest = split_low(term, 2)
        turned = [piece.T for piece in (high, rest)]
        small_ref[...] = (dot_nn(turned[0], rows) + dot_nn(turned[1], rows))[0 : 2 * SMALL, :]
        drow_ref[...] = (acc_row[...] + dot_nt(high, router_ref[...]) + dot_nt(rest, router_ref[...])).astype(bf16)


def expert_pass(group, home, rows, early, router_pad, w_gate, w_up, w_down):
    count, width = rows.shape
    ff = w_gate.shape[2]
    tile = min(512, ff)
    full = pl.BlockSpec((count, width), lambda j: (0, 0))
    wide = pl.BlockSpec((count, width + EXTRA), lambda j: (0, 0))
    tall = pl.BlockSpec((1, width, tile), lambda j: (0, 0, j))
    piece = pl.BlockSpec((count, tile), lambda j: (0, j))
    return pl.pallas_call(
        functools.partial(expert_kernel, group),
        grid=(ff // tile,),
        in_specs=[
            pl.BlockSpec(memory_space=pltpu.SMEM),
            full,
            pl.BlockSpec(early.shape, lambda j: (0, 0, 0)),
            pl.BlockSpec((width, EXTRA), lambda j: (0, 0)),
            tall,
            tall,
            pl.BlockSpec((1, tile, width), lambda j: (0, j, 0)),
        ],
        out_specs=[wide, full, full, piece, piece, piece, pl.BlockSpec((2 * SMALL, width), lambda j: (0, 0))],
        out_shape=[
            jax.ShapeDtypeStruct((count, width + EXTRA), bf16),
            jax.ShapeDtypeStruct((count, width), bf16),
            jax.ShapeDtypeStruct((count, width), bf16),
        ]
        + [jax.ShapeDtypeStruct((count, ff), bf16)] * 3
        + [jax.ShapeDtypeStruct((2 * SMALL, width), f32)],
        scratch_shapes=[pltpu.VMEM((count, width), f32), pltpu.VMEM((count, width), f32), pltpu.VMEM((count, EXTRA), f32)],
        compiler_params=pltpu.CompilerParams(vmem_limit_bytes=60 * 2**20),
        cost_estimate=pl.CostEstimate(flops=12 * count * width * ff, bytes_accessed=6 * width * ff + 2 * count * (5 * width + 3 * ff), transcendentals=count * ff),
        name="expert_pass",
    )(home, rows, early, router_pad, w_gate, w_up, w_down)


def weight_kernel(count, *refs):
    rows, douts, inners, dgates, dups = (refs[i * count : (i + 1) * count] for i in range(5))
    gate_up_ref, down_ref = refs[5 * count : 5 * count + 2]
    turned = refs[5 * count + 2 :]

    @pl.when(pl.program_id(0) == 0)
    def _():
        for ref, scratch in zip(rows, turned):
            scratch[...] = ref[...].T

    gate_up_ref[0] = sum(dot_nn(t[...], d[...]) for t, d in zip(turned, dgates)).astype(bf16)
    gate_up_ref[1] = sum(dot_nn(t[...], d[...]) for t, d in zip(turned, dups)).astype(bf16)
    down_ref[...] = sum(dot_nn(i[...].T, d[...]) for i, d in zip(inners, douts)).astype(bf16)


def weight_gradients(rows, douts, inners, dgates, dups):
    count = len(rows)
    width, ff = rows[0].shape[1], inners[0].shape[1]
    tile = min(512, ff)
    total = sum(r.shape[0] for r in rows)
    full = [pl.BlockSpec(r.shape, lambda j: (0, 0)) for r in rows]
    piece = [pl.BlockSpec((r.shape[0], tile), lambda j: (0, j)) for r in rows]
    return pl.pallas_call(
        functools.partial(weight_kernel, count),
        grid=(ff // tile,),
        in_specs=full + full + piece * 3,
        out_specs=[pl.BlockSpec((2, width, tile), lambda j: (0, 0, j)), pl.BlockSpec((tile, width), lambda j: (j, 0))],
        out_shape=[jax.ShapeDtypeStruct((2, width, ff), bf16), jax.ShapeDtypeStruct((ff, width), bf16)],
        scratch_shapes=[pltpu.VMEM((width, r.shape[0]), bf16) for r in rows],
        compiler_params=pltpu.CompilerParams(vmem_limit_bytes=60 * 2**20),
        cost_estimate=pl.CostEstimate(flops=6 * total * width * ff, bytes_accessed=6 * width * ff + 2 * total * (2 * width + 3 * ff), transcendentals=0),
        name="weight_gradients",
    )(*rows, *douts, *inners, *dgates, *dups)


ANYWHERE = pl.BlockSpec(memory_space=pltpu.VMEM)
SCALARS = pl.BlockSpec(memory_space=pltpu.SMEM)


def inverse_rms(value):
    return lax.rsqrt(jnp.mean(value * value, axis=1, keepdims=True) + epsilon)


def turn_kernel(in_ref, out_ref):
    out_ref[...] = in_ref[...].T


def turn(value):
    rows, columns = value.shape
    block = 256 if rows % 256 == 0 else 128
    return pl.pallas_call(
        turn_kernel,
        grid=(rows // block,),
        in_specs=[pl.BlockSpec((block, columns), lambda i: (i, 0))],
        out_specs=pl.BlockSpec((columns, block), lambda i: (0, i)),
        out_shape=jax.ShapeDtypeStruct((columns, rows), value.dtype),
        compiler_params=pltpu.CompilerParams(vmem_limit_bytes=60 * 2**20),
        cost_estimate=pl.CostEstimate(flops=0, bytes_accessed=4 * rows * columns, transcendentals=0),
        name="turn",
    )(value)


def place(value, lane, at):
    return jnp.where(lane == at, value, 0.0)


def local_kernel(hidden_ref, low_ref, grad_ref, prev_ref, ids_ref, mix_ref, gain_ref, vec_ref, out_ref, dnormed_ref, probs_ref, dprobs_ref, small_ref):
    lane = lax.broadcasted_iota(jnp.int32, (1, EXTRA), 1)
    hidden = hidden_ref[...]
    normed = hidden * inverse_rms(hidden) * gain_ref[...]
    low = low_ref[...]
    grad = grad_ref[...].astype(f32)
    raw = dot_nn(low, mix_ref[...])
    prev = jnp.concatenate([prev_ref[...], jnp.zeros((raw.shape[0], EXTRA - ALL_EXPERTS), f32)], axis=1)
    logits = jnp.where(lane < ALL_EXPERTS, raw + prev, NEG)
    unnormed = jnp.exp(logits - jnp.max(logits, axis=1, keepdims=True))
    probs = unnormed / jnp.sum(unnormed, axis=1, keepdims=True)
    named = (ids_ref[:, 0:1] == lane) | (ids_ref[:, 1:2] == lane)
    gates = jnp.where(named, probs, 0.0)
    copy_gate = gates[:, FFN_EXPERTS + 1 : FFN_EXPERTS + 2]
    dots = jnp.sum(grad * normed, axis=1, keepdims=True)
    out = hidden
    weight = copy_gate
    d_probs = place(dots, lane, FFN_EXPERTS + 1)
    logit_grads = jnp.zeros_like(probs)
    vec_terms = jnp.zeros_like(probs)
    for c in range(2):
        vec = vec_ref[c : c + 1, :]
        gate = gates[:, FFN_EXPERTS + 2 + c : FFN_EXPERTS + 3 + c]
        at = 16 + 2 * c
        a0 = jax.nn.sigmoid(raw[:, at : at + 1] - raw[:, at + 1 : at + 2])
        a1 = jax.nn.sigmoid(raw[:, at + 1 : at + 2] - raw[:, at : at + 1])
        vec_dots = jnp.sum(grad * vec, axis=1, keepdims=True)
        weight = weight + gate * a0
        out = out + (gate * a1) * vec
        d_probs = d_probs + place(a0 * dots + a1 * vec_dots, lane, FFN_EXPERTS + 2 + c)
        d0, d1 = gate * dots, gate * vec_dots
        mean = a0 * d0 + a1 * d1
        d0, d1 = a0 * (d0 - mean), a1 * (d1 - mean)
        logit_grads = logit_grads + place(d0, lane, at) + place(d1, lane, at + 1)
        vec_terms = vec_terms + place(gate * a1, lane, 20 + c)
    d_probs = jnp.where(named, d_probs, 0.0)
    logit_grads = logit_grads + probs * (d_probs - jnp.sum(probs * d_probs, axis=1, keepdims=True))
    high, rest = split_low(logit_grads, 2)
    out_ref[...] = out + weight * normed
    dnormed_ref[...] = weight * grad + dot_nt(high, mix_ref[...]) + dot_nt(rest, mix_ref[...])
    probs_ref[...] = probs
    dprobs_ref[...] = d_probs
    sums = None
    for terms, rows in ((logit_grads, low), (vec_terms, grad_ref[...])):
        for piece in split_low(terms.T, 2):
            part = dot_nn(piece, rows)
            sums = part if sums is None else sums + part
    sums = sums[0 : 3 * SMALL, :]

    @pl.when(pl.program_id(0) == 0)
    def _():
        small_ref[...] = sums

    @pl.when(pl.program_id(0) > 0)
    def _():
        small_ref[...] += sums


def local_part(hidden, low, grad, prev, ids, mix, gain, vec):
    tok, width = hidden.shape
    block, tiles = row_tiles(tok)
    shapes = [(tok, width), (tok, width), (tok, EXTRA), (tok, EXTRA), (3 * SMALL, width)]
    return pl.pallas_call(
        local_kernel,
        grid=(tok // block,),
        in_specs=[tiles(width), tiles(width), tiles(width), tiles(ALL_EXPERTS), tiles(2), fixed(mix), fixed(gain), fixed(vec)],
        out_specs=[tiles(width), tiles(width), tiles(EXTRA), tiles(EXTRA), pl.BlockSpec((3 * SMALL, width), lambda i: (0, 0))],
        out_shape=[jax.ShapeDtypeStruct(s, f32) for s in shapes],
        compiler_params=pltpu.CompilerParams(vmem_limit_bytes=60 * 2**20),
        cost_estimate=pl.CostEstimate(flops=14 * tok * width * EXTRA, bytes_accessed=16 * tok * width, transcendentals=tok * EXTRA),
        name="local_part",
    )(hidden, low, grad, prev, ids, mix, gain, vec)


def row_tiles(tok):
    block = 256 if tok % 256 == 0 else 128
    return block, lambda columns: pl.BlockSpec((block, columns), lambda i: (i, 0))


def fixed(value):
    return pl.BlockSpec(value.shape, lambda i: (0,) * value.ndim)


def combine_kernel(count, parts, core_ref, *refs):
    chosen, got, refs = refs[:count], refs[count : count * (1 + parts)], refs[count * (1 + parts) :]
    smalls, refs = refs[: count + 1], refs[count + 1 :]
    local_ref, hidden_ref, gain_ref, grad_ref, mixed_ref, w_ref, dhidden_ref, dmixed_ref, mine_ref, theirs_ref, total_w, total_gain, small_t = refs
    step = pl.program_id(0)

    @pl.when(step == 0)
    def _():
        total_w[...] = jnp.zeros_like(total_w)
        total_gain[...] = jnp.zeros_like(total_gain)

    d_normed = local_ref[...]
    for g in range(count):
        for r in range(parts):
            d_normed = d_normed + dot_nn(chosen[g][...], got[g * parts + r][...])
    hidden = hidden_ref[...]
    inverse = inverse_rms(hidden)
    scaled = d_normed * gain_ref[...]
    mean = jnp.mean(scaled * hidden, axis=1, keepdims=True)
    d_hidden = grad_ref[...].astype(f32) + inverse * scaled - hidden * (inverse * inverse * inverse * mean)
    low = d_hidden.astype(bf16)
    dhidden_ref[...] = d_hidden
    dmixed_ref[...] = dot_nt(low, w_ref[...]).astype(bf16)
    total_w[...] += dot_nn(mixed_ref[...].T, low)
    total_gain[...] += jnp.sum(d_normed * hidden * inverse, axis=0, keepdims=True)

    @pl.when(step == pl.num_programs(0) - 1)
    def _():
        width = w_ref.shape[0]
        half = width // 2
        row = lax.broadcasted_iota(jnp.int32, (SMALL, 1), 0)
        top = smalls[0][0 : 2 * SMALL, :]
        for small in smalls[1:]:
            top = top + small[...]
        rest = jnp.zeros((EXTRA - 4 * SMALL, width), f32)
        rows = [top, smalls[0][2 * SMALL : 3 * SMALL, :], jnp.where(row == 0, total_gain[...], 0.0), rest]
        small_t[...] = jnp.concatenate(rows, axis=0).T
        at = mine_ref.shape[1] - width - EXTRA
        for out_ref, which in ((theirs_ref, 1 - core_ref[0]), (mine_ref, core_ref[0])):
            place_rows = pl.ds(pl.multiple_of(which * half, half), half)
            out_ref[:, at : at + width] = total_w[place_rows, :].astype(bf16)
            out_ref[:, at + width : at + width + EXTRA] = small_t[place_rows, :].astype(bf16)


def combine(core, chosen, got, smalls, local, hidden, gain, grad, mixed, w_out, columns):
    tok, width = hidden.shape
    rows = sum(c.shape[1] for c in chosen)
    arrays = [a for group in got for a in group]
    block, tiles = row_tiles(tok)
    half = (width // 2, columns + width + EXTRA)
    return pl.pallas_call(
        functools.partial(combine_kernel, len(chosen), len(got[0])),
        grid=(tok // block,),
        in_specs=[SCALARS] + [tiles(c.shape[1]) for c in chosen] + [fixed(a) for a in arrays + smalls]
        + [tiles(width), tiles(width), fixed(gain), tiles(width), tiles(width), fixed(w_out)],
        out_specs=[tiles(width)] * 2 + [pl.BlockSpec(half, lambda i: (0, 0))] * 2,
        out_shape=[jax.ShapeDtypeStruct((tok, width), f32), jax.ShapeDtypeStruct((tok, width), bf16)] + [jax.ShapeDtypeStruct(half, bf16)] * 2,
        scratch_shapes=[pltpu.VMEM((width, width), f32), pltpu.VMEM((1, width), f32), pltpu.VMEM((width, EXTRA), f32)],
        compiler_params=pltpu.CompilerParams(vmem_limit_bytes=60 * 2**20),
        cost_estimate=pl.CostEstimate(flops=2 * tok * width * (rows + 2 * width), bytes_accessed=2 * width * (10 * tok + 2 * rows), transcendentals=0),
        name="combine_gradients",
    )(core, *chosen, *arrays, *smalls, local, hidden, gain, grad, mixed, w_out)


def flat_rows(value):
    if value.shape[1] % 16:
        return value.astype(f32).reshape(-1, value.shape[2]).astype(bf16)
    return value.reshape(-1, value.shape[2])


def finish_kernel(groups, parts, *refs):
    chosen, got = refs[: len(groups)], refs[len(groups) : len(groups) + parts]
    local_ref, probs_ref, dprobs_ref, out_ref, dlogits_ref = refs[len(groups) + parts :]
    width = local_ref.shape[1]
    lane = lax.broadcasted_iota(jnp.int32, (1, EXTRA), 1)
    picked = None
    for c, (at, size) in zip(chosen, groups):
        for r in range(parts):
            part = dot_nn(c[...], flat_rows(got[r][:, at : at + size, :]))
            picked = part if picked is None else picked + part
    out_ref[...] = (local_ref[...] + picked[:, 0:width]).astype(bf16)
    extra = picked[:, width : width + EXTRA]
    extra = extra + pltpu.roll(extra, EXTRA - 16, 1) + pltpu.roll(extra, EXTRA - 32, 1)
    d_probs = dprobs_ref[...] + jnp.where(lane < ALL_EXPERTS, extra, 0.0)
    probs = probs_ref[...]
    d_logits = probs * (d_probs - jnp.sum(probs * d_probs, axis=1, keepdims=True))
    dlogits_ref[...] = d_logits.T


def finish(chosen, got, groups, local, probs, d_probs):
    tok, width = local.shape
    block, tiles = row_tiles(tok)
    return pl.pallas_call(
        functools.partial(finish_kernel, groups, len(got)),
        grid=(tok // block,),
        in_specs=[tiles(c.shape[1]) for c in chosen] + [fixed(g) for g in got] + [tiles(width), tiles(EXTRA), tiles(EXTRA)],
        out_specs=[tiles(width), pl.BlockSpec((EXTRA, block), lambda i: (0, i))],
        out_shape=[jax.ShapeDtypeStruct((tok, width), bf16), jax.ShapeDtypeStruct((EXTRA, tok), f32)],
        compiler_params=pltpu.CompilerParams(vmem_limit_bytes=60 * 2**20),
        cost_estimate=pl.CostEstimate(flops=2 * tok * 1152 * (width + EXTRA), bytes_accessed=16 * tok * width, transcendentals=0),
        name="finish_outputs",
    )(*chosen, *got, local, probs, d_probs)


def input_kernel(count, x_ref, gain_ref, dhidden_ref, w_ref, *refs):
    grads, far, (out_ref, weights) = refs[:count], refs[count:-2], refs[-2:]
    width = x_ref.shape[1]

    @pl.when(pl.program_id(0) == 0)
    def _():
        for i in range(width // 128):
            for p in range(3):
                weights[:, i * 384 + p * 128 : i * 384 + (p + 1) * 128] = w_ref[:, p * width + i * 128 : p * width + (i + 1) * 128]

    total = None
    for ref in far:
        total = ref[...].astype(f32) if total is None else total + ref[...].astype(f32)
    d_act = jnp.where(pl.program_id(0) == 0, total, 0.0)
    at = 0
    for ref in grads:
        columns = ref.shape[1]
        d_act = d_act + dot_nt(ref[...], weights[:, at : at + columns])
        at += columns
    x = x_ref[...].astype(f32)
    inverse = inverse_rms(x)
    scaled = d_act * gain_ref[...]
    mean = jnp.mean(scaled * x, axis=1, keepdims=True)
    out_ref[...] = dhidden_ref[...] + inverse * scaled - x * (inverse * inverse * inverse * mean)


def input_gradient(grads, x, gain, d_hidden, w_qkv, far):
    tok, width = x.shape
    block = far[0].shape[0]
    tiles = lambda columns: pl.BlockSpec((block, columns), lambda i: (i, 0))
    return pl.pallas_call(
        functools.partial(input_kernel, len(grads)),
        grid=(tok // block,),
        in_specs=[tiles(width), fixed(gain), tiles(width), fixed(w_qkv)] + [tiles(g.shape[1]) for g in grads] + [fixed(f) for f in far],
        out_specs=tiles(width),
        out_shape=jax.ShapeDtypeStruct((tok, width), f32),
        scratch_shapes=[pltpu.VMEM((width, 3 * width), bf16)],
        compiler_params=pltpu.CompilerParams(vmem_limit_bytes=60 * 2**20),
        cost_estimate=pl.CostEstimate(flops=6 * tok * width * width, bytes_accessed=22 * tok * width, transcendentals=0),
        name="input_gradient",
    )(x, gain, d_hidden, w_qkv, *grads, *far)


def far_kernel(count, gain_ref, wk_ref, wv_ref, *refs):
    far, (act_ref, kv_ref) = refs[:count], refs[count:]
    width = wk_ref.shape[0]
    for k, ref in enumerate(far):

        @pl.when(pl.program_id(0) == k)
        def _():
            x = ref[...].astype(f32)
            act = (x * inverse_rms(x) * gain_ref[...]).astype(bf16)
            act_ref[...] = act
            kv_ref[:, 0:width] = dot_nn(act, wk_ref[...]).astype(bf16)
            kv_ref[:, width : 2 * width] = dot_nn(act, wv_ref[...]).astype(bf16)


def far_projection(far, gain, w_qkv):
    rows, width = far[0].shape
    count = len(far)
    return pl.pallas_call(
        functools.partial(far_kernel, count),
        grid=(count,),
        in_specs=[fixed(gain), pl.BlockSpec((width, width), lambda i: (0, 1)), pl.BlockSpec((width, width), lambda i: (0, 2))] + [fixed(f) for f in far],
        out_specs=[pl.BlockSpec((rows, width), lambda i: (i, 0)), pl.BlockSpec((rows, 2 * width), lambda i: (i, 0))],
        out_shape=[jax.ShapeDtypeStruct((count * rows, width), bf16), jax.ShapeDtypeStruct((count * rows, 2 * width), bf16)],
        compiler_params=pltpu.CompilerParams(vmem_limit_bytes=60 * 2**20),
        cost_estimate=pl.CostEstimate(flops=4 * count * rows * width * width, bytes_accessed=2 * width * (4 * count * rows + 2 * width), transcendentals=0),
        name="far_projection",
    )(gain, w_qkv, w_qkv, *far)


def xor_pairs(size, mask):
    return [(i, i ^ mask) for i in range(size)]


def sum_kernel(terms, index_ref, *refs):
    count = len(refs) // (sum(terms) + 1)
    outs = refs[-count:]
    for k, out_ref in enumerate(outs):
        at = 0
        first = 0
        for number in terms:
            total = None
            for t in range(first, first + number):
                value = refs[t * count + k][0].astype(f32)
                total = value if total is None else total + value
            out_ref[0, :, at : at + total.shape[1]] = total.astype(bf16)
            at += total.shape[1]
            first += number


def sum_pieces(index, groups):
    arrays = [a for group in groups for a in group]
    n, rows = arrays[0].shape[:2]
    columns = sum(group[0].shape[2] for group in groups)
    view = lambda a, k: pl.BlockSpec((1, rows, a.shape[2]), lambda i, s: (s[0] ^ k if n > 1 else 0, 0, 0))
    return pl.pallas_call(
        functools.partial(sum_kernel, [len(g) for g in groups]),
        grid_spec=pltpu.PrefetchScalarGridSpec(
            num_scalar_prefetch=1,
            grid=(1,),
            in_specs=[view(a, k) for a in arrays for k in range(n)],
            out_specs=[pl.BlockSpec((1, rows, columns), lambda i, s: (0, 0, 0))] * n,
        ),
        out_shape=[jax.ShapeDtypeStruct((1, rows, columns), bf16)] * n,
        compiler_params=pltpu.CompilerParams(vmem_limit_bytes=60 * 2**20),
        cost_estimate=pl.CostEstimate(flops=0, bytes_accessed=2 * n * rows * columns * 5, transcendentals=0),
        name="sum_pieces",
    )(index, *[a for a in arrays for _ in range(n)])


def quarters(value):
    return value.reshape(4, -1, value.shape[-1])


def swap(pieces, along):
    axis, size, unit = along
    return [pieces[0]] + [lax.ppermute(pieces[k], axis, xor_pairs(size, unit * k)) for k in range(1, 4)]


def spread(value, along):
    return swap([value] * 4, along)


def stack_kernel(*refs):
    n = len(refs) - 1
    size = refs[0].shape[0]
    for k in range(n):
        refs[n][k * size : (k + 1) * size] = refs[k][...]


def stack_pieces(pieces):
    shape = (len(pieces) * pieces[0].shape[0],) + pieces[0].shape[1:]
    return pl.pallas_call(
        stack_kernel,
        in_specs=[ANYWHERE] * len(pieces),
        out_specs=ANYWHERE,
        out_shape=jax.ShapeDtypeStruct(shape, bf16),
        compiler_params=pltpu.CompilerParams(vmem_limit_bytes=60 * 2**20),
        cost_estimate=pl.CostEstimate(flops=0, bytes_accessed=4 * math.prod(shape), transcendentals=0),
        name="stack_pieces",
    )(*pieces)


def unpack_kernel(left, last, index_ref, *refs):
    pieces, (w_ref, *refs) = refs[:4], refs[4:]
    if last:
        scale_ref, first_ref, _, _, out_ref, qkv_ref, router_ref, mixing_ref, vec_ref, gain_ref, attn_ref, small = refs
    else:
        out_ref, qkv_ref, small = refs
    width = out_ref.shape[1]
    size = pieces[0].shape[1]
    lane = lax.broadcasted_iota(jnp.int32, (1, EXTRA), 1)
    step = pl.program_id(0)
    half = index_ref[0]
    base = (half * width // 2 if last else 0) + step * 4 * size
    for k in range(4):
        at_ctx = pl.multiple_of((k ^ index_ref[1]) * size, size)
        rows = pl.ds(at_ctx, size)
        total = pieces[k][0].astype(f32)
        out_ref[rows, :] = total[:, left : left + width]
        gain = None
        for p in range(3):
            for i in range(width // 128):
                at = i * 384 + p * 128 + (0 if i * 384 < left else width + EXTRA)
                value = total[:, at : at + 128]
                columns = slice(p * width + i * 128, p * width + (i + 1) * 128)
                qkv_ref[rows, columns] = value
                part = value * w_ref[rows, columns].astype(f32)
                gain = part if gain is None else gain + part
        gain = jnp.sum(gain, axis=1, keepdims=True)
        small[pl.ds(pl.multiple_of(base + at_ctx, size), size), :] = total[:, left + width : left + width + EXTRA] + place(gain, lane, EXTRA - 1)
    if last:

        @pl.when(step == 3)
        def _():
            small[pl.ds(pl.multiple_of((1 - half) * (width // 2), width // 2), width // 2), :] = first_ref[...]
            turned = small[...].T
            router_ref[...] = turned[0:ALL_EXPERTS]
            mixing_ref[0] = turned[16:18]
            mixing_ref[1] = turned[18:20]
            vec_ref[...] = turned[20:22]
            gain_ref[...] = turned[24]
            attn_ref[...] = (turned[EXTRA - 1 : EXTRA] / scale_ref[...])[0]


def unpack_half(index, pieces, w_qkv, left, scale, before):
    width = w_qkv.shape[0]
    size = width // 32
    last = before is not None
    row = lambda a, s: (s[0] * 4 + a, 0)
    source = pl.BlockSpec((1, size, pieces[0].shape[2]), lambda a, s: (a ^ s[2], 0, 0))
    whole = lambda shape: pl.BlockSpec(shape, lambda a, s: (0,) * len(shape))
    in_specs = [source] * 4 + [pl.BlockSpec((4 * size, 3 * width), row)]
    out_specs = [pl.BlockSpec((4 * size, width), row), pl.BlockSpec((4 * size, 3 * width), row)]
    out_shape = [jax.ShapeDtypeStruct((width, width), f32), jax.ShapeDtypeStruct((width, 3 * width), f32)]
    arrays = [*pieces, w_qkv]
    if last:
        shapes = ((ALL_EXPERTS, width), (2, 2, width), (2, width), (width,), (width,))
        in_specs += [whole((1, width)), whole((width // 2, EXTRA))] + [pl.BlockSpec(memory_space=pl.ANY)] * 2
        arrays += [scale, before[2], before[0], before[1]]
        scratch = [pltpu.VMEM((width, EXTRA), f32)]
        aliases = {len(arrays) - 1: 0, len(arrays): 1}
    else:
        shapes = ((width // 2, EXTRA),)
        scratch = []
        aliases = {}
    return pl.pallas_call(
        functools.partial(unpack_kernel, left, last),
        grid_spec=pltpu.PrefetchScalarGridSpec(
            num_scalar_prefetch=1,
            grid=(4,),
            in_specs=in_specs,
            out_specs=out_specs + [whole(s) for s in shapes],
            scratch_shapes=scratch,
        ),
        out_shape=out_shape + [jax.ShapeDtypeStruct(s, f32) for s in shapes],
        input_output_aliases=aliases,
        compiler_params=pltpu.CompilerParams(vmem_limit_bytes=60 * 2**20),
        cost_estimate=pl.CostEstimate(flops=0, bytes_accessed=14 * width * width, transcendentals=0),
        name="unpack_half",
    )(index, *arrays)

P = jax.sharding.PartitionSpec


def rms_inverse(tensor):
    return lax.rsqrt(jnp.mean(tensor * tensor, axis=-1, keepdims=True) + epsilon)


def after(values, *others):
    return lax.optimization_barrier((values, others))[0]


def body(inputs, prev_logits, routes, attn_gain, w_qkv, w_out, moe_gain, router, const_gate, const_vec, w_gate, w_up, w_down, out_grad):
    n_ctx, n_exp = lax.axis_size("ctx"), lax.axis_size("exp")
    me_c, me_e = lax.axis_index("ctx"), lax.axis_index("exp")
    tok, width = inputs.shape[1], inputs.shape[2]
    plen = tok - CONT_LEN
    split = n_exp // FFN_EXPERTS
    capacity = max(4, tok // 64 * 12)
    first = -(-capacity // 32) * 16
    groups = ((0, first), (first, capacity - first))
    home = (me_e // split).reshape(1)

    def deal(value):
        value = jnp.repeat(value, split, axis=0) if split > 1 else value
        return lax.all_to_all(value, "exp", 0, 0, tiled=True)

    def give_back(value):
        value = lax.all_to_all(value, "exp", 0, 0, tiled=True)
        return [value[r::split] if split > 1 else value for r in range(split)]

    x_low = inputs[0]
    upstream_low = out_grad[0]
    flags = jnp.where((me_c ^ jnp.arange(1, n_ctx)) < me_c, 0.0, NEG).astype(f32)

    prev = prev_logits[0]
    mix = jnp.concatenate([router, jnp.zeros((width, 4), bf16), const_gate[0], const_gate[1], jnp.zeros((width, EXTRA - 20), bf16)], axis=1)
    router_pad = jnp.pad(router, ((0, 0), (0, EXTRA - ALL_EXPERTS)))
    turned, chosen, early_sent, x_prompt = route_plan(home, routes[0].T, upstream_low, prev.T, x_low, plen, groups)
    far = [lax.ppermute(x_prompt, "ctx", xor_pairs(n_ctx, k)) for k in range(1, n_ctx)]

    tokens_in = x_low.astype(f32)
    inverse_attn = rms_inverse(tokens_in)
    act_low = (tokens_in * inverse_attn * attn_gain).astype(bf16)
    projected = dot_nn(act_low, w_qkv).astype(bf16)
    early = deal(early_sent)
    act_t = turn(act_low)
    act_far, kv_far = far_projection(after(far, projected, act_t), attn_gain[None], w_qkv)

    mixed_low, lse, hidden, moe_low, sent = attention_forward(flags, projected, kv_far, plen, x_low, w_out, moe_gain[None], turned)
    sent, hidden, early = lax.optimization_barrier((sent, hidden, early))

    local_out, d_normed_local, probs, d_probs, small_local = local_part(hidden, moe_low, upstream_low, prev, routes[0], mix, moe_gain[None], const_vec)
    far_t = turn(act_far)
    sent = [after(sent[0], local_out, d_normed_local, far_t), sent[1]]
    got = [deal(part.reshape(FFN_EXPERTS, -1, width)) for part in sent]

    got = [part.reshape(-1, width) for part in got]
    passes = [expert_pass(group, home, r, early, router_pad, w_gate, w_up, w_down) for group, r in zip(groups, got)]
    d_got = [give_back(p[1].reshape(n_exp, -1, width)) for p in passes]
    gate_up_low, down_low = weight_gradients(got, [p[2] for p in passes], [p[3] for p in passes], [p[4] for p in passes], [p[5] for p in passes])
    outs = jnp.concatenate([p[0].reshape(n_exp, -1, width + EXTRA) for p in passes], axis=1)
    d_got, gate_up_low, down_low, outs = lax.optimization_barrier((d_got, gate_up_low, down_low, outs))
    out_got = give_back(outs)

    d_got = [[part.reshape(-1, width) for part in group] for group in d_got]
    pairs = width // 128
    cut = pairs // 3
    core = (me_e & 1).reshape(1)
    smalls = [small_local] + [p[6] for p in passes]
    d_hidden, d_mixed, *buffers = combine(core, chosen, d_got, smalls, d_normed_local, hidden, moe_gain[None], upstream_low, mixed_low, w_out, cut * 384)

    sum_gate_up = lax.psum_scatter(gate_up_low, "ctx", scatter_dimension=1, tiled=True).astype(f32)
    sum_down = lax.psum_scatter(down_low, "ctx", scatter_dimension=0, tiled=True).astype(f32)

    def attention(upstream, begin, count, buffers, at, starts, last):
        return attention_backward(flags, core, projected, kv_far, mixed_low, upstream, lse, act_t, far_t, w_qkv, plen, begin, count, buffers, at, starts, last)

    dense = n_ctx == 4 and n_exp == 8
    left, right = cut * 384, (pairs - cut) * 384
    z = me_e >> 1
    at_ctx, at_z = me_c.reshape(1), z.reshape(1)
    along_ctx, along_z = ("ctx", 4, 1), ("exp", 8, 2)
    across = lambda value: lax.ppermute(value, "exp", xor_pairs(n_exp, 1))
    mine_1, theirs_1, grads_1, *starts = attention(d_mixed, 0, cut, buffers, 0, None, False)
    if dense:
        got_1 = across(theirs_1)
    mine_2, theirs_2, grads_2, *starts = attention(d_mixed, cut, 1, right, 0, starts, False)
    if dense:
        mine_2, theirs_2, starts, got_1 = lax.optimization_barrier((mine_2, theirs_2, starts, got_1))
        sums_1 = sum_pieces(at_z, [[quarters(mine_1), quarters(got_1)]])
        parts_1 = swap(sums_1, along_z)
        mine_2 = after(mine_2, sums_1[0])
    mine_2, theirs_2, grads_3, *d_far = attention(d_mixed, cut + 1, pairs - cut - 1, (mine_2, theirs_2), 1, starts, True)
    if dense:
        mine_2, theirs_2, grads_3, d_far, parts_1 = lax.optimization_barrier((mine_2, theirs_2, grads_3, d_far, parts_1))
    send_far = lambda k: lax.ppermute(d_far[k - 1], "ctx", xor_pairs(n_ctx, k))
    far_back = [send_far(k) for k in range(1, n_ctx - 1)]
    if dense:
        sums_2 = sum_pieces(at_z, [[quarters(mine_2), quarters(across(theirs_2))]])
        parts_2 = swap(sums_2, along_z)
        mixed_out, d_logits = finish(chosen, out_got, groups, after(local_out, sums_2[0]), probs, d_probs)
        mixed_out, d_logits, far_back, d_far = lax.optimization_barrier((mixed_out, d_logits, far_back, d_far))
        far_back = far_back + [send_far(n_ctx - 1)]
        mixed_out, parts_2 = lax.optimization_barrier((mixed_out, parts_2))
        parts_1, parts_2 = ([quarters(p) for p in parts] for parts in (parts_1, parts_2))
        parts = swap(sum_pieces(at_ctx, [parts_1, parts_2]), along_ctx)
        [piece] = sum_pieces(at_ctx, [parts])
        spread_z = spread(piece, along_z)
    else:
        mixed_out, d_logits = finish(chosen, out_got, groups, local_out, probs, d_probs)
        far_back = far_back + [send_far(n_ctx - 1)]
    d_inputs = input_gradient([grads_1, grads_2, grads_3], x_low, attn_gain[None], d_hidden, w_qkv, far_back)

    d_prev = d_logits[:ALL_EXPERTS].T[None]
    total_gate, total_up, total_down = sum_gate_up[0][None], sum_gate_up[1][None], sum_down[None]
    if dense:
        d_inputs, spread_z = lax.optimization_barrier((d_inputs, spread_z))
        column = stack_pieces(spread_z)
        own = after(spread(column, along_ctx), total_gate, total_up, total_down, d_prev)
        other = [across(piece) for piece in own]
        place_of = lambda half: jnp.stack([half, me_c, z])
        first = unpack_half(place_of(core[0]), own, w_qkv, left, None, None)
        first, other = lax.optimization_barrier((first, other))
        out_sum, qkv_sum, d_router, d_mixing, d_const_vec, d_moe_gain, d_attn_gain = unpack_half(place_of(1 - core[0]), other, w_qkv, left, attn_gain[None], first)
    else:
        whole = lambda mine, theirs: jnp.where(core == 0, jnp.concatenate([mine, theirs], axis=0), jnp.concatenate([theirs, mine], axis=0))
        total_1, total_2 = [v.astype(f32) for v in lax.psum((whole(mine_1, theirs_1), whole(mine_2, theirs_2)), ("ctx", "exp"))]
        columns = jnp.concatenate([total_1[:, :left], total_2], axis=1).reshape(width, pairs, 3, 128)
        qkv_sum = columns.transpose(0, 2, 1, 3).reshape(width, 3 * width)
        out_sum, small = total_1[:, left : left + width], total_1[:, left + width :].T
        d_attn_gain = (jnp.sum(qkv_sum * w_qkv.astype(f32), axis=1) / attn_gain)
        d_router, d_mixing, d_const_vec, d_moe_gain = small[:ALL_EXPERTS], small[16:20].reshape(2, 2, width), small[20:22], small[24]
    return (
        mixed_out[None],
        d_inputs[None],
        d_prev,
        d_attn_gain,
        qkv_sum,
        out_sum,
        d_moe_gain,
        d_router.T,
        d_mixing.transpose(0, 2, 1),
        d_const_vec,
        total_gate,
        total_up,
        total_down,
    )


def solution(mesh):
    rows = P("ctx", "exp", None)
    expert = P("exp", None, None)
    summed = P("exp", "ctx", None)
    return jax.shard_map(
        body,
        mesh=mesh,
        in_specs=(rows, rows, rows, P(), P(), P(), P(), P(), P(), P(), expert, expert, expert, rows),
        out_specs=(rows, rows, rows, P(), P(), P(), P(), P(), P(), P(), summed, summed, summed),
        check_vma=False,
    )
```

```python
import functools, math
import jax, jax.numpy as jnp
from jax import lax
from jax.experimental import pallas as pl
from jax.experimental.pallas import tpu as pltpu

HEADS = 12
HEAD_DIM = 64
CONT_LEN = 512
LOG2E = 1.4426950408889634
SCALE = HEAD_DIM ** -0.5
bf16 = jnp.bfloat16
f32 = jnp.float32
NEG = -1e30
epsilon = 1e-06


def dot_nt(a, b):
    return lax.dot_general(a, b, (((1,), (1,)), ((), ())), preferred_element_type=f32)


def dot_nn(a, b):
    return jnp.dot(a, b, preferred_element_type=f32)


def query_tiles(tok, plen):
    tiles = [(0, plen, True)]
    step = 256
    for start in range(plen, tok, step):
        tiles.append((start, step, False))
    return tiles


def split_high(value):
    high = value.astype(bf16)
    return high, (value - high.astype(f32)).astype(bf16)


def both_halves(value, head, low_half):
    turned = pltpu.roll(value, HEAD_DIM, 1)
    return jnp.where(low_half, value, turned) if head == 0 else jnp.where(low_half, turned, value)


def scaled_queries(value, head, low_half):
    high, rest = split_high(value.astype(f32) * (SCALE * LOG2E))
    rest = pltpu.roll(rest, HEAD_DIM, 1)
    return jnp.where(low_half, high, rest) if head == 0 else jnp.where(low_half, rest, high)


def attention_forward_kernel(plen, count, flags_ref, q_ref, k_ref, v_ref, kr_ref, vr_ref, gain_ref, x_any, w_any, *refs):
    turned_any, (o_ref, lse_ref, hidden_ref, low_ref), sent = refs[:count], refs[count : count + 4], refs[count + 4 : 2 * count + 4]
    kd, krd, vd, vrd, mixed, x_ref, w_ref, *select, sems = refs[2 * count + 4 :]
    step = pl.program_id(0)
    copies = [pltpu.make_async_copy(a, r, sems.at[i]) for i, (a, r) in enumerate(zip((x_any, w_any, *turned_any), (x_ref, w_ref, *select)))]

    @pl.when(step == 0)
    def _():
        for copy in copies:
            copy.start()

    tok = q_ref.shape[0]
    remote = kr_ref.shape[0]
    low_half = lax.broadcasted_iota(jnp.int32, (1, 128), 1) < HEAD_DIM
    one = jnp.ones((), bf16)
    for head in range(2):
        mine = low_half if head == 0 else ~low_half
        kd[head] = both_halves(k_ref[...], head, low_half)
        krd[head] = both_halves(kr_ref[...], head, low_half)
        vd[head] = jnp.where(mine, v_ref[...], one)
        vrd[head] = jnp.where(mine, vr_ref[...], one)
    for start, size, is_prompt in query_tiles(tok, plen):
        row = lax.broadcasted_iota(jnp.int32, (size, size), 0)
        col = lax.broadcasted_iota(jnp.int32, (size, size), 1)
        queries = q_ref[start : start + size, :]
        units = []
        for head in range(2):
            qh = scaled_queries(queries, head, low_half)
            pieces = []
            diag = dot_nt(qh, kd[head, start : start + size, :])
            pieces.append((jnp.where(col <= row, diag, NEG), vd, start, size))
            if is_prompt:
                for j in range(remote // plen):
                    s = dot_nt(qh, krd[head, j * plen : (j + 1) * plen, :])
                    pieces.append((s + flags_ref[j], vrd, j * plen, plen))
            else:
                s = dot_nt(qh, kd[head, 0:start, :])
                pieces.append((s, vd, 0, start))
                s = dot_nt(qh, krd[head])
                pieces.append((s, vrd, 0, remote))
            units.append(pieces)
        accs, peaks = [], []
        for head, pieces in enumerate(units):
            peak = None
            for s, _, _, _ in pieces:
                m = jnp.max(s, axis=1, keepdims=True)
                peak = m if peak is None else jnp.maximum(peak, m)
            acc = None
            for s, ref, at, n in pieces:
                p = jnp.exp2(s - peak).astype(bf16)
                part = dot_nn(p, ref[head, at : at + n, :])
                acc = part if acc is None else acc + part
            accs.append(acc)
            peaks.append(peak)
        num = jnp.where(low_half, accs[0], accs[1])
        den = pltpu.roll(jnp.where(low_half, accs[1], accs[0]), HEAD_DIM, 1)
        value = (num / den).astype(bf16)
        o_ref[start : start + size, :] = value
        mixed[step, start : start + size, :] = value
        turned = (jnp.where(low_half, peaks[0], peaks[1]) + jnp.log2(den)).T
        lse_ref[0, 0:8, start : start + size] = turned[0:8, :]
        lse_ref[0, 8:16, start : start + size] = turned[HEAD_DIM : HEAD_DIM + 8, :]


    @pl.when(step == pl.num_programs(0) - 1)
    def _():
        for copy in copies:
            copy.wait()
        joined = jnp.concatenate([mixed[i] for i in range(mixed.shape[0])], axis=1)
        hidden = x_ref[...].astype(f32) + dot_nn(joined, w_ref[...])
        inverse = lax.rsqrt(jnp.mean(hidden * hidden, axis=1, keepdims=True) + epsilon)
        low = (hidden * inverse * gain_ref[...]).astype(bf16)
        hidden_ref[...] = hidden
        low_ref[...] = low
        for rows_ref, s in zip(select, sent):
            s[...] = dot_nn(rows_ref[...], low).astype(bf16)


def attention_forward(flags, proj, kv_rem, plen, x, w_out, gain, turned):
    tok, width = proj.shape[0], proj.shape[1] // 3
    remote = kv_rem.shape[0]
    pairs = width // 128
    still = lambda shape: pl.BlockSpec(shape, lambda i: (0, 0))
    sent = [(r.shape[0], width) for r in turned]
    out = pl.pallas_call(
        functools.partial(attention_forward_kernel, plen, len(turned)),
        grid=(pairs,),
        in_specs=[
            pl.BlockSpec(memory_space=pltpu.SMEM),
            pl.BlockSpec((tok, 128), lambda i: (0, i)),
            pl.BlockSpec((tok, 128), lambda i: (0, pairs + i)),
            pl.BlockSpec((tok, 128), lambda i: (0, 2 * pairs + i)),
            pl.BlockSpec((remote, 128), lambda i: (0, i)),
            pl.BlockSpec((remote, 128), lambda i: (0, pairs + i)),
            still((1, width)),
        ]
        + [pl.BlockSpec(memory_space=pl.ANY)] * (2 + len(turned)),
        out_specs=[
            pl.BlockSpec((tok, 128), lambda i: (0, i)),
            pl.BlockSpec((1, 16, tok), lambda i: (i, 0, 0)),
            still((tok, width)),
            still((tok, width)),
        ]
        + [still(s) for s in sent],
        out_shape=[
            jax.ShapeDtypeStruct((tok, width), bf16),
            jax.ShapeDtypeStruct((pairs, 16, tok), f32),
            jax.ShapeDtypeStruct((tok, width), f32),
            jax.ShapeDtypeStruct((tok, width), bf16),
        ]
        + [jax.ShapeDtypeStruct(s, bf16) for s in sent],
        scratch_shapes=[pltpu.VMEM((2, n, 128), bf16) for n in (tok, remote, tok, remote)]
        + [pltpu.VMEM((pairs, tok, 128), bf16)]
        + [pltpu.VMEM(a.shape, bf16) for a in (x, w_out, *turned)]
        + [pltpu.SemaphoreType.DMA((2 + len(turned),))],
        compiler_params=pltpu.CompilerParams(vmem_limit_bytes=60 * 2**20),
        cost_estimate=pl.CostEstimate(flops=4 * tok * (tok + remote) * width + 4 * tok * width * width, bytes_accessed=2 * (tok * 10 + remote * 2) * width, transcendentals=tok * (tok + remote) * HEADS),
        name="attention_forward",
    )(flags, proj, proj, proj, kv_rem, kv_rem, gain, x, w_out, *turned)
    return out[0], out[1], out[2], out[3], out[4:]


def attention_backward_kernel(plen, started, last, skip, flags_ref, core_ref, q_ref, k_ref, v_ref, kr_ref, vr_ref, o_ref, do_ref, lse_ref, act_ref, far_ref, wk_ref, wv_ref, *refs):
    refs = refs[skip:]
    if started:
        start_far_ref, *refs = refs
    mine_ref, theirs_ref, own_grads, *refs = refs
    dfar_ref, *dfar_refs = (refs[-1:] + refs[:-10]) if last else refs[:1]
    kt, krt, dka, dva, dkra, dvra, weights, kd, krd = refs[-10:-1] if last else refs[-9:]
    tok = q_ref.shape[0]
    remote = kr_ref.shape[0]
    lane = lax.broadcasted_iota(jnp.int32, (1, 128), 1)
    low_half = lane < HEAD_DIM
    c = SCALE * LOG2E
    zero = jnp.zeros((), bf16)
    for head in range(2):
        kd[head] = both_halves(k_ref[...], head, low_half)
        krd[head] = both_halves(kr_ref[...], head, low_half)
    kt[...] = k_ref[...].T
    krt[...] = kr_ref[...].T
    dka[...] = jnp.zeros_like(dka)
    dva[...] = jnp.zeros_like(dva)
    dkra[...] = jnp.zeros_like(dkra)
    dvra[...] = jnp.zeros_like(dvra)
    pick = lax.broadcasted_iota(jnp.int32, (16, 128), 0) // 8 == lax.broadcasted_iota(jnp.int32, (16, 128), 1) // HEAD_DIM
    pick = jnp.where(pick, 1.0, 0.0).astype(bf16)
    for start, size, is_prompt in query_tiles(tok, plen):
        rows = slice(start, start + size)
        product = do_ref[rows, :].astype(f32) * o_ref[rows, :].astype(f32)
        high = product.astype(bf16)
        rest = (product - high.astype(f32)).astype(bf16)
        delta = dot_nt(pick, high) + dot_nt(pick, rest)
        totals = [None, None]
        masks = [low_half, ~low_half]
        qh = [jnp.where(m, q_ref[rows, :], zero) for m in masks]
        qs = [scaled_queries(q_ref[rows, :], head, low_half) for head in range(2)]
        doh = [jnp.where(m, do_ref[rows, :], zero) for m in masks]
        segments = [(kd, v_ref, kt, dka, dva, start, size, "diag")]
        if is_prompt:
            for j in range(remote // plen):
                segments.append((krd, vr_ref, krt, dkra, dvra, j * plen, plen, j))
        else:
            segments.append((kd, v_ref, kt, dka, dva, 0, start, None))
            segments.append((krd, vr_ref, krt, dkra, dvra, 0, remote, None))
        for kk, vv, tt, dk_acc, dv_acc, at, n, mode in segments:
            keys = slice(at, at + n)
            scores = [dot_nt(kk[head, keys, :], qs[head]) for head in range(2)]
            d_probs = [dot_nt(vv[keys, :], doh[head]) for head in range(2)]
            low_p, low_d = [], []
            for head in range(2):
                st = scores[head] - lse_ref[0, 8 * head : 8 * head + 1, rows]
                if mode == "diag":
                    key = lax.broadcasted_iota(jnp.int32, (n, size), 0)
                    query = lax.broadcasted_iota(jnp.int32, (n, size), 1)
                    st = jnp.where(key <= query, st, NEG)
                elif mode is not None:
                    st = st + flags_ref[mode]
                pt = jnp.exp2(st)
                low_p.append(pt.astype(bf16))
                low_d.append((pt * (d_probs[head] - delta[8 * head : 8 * head + 1, :])).astype(bf16))
            dv_acc[keys, :] += dot_nn(low_p[0], doh[0]) + dot_nn(low_p[1], doh[1])
            dk_acc[keys, :] += dot_nn(low_d[0], qh[0]) + dot_nn(low_d[1], qh[1])
            for head in range(2):
                part = dot_nn(tt[head * HEAD_DIM : (head + 1) * HEAD_DIM, keys], low_d[head])
                totals[head] = part if totals[head] is None else totals[head] + part
        dqt = totals
        own_grads[rows, 0:128] = (jnp.concatenate(dqt, axis=0).T * SCALE).astype(bf16)
    own_grads[:, 128:256] = (dka[...] * SCALE).astype(bf16)
    own_grads[:, 256:384] = dva[...].astype(bf16)
    far_grads = jnp.concatenate([(dkra[...] * SCALE).astype(bf16), dvra[...].astype(bf16)], axis=1)
    weights[:, 0:128] = wk_ref[...]
    weights[:, 128:256] = wv_ref[...]
    half = mine_ref.shape[0]
    for out_ref, which in ((theirs_ref, 1 - core_ref[0]), (mine_ref, core_ref[0])):
        rows = pl.ds(pl.multiple_of(which * half, half), half)
        total = dot_nn(act_ref[rows, :], own_grads[...])
        out_ref[:, 0:128] = total[:, 0:128].astype(bf16)
        out_ref[:, 128:384] = (total[:, 128:384] + dot_nn(far_ref[rows, :], far_grads)).astype(bf16)
    d_far = dot_nt(far_grads, weights[...])
    step = pl.program_id(0)

    @pl.when(step == 0)
    def _():
        dfar_ref[...] = d_far + start_far_ref[...] if started else d_far

    @pl.when(step > 0)
    def _():
        dfar_ref[...] += d_far

    if last:

        @pl.when(step == pl.num_programs(0) - 1)
        def _():
            for k, ref in enumerate(dfar_refs):
                ref[...] = dfar_ref[k * plen : (k + 1) * plen, :].astype(bf16)


def attention_backward(flags, core, proj, kv_rem, mixed, d_mixed, lse, act_t, far_t, w_qkv, plen, begin, count, buffers, at, starts, last):
    tok, width = mixed.shape
    remote = kv_rem.shape[0]
    pairs = width // 128
    own = lambda shift: pl.BlockSpec((tok, 128), lambda i: (0, shift + i))
    far = lambda shift: pl.BlockSpec((remote, 128), lambda i: (0, shift + i))
    weight = lambda shift: pl.BlockSpec((width, 128), lambda i: (0, shift + i))
    still = lambda shape: pl.BlockSpec(shape, lambda i: (0, 0))
    half = pl.BlockSpec((width // 2, 384), lambda i: (0, at + i))
    in_specs = [
        pl.BlockSpec(memory_space=pltpu.SMEM),
        pl.BlockSpec(memory_space=pltpu.SMEM),
        own(begin),
        own(pairs + begin),
        own(2 * pairs + begin),
        far(begin),
        far(pairs + begin),
        own(begin),
        own(begin),
        pl.BlockSpec((1, 16, tok), lambda i: (begin + i, 0, 0)),
        still((width, tok)),
        still((width, remote)),
        weight(pairs + begin),
        weight(2 * pairs + begin),
    ]
    arrays = [flags, core, proj, proj, proj, kv_rem, kv_rem, mixed, d_mixed, lse, act_t, far_t, w_qkv, w_qkv]
    scratch = [
        pltpu.VMEM((128, tok), bf16),
        pltpu.VMEM((128, remote), bf16),
        pltpu.VMEM((tok, 128), f32),
        pltpu.VMEM((tok, 128), f32),
        pltpu.VMEM((remote, 128), f32),
        pltpu.VMEM((remote, 128), f32),
        pltpu.VMEM((width, 256), bf16),
        pltpu.VMEM((2, tok, 128), bf16),
        pltpu.VMEM((2, remote, 128), bf16),
    ]
    aliases = {}
    skip = 0
    if not isinstance(buffers, int):
        aliases = {len(arrays): 0, len(arrays) + 1: 1}
        in_specs += [pl.BlockSpec(memory_space=pl.ANY)] * 2
        arrays += list(buffers)
        skip = 2
        buffers = buffers[0].shape[1]
    if starts:
        in_specs += [still((remote, width))]
        arrays += list(starts)
    out_specs = [half, half, pl.BlockSpec((tok, 384), lambda i: (0, i))]
    out_shape = [jax.ShapeDtypeStruct((width // 2, buffers), bf16)] * 2 + [jax.ShapeDtypeStruct((tok, count * 384), bf16)]
    if last:
        out_specs += [still((plen, width))] * (remote // plen)
        out_shape += [jax.ShapeDtypeStruct((plen, width), bf16)] * (remote // plen)
        scratch = scratch + [pltpu.VMEM((remote, width), f32)]
    else:
        out_specs += [still((remote, width))]
        out_shape += [jax.ShapeDtypeStruct((remote, width), f32)]
    return pl.pallas_call(
        functools.partial(attention_backward_kernel, plen, bool(starts), last, skip),
        grid=(count,),
        in_specs=in_specs,
        out_specs=out_specs,
        out_shape=out_shape,
        scratch_shapes=scratch,
        input_output_aliases=aliases,
        compiler_params=pltpu.CompilerParams(vmem_limit_bytes=60 * 2**20),
        cost_estimate=pl.CostEstimate(flops=10 * tok * (tok + remote) * count * 128 + 20 * tok * width * count * 128, bytes_accessed=2 * (tok * 8 + remote * 4) * count * 128 + 16 * tok * width, transcendentals=tok * (tok + remote) * 2 * count),
        name="attention_backward",
    )(*arrays)


FFN_EXPERTS = 8
ALL_EXPERTS = 12
EXTRA = 128
SMALL = 8


def dot_tn(a, b):
    return lax.dot_general(a, b, (((0,), (0,)), ((), ())), preferred_element_type=f32)


def split_low(value, parts):
    pieces = []
    for _ in range(parts):
        piece = value.astype(bf16)
        pieces.append(piece)
        value = value - piece.astype(f32)
    return pieces


def route_kernel(groups, home_ref, ids_ref, grad_ref, prev_ref, x_ref, *out_refs):
    tok, width = grad_ref.shape
    count = len(groups)
    turned_refs, chosen_refs, (early_ref, prompt_ref) = out_refs[:count], out_refs[count : 2 * count], out_refs[2 * count :]
    prompt_ref[...] = x_ref[0 : prompt_ref.shape[0], :]
    capacity = early_ref.shape[1] - SMALL
    expert = lax.broadcasted_iota(jnp.int32, (16, tok), 0)
    ids = [ids_ref[k : k + 1, :] for k in range(2)]
    names = [row == expert for row in ids]
    both = jnp.where(names[0] | names[1], 1.0, 0.0).astype(bf16)
    earlier = lax.broadcasted_iota(jnp.int32, (tok, tok), 0) < lax.broadcasted_iota(jnp.int32, (tok, tok), 1)
    before = dot_nn(both, jnp.where(earlier, 1.0, 0.0).astype(bf16))
    pieces = [piece.astype(f32) for piece in split_low(prev_ref[:, 0, :], 3)]
    extra = jnp.concatenate(pieces + [jnp.zeros((EXTRA - 3 * ALL_EXPERTS, tok), f32)], axis=0).T.astype(bf16)
    slot = [jnp.sum(jnp.where(n, before, 0.0), axis=0, keepdims=True).astype(jnp.int32) for n in names]
    extras = []
    for (first, size), turned_ref, chosen_ref in zip(groups, turned_refs, chosen_refs):
        spots = lax.broadcasted_iota(jnp.int32, (FFN_EXPERTS * size, tok), 0)
        hit = None
        for k in range(2):
            inside = (ids[k] < FFN_EXPERTS) & (slot[k] >= first) & (slot[k] < first + size)
            place = jnp.where(inside, ids[k] * size + slot[k] - first, -1)
            hit = spots == place if hit is None else hit | (spots == place)
        turned = jnp.where(hit, 1.0, 0.0).astype(bf16)
        turned_ref[...] = turned
        chosen_ref[...] = turned.T
        grads = dot_nn(turned, grad_ref[...]).astype(bf16)
        extras.append(dot_nn(turned, extra))
        for e in range(FFN_EXPERTS):
            early_ref[e, first : first + size, :] = grads[e * size : (e + 1) * size]
    third = capacity // 3
    for e in range(FFN_EXPERTS):
        rows = jnp.concatenate([x[e * size : (e + 1) * size] for x, (_, size) in zip(extras, groups)], axis=0)
        rows = rows[0:third] + pltpu.roll(rows[third : 2 * third], 40, 1) + pltpu.roll(rows[2 * third : capacity], 80, 1)
        early_ref[e, capacity : capacity + SMALL, :] = jnp.zeros((SMALL, width), bf16)
        for g in range(third // SMALL):
            early_ref[e, capacity : capacity + SMALL, g * EXTRA : (g + 1) * EXTRA] = rows[g * SMALL : (g + 1) * SMALL].astype(bf16)


def route_plan(home, ids, grad, prev, x, plen, groups):
    tok, width = grad.shape
    counts = [FFN_EXPERTS * size for _, size in groups]
    whole = pl.BlockSpec(memory_space=pltpu.VMEM)
    early = (FFN_EXPERTS, sum(counts) // FFN_EXPERTS + SMALL, width)
    out = pl.pallas_call(
        functools.partial(route_kernel, groups),
        in_specs=[pl.BlockSpec(memory_space=pltpu.SMEM), whole, whole, whole, whole],
        out_specs=[whole] * (2 * len(groups) + 2),
        out_shape=[jax.ShapeDtypeStruct((n, tok), bf16) for n in counts]
        + [jax.ShapeDtypeStruct((tok, n), bf16) for n in counts]
        + [jax.ShapeDtypeStruct(early, bf16), jax.ShapeDtypeStruct((plen, width), bf16)],
        compiler_params=pltpu.CompilerParams(vmem_limit_bytes=60 * 2**20),
        cost_estimate=pl.CostEstimate(flops=2 * sum(counts) * tok * (width + EXTRA), bytes_accessed=4 * sum(counts) * width, transcendentals=0),
        name="route_plan",
    )(home, ids, grad, prev, x)
    return out[: len(groups)], out[len(groups) : -2], out[-2], out[-1]


def router_inputs(early_ref, slots):
    capacity = early_ref.shape[1] - SMALL
    groups = capacity // 3 // SMALL
    rows = []
    for sender in range(early_ref.shape[0]):
        packed = early_ref[sender, capacity : capacity + SMALL, :].astype(f32)
        third = jnp.concatenate([packed[:, g * EXTRA : (g + 1) * EXTRA] for g in range(groups)], axis=0)
        every = jnp.concatenate([third, pltpu.roll(third, EXTRA - 40, 1), pltpu.roll(third, EXTRA - 80, 1)], axis=0)
        rows.append(every[slots])
    rows = jnp.concatenate(rows, axis=0)
    return rows + pltpu.roll(rows, EXTRA - ALL_EXPERTS, 1) + pltpu.roll(rows, EXTRA - 2 * ALL_EXPERTS, 1)


def expert_kernel(group, home_ref, rows_ref, early_ref, router_ref, wg_ref, wu_ref, wd_ref,
                  out_ref, drow_ref, dout_ref, inner_ref, dgate_ref, dup_ref, small_ref, acc_out, acc_row, probs_ref):
    width = rows_ref.shape[1]
    step, steps = pl.program_id(0), pl.num_programs(0)
    home = home_ref[0]
    lane = lax.broadcasted_iota(jnp.int32, (1, EXTRA), 1)
    slots = slice(group[0], group[0] + group[1])

    @pl.when(step == 0)
    def _():
        logits = router_inputs(early_ref, slots) + dot_nn(rows_ref[...], router_ref[...])
        logits = jnp.where(lane < ALL_EXPERTS, logits, NEG)
        unnormed = jnp.exp(logits - jnp.max(logits, axis=1, keepdims=True))
        probs = unnormed / jnp.sum(unnormed, axis=1, keepdims=True)
        probs_ref[...] = probs
        gate = jnp.sum(jnp.where(lane == home, probs, 0.0), axis=1, keepdims=True)
        dout_ref[...] = (gate * early_ref[:, slots, 0:width].astype(f32).reshape(-1, width)).astype(bf16)
        acc_out[...] = jnp.zeros_like(acc_out)
        acc_row[...] = jnp.zeros_like(acc_row)

    rows = rows_ref[...]
    gate_pre = dot_nn(rows, wg_ref[0])
    up_pre = dot_nn(rows, wu_ref[0])
    d_inner = dot_nt(dout_ref[...], wd_ref[0])
    sigmoid = jax.nn.sigmoid(gate_pre)
    silu = gate_pre * sigmoid
    inner = (silu * up_pre).astype(bf16)
    d_gate = (d_inner * up_pre * (sigmoid * (1.0 + gate_pre * (1.0 - sigmoid)))).astype(bf16)
    d_up = (d_inner * silu).astype(bf16)
    inner_ref[...] = inner
    dgate_ref[...] = d_gate
    dup_ref[...] = d_up
    acc_out[...] += dot_nn(inner, wd_ref[0])
    acc_row[...] += dot_nt(d_gate, wg_ref[0]) + dot_nt(d_up, wu_ref[0])

    @pl.when(step == steps - 1)
    def _():
        probs = probs_ref[...]
        gate = jnp.sum(jnp.where(lane == home, probs, 0.0), axis=1, keepdims=True)
        out = acc_out[...].astype(bf16).astype(f32)
        d_row_gate = jnp.sum(out * early_ref[:, slots, 0:width].astype(f32).reshape(-1, width), axis=1, keepdims=True)
        out_ref[:, 0:width] = (gate * out).astype(bf16)
        extra = jnp.zeros((out.shape[0], EXTRA), f32)
        for i, piece in enumerate(split_low(d_row_gate, 3)):
            extra = jnp.where(lane == home + 16 * i, piece.astype(f32), extra)
        out_ref[:, width : width + EXTRA] = extra.astype(bf16)
        term = d_row_gate * gate * (jnp.where(lane == home, 1.0, 0.0) - probs)
        high, rest = split_low(term, 2)
        turned = [piece.T for piece in (high, rest)]
        small_ref[...] = (dot_nn(turned[0], rows) + dot_nn(turned[1], rows))[0 : 2 * SMALL, :]
        drow_ref[...] = (acc_row[...] + dot_nt(high, router_ref[...]) + dot_nt(rest, router_ref[...])).astype(bf16)


def expert_pass(group, home, rows, early, router_pad, w_gate, w_up, w_down):
    count, width = rows.shape
    ff = w_gate.shape[2]
    tile = min(512, ff)
    full = pl.BlockSpec((count, width), lambda j: (0, 0))
    wide = pl.BlockSpec((count, width + EXTRA), lambda j: (0, 0))
    tall = pl.BlockSpec((1, width, tile), lambda j: (0, 0, j))
    piece = pl.BlockSpec((count, tile), lambda j: (0, j))
    return pl.pallas_call(
        functools.partial(expert_kernel, group),
        grid=(ff // tile,),
        in_specs=[
            pl.BlockSpec(memory_space=pltpu.SMEM),
            full,
            pl.BlockSpec(early.shape, lambda j: (0, 0, 0)),
            pl.BlockSpec((width, EXTRA), lambda j: (0, 0)),
            tall,
            tall,
            pl.BlockSpec((1, tile, width), lambda j: (0, j, 0)),
        ],
        out_specs=[wide, full, full, piece, piece, piece, pl.BlockSpec((2 * SMALL, width), lambda j: (0, 0))],
        out_shape=[
            jax.ShapeDtypeStruct((count, width + EXTRA), bf16),
            jax.ShapeDtypeStruct((count, width), bf16),
            jax.ShapeDtypeStruct((count, width), bf16),
        ]
        + [jax.ShapeDtypeStruct((count, ff), bf16)] * 3
        + [jax.ShapeDtypeStruct((2 * SMALL, width), f32)],
        scratch_shapes=[pltpu.VMEM((count, width), f32), pltpu.VMEM((count, width), f32), pltpu.VMEM((count, EXTRA), f32)],
        compiler_params=pltpu.CompilerParams(vmem_limit_bytes=60 * 2**20),
        cost_estimate=pl.CostEstimate(flops=12 * count * width * ff, bytes_accessed=6 * width * ff + 2 * count * (5 * width + 3 * ff), transcendentals=count * ff),
        name="expert_pass",
    )(home, rows, early, router_pad, w_gate, w_up, w_down)


def weight_kernel(count, *refs):
    rows, douts, inners, dgates, dups = (refs[i * count : (i + 1) * count] for i in range(5))
    gate_up_ref, down_ref = refs[5 * count : 5 * count + 2]
    turned = refs[5 * count + 2 :]

    @pl.when(pl.program_id(0) == 0)
    def _():
        for ref, scratch in zip(rows, turned):
            scratch[...] = ref[...].T

    gate_up_ref[0] = sum(dot_nn(t[...], d[...]) for t, d in zip(turned, dgates)).astype(bf16)
    gate_up_ref[1] = sum(dot_nn(t[...], d[...]) for t, d in zip(turned, dups)).astype(bf16)
    down_ref[...] = sum(dot_nn(i[...].T, d[...]) for i, d in zip(inners, douts)).astype(bf16)


def weight_gradients(rows, douts, inners, dgates, dups):
    count = len(rows)
    width, ff = rows[0].shape[1], inners[0].shape[1]
    tile = min(512, ff)
    total = sum(r.shape[0] for r in rows)
    full = [pl.BlockSpec(r.shape, lambda j: (0, 0)) for r in rows]
    piece = [pl.BlockSpec((r.shape[0], tile), lambda j: (0, j)) for r in rows]
    return pl.pallas_call(
        functools.partial(weight_kernel, count),
        grid=(ff // tile,),
        in_specs=full + full + piece * 3,
        out_specs=[pl.BlockSpec((2, width, tile), lambda j: (0, 0, j)), pl.BlockSpec((tile, width), lambda j: (j, 0))],
        out_shape=[jax.ShapeDtypeStruct((2, width, ff), bf16), jax.ShapeDtypeStruct((ff, width), bf16)],
        scratch_shapes=[pltpu.VMEM((width, r.shape[0]), bf16) for r in rows],
        compiler_params=pltpu.CompilerParams(vmem_limit_bytes=60 * 2**20),
        cost_estimate=pl.CostEstimate(flops=6 * total * width * ff, bytes_accessed=6 * width * ff + 2 * total * (2 * width + 3 * ff), transcendentals=0),
        name="weight_gradients",
    )(*rows, *douts, *inners, *dgates, *dups)


ANYWHERE = pl.BlockSpec(memory_space=pltpu.VMEM)
SCALARS = pl.BlockSpec(memory_space=pltpu.SMEM)


def inverse_rms(value):
    return lax.rsqrt(jnp.mean(value * value, axis=1, keepdims=True) + epsilon)


def turn_kernel(in_ref, out_ref):
    out_ref[...] = in_ref[...].T


def turn(value):
    rows, columns = value.shape
    block = 256 if rows % 256 == 0 else 128
    return pl.pallas_call(
        turn_kernel,
        grid=(rows // block,),
        in_specs=[pl.BlockSpec((block, columns), lambda i: (i, 0))],
        out_specs=pl.BlockSpec((columns, block), lambda i: (0, i)),
        out_shape=jax.ShapeDtypeStruct((columns, rows), value.dtype),
        compiler_params=pltpu.CompilerParams(vmem_limit_bytes=60 * 2**20),
        cost_estimate=pl.CostEstimate(flops=0, bytes_accessed=4 * rows * columns, transcendentals=0),
        name="turn",
    )(value)


def place(value, lane, at):
    return jnp.where(lane == at, value, 0.0)


def local_kernel(hidden_ref, low_ref, grad_ref, prev_ref, ids_ref, mix_ref, gain_ref, vec_ref, out_ref, dnormed_ref, probs_ref, dprobs_ref, small_ref):
    lane = lax.broadcasted_iota(jnp.int32, (1, EXTRA), 1)
    hidden = hidden_ref[...]
    normed = hidden * inverse_rms(hidden) * gain_ref[...]
    low = low_ref[...]
    grad = grad_ref[...].astype(f32)
    raw = dot_nn(low, mix_ref[...])
    block = raw.shape[0]
    prev = jnp.concatenate([prev_ref[:, 0, :], jnp.zeros((EXTRA - ALL_EXPERTS, block), f32)], axis=0).T
    logits = jnp.where(lane < ALL_EXPERTS, raw + prev, NEG)
    unnormed = jnp.exp(logits - jnp.max(logits, axis=1, keepdims=True))
    probs = unnormed / jnp.sum(unnormed, axis=1, keepdims=True)
    ids = jnp.concatenate([ids_ref[...].astype(f32), jnp.zeros((SMALL - 2, block), f32)], axis=0).T
    named = (ids[:, 0:1] == lane.astype(f32)) | (ids[:, 1:2] == lane.astype(f32))
    gates = jnp.where(named, probs, 0.0)
    copy_gate = gates[:, FFN_EXPERTS + 1 : FFN_EXPERTS + 2]
    dots = jnp.sum(grad * normed, axis=1, keepdims=True)
    out = hidden
    weight = copy_gate
    d_probs = place(dots, lane, FFN_EXPERTS + 1)
    logit_grads = jnp.zeros_like(probs)
    vec_terms = jnp.zeros_like(probs)
    for c in range(2):
        vec = vec_ref[c : c + 1, :]
        gate = gates[:, FFN_EXPERTS + 2 + c : FFN_EXPERTS + 3 + c]
        at = 16 + 2 * c
        a0 = jax.nn.sigmoid(raw[:, at : at + 1] - raw[:, at + 1 : at + 2])
        a1 = jax.nn.sigmoid(raw[:, at + 1 : at + 2] - raw[:, at : at + 1])
        vec_dots = jnp.sum(grad * vec, axis=1, keepdims=True)
        weight = weight + gate * a0
        out = out + (gate * a1) * vec
        d_probs = d_probs + place(a0 * dots + a1 * vec_dots, lane, FFN_EXPERTS + 2 + c)
        d0, d1 = gate * dots, gate * vec_dots
        mean = a0 * d0 + a1 * d1
        d0, d1 = a0 * (d0 - mean), a1 * (d1 - mean)
        logit_grads = logit_grads + place(d0, lane, at) + place(d1, lane, at + 1)
        vec_terms = vec_terms + place(gate * a1, lane, 20 + c)
    d_probs = jnp.where(named, d_probs, 0.0)
    logit_grads = logit_grads + probs * (d_probs - jnp.sum(probs * d_probs, axis=1, keepdims=True))
    high, rest = split_low(logit_grads, 2)
    out_ref[...] = out + weight * normed
    dnormed_ref[...] = weight * grad + dot_nt(high, mix_ref[...]) + dot_nt(rest, mix_ref[...])
    probs_ref[...] = probs
    dprobs_ref[...] = d_probs
    sums = None
    for terms, rows in ((logit_grads, low), (vec_terms, grad_ref[...])):
        for piece in split_low(terms.T, 2):
            part = dot_nn(piece, rows)
            sums = part if sums is None else sums + part
    sums = sums[0 : 3 * SMALL, :]

    @pl.when(pl.program_id(0) == 0)
    def _():
        small_ref[...] = sums

    @pl.when(pl.program_id(0) > 0)
    def _():
        small_ref[...] += sums


def local_part(hidden, low, grad, prev, ids, mix, gain, vec):
    tok, width = hidden.shape
    block, tiles = row_tiles(tok)
    shapes = [(tok, width), (tok, width), (tok, EXTRA), (tok, EXTRA), (3 * SMALL, width)]
    return pl.pallas_call(
        local_kernel,
        grid=(tok // block,),
        in_specs=[tiles(width), tiles(width), tiles(width), pl.BlockSpec((ALL_EXPERTS, 1, block), lambda i: (0, 0, i)), pl.BlockSpec((2, block), lambda i: (0, i)), fixed(mix), fixed(gain), fixed(vec)],
        out_specs=[tiles(width), tiles(width), tiles(EXTRA), tiles(EXTRA), pl.BlockSpec((3 * SMALL, width), lambda i: (0, 0))],
        out_shape=[jax.ShapeDtypeStruct(s, f32) for s in shapes],
        compiler_params=pltpu.CompilerParams(vmem_limit_bytes=60 * 2**20),
        cost_estimate=pl.CostEstimate(flops=14 * tok * width * EXTRA, bytes_accessed=16 * tok * width, transcendentals=tok * EXTRA),
        name="local_part",
    )(hidden, low, grad, prev, ids, mix, gain, vec)


def row_tiles(tok):
    block = 256 if tok % 256 == 0 else 128
    return block, lambda columns: pl.BlockSpec((block, columns), lambda i: (i, 0))


def fixed(value):
    return pl.BlockSpec(value.shape, lambda i: (0,) * value.ndim)


def combine_kernel(count, parts, core_ref, *refs):
    chosen, got, refs = refs[:count], refs[count : count * (1 + parts)], refs[count * (1 + parts) :]
    smalls, refs = refs[: count + 1], refs[count + 1 :]
    local_ref, hidden_ref, gain_ref, grad_ref, mixed_ref, w_ref, dhidden_ref, dmixed_ref, mine_ref, theirs_ref, total_w, total_gain, small_t = refs
    step = pl.program_id(0)

    @pl.when(step == 0)
    def _():
        total_w[...] = jnp.zeros_like(total_w)
        total_gain[...] = jnp.zeros_like(total_gain)

    d_normed = local_ref[...]
    for g in range(count):
        for r in range(parts):
            d_normed = d_normed + dot_nn(chosen[g][...], got[g * parts + r][...])
    hidden = hidden_ref[...]
    inverse = inverse_rms(hidden)
    scaled = d_normed * gain_ref[...]
    mean = jnp.mean(scaled * hidden, axis=1, keepdims=True)
    d_hidden = grad_ref[...].astype(f32) + inverse * scaled - hidden * (inverse * inverse * inverse * mean)
    low = d_hidden.astype(bf16)
    dhidden_ref[...] = d_hidden
    dmixed_ref[...] = dot_nt(low, w_ref[...]).astype(bf16)
    total_w[...] += dot_nn(mixed_ref[...].T, low)
    total_gain[...] += jnp.sum(d_normed * hidden * inverse, axis=0, keepdims=True)

    @pl.when(step == pl.num_programs(0) - 1)
    def _():
        width = w_ref.shape[0]
        half = width // 2
        row = lax.broadcasted_iota(jnp.int32, (SMALL, 1), 0)
        top = smalls[0][0 : 2 * SMALL, :]
        for small in smalls[1:]:
            top = top + small[...]
        rest = jnp.zeros((EXTRA - 4 * SMALL, width), f32)
        rows = [top, smalls[0][2 * SMALL : 3 * SMALL, :], jnp.where(row == 0, total_gain[...], 0.0), rest]
        small_t[...] = jnp.concatenate(rows, axis=0).T
        at = mine_ref.shape[1] - width - EXTRA
        for out_ref, which in ((theirs_ref, 1 - core_ref[0]), (mine_ref, core_ref[0])):
            place_rows = pl.ds(pl.multiple_of(which * half, half), half)
            out_ref[:, at : at + width] = total_w[place_rows, :].astype(bf16)
            out_ref[:, at + width : at + width + EXTRA] = small_t[place_rows, :].astype(bf16)


def combine(core, chosen, got, smalls, local, hidden, gain, grad, mixed, w_out, columns):
    tok, width = hidden.shape
    rows = sum(c.shape[1] for c in chosen)
    arrays = [a for group in got for a in group]
    block, tiles = row_tiles(tok)
    half = (width // 2, columns + width + EXTRA)
    return pl.pallas_call(
        functools.partial(combine_kernel, len(chosen), len(got[0])),
        grid=(tok // block,),
        in_specs=[SCALARS] + [tiles(c.shape[1]) for c in chosen] + [fixed(a) for a in arrays + smalls]
        + [tiles(width), tiles(width), fixed(gain), tiles(width), tiles(width), fixed(w_out)],
        out_specs=[tiles(width)] * 2 + [pl.BlockSpec(half, lambda i: (0, 0))] * 2,
        out_shape=[jax.ShapeDtypeStruct((tok, width), f32), jax.ShapeDtypeStruct((tok, width), bf16)] + [jax.ShapeDtypeStruct(half, bf16)] * 2,
        scratch_shapes=[pltpu.VMEM((width, width), f32), pltpu.VMEM((1, width), f32), pltpu.VMEM((width, EXTRA), f32)],
        compiler_params=pltpu.CompilerParams(vmem_limit_bytes=60 * 2**20),
        cost_estimate=pl.CostEstimate(flops=2 * tok * width * (rows + 2 * width), bytes_accessed=2 * width * (10 * tok + 2 * rows), transcendentals=0),
        name="combine_gradients",
    )(core, *chosen, *arrays, *smalls, local, hidden, gain, grad, mixed, w_out)


def flat_rows(value):
    if value.shape[1] % 16:
        return value.astype(f32).reshape(-1, value.shape[2]).astype(bf16)
    return value.reshape(-1, value.shape[2])


def finish_kernel(groups, parts, *refs):
    chosen, got = refs[: len(groups)], refs[len(groups) : len(groups) + parts]
    local_ref, probs_ref, dprobs_ref, out_ref, dlogits_ref = refs[len(groups) + parts :]
    width = local_ref.shape[1]
    lane = lax.broadcasted_iota(jnp.int32, (1, EXTRA), 1)
    picked = None
    for c, (at, size) in zip(chosen, groups):
        for r in range(parts):
            part = dot_nn(c[...], flat_rows(got[r][:, at : at + size, :]))
            picked = part if picked is None else picked + part
    out_ref[...] = (local_ref[...] + picked[:, 0:width]).astype(bf16)
    extra = picked[:, width : width + EXTRA]
    extra = extra + pltpu.roll(extra, EXTRA - 16, 1) + pltpu.roll(extra, EXTRA - 32, 1)
    d_probs = dprobs_ref[...] + jnp.where(lane < ALL_EXPERTS, extra, 0.0)
    probs = probs_ref[...]
    d_logits = probs * (d_probs - jnp.sum(probs * d_probs, axis=1, keepdims=True))
    dlogits_ref[...] = d_logits.T


def finish(chosen, got, groups, local, probs, d_probs):
    tok, width = local.shape
    block, tiles = row_tiles(tok)
    return pl.pallas_call(
        functools.partial(finish_kernel, groups, len(got)),
        grid=(tok // block,),
        in_specs=[tiles(c.shape[1]) for c in chosen] + [fixed(g) for g in got] + [tiles(width), tiles(EXTRA), tiles(EXTRA)],
        out_specs=[tiles(width), pl.BlockSpec((EXTRA, block), lambda i: (0, i))],
        out_shape=[jax.ShapeDtypeStruct((tok, width), bf16), jax.ShapeDtypeStruct((EXTRA, tok), f32)],
        compiler_params=pltpu.CompilerParams(vmem_limit_bytes=60 * 2**20),
        cost_estimate=pl.CostEstimate(flops=2 * tok * 1152 * (width + EXTRA), bytes_accessed=16 * tok * width, transcendentals=0),
        name="finish_outputs",
    )(*chosen, *got, local, probs, d_probs)


def input_kernel(count, x_ref, gain_ref, dhidden_ref, w_ref, *refs):
    grads, far, (out_ref, weights) = refs[:count], refs[count:-2], refs[-2:]
    width = x_ref.shape[1]

    @pl.when(pl.program_id(0) == 0)
    def _():
        for i in range(width // 128):
            for p in range(3):
                weights[:, i * 384 + p * 128 : i * 384 + (p + 1) * 128] = w_ref[:, p * width + i * 128 : p * width + (i + 1) * 128]

    total = None
    for ref in far:
        total = ref[...].astype(f32) if total is None else total + ref[...].astype(f32)
    d_act = jnp.where(pl.program_id(0) == 0, total, 0.0)
    at = 0
    for ref in grads:
        columns = ref.shape[1]
        d_act = d_act + dot_nt(ref[...], weights[:, at : at + columns])
        at += columns
    x = x_ref[...].astype(f32)
    inverse = inverse_rms(x)
    scaled = d_act * gain_ref[...]
    mean = jnp.mean(scaled * x, axis=1, keepdims=True)
    out_ref[...] = dhidden_ref[...] + inverse * scaled - x * (inverse * inverse * inverse * mean)


def input_gradient(grads, x, gain, d_hidden, w_qkv, far):
    tok, width = x.shape
    block = far[0].shape[0]
    tiles = lambda columns: pl.BlockSpec((block, columns), lambda i: (i, 0))
    return pl.pallas_call(
        functools.partial(input_kernel, len(grads)),
        grid=(tok // block,),
        in_specs=[tiles(width), fixed(gain), tiles(width), fixed(w_qkv)] + [tiles(g.shape[1]) for g in grads] + [fixed(f) for f in far],
        out_specs=tiles(width),
        out_shape=jax.ShapeDtypeStruct((tok, width), f32),
        scratch_shapes=[pltpu.VMEM((width, 3 * width), bf16)],
        compiler_params=pltpu.CompilerParams(vmem_limit_bytes=60 * 2**20),
        cost_estimate=pl.CostEstimate(flops=6 * tok * width * width, bytes_accessed=22 * tok * width, transcendentals=0),
        name="input_gradient",
    )(x, gain, d_hidden, w_qkv, *grads, *far)


def far_kernel(count, gain_ref, wk_ref, wv_ref, *refs):
    far, (act_ref, kv_ref) = refs[:count], refs[count:]
    width = wk_ref.shape[0]
    for k, ref in enumerate(far):

        @pl.when(pl.program_id(0) == k)
        def _():
            x = ref[...].astype(f32)
            act = (x * inverse_rms(x) * gain_ref[...]).astype(bf16)
            act_ref[...] = act
            kv_ref[:, 0:width] = dot_nn(act, wk_ref[...]).astype(bf16)
            kv_ref[:, width : 2 * width] = dot_nn(act, wv_ref[...]).astype(bf16)


def far_projection(far, gain, w_qkv):
    rows, width = far[0].shape
    count = len(far)
    return pl.pallas_call(
        functools.partial(far_kernel, count),
        grid=(count,),
        in_specs=[fixed(gain), pl.BlockSpec((width, width), lambda i: (0, 1)), pl.BlockSpec((width, width), lambda i: (0, 2))] + [fixed(f) for f in far],
        out_specs=[pl.BlockSpec((rows, width), lambda i: (i, 0)), pl.BlockSpec((rows, 2 * width), lambda i: (i, 0))],
        out_shape=[jax.ShapeDtypeStruct((count * rows, width), bf16), jax.ShapeDtypeStruct((count * rows, 2 * width), bf16)],
        compiler_params=pltpu.CompilerParams(vmem_limit_bytes=60 * 2**20),
        cost_estimate=pl.CostEstimate(flops=4 * count * rows * width * width, bytes_accessed=2 * width * (4 * count * rows + 2 * width), transcendentals=0),
        name="far_projection",
    )(gain, w_qkv, w_qkv, *far)


def xor_pairs(size, mask):
    return [(i, i ^ mask) for i in range(size)]


def sum_kernel(terms, index_ref, *refs):
    count = len(refs) // (sum(terms) + 1)
    outs = refs[-count:]
    for k, out_ref in enumerate(outs):
        at = 0
        first = 0
        for number in terms:
            total = None
            for t in range(first, first + number):
                value = refs[t * count + k][0].astype(f32)
                total = value if total is None else total + value
            out_ref[0, :, at : at + total.shape[1]] = total.astype(bf16)
            at += total.shape[1]
            first += number


def sum_pieces(index, groups):
    arrays = [a for group in groups for a in group]
    n, rows = arrays[0].shape[:2]
    columns = sum(group[0].shape[2] for group in groups)
    view = lambda a, k: pl.BlockSpec((1, rows, a.shape[2]), lambda i, s: (s[0] ^ k if n > 1 else 0, 0, 0))
    return pl.pallas_call(
        functools.partial(sum_kernel, [len(g) for g in groups]),
        grid_spec=pltpu.PrefetchScalarGridSpec(
            num_scalar_prefetch=1,
            grid=(1,),
            in_specs=[view(a, k) for a in arrays for k in range(n)],
            out_specs=[pl.BlockSpec((1, rows, columns), lambda i, s: (0, 0, 0))] * n,
        ),
        out_shape=[jax.ShapeDtypeStruct((1, rows, columns), bf16)] * n,
        compiler_params=pltpu.CompilerParams(vmem_limit_bytes=60 * 2**20),
        cost_estimate=pl.CostEstimate(flops=0, bytes_accessed=2 * n * rows * columns * 5, transcendentals=0),
        name="sum_pieces",
    )(index, *[a for a in arrays for _ in range(n)])


def quarters(value):
    return value.reshape(4, -1, value.shape[-1])


def swap(pieces, along):
    axis, size, unit = along
    return [pieces[0]] + [lax.ppermute(pieces[k], axis, xor_pairs(size, unit * k)) for k in range(1, 4)]


def spread(value, along):
    return swap([value] * 4, along)


def stack_kernel(*refs):
    n = len(refs) - 1
    size = refs[0].shape[0]
    for k in range(n):
        refs[n][k * size : (k + 1) * size] = refs[k][...]


def stack_pieces(pieces):
    shape = (len(pieces) * pieces[0].shape[0],) + pieces[0].shape[1:]
    return pl.pallas_call(
        stack_kernel,
        in_specs=[ANYWHERE] * len(pieces),
        out_specs=ANYWHERE,
        out_shape=jax.ShapeDtypeStruct(shape, bf16),
        compiler_params=pltpu.CompilerParams(vmem_limit_bytes=60 * 2**20),
        cost_estimate=pl.CostEstimate(flops=0, bytes_accessed=4 * math.prod(shape), transcendentals=0),
        name="stack_pieces",
    )(*pieces)


def unpack_kernel(left, last, index_ref, *refs):
    pieces, (w_ref, *refs) = refs[:4], refs[4:]
    if last:
        scale_ref, first_ref, _, _, out_ref, qkv_ref, router_ref, mixing_ref, vec_ref, gain_ref, attn_ref, small = refs
    else:
        out_ref, qkv_ref, small = refs
    width = out_ref.shape[1]
    size = pieces[0].shape[1]
    lane = lax.broadcasted_iota(jnp.int32, (1, EXTRA), 1)
    step = pl.program_id(0)
    half = index_ref[0]
    base = (half * width // 2 if last else 0) + step * 4 * size
    for k in range(4):
        at_ctx = pl.multiple_of((k ^ index_ref[1]) * size, size)
        rows = pl.ds(at_ctx, size)
        total = pieces[k][0].astype(f32)
        out_ref[rows, :] = total[:, left : left + width]
        gain = None
        for p in range(3):
            for i in range(width // 128):
                at = i * 384 + p * 128 + (0 if i * 384 < left else width + EXTRA)
                value = total[:, at : at + 128]
                columns = slice(p * width + i * 128, p * width + (i + 1) * 128)
                qkv_ref[rows, columns] = value
                part = value * w_ref[rows, columns].astype(f32)
                gain = part if gain is None else gain + part
        gain = jnp.sum(gain, axis=1, keepdims=True)
        small[pl.ds(pl.multiple_of(base + at_ctx, size), size), :] = total[:, left + width : left + width + EXTRA] + place(gain, lane, EXTRA - 1)
    if last:

        @pl.when(step == 3)
        def _():
            small[pl.ds(pl.multiple_of((1 - half) * (width // 2), width // 2), width // 2), :] = first_ref[...]
            turned = small[...].T
            router_ref[...] = turned[0:ALL_EXPERTS]
            mixing_ref[0] = turned[16:18]
            mixing_ref[1] = turned[18:20]
            vec_ref[...] = turned[20:22]
            gain_ref[...] = turned[24]
            attn_ref[...] = (turned[EXTRA - 1 : EXTRA] / scale_ref[...])[0]


def unpack_half(index, pieces, w_qkv, left, scale, before):
    width = w_qkv.shape[0]
    size = width // 32
    last = before is not None
    row = lambda a, s: (s[0] * 4 + a, 0)
    source = pl.BlockSpec((1, size, pieces[0].shape[2]), lambda a, s: (a ^ s[2], 0, 0))
    whole = lambda shape: pl.BlockSpec(shape, lambda a, s: (0,) * len(shape))
    in_specs = [source] * 4 + [pl.BlockSpec((4 * size, 3 * width), row)]
    out_specs = [pl.BlockSpec((4 * size, width), row), pl.BlockSpec((4 * size, 3 * width), row)]
    out_shape = [jax.ShapeDtypeStruct((width, width), f32), jax.ShapeDtypeStruct((width, 3 * width), f32)]
    arrays = [*pieces, w_qkv]
    if last:
        shapes = ((ALL_EXPERTS, width), (2, 2, width), (2, width), (width,), (width,))
        in_specs += [whole((1, width)), whole((width // 2, EXTRA))] + [pl.BlockSpec(memory_space=pl.ANY)] * 2
        arrays += [scale, before[2], before[0], before[1]]
        scratch = [pltpu.VMEM((width, EXTRA), f32)]
        aliases = {len(arrays) - 1: 0, len(arrays): 1}
    else:
        shapes = ((width // 2, EXTRA),)
        scratch = []
        aliases = {}
    return pl.pallas_call(
        functools.partial(unpack_kernel, left, last),
        grid_spec=pltpu.PrefetchScalarGridSpec(
            num_scalar_prefetch=1,
            grid=(4,),
            in_specs=in_specs,
            out_specs=out_specs + [whole(s) for s in shapes],
            scratch_shapes=scratch,
        ),
        out_shape=out_shape + [jax.ShapeDtypeStruct(s, f32) for s in shapes],
        input_output_aliases=aliases,
        compiler_params=pltpu.CompilerParams(vmem_limit_bytes=60 * 2**20),
        cost_estimate=pl.CostEstimate(flops=0, bytes_accessed=14 * width * width, transcendentals=0),
        name="unpack_half",
    )(index, *arrays)

P = jax.sharding.PartitionSpec


def rms_inverse(tensor):
    return lax.rsqrt(jnp.mean(tensor * tensor, axis=-1, keepdims=True) + epsilon)


def after(values, *others):
    return lax.optimization_barrier((values, others))[0]


def body(inputs, prev_logits, routes, attn_gain, w_qkv, w_out, moe_gain, router, const_gate, const_vec, w_gate, w_up, w_down, out_grad):
    n_ctx, n_exp = lax.axis_size("ctx"), lax.axis_size("exp")
    me_c, me_e = lax.axis_index("ctx"), lax.axis_index("exp")
    tok, width = inputs.shape[1], inputs.shape[2]
    plen = tok - CONT_LEN
    split = n_exp // FFN_EXPERTS
    capacity = max(4, tok // 64 * 12)
    first = -(-capacity // 32) * 16
    groups = ((0, first), (first, capacity - first))
    home = (me_e // split).reshape(1)

    def deal(value):
        value = jnp.repeat(value, split, axis=0) if split > 1 else value
        return lax.all_to_all(value, "exp", 0, 0, tiled=True)

    def give_back(value):
        value = lax.all_to_all(value, "exp", 0, 0, tiled=True)
        return [value[r::split] if split > 1 else value for r in range(split)]

    x_low = inputs[0]
    upstream_low = out_grad[0]
    flags = jnp.where((me_c ^ jnp.arange(1, n_ctx)) < me_c, 0.0, NEG).astype(f32)

    prev = prev_logits.transpose(2, 0, 1)
    ids = routes.transpose(0, 2, 1)[0]
    mix = jnp.concatenate([router, jnp.zeros((width, 4), bf16), const_gate[0], const_gate[1], jnp.zeros((width, EXTRA - 20), bf16)], axis=1)
    router_pad = jnp.pad(router, ((0, 0), (0, EXTRA - ALL_EXPERTS)))
    turned, chosen, early_sent, x_prompt = route_plan(home, ids, upstream_low, prev, x_low, plen, groups)
    far = [lax.ppermute(x_prompt, "ctx", xor_pairs(n_ctx, k)) for k in range(1, n_ctx)]

    tokens_in = x_low.astype(f32)
    inverse_attn = rms_inverse(tokens_in)
    act_low = (tokens_in * inverse_attn * attn_gain).astype(bf16)
    projected = dot_nn(act_low, w_qkv).astype(bf16)
    early = deal(early_sent)
    act_t = turn(act_low)
    act_far, kv_far = far_projection(after(far, projected, act_t), attn_gain[None], w_qkv)

    mixed_low, lse, hidden, moe_low, sent = attention_forward(flags, projected, kv_far, plen, x_low, w_out, moe_gain[None], turned)
    sent, hidden, early = lax.optimization_barrier((sent, hidden, early))

    local_out, d_normed_local, probs, d_probs, small_local = local_part(hidden, moe_low, upstream_low, prev, ids, mix, moe_gain[None], const_vec)
    far_t = turn(act_far)
    sent = [after(sent[0], local_out, d_normed_local, far_t), sent[1]]
    got = [deal(part.reshape(FFN_EXPERTS, -1, width)) for part in sent]

    got = [part.reshape(-1, width) for part in got]
    passes = [expert_pass(group, home, r, early, router_pad, w_gate, w_up, w_down) for group, r in zip(groups, got)]
    d_got = [give_back(p[1].reshape(n_exp, -1, width)) for p in passes]
    gate_up_low, down_low = weight_gradients(got, [p[2] for p in passes], [p[3] for p in passes], [p[4] for p in passes], [p[5] for p in passes])
    outs = jnp.concatenate([p[0].reshape(n_exp, -1, width + EXTRA) for p in passes], axis=1)
    d_got, gate_up_low, down_low, outs = lax.optimization_barrier((d_got, gate_up_low, down_low, outs))
    out_got = give_back(outs)

    d_got = [[part.reshape(-1, width) for part in group] for group in d_got]
    pairs = width // 128
    cut = pairs // 3
    core = (me_e & 1).reshape(1)
    smalls = [small_local] + [p[6] for p in passes]
    d_hidden, d_mixed, *buffers = combine(core, chosen, d_got, smalls, d_normed_local, hidden, moe_gain[None], upstream_low, mixed_low, w_out, cut * 384)

    sum_gate_up = lax.psum_scatter(gate_up_low, "ctx", scatter_dimension=1, tiled=True).astype(f32)
    sum_down = lax.psum_scatter(down_low, "ctx", scatter_dimension=0, tiled=True).astype(f32)

    def attention(upstream, begin, count, buffers, at, starts, last):
        return attention_backward(flags, core, projected, kv_far, mixed_low, upstream, lse, act_t, far_t, w_qkv, plen, begin, count, buffers, at, starts, last)

    dense = n_ctx == 4 and n_exp == 8
    left, right = cut * 384, (pairs - cut) * 384
    z = me_e >> 1
    at_ctx, at_z = me_c.reshape(1), z.reshape(1)
    along_ctx, along_z = ("ctx", 4, 1), ("exp", 8, 2)
    across = lambda value: lax.ppermute(value, "exp", xor_pairs(n_exp, 1))
    mine_1, theirs_1, grads_1, *starts = attention(d_mixed, 0, cut, buffers, 0, None, False)
    if dense:
        got_1 = across(theirs_1)
    mine_2, theirs_2, grads_2, *starts = attention(d_mixed, cut, 1, right, 0, starts, False)
    if dense:
        mine_2, theirs_2, starts, got_1 = lax.optimization_barrier((mine_2, theirs_2, starts, got_1))
        sums_1 = sum_pieces(at_z, [[quarters(mine_1), quarters(got_1)]])
        parts_1 = swap(sums_1, along_z)
        mine_2 = after(mine_2, sums_1[0])
    mine_2, theirs_2, grads_3, *d_far = attention(d_mixed, cut + 1, pairs - cut - 1, (mine_2, theirs_2), 1, starts, True)
    if dense:
        mine_2, theirs_2, grads_3, d_far, parts_1 = lax.optimization_barrier((mine_2, theirs_2, grads_3, d_far, parts_1))
    send_far = lambda k: lax.ppermute(d_far[k - 1], "ctx", xor_pairs(n_ctx, k))
    far_back = [send_far(k) for k in range(1, n_ctx - 1)]
    if dense:
        sums_2 = sum_pieces(at_z, [[quarters(mine_2), quarters(across(theirs_2))]])
        parts_2 = swap(sums_2, along_z)
        mixed_out, d_logits = finish(chosen, out_got, groups, after(local_out, sums_2[0]), probs, d_probs)
        mixed_out, d_logits, far_back, d_far = lax.optimization_barrier((mixed_out, d_logits, far_back, d_far))
        far_back = far_back + [send_far(n_ctx - 1)]
        mixed_out, parts_2 = lax.optimization_barrier((mixed_out, parts_2))
        parts_1, parts_2 = ([quarters(p) for p in parts] for parts in (parts_1, parts_2))
        parts = swap(sum_pieces(at_ctx, [parts_1, parts_2]), along_ctx)
        [piece] = sum_pieces(at_ctx, [parts])
        spread_z = spread(piece, along_z)
    else:
        mixed_out, d_logits = finish(chosen, out_got, groups, local_out, probs, d_probs)
        far_back = far_back + [send_far(n_ctx - 1)]
    d_inputs = input_gradient([grads_1, grads_2, grads_3], x_low, attn_gain[None], d_hidden, w_qkv, far_back)

    d_prev = d_logits[:ALL_EXPERTS].T[None]
    total_gate, total_up, total_down = sum_gate_up[0][None], sum_gate_up[1][None], sum_down[None]
    if dense:
        d_inputs, spread_z = lax.optimization_barrier((d_inputs, spread_z))
        column = stack_pieces(spread_z)
        own = after(spread(column, along_ctx), total_gate, total_up, total_down, d_prev)
        other = [across(piece) for piece in own]
        place_of = lambda half: jnp.stack([half, me_c, z])
        first = unpack_half(place_of(core[0]), own, w_qkv, left, None, None)
        first, other = lax.optimization_barrier((first, other))
        out_sum, qkv_sum, d_router, d_mixing, d_const_vec, d_moe_gain, d_attn_gain = unpack_half(place_of(1 - core[0]), other, w_qkv, left, attn_gain[None], first)
    else:
        whole = lambda mine, theirs: jnp.where(core == 0, jnp.concatenate([mine, theirs], axis=0), jnp.concatenate([theirs, mine], axis=0))
        total_1, total_2 = [v.astype(f32) for v in lax.psum((whole(mine_1, theirs_1), whole(mine_2, theirs_2)), ("ctx", "exp"))]
        columns = jnp.concatenate([total_1[:, :left], total_2], axis=1).reshape(width, pairs, 3, 128)
        qkv_sum = columns.transpose(0, 2, 1, 3).reshape(width, 3 * width)
        out_sum, small = total_1[:, left : left + width], total_1[:, left + width :].T
        d_attn_gain = (jnp.sum(qkv_sum * w_qkv.astype(f32), axis=1) / attn_gain)
        d_router, d_mixing, d_const_vec, d_moe_gain = small[:ALL_EXPERTS], small[16:20].reshape(2, 2, width), small[20:22], small[24]
    return (
        mixed_out[None],
        d_inputs[None],
        d_prev,
        d_attn_gain,
        qkv_sum,
        out_sum,
        d_moe_gain,
        d_router.T,
        d_mixing.transpose(0, 2, 1),
        d_const_vec,
        total_gate,
        total_up,
        total_down,
    )


def solution(mesh):
    rows = P("ctx", "exp", None)
    expert = P("exp", None, None)
    summed = P("exp", "ctx", None)
    return jax.shard_map(
        body,
        mesh=mesh,
        in_specs=(rows, rows, rows, P(), P(), P(), P(), P(), P(), P(), expert, expert, expert, rows),
        out_specs=(rows, rows, rows, P(), P(), P(), P(), P(), P(), P(), summed, summed, summed),
        check_vma=False,
    )
```

```python
import functools, math
import jax, jax.numpy as jnp
from jax import lax
from jax.experimental import pallas as pl
from jax.experimental.pallas import tpu as pltpu

HEADS = 12
HEAD_DIM = 64
CONT_LEN = 512
LOG2E = 1.4426950408889634
SCALE = HEAD_DIM ** -0.5
bf16 = jnp.bfloat16
f32 = jnp.float32
NEG = -1e30
epsilon = 1e-06


def dot_nt(a, b):
    return lax.dot_general(a, b, (((1,), (1,)), ((), ())), preferred_element_type=f32)


def dot_nn(a, b):
    return jnp.dot(a, b, preferred_element_type=f32)


def query_tiles(tok, plen):
    tiles = [(0, plen, True)]
    step = 256
    for start in range(plen, tok, step):
        tiles.append((start, step, False))
    return tiles


def split_high(value):
    high = value.astype(bf16)
    return high, (value - high.astype(f32)).astype(bf16)


def both_halves(value, head, low_half):
    turned = pltpu.roll(value, HEAD_DIM, 1)
    return jnp.where(low_half, value, turned) if head == 0 else jnp.where(low_half, turned, value)


def scaled_queries(value, head, low_half):
    high, rest = split_high(value.astype(f32) * (SCALE * LOG2E))
    rest = pltpu.roll(rest, HEAD_DIM, 1)
    return jnp.where(low_half, high, rest) if head == 0 else jnp.where(low_half, rest, high)


def attention_forward_kernel(plen, count, flags_ref, q_ref, k_ref, v_ref, kr_ref, vr_ref, gain_ref, x_any, w_any, *refs):
    turned_any, (o_ref, lse_ref, hidden_ref, low_ref), sent = refs[:count], refs[count : count + 4], refs[count + 4 : 2 * count + 4]
    kd, krd, vd, vrd, mixed, x_ref, w_ref, *select, sems = refs[2 * count + 4 :]
    step = pl.program_id(0)
    copies = [pltpu.make_async_copy(a, r, sems.at[i]) for i, (a, r) in enumerate(zip((x_any, w_any, *turned_any), (x_ref, w_ref, *select)))]

    @pl.when(step == 0)
    def _():
        for copy in copies:
            copy.start()

    tok = q_ref.shape[0]
    remote = kr_ref.shape[0]
    low_half = lax.broadcasted_iota(jnp.int32, (1, 128), 1) < HEAD_DIM
    one = jnp.ones((), bf16)
    for head in range(2):
        mine = low_half if head == 0 else ~low_half
        kd[head] = both_halves(k_ref[...], head, low_half)
        krd[head] = both_halves(kr_ref[...], head, low_half)
        vd[head] = jnp.where(mine, v_ref[...], one)
        vrd[head] = jnp.where(mine, vr_ref[...], one)
    for start, size, is_prompt in query_tiles(tok, plen):
        row = lax.broadcasted_iota(jnp.int32, (size, size), 0)
        col = lax.broadcasted_iota(jnp.int32, (size, size), 1)
        queries = q_ref[start : start + size, :]
        units = []
        for head in range(2):
            qh = scaled_queries(queries, head, low_half)
            pieces = []
            diag = dot_nt(qh, kd[head, start : start + size, :])
            pieces.append((jnp.where(col <= row, diag, NEG), vd, start, size))
            if is_prompt:
                for j in range(remote // plen):
                    s = dot_nt(qh, krd[head, j * plen : (j + 1) * plen, :])
                    pieces.append((s + flags_ref[j], vrd, j * plen, plen))
            else:
                s = dot_nt(qh, kd[head, 0:start, :])
                pieces.append((s, vd, 0, start))
                s = dot_nt(qh, krd[head])
                pieces.append((s, vrd, 0, remote))
            units.append(pieces)
        accs, peaks = [], []
        for head, pieces in enumerate(units):
            peak = None
            for s, _, _, _ in pieces:
                m = jnp.max(s, axis=1, keepdims=True)
                peak = m if peak is None else jnp.maximum(peak, m)
            acc = None
            for s, ref, at, n in pieces:
                p = jnp.exp2(s - peak).astype(bf16)
                part = dot_nn(p, ref[head, at : at + n, :])
                acc = part if acc is None else acc + part
            accs.append(acc)
            peaks.append(peak)
        num = jnp.where(low_half, accs[0], accs[1])
        den = pltpu.roll(jnp.where(low_half, accs[1], accs[0]), HEAD_DIM, 1)
        value = (num / den).astype(bf16)
        o_ref[start : start + size, :] = value
        mixed[step, start : start + size, :] = value
        turned = (jnp.where(low_half, peaks[0], peaks[1]) + jnp.log2(den)).T
        lse_ref[0, 0:8, start : start + size] = turned[0:8, :]
        lse_ref[0, 8:16, start : start + size] = turned[HEAD_DIM : HEAD_DIM + 8, :]


    @pl.when(step == pl.num_programs(0) - 1)
    def _():
        for copy in copies:
            copy.wait()
        joined = jnp.concatenate([mixed[i] for i in range(mixed.shape[0])], axis=1)
        hidden = x_ref[...].astype(f32) + dot_nn(joined, w_ref[...])
        inverse = lax.rsqrt(jnp.mean(hidden * hidden, axis=1, keepdims=True) + epsilon)
        low = (hidden * inverse * gain_ref[...]).astype(bf16)
        hidden_ref[...] = hidden
        low_ref[...] = low
        for rows_ref, s in zip(select, sent):
            s[...] = dot_nn(rows_ref[...], low).astype(bf16)


def attention_forward(flags, proj, kv_rem, plen, x, w_out, gain, turned):
    tok, width = proj.shape[0], proj.shape[1] // 3
    remote = kv_rem.shape[0]
    pairs = width // 128
    still = lambda shape: pl.BlockSpec(shape, lambda i: (0, 0))
    sent = [(r.shape[0], width) for r in turned]
    out = pl.pallas_call(
        functools.partial(attention_forward_kernel, plen, len(turned)),
        grid=(pairs,),
        in_specs=[
            pl.BlockSpec(memory_space=pltpu.SMEM),
            pl.BlockSpec((tok, 128), lambda i: (0, i)),
            pl.BlockSpec((tok, 128), lambda i: (0, pairs + i)),
            pl.BlockSpec((tok, 128), lambda i: (0, 2 * pairs + i)),
            pl.BlockSpec((remote, 128), lambda i: (0, i)),
            pl.BlockSpec((remote, 128), lambda i: (0, pairs + i)),
            still((1, width)),
        ]
        + [pl.BlockSpec(memory_space=pl.ANY)] * (2 + len(turned)),
        out_specs=[
            pl.BlockSpec((tok, 128), lambda i: (0, i)),
            pl.BlockSpec((1, 16, tok), lambda i: (i, 0, 0)),
            still((tok, width)),
            still((tok, width)),
        ]
        + [still(s) for s in sent],
        out_shape=[
            jax.ShapeDtypeStruct((tok, width), bf16),
            jax.ShapeDtypeStruct((pairs, 16, tok), f32),
            jax.ShapeDtypeStruct((tok, width), f32),
            jax.ShapeDtypeStruct((tok, width), bf16),
        ]
        + [jax.ShapeDtypeStruct(s, bf16) for s in sent],
        scratch_shapes=[pltpu.VMEM((2, n, 128), bf16) for n in (tok, remote, tok, remote)]
        + [pltpu.VMEM((pairs, tok, 128), bf16)]
        + [pltpu.VMEM(a.shape, bf16) for a in (x, w_out, *turned)]
        + [pltpu.SemaphoreType.DMA((2 + len(turned),))],
        compiler_params=pltpu.CompilerParams(vmem_limit_bytes=60 * 2**20),
        cost_estimate=pl.CostEstimate(flops=4 * tok * (tok + remote) * width + 4 * tok * width * width, bytes_accessed=2 * (tok * 10 + remote * 2) * width, transcendentals=tok * (tok + remote) * HEADS),
        name="attention_forward",
    )(flags, proj, proj, proj, kv_rem, kv_rem, gain, x, w_out, *turned)
    return out[0], out[1], out[2], out[3], out[4:]


def attention_backward_kernel(plen, started, last, skip, flags_ref, core_ref, q_ref, k_ref, v_ref, kr_ref, vr_ref, o_ref, do_ref, lse_ref, act_ref, far_ref, wk_ref, wv_ref, *refs):
    refs = refs[skip:]
    if started:
        start_far_ref, *refs = refs
    mine_ref, theirs_ref, own_grads, *refs = refs
    dfar_ref, *dfar_refs = (refs[-1:] + refs[:-10]) if last else refs[:1]
    kt, krt, dka, dva, dkra, dvra, weights, kd, krd = refs[-10:-1] if last else refs[-9:]
    tok = q_ref.shape[0]
    remote = kr_ref.shape[0]
    lane = lax.broadcasted_iota(jnp.int32, (1, 128), 1)
    low_half = lane < HEAD_DIM
    c = SCALE * LOG2E
    zero = jnp.zeros((), bf16)
    for head in range(2):
        kd[head] = both_halves(k_ref[...], head, low_half)
        krd[head] = both_halves(kr_ref[...], head, low_half)
    kt[...] = k_ref[...].T
    krt[...] = kr_ref[...].T
    dka[...] = jnp.zeros_like(dka)
    dva[...] = jnp.zeros_like(dva)
    dkra[...] = jnp.zeros_like(dkra)
    dvra[...] = jnp.zeros_like(dvra)
    pick = lax.broadcasted_iota(jnp.int32, (16, 128), 0) // 8 == lax.broadcasted_iota(jnp.int32, (16, 128), 1) // HEAD_DIM
    pick = jnp.where(pick, 1.0, 0.0).astype(bf16)
    for start, size, is_prompt in query_tiles(tok, plen):
        rows = slice(start, start + size)
        product = do_ref[rows, :].astype(f32) * o_ref[rows, :].astype(f32)
        high = product.astype(bf16)
        rest = (product - high.astype(f32)).astype(bf16)
        delta = dot_nt(pick, high) + dot_nt(pick, rest)
        totals = [None, None]
        masks = [low_half, ~low_half]
        qh = [jnp.where(m, q_ref[rows, :], zero) for m in masks]
        qs = [scaled_queries(q_ref[rows, :], head, low_half) for head in range(2)]
        doh = [jnp.where(m, do_ref[rows, :], zero) for m in masks]
        segments = [(kd, v_ref, kt, dka, dva, start, size, "diag")]
        if is_prompt:
            for j in range(remote // plen):
                segments.append((krd, vr_ref, krt, dkra, dvra, j * plen, plen, j))
        else:
            segments.append((kd, v_ref, kt, dka, dva, 0, start, None))
            segments.append((krd, vr_ref, krt, dkra, dvra, 0, remote, None))
        for kk, vv, tt, dk_acc, dv_acc, at, n, mode in segments:
            keys = slice(at, at + n)
            scores = [dot_nt(kk[head, keys, :], qs[head]) for head in range(2)]
            d_probs = [dot_nt(vv[keys, :], doh[head]) for head in range(2)]
            low_p, low_d = [], []
            for head in range(2):
                st = scores[head] - lse_ref[0, 8 * head : 8 * head + 1, rows]
                if mode == "diag":
                    key = lax.broadcasted_iota(jnp.int32, (n, size), 0)
                    query = lax.broadcasted_iota(jnp.int32, (n, size), 1)
                    st = jnp.where(key <= query, st, NEG)
                elif mode is not None:
                    st = st + flags_ref[mode]
                pt = jnp.exp2(st)
                low_p.append(pt.astype(bf16))
                low_d.append((pt * (d_probs[head] - delta[8 * head : 8 * head + 1, :])).astype(bf16))
            dv_acc[keys, :] += dot_nn(low_p[0], doh[0]) + dot_nn(low_p[1], doh[1])
            dk_acc[keys, :] += dot_nn(low_d[0], qh[0]) + dot_nn(low_d[1], qh[1])
            for head in range(2):
                part = dot_nn(tt[head * HEAD_DIM : (head + 1) * HEAD_DIM, keys], low_d[head])
                totals[head] = part if totals[head] is None else totals[head] + part
        dqt = totals
        own_grads[rows, 0:128] = (jnp.concatenate(dqt, axis=0).T * SCALE).astype(bf16)
    own_grads[:, 128:256] = (dka[...] * SCALE).astype(bf16)
    own_grads[:, 256:384] = dva[...].astype(bf16)
    far_grads = jnp.concatenate([(dkra[...] * SCALE).astype(bf16), dvra[...].astype(bf16)], axis=1)
    weights[:, 0:128] = wk_ref[...]
    weights[:, 128:256] = wv_ref[...]
    half = mine_ref.shape[0]
    for out_ref, which in ((theirs_ref, 1 - core_ref[0]), (mine_ref, core_ref[0])):
        rows = pl.ds(pl.multiple_of(which * half, half), half)
        total = dot_nn(act_ref[rows, :], own_grads[...])
        out_ref[:, 0:128] = total[:, 0:128].astype(bf16)
        out_ref[:, 128:384] = (total[:, 128:384] + dot_nn(far_ref[rows, :], far_grads)).astype(bf16)
    d_far = dot_nt(far_grads, weights[...])
    step = pl.program_id(0)

    @pl.when(step == 0)
    def _():
        dfar_ref[...] = d_far + start_far_ref[...] if started else d_far

    @pl.when(step > 0)
    def _():
        dfar_ref[...] += d_far

    if last:

        @pl.when(step == pl.num_programs(0) - 1)
        def _():
            for k, ref in enumerate(dfar_refs):
                ref[...] = dfar_ref[k * plen : (k + 1) * plen, :].astype(bf16)


def attention_backward(flags, core, proj, kv_rem, mixed, d_mixed, lse, act_t, far_t, w_qkv, plen, begin, count, buffers, at, starts, last):
    tok, width = mixed.shape
    remote = kv_rem.shape[0]
    pairs = width // 128
    own = lambda shift: pl.BlockSpec((tok, 128), lambda i: (0, shift + i))
    far = lambda shift: pl.BlockSpec((remote, 128), lambda i: (0, shift + i))
    weight = lambda shift: pl.BlockSpec((width, 128), lambda i: (0, shift + i))
    still = lambda shape: pl.BlockSpec(shape, lambda i: (0, 0))
    half = pl.BlockSpec((width // 2, 384), lambda i: (0, at + i))
    in_specs = [
        pl.BlockSpec(memory_space=pltpu.SMEM),
        pl.BlockSpec(memory_space=pltpu.SMEM),
        own(begin),
        own(pairs + begin),
        own(2 * pairs + begin),
        far(begin),
        far(pairs + begin),
        own(begin),
        own(begin),
        pl.BlockSpec((1, 16, tok), lambda i: (begin + i, 0, 0)),
        still((width, tok)),
        still((width, remote)),
        weight(pairs + begin),
        weight(2 * pairs + begin),
    ]
    arrays = [flags, core, proj, proj, proj, kv_rem, kv_rem, mixed, d_mixed, lse, act_t, far_t, w_qkv, w_qkv]
    scratch = [
        pltpu.VMEM((128, tok), bf16),
        pltpu.VMEM((128, remote), bf16),
        pltpu.VMEM((tok, 128), f32),
        pltpu.VMEM((tok, 128), f32),
        pltpu.VMEM((remote, 128), f32),
        pltpu.VMEM((remote, 128), f32),
        pltpu.VMEM((width, 256), bf16),
        pltpu.VMEM((2, tok, 128), bf16),
        pltpu.VMEM((2, remote, 128), bf16),
    ]
    aliases = {}
    skip = 0
    if not isinstance(buffers, int):
        aliases = {len(arrays): 0, len(arrays) + 1: 1}
        in_specs += [pl.BlockSpec(memory_space=pl.ANY)] * 2
        arrays += list(buffers)
        skip = 2
        buffers = buffers[0].shape[1]
    if starts:
        in_specs += [still((remote, width))]
        arrays += list(starts)
    out_specs = [half, half, pl.BlockSpec((tok, 384), lambda i: (0, i))]
    out_shape = [jax.ShapeDtypeStruct((width // 2, buffers), bf16)] * 2 + [jax.ShapeDtypeStruct((tok, count * 384), bf16)]
    if last:
        out_specs += [still((plen, width))] * (remote // plen)
        out_shape += [jax.ShapeDtypeStruct((plen, width), bf16)] * (remote // plen)
        scratch = scratch + [pltpu.VMEM((remote, width), f32)]
    else:
        out_specs += [still((remote, width))]
        out_shape += [jax.ShapeDtypeStruct((remote, width), f32)]
    return pl.pallas_call(
        functools.partial(attention_backward_kernel, plen, bool(starts), last, skip),
        grid=(count,),
        in_specs=in_specs,
        out_specs=out_specs,
        out_shape=out_shape,
        scratch_shapes=scratch,
        input_output_aliases=aliases,
        compiler_params=pltpu.CompilerParams(vmem_limit_bytes=60 * 2**20),
        cost_estimate=pl.CostEstimate(flops=10 * tok * (tok + remote) * count * 128 + 20 * tok * width * count * 128, bytes_accessed=2 * (tok * 8 + remote * 4) * count * 128 + 16 * tok * width, transcendentals=tok * (tok + remote) * 2 * count),
        name="attention_backward",
    )(*arrays)


FFN_EXPERTS = 8
ALL_EXPERTS = 12
EXTRA = 128
SMALL = 8


def dot_tn(a, b):
    return lax.dot_general(a, b, (((0,), (0,)), ((), ())), preferred_element_type=f32)


def split_low(value, parts):
    pieces = []
    for _ in range(parts):
        piece = value.astype(bf16)
        pieces.append(piece)
        value = value - piece.astype(f32)
    return pieces


def route_kernel(groups, home_ref, ids_ref, grad_ref, prev_ref, x_ref, *out_refs):
    tok, width = grad_ref.shape
    count = len(groups)
    turned_refs, chosen_refs, (early_ref, prompt_ref) = out_refs[:count], out_refs[count : 2 * count], out_refs[2 * count :]
    prompt_ref[...] = x_ref[0 : prompt_ref.shape[0], :]
    capacity = early_ref.shape[1] - SMALL
    expert = lax.broadcasted_iota(jnp.int32, (16, tok), 0)
    ids = [ids_ref[k : k + 1, :] for k in range(2)]
    names = [row == expert for row in ids]
    both = jnp.where(names[0] | names[1], 1.0, 0.0).astype(bf16)
    earlier = lax.broadcasted_iota(jnp.int32, (tok, tok), 0) < lax.broadcasted_iota(jnp.int32, (tok, tok), 1)
    before = dot_nn(both, jnp.where(earlier, 1.0, 0.0).astype(bf16))
    pieces = [piece.astype(f32) for piece in split_low(prev_ref[:, 0, :], 3)]
    extra = jnp.concatenate(pieces + [jnp.zeros((EXTRA - 3 * ALL_EXPERTS, tok), f32)], axis=0).T.astype(bf16)
    slot = [jnp.sum(jnp.where(n, before, 0.0), axis=0, keepdims=True).astype(jnp.int32) for n in names]
    extras = []
    for (first, size), turned_ref, chosen_ref in zip(groups, turned_refs, chosen_refs):
        spots = lax.broadcasted_iota(jnp.int32, (FFN_EXPERTS * size, tok), 0)
        hit = None
        for k in range(2):
            inside = (ids[k] < FFN_EXPERTS) & (slot[k] >= first) & (slot[k] < first + size)
            place = jnp.where(inside, ids[k] * size + slot[k] - first, -1)
            hit = spots == place if hit is None else hit | (spots == place)
        turned = jnp.where(hit, 1.0, 0.0).astype(bf16)
        turned_ref[...] = turned
        chosen_ref[...] = turned.T
        grads = dot_nn(turned, grad_ref[...]).astype(bf16)
        extras.append(dot_nn(turned, extra))
        for e in range(FFN_EXPERTS):
            early_ref[e, first : first + size, :] = grads[e * size : (e + 1) * size]
    third = capacity // 3
    for e in range(FFN_EXPERTS):
        rows = jnp.concatenate([x[e * size : (e + 1) * size] for x, (_, size) in zip(extras, groups)], axis=0)
        rows = rows[0:third] + pltpu.roll(rows[third : 2 * third], 40, 1) + pltpu.roll(rows[2 * third : capacity], 80, 1)
        early_ref[e, capacity : capacity + SMALL, :] = jnp.zeros((SMALL, width), bf16)
        for g in range(third // SMALL):
            early_ref[e, capacity : capacity + SMALL, g * EXTRA : (g + 1) * EXTRA] = rows[g * SMALL : (g + 1) * SMALL].astype(bf16)


def route_plan(home, ids, grad, prev, x, plen, groups):
    tok, width = grad.shape
    counts = [FFN_EXPERTS * size for _, size in groups]
    whole = pl.BlockSpec(memory_space=pltpu.VMEM)
    early = (FFN_EXPERTS, sum(counts) // FFN_EXPERTS + SMALL, width)
    out = pl.pallas_call(
        functools.partial(route_kernel, groups),
        in_specs=[pl.BlockSpec(memory_space=pltpu.SMEM), whole, whole, whole, whole],
        out_specs=[whole] * (2 * len(groups) + 2),
        out_shape=[jax.ShapeDtypeStruct((n, tok), bf16) for n in counts]
        + [jax.ShapeDtypeStruct((tok, n), bf16) for n in counts]
        + [jax.ShapeDtypeStruct(early, bf16), jax.ShapeDtypeStruct((plen, width), bf16)],
        compiler_params=pltpu.CompilerParams(vmem_limit_bytes=60 * 2**20),
        cost_estimate=pl.CostEstimate(flops=2 * sum(counts) * tok * (width + EXTRA), bytes_accessed=4 * sum(counts) * width, transcendentals=0),
        name="route_plan",
    )(home, ids, grad, prev, x)
    return out[: len(groups)], out[len(groups) : -2], out[-2], out[-1]


def router_inputs(early_ref, slots):
    capacity = early_ref.shape[1] - SMALL
    groups = capacity // 3 // SMALL
    rows = []
    for sender in range(early_ref.shape[0]):
        packed = early_ref[sender, capacity : capacity + SMALL, :].astype(f32)
        third = jnp.concatenate([packed[:, g * EXTRA : (g + 1) * EXTRA] for g in range(groups)], axis=0)
        every = jnp.concatenate([third, pltpu.roll(third, EXTRA - 40, 1), pltpu.roll(third, EXTRA - 80, 1)], axis=0)
        rows.append(every[slots])
    rows = jnp.concatenate(rows, axis=0)
    return rows + pltpu.roll(rows, EXTRA - ALL_EXPERTS, 1) + pltpu.roll(rows, EXTRA - 2 * ALL_EXPERTS, 1)


def expert_kernel(group, home_ref, rows_ref, early_ref, router_ref, wg_ref, wu_ref, wd_ref,
                  out_ref, drow_ref, dout_ref, inner_ref, dgate_ref, dup_ref, small_ref, acc_out, acc_row, probs_ref):
    width = rows_ref.shape[1]
    step, steps = pl.program_id(0), pl.num_programs(0)
    home = home_ref[0]
    lane = lax.broadcasted_iota(jnp.int32, (1, EXTRA), 1)
    slots = slice(group[0], group[0] + group[1])

    @pl.when(step == 0)
    def _():
        logits = router_inputs(early_ref, slots) + dot_nn(rows_ref[...], router_ref[...])
        logits = jnp.where(lane < ALL_EXPERTS, logits, NEG)
        unnormed = jnp.exp(logits - jnp.max(logits, axis=1, keepdims=True))
        probs = unnormed / jnp.sum(unnormed, axis=1, keepdims=True)
        probs_ref[...] = probs
        gate = jnp.sum(jnp.where(lane == home, probs, 0.0), axis=1, keepdims=True)
        dout_ref[...] = (gate * early_ref[:, slots, 0:width].astype(f32).reshape(-1, width)).astype(bf16)
        acc_out[...] = jnp.zeros_like(acc_out)
        acc_row[...] = jnp.zeros_like(acc_row)

    rows = rows_ref[...]
    gate_pre = dot_nn(rows, wg_ref[0])
    up_pre = dot_nn(rows, wu_ref[0])
    d_inner = dot_nt(dout_ref[...], wd_ref[0])
    sigmoid = jax.nn.sigmoid(gate_pre)
    silu = gate_pre * sigmoid
    inner = (silu * up_pre).astype(bf16)
    d_gate = (d_inner * up_pre * (sigmoid * (1.0 + gate_pre * (1.0 - sigmoid)))).astype(bf16)
    d_up = (d_inner * silu).astype(bf16)
    inner_ref[...] = inner
    dgate_ref[...] = d_gate
    dup_ref[...] = d_up
    acc_out[...] += dot_nn(inner, wd_ref[0])
    acc_row[...] += dot_nt(d_gate, wg_ref[0]) + dot_nt(d_up, wu_ref[0])

    @pl.when(step == steps - 1)
    def _():
        probs = probs_ref[...]
        gate = jnp.sum(jnp.where(lane == home, probs, 0.0), axis=1, keepdims=True)
        out = acc_out[...].astype(bf16).astype(f32)
        d_row_gate = jnp.sum(out * early_ref[:, slots, 0:width].astype(f32).reshape(-1, width), axis=1, keepdims=True)
        out_ref[:, 0:width] = (gate * out).astype(bf16)
        extra = jnp.zeros((out.shape[0], EXTRA), f32)
        for i, piece in enumerate(split_low(d_row_gate, 3)):
            extra = jnp.where(lane == home + 16 * i, piece.astype(f32), extra)
        out_ref[:, width : width + EXTRA] = extra.astype(bf16)
        term = d_row_gate * gate * (jnp.where(lane == home, 1.0, 0.0) - probs)
        high, rest = split_low(term, 2)
        turned = [piece.T for piece in (high, rest)]
        small_ref[...] = (dot_nn(turned[0], rows) + dot_nn(turned[1], rows))[0 : 2 * SMALL, :]
        drow_ref[...] = (acc_row[...] + dot_nt(high, router_ref[...]) + dot_nt(rest, router_ref[...])).astype(bf16)


def expert_pass(group, home, rows, early, router_pad, w_gate, w_up, w_down):
    count, width = rows.shape
    ff = w_gate.shape[2]
    tile = min(512, ff)
    full = pl.BlockSpec((count, width), lambda j: (0, 0))
    wide = pl.BlockSpec((count, width + EXTRA), lambda j: (0, 0))
    tall = pl.BlockSpec((1, width, tile), lambda j: (0, 0, j))
    piece = pl.BlockSpec((count, tile), lambda j: (0, j))
    return pl.pallas_call(
        functools.partial(expert_kernel, group),
        grid=(ff // tile,),
        in_specs=[
            pl.BlockSpec(memory_space=pltpu.SMEM),
            full,
            pl.BlockSpec(early.shape, lambda j: (0, 0, 0)),
            pl.BlockSpec((width, EXTRA), lambda j: (0, 0)),
            tall,
            tall,
            pl.BlockSpec((1, tile, width), lambda j: (0, j, 0)),
        ],
        out_specs=[wide, full, full, piece, piece, piece, pl.BlockSpec((2 * SMALL, width), lambda j: (0, 0))],
        out_shape=[
            jax.ShapeDtypeStruct((count, width + EXTRA), bf16),
            jax.ShapeDtypeStruct((count, width), bf16),
            jax.ShapeDtypeStruct((count, width), bf16),
        ]
        + [jax.ShapeDtypeStruct((count, ff), bf16)] * 3
        + [jax.ShapeDtypeStruct((2 * SMALL, width), f32)],
        scratch_shapes=[pltpu.VMEM((count, width), f32), pltpu.VMEM((count, width), f32), pltpu.VMEM((count, EXTRA), f32)],
        compiler_params=pltpu.CompilerParams(vmem_limit_bytes=60 * 2**20),
        cost_estimate=pl.CostEstimate(flops=12 * count * width * ff, bytes_accessed=6 * width * ff + 2 * count * (5 * width + 3 * ff), transcendentals=count * ff),
        name="expert_pass",
    )(home, rows, early, router_pad, w_gate, w_up, w_down)


def weight_kernel(count, *refs):
    rows, douts, inners, dgates, dups = (refs[i * count : (i + 1) * count] for i in range(5))
    gate_up_ref, down_ref = refs[5 * count : 5 * count + 2]
    turned = refs[5 * count + 2 :]

    @pl.when(pl.program_id(0) == 0)
    def _():
        for ref, scratch in zip(rows, turned):
            scratch[...] = ref[...].T

    gate_up_ref[0] = sum(dot_nn(t[...], d[...]) for t, d in zip(turned, dgates)).astype(bf16)
    gate_up_ref[1] = sum(dot_nn(t[...], d[...]) for t, d in zip(turned, dups)).astype(bf16)
    down_ref[...] = sum(dot_nn(i[...].T, d[...]) for i, d in zip(inners, douts)).astype(bf16)


def weight_gradients(rows, douts, inners, dgates, dups):
    count = len(rows)
    width, ff = rows[0].shape[1], inners[0].shape[1]
    tile = min(512, ff)
    total = sum(r.shape[0] for r in rows)
    full = [pl.BlockSpec(r.shape, lambda j: (0, 0)) for r in rows]
    piece = [pl.BlockSpec((r.shape[0], tile), lambda j: (0, j)) for r in rows]
    return pl.pallas_call(
        functools.partial(weight_kernel, count),
        grid=(ff // tile,),
        in_specs=full + full + piece * 3,
        out_specs=[pl.BlockSpec((2, width, tile), lambda j: (0, 0, j)), pl.BlockSpec((tile, width), lambda j: (j, 0))],
        out_shape=[jax.ShapeDtypeStruct((2, width, ff), bf16), jax.ShapeDtypeStruct((ff, width), bf16)],
        scratch_shapes=[pltpu.VMEM((width, r.shape[0]), bf16) for r in rows],
        compiler_params=pltpu.CompilerParams(vmem_limit_bytes=60 * 2**20),
        cost_estimate=pl.CostEstimate(flops=6 * total * width * ff, bytes_accessed=6 * width * ff + 2 * total * (2 * width + 3 * ff), transcendentals=0),
        name="weight_gradients",
    )(*rows, *douts, *inners, *dgates, *dups)


ANYWHERE = pl.BlockSpec(memory_space=pltpu.VMEM)
SCALARS = pl.BlockSpec(memory_space=pltpu.SMEM)


def inverse_rms(value):
    return lax.rsqrt(jnp.mean(value * value, axis=1, keepdims=True) + epsilon)


def turn_kernel(in_ref, out_ref):
    out_ref[...] = in_ref[...].T


def turn(value):
    rows, columns = value.shape
    block = 256 if rows % 256 == 0 else 128
    return pl.pallas_call(
        turn_kernel,
        grid=(rows // block,),
        in_specs=[pl.BlockSpec((block, columns), lambda i: (i, 0))],
        out_specs=pl.BlockSpec((columns, block), lambda i: (0, i)),
        out_shape=jax.ShapeDtypeStruct((columns, rows), value.dtype),
        compiler_params=pltpu.CompilerParams(vmem_limit_bytes=60 * 2**20),
        cost_estimate=pl.CostEstimate(flops=0, bytes_accessed=4 * rows * columns, transcendentals=0),
        name="turn",
    )(value)


def place(value, lane, at):
    return jnp.where(lane == at, value, 0.0)


def local_kernel(hidden_ref, low_ref, grad_ref, prev_ref, ids_ref, mix_ref, gain_ref, vec_ref, out_ref, dnormed_ref, probs_ref, dprobs_ref, small_ref):
    lane = lax.broadcasted_iota(jnp.int32, (1, EXTRA), 1)
    hidden = hidden_ref[...]
    normed = hidden * inverse_rms(hidden) * gain_ref[...]
    low = low_ref[...]
    grad = grad_ref[...].astype(f32)
    raw = dot_nn(low, mix_ref[...])
    block = raw.shape[0]
    prev = jnp.concatenate([prev_ref[:, 0, :], jnp.zeros((EXTRA - ALL_EXPERTS, block), f32)], axis=0).T
    logits = jnp.where(lane < ALL_EXPERTS, raw + prev, NEG)
    unnormed = jnp.exp(logits - jnp.max(logits, axis=1, keepdims=True))
    probs = unnormed / jnp.sum(unnormed, axis=1, keepdims=True)
    ids = jnp.concatenate([ids_ref[...].astype(f32), jnp.zeros((SMALL - 2, block), f32)], axis=0).T
    named = (ids[:, 0:1] == lane.astype(f32)) | (ids[:, 1:2] == lane.astype(f32))
    gates = jnp.where(named, probs, 0.0)
    copy_gate = gates[:, FFN_EXPERTS + 1 : FFN_EXPERTS + 2]
    dots = jnp.sum(grad * normed, axis=1, keepdims=True)
    out = hidden
    weight = copy_gate
    d_probs = place(dots, lane, FFN_EXPERTS + 1)
    logit_grads = jnp.zeros_like(probs)
    vec_terms = jnp.zeros_like(probs)
    for c in range(2):
        vec = vec_ref[c : c + 1, :]
        gate = gates[:, FFN_EXPERTS + 2 + c : FFN_EXPERTS + 3 + c]
        at = 16 + 2 * c
        a0 = jax.nn.sigmoid(raw[:, at : at + 1] - raw[:, at + 1 : at + 2])
        a1 = jax.nn.sigmoid(raw[:, at + 1 : at + 2] - raw[:, at : at + 1])
        vec_dots = jnp.sum(grad * vec, axis=1, keepdims=True)
        weight = weight + gate * a0
        out = out + (gate * a1) * vec
        d_probs = d_probs + place(a0 * dots + a1 * vec_dots, lane, FFN_EXPERTS + 2 + c)
        d0, d1 = gate * dots, gate * vec_dots
        mean = a0 * d0 + a1 * d1
        d0, d1 = a0 * (d0 - mean), a1 * (d1 - mean)
        logit_grads = logit_grads + place(d0, lane, at) + place(d1, lane, at + 1)
        vec_terms = vec_terms + place(gate * a1, lane, 20 + c)
    d_probs = jnp.where(named, d_probs, 0.0)
    logit_grads = logit_grads + probs * (d_probs - jnp.sum(probs * d_probs, axis=1, keepdims=True))
    high, rest = split_low(logit_grads, 2)
    out_ref[...] = out + weight * normed
    dnormed_ref[...] = weight * grad + dot_nt(high, mix_ref[...]) + dot_nt(rest, mix_ref[...])
    probs_ref[...] = probs
    dprobs_ref[...] = d_probs
    sums = None
    for terms, rows in ((logit_grads, low), (vec_terms, grad_ref[...])):
        for piece in split_low(terms.T, 2):
            part = dot_nn(piece, rows)
            sums = part if sums is None else sums + part
    sums = sums[0 : 3 * SMALL, :]

    @pl.when(pl.program_id(0) == 0)
    def _():
        small_ref[...] = sums

    @pl.when(pl.program_id(0) > 0)
    def _():
        small_ref[...] += sums


def local_part(hidden, low, grad, prev, ids, mix, gain, vec):
    tok, width = hidden.shape
    block, tiles = row_tiles(tok)
    shapes = [(tok, width), (tok, width), (tok, EXTRA), (tok, EXTRA), (3 * SMALL, width)]
    return pl.pallas_call(
        local_kernel,
        grid=(tok // block,),
        in_specs=[tiles(width), tiles(width), tiles(width), pl.BlockSpec((ALL_EXPERTS, 1, block), lambda i: (0, 0, i)), pl.BlockSpec((2, block), lambda i: (0, i)), fixed(mix), fixed(gain), fixed(vec)],
        out_specs=[tiles(width), tiles(width), tiles(EXTRA), tiles(EXTRA), pl.BlockSpec((3 * SMALL, width), lambda i: (0, 0))],
        out_shape=[jax.ShapeDtypeStruct(s, f32) for s in shapes],
        compiler_params=pltpu.CompilerParams(vmem_limit_bytes=60 * 2**20),
        cost_estimate=pl.CostEstimate(flops=14 * tok * width * EXTRA, bytes_accessed=16 * tok * width, transcendentals=tok * EXTRA),
        name="local_part",
    )(hidden, low, grad, prev, ids, mix, gain, vec)


def row_tiles(tok):
    block = 256 if tok % 256 == 0 else 128
    return block, lambda columns: pl.BlockSpec((block, columns), lambda i: (i, 0))


def fixed(value):
    return pl.BlockSpec(value.shape, lambda i: (0,) * value.ndim)


def combine_kernel(count, parts, core_ref, *refs):
    chosen, got, refs = refs[:count], refs[count : count * (1 + parts)], refs[count * (1 + parts) :]
    smalls, refs = refs[: count + 1], refs[count + 1 :]
    local_ref, hidden_ref, gain_ref, grad_ref, mixed_ref, w_ref, dhidden_ref, dmixed_ref, mine_ref, theirs_ref, total_w, total_gain, small_t = refs
    step = pl.program_id(0)

    @pl.when(step == 0)
    def _():
        total_w[...] = jnp.zeros_like(total_w)
        total_gain[...] = jnp.zeros_like(total_gain)

    d_normed = local_ref[...]
    for g in range(count):
        for r in range(parts):
            d_normed = d_normed + dot_nn(chosen[g][...], got[g * parts + r][...])
    hidden = hidden_ref[...]
    inverse = inverse_rms(hidden)
    scaled = d_normed * gain_ref[...]
    mean = jnp.mean(scaled * hidden, axis=1, keepdims=True)
    d_hidden = grad_ref[...].astype(f32) + inverse * scaled - hidden * (inverse * inverse * inverse * mean)
    low = d_hidden.astype(bf16)
    dhidden_ref[...] = d_hidden
    dmixed_ref[...] = dot_nt(low, w_ref[...]).astype(bf16)
    total_w[...] += dot_nn(mixed_ref[...].T, low)
    total_gain[...] += jnp.sum(d_normed * hidden * inverse, axis=0, keepdims=True)

    @pl.when(step == pl.num_programs(0) - 1)
    def _():
        width = w_ref.shape[0]
        half = width // 2
        row = lax.broadcasted_iota(jnp.int32, (SMALL, 1), 0)
        top = smalls[0][0 : 2 * SMALL, :]
        for small in smalls[1:]:
            top = top + small[...]
        rest = jnp.zeros((EXTRA - 4 * SMALL, width), f32)
        rows = [top, smalls[0][2 * SMALL : 3 * SMALL, :], jnp.where(row == 0, total_gain[...], 0.0), rest]
        small_t[...] = jnp.concatenate(rows, axis=0).T
        at = mine_ref.shape[1] - width - EXTRA
        for out_ref, which in ((theirs_ref, 1 - core_ref[0]), (mine_ref, core_ref[0])):
            place_rows = pl.ds(pl.multiple_of(which * half, half), half)
            out_ref[:, at : at + width] = total_w[place_rows, :].astype(bf16)
            out_ref[:, at + width : at + width + EXTRA] = small_t[place_rows, :].astype(bf16)


def combine(core, chosen, got, smalls, local, hidden, gain, grad, mixed, w_out, columns):
    tok, width = hidden.shape
    rows = sum(c.shape[1] for c in chosen)
    arrays = [a for group in got for a in group]
    block, tiles = row_tiles(tok)
    half = (width // 2, columns + width + EXTRA)
    return pl.pallas_call(
        functools.partial(combine_kernel, len(chosen), len(got[0])),
        grid=(tok // block,),
        in_specs=[SCALARS] + [tiles(c.shape[1]) for c in chosen] + [fixed(a) for a in arrays + smalls]
        + [tiles(width), tiles(width), fixed(gain), tiles(width), tiles(width), fixed(w_out)],
        out_specs=[tiles(width)] * 2 + [pl.BlockSpec(half, lambda i: (0, 0))] * 2,
        out_shape=[jax.ShapeDtypeStruct((tok, width), f32), jax.ShapeDtypeStruct((tok, width), bf16)] + [jax.ShapeDtypeStruct(half, bf16)] * 2,
        scratch_shapes=[pltpu.VMEM((width, width), f32), pltpu.VMEM((1, width), f32), pltpu.VMEM((width, EXTRA), f32)],
        compiler_params=pltpu.CompilerParams(vmem_limit_bytes=60 * 2**20),
        cost_estimate=pl.CostEstimate(flops=2 * tok * width * (rows + 2 * width), bytes_accessed=2 * width * (10 * tok + 2 * rows), transcendentals=0),
        name="combine_gradients",
    )(core, *chosen, *arrays, *smalls, local, hidden, gain, grad, mixed, w_out)


def flat_rows(value):
    if value.shape[1] % 16:
        return value.astype(f32).reshape(-1, value.shape[2]).astype(bf16)
    return value.reshape(-1, value.shape[2])


def finish_kernel(groups, parts, *refs):
    chosen, got = refs[: len(groups)], refs[len(groups) : len(groups) + parts]
    local_ref, probs_ref, dprobs_ref, out_ref, dlogits_ref = refs[len(groups) + parts :]
    width = local_ref.shape[1]
    lane = lax.broadcasted_iota(jnp.int32, (1, EXTRA), 1)
    picked = None
    for c, (at, size) in zip(chosen, groups):
        for r in range(parts):
            part = dot_nn(c[...], flat_rows(got[r][:, at : at + size, :]))
            picked = part if picked is None else picked + part
    out_ref[...] = (local_ref[...] + picked[:, 0:width]).astype(bf16)
    extra = picked[:, width : width + EXTRA]
    extra = extra + pltpu.roll(extra, EXTRA - 16, 1) + pltpu.roll(extra, EXTRA - 32, 1)
    d_probs = dprobs_ref[...] + jnp.where(lane < ALL_EXPERTS, extra, 0.0)
    probs = probs_ref[...]
    d_logits = probs * (d_probs - jnp.sum(probs * d_probs, axis=1, keepdims=True))
    dlogits_ref[:, 0, :] = d_logits.T[0:ALL_EXPERTS]


def finish(chosen, got, groups, local, probs, d_probs):
    tok, width = local.shape
    block, tiles = row_tiles(tok)
    return pl.pallas_call(
        functools.partial(finish_kernel, groups, len(got)),
        grid=(tok // block,),
        in_specs=[tiles(c.shape[1]) for c in chosen] + [fixed(g) for g in got] + [tiles(width), tiles(EXTRA), tiles(EXTRA)],
        out_specs=[tiles(width), pl.BlockSpec((ALL_EXPERTS, 1, block), lambda i: (0, 0, i))],
        out_shape=[jax.ShapeDtypeStruct((tok, width), bf16), jax.ShapeDtypeStruct((ALL_EXPERTS, 1, tok), f32)],
        compiler_params=pltpu.CompilerParams(vmem_limit_bytes=60 * 2**20),
        cost_estimate=pl.CostEstimate(flops=2 * tok * 1152 * (width + EXTRA), bytes_accessed=16 * tok * width, transcendentals=0),
        name="finish_outputs",
    )(*chosen, *got, local, probs, d_probs)


def input_kernel(count, x_ref, gain_ref, dhidden_ref, w_ref, *refs):
    grads, far, (out_ref, weights) = refs[:count], refs[count:-2], refs[-2:]
    width = x_ref.shape[1]

    @pl.when(pl.program_id(0) == 0)
    def _():
        for i in range(width // 128):
            for p in range(3):
                weights[:, i * 384 + p * 128 : i * 384 + (p + 1) * 128] = w_ref[:, p * width + i * 128 : p * width + (i + 1) * 128]

    total = None
    for ref in far:
        total = ref[...].astype(f32) if total is None else total + ref[...].astype(f32)
    d_act = jnp.where(pl.program_id(0) == 0, total, 0.0)
    at = 0
    for ref in grads:
        columns = ref.shape[1]
        d_act = d_act + dot_nt(ref[...], weights[:, at : at + columns])
        at += columns
    x = x_ref[...].astype(f32)
    inverse = inverse_rms(x)
    scaled = d_act * gain_ref[...]
    mean = jnp.mean(scaled * x, axis=1, keepdims=True)
    out_ref[...] = dhidden_ref[...] + inverse * scaled - x * (inverse * inverse * inverse * mean)


def input_gradient(grads, x, gain, d_hidden, w_qkv, far):
    tok, width = x.shape
    block = far[0].shape[0]
    tiles = lambda columns: pl.BlockSpec((block, columns), lambda i: (i, 0))
    return pl.pallas_call(
        functools.partial(input_kernel, len(grads)),
        grid=(tok // block,),
        in_specs=[tiles(width), fixed(gain), tiles(width), fixed(w_qkv)] + [tiles(g.shape[1]) for g in grads] + [fixed(f) for f in far],
        out_specs=tiles(width),
        out_shape=jax.ShapeDtypeStruct((tok, width), f32),
        scratch_shapes=[pltpu.VMEM((width, 3 * width), bf16)],
        compiler_params=pltpu.CompilerParams(vmem_limit_bytes=60 * 2**20),
        cost_estimate=pl.CostEstimate(flops=6 * tok * width * width, bytes_accessed=22 * tok * width, transcendentals=0),
        name="input_gradient",
    )(x, gain, d_hidden, w_qkv, *grads, *far)


def far_kernel(count, gain_ref, wk_ref, wv_ref, *refs):
    far, (act_ref, kv_ref) = refs[:count], refs[count:]
    width = wk_ref.shape[0]
    for k, ref in enumerate(far):

        @pl.when(pl.program_id(0) == k)
        def _():
            x = ref[...].astype(f32)
            act = (x * inverse_rms(x) * gain_ref[...]).astype(bf16)
            act_ref[...] = act
            kv_ref[:, 0:width] = dot_nn(act, wk_ref[...]).astype(bf16)
            kv_ref[:, width : 2 * width] = dot_nn(act, wv_ref[...]).astype(bf16)


def far_projection(far, gain, w_qkv):
    rows, width = far[0].shape
    count = len(far)
    return pl.pallas_call(
        functools.partial(far_kernel, count),
        grid=(count,),
        in_specs=[fixed(gain), pl.BlockSpec((width, width), lambda i: (0, 1)), pl.BlockSpec((width, width), lambda i: (0, 2))] + [fixed(f) for f in far],
        out_specs=[pl.BlockSpec((rows, width), lambda i: (i, 0)), pl.BlockSpec((rows, 2 * width), lambda i: (i, 0))],
        out_shape=[jax.ShapeDtypeStruct((count * rows, width), bf16), jax.ShapeDtypeStruct((count * rows, 2 * width), bf16)],
        compiler_params=pltpu.CompilerParams(vmem_limit_bytes=60 * 2**20),
        cost_estimate=pl.CostEstimate(flops=4 * count * rows * width * width, bytes_accessed=2 * width * (4 * count * rows + 2 * width), transcendentals=0),
        name="far_projection",
    )(gain, w_qkv, w_qkv, *far)


def xor_pairs(size, mask):
    return [(i, i ^ mask) for i in range(size)]


def sum_kernel(terms, index_ref, *refs):
    count = len(refs) // (sum(terms) + 1)
    outs = refs[-count:]
    for k, out_ref in enumerate(outs):
        at = 0
        first = 0
        for number in terms:
            total = None
            for t in range(first, first + number):
                value = refs[t * count + k][0].astype(f32)
                total = value if total is None else total + value
            out_ref[0, :, at : at + total.shape[1]] = total.astype(bf16)
            at += total.shape[1]
            first += number


def sum_pieces(index, groups):
    arrays = [a for group in groups for a in group]
    n, rows = arrays[0].shape[:2]
    columns = sum(group[0].shape[2] for group in groups)
    view = lambda a, k: pl.BlockSpec((1, rows, a.shape[2]), lambda i, s: (s[0] ^ k if n > 1 else 0, 0, 0))
    return pl.pallas_call(
        functools.partial(sum_kernel, [len(g) for g in groups]),
        grid_spec=pltpu.PrefetchScalarGridSpec(
            num_scalar_prefetch=1,
            grid=(1,),
            in_specs=[view(a, k) for a in arrays for k in range(n)],
            out_specs=[pl.BlockSpec((1, rows, columns), lambda i, s: (0, 0, 0))] * n,
        ),
        out_shape=[jax.ShapeDtypeStruct((1, rows, columns), bf16)] * n,
        compiler_params=pltpu.CompilerParams(vmem_limit_bytes=60 * 2**20),
        cost_estimate=pl.CostEstimate(flops=0, bytes_accessed=2 * n * rows * columns * 5, transcendentals=0),
        name="sum_pieces",
    )(index, *[a for a in arrays for _ in range(n)])


def quarters(value):
    return value.reshape(4, -1, value.shape[-1])


def swap(pieces, along):
    axis, size, unit = along
    return [pieces[0]] + [lax.ppermute(pieces[k], axis, xor_pairs(size, unit * k)) for k in range(1, 4)]


def spread(value, along):
    return swap([value] * 4, along)


def stack_kernel(*refs):
    n = len(refs) - 1
    size = refs[0].shape[0]
    for k in range(n):
        refs[n][k * size : (k + 1) * size] = refs[k][...]


def stack_pieces(pieces):
    shape = (len(pieces) * pieces[0].shape[0],) + pieces[0].shape[1:]
    return pl.pallas_call(
        stack_kernel,
        in_specs=[ANYWHERE] * len(pieces),
        out_specs=ANYWHERE,
        out_shape=jax.ShapeDtypeStruct(shape, bf16),
        compiler_params=pltpu.CompilerParams(vmem_limit_bytes=60 * 2**20),
        cost_estimate=pl.CostEstimate(flops=0, bytes_accessed=4 * math.prod(shape), transcendentals=0),
        name="stack_pieces",
    )(*pieces)


def unpack_kernel(left, last, index_ref, *refs):
    pieces, (w_ref, *refs) = refs[:4], refs[4:]
    if last:
        scale_ref, first_ref, _, _, out_ref, qkv_ref, router_ref, mixing_ref, vec_ref, gain_ref, attn_ref, small = refs
    else:
        out_ref, qkv_ref, small = refs
    width = out_ref.shape[1]
    size = pieces[0].shape[1]
    lane = lax.broadcasted_iota(jnp.int32, (1, EXTRA), 1)
    step = pl.program_id(0)
    half = index_ref[0]
    base = (half * width // 2 if last else 0) + step * 4 * size
    for k in range(4):
        at_ctx = pl.multiple_of((k ^ index_ref[1]) * size, size)
        rows = pl.ds(at_ctx, size)
        total = pieces[k][0].astype(f32)
        out_ref[rows, :] = total[:, left : left + width]
        gain = None
        for p in range(3):
            for i in range(width // 128):
                at = i * 384 + p * 128 + (0 if i * 384 < left else width + EXTRA)
                value = total[:, at : at + 128]
                columns = slice(p * width + i * 128, p * width + (i + 1) * 128)
                qkv_ref[rows, columns] = value
                part = value * w_ref[rows, columns].astype(f32)
                gain = part if gain is None else gain + part
        gain = jnp.sum(gain, axis=1, keepdims=True)
        small[pl.ds(pl.multiple_of(base + at_ctx, size), size), :] = total[:, left + width : left + width + EXTRA] + place(gain, lane, EXTRA - 1)
    if last:

        @pl.when(step == 3)
        def _():
            small[pl.ds(pl.multiple_of((1 - half) * (width // 2), width // 2), width // 2), :] = first_ref[...]
            turned = small[...].T
            router_ref[...] = turned[0:ALL_EXPERTS]
            mixing_ref[0] = turned[16:18]
            mixing_ref[1] = turned[18:20]
            vec_ref[...] = turned[20:22]
            gain_ref[...] = turned[24]
            attn_ref[...] = (turned[EXTRA - 1 : EXTRA] / scale_ref[...])[0]


def unpack_half(index, pieces, w_qkv, left, scale, before):
    width = w_qkv.shape[0]
    size = width // 32
    last = before is not None
    row = lambda a, s: (s[0] * 4 + a, 0)
    source = pl.BlockSpec((1, size, pieces[0].shape[2]), lambda a, s: (a ^ s[2], 0, 0))
    whole = lambda shape: pl.BlockSpec(shape, lambda a, s: (0,) * len(shape))
    in_specs = [source] * 4 + [pl.BlockSpec((4 * size, 3 * width), row)]
    out_specs = [pl.BlockSpec((4 * size, width), row), pl.BlockSpec((4 * size, 3 * width), row)]
    out_shape = [jax.ShapeDtypeStruct((width, width), f32), jax.ShapeDtypeStruct((width, 3 * width), f32)]
    arrays = [*pieces, w_qkv]
    if last:
        shapes = ((ALL_EXPERTS, width), (2, 2, width), (2, width), (width,), (width,))
        in_specs += [whole((1, width)), whole((width // 2, EXTRA))] + [pl.BlockSpec(memory_space=pl.ANY)] * 2
        arrays += [scale, before[2], before[0], before[1]]
        scratch = [pltpu.VMEM((width, EXTRA), f32)]
        aliases = {len(arrays) - 1: 0, len(arrays): 1}
    else:
        shapes = ((width // 2, EXTRA),)
        scratch = []
        aliases = {}
    return pl.pallas_call(
        functools.partial(unpack_kernel, left, last),
        grid_spec=pltpu.PrefetchScalarGridSpec(
            num_scalar_prefetch=1,
            grid=(4,),
            in_specs=in_specs,
            out_specs=out_specs + [whole(s) for s in shapes],
            scratch_shapes=scratch,
        ),
        out_shape=out_shape + [jax.ShapeDtypeStruct(s, f32) for s in shapes],
        input_output_aliases=aliases,
        compiler_params=pltpu.CompilerParams(vmem_limit_bytes=60 * 2**20),
        cost_estimate=pl.CostEstimate(flops=0, bytes_accessed=14 * width * width, transcendentals=0),
        name="unpack_half",
    )(index, *arrays)

P = jax.sharding.PartitionSpec


def rms_inverse(tensor):
    return lax.rsqrt(jnp.mean(tensor * tensor, axis=-1, keepdims=True) + epsilon)


def after(values, *others):
    return lax.optimization_barrier((values, others))[0]


def body(inputs, prev_logits, routes, attn_gain, w_qkv, w_out, moe_gain, router, const_gate, const_vec, w_gate, w_up, w_down, out_grad):
    n_ctx, n_exp = lax.axis_size("ctx"), lax.axis_size("exp")
    me_c, me_e = lax.axis_index("ctx"), lax.axis_index("exp")
    tok, width = inputs.shape[1], inputs.shape[2]
    plen = tok - CONT_LEN
    split = n_exp // FFN_EXPERTS
    capacity = max(4, tok // 64 * 12)
    first = -(-capacity // 32) * 16
    groups = ((0, first), (first, capacity - first))
    home = (me_e // split).reshape(1)

    def deal(value):
        value = jnp.repeat(value, split, axis=0) if split > 1 else value
        return lax.all_to_all(value, "exp", 0, 0, tiled=True)

    def give_back(value):
        value = lax.all_to_all(value, "exp", 0, 0, tiled=True)
        return [value[r::split] if split > 1 else value for r in range(split)]

    x_low = inputs[0]
    upstream_low = out_grad[0]
    flags = jnp.where((me_c ^ jnp.arange(1, n_ctx)) < me_c, 0.0, NEG).astype(f32)

    prev = prev_logits.transpose(2, 0, 1)
    ids = routes.transpose(0, 2, 1)[0]
    mix = jnp.concatenate([router, jnp.zeros((width, 4), bf16), const_gate[0], const_gate[1], jnp.zeros((width, EXTRA - 20), bf16)], axis=1)
    router_pad = jnp.pad(router, ((0, 0), (0, EXTRA - ALL_EXPERTS)))
    turned, chosen, early_sent, x_prompt = route_plan(home, ids, upstream_low, prev, x_low, plen, groups)
    far = [lax.ppermute(x_prompt, "ctx", xor_pairs(n_ctx, k)) for k in range(1, n_ctx)]

    tokens_in = x_low.astype(f32)
    inverse_attn = rms_inverse(tokens_in)
    act_low = (tokens_in * inverse_attn * attn_gain).astype(bf16)
    projected = dot_nn(act_low, w_qkv).astype(bf16)
    early = deal(early_sent)
    act_t = turn(act_low)
    act_far, kv_far = far_projection(after(far, projected, act_t), attn_gain[None], w_qkv)

    mixed_low, lse, hidden, moe_low, sent = attention_forward(flags, projected, kv_far, plen, x_low, w_out, moe_gain[None], turned)
    sent, hidden, early = lax.optimization_barrier((sent, hidden, early))

    local_out, d_normed_local, probs, d_probs, small_local = local_part(hidden, moe_low, upstream_low, prev, ids, mix, moe_gain[None], const_vec)
    far_t = turn(act_far)
    sent = [after(sent[0], local_out, d_normed_local, far_t), sent[1]]
    got = [deal(part.reshape(FFN_EXPERTS, -1, width)) for part in sent]

    got = [part.reshape(-1, width) for part in got]
    passes = [expert_pass(group, home, r, early, router_pad, w_gate, w_up, w_down) for group, r in zip(groups, got)]
    d_got = [give_back(p[1].reshape(n_exp, -1, width)) for p in passes]
    gate_up_low, down_low = weight_gradients(got, [p[2] for p in passes], [p[3] for p in passes], [p[4] for p in passes], [p[5] for p in passes])
    outs = jnp.concatenate([p[0].reshape(n_exp, -1, width + EXTRA) for p in passes], axis=1)
    d_got, gate_up_low, down_low, outs = lax.optimization_barrier((d_got, gate_up_low, down_low, outs))
    out_got = give_back(outs)

    d_got = [[part.reshape(-1, width) for part in group] for group in d_got]
    pairs = width // 128
    cut = pairs // 3
    core = (me_e & 1).reshape(1)
    smalls = [small_local] + [p[6] for p in passes]
    d_hidden, d_mixed, *buffers = combine(core, chosen, d_got, smalls, d_normed_local, hidden, moe_gain[None], upstream_low, mixed_low, w_out, cut * 384)

    sum_gate_up = lax.psum_scatter(gate_up_low, "ctx", scatter_dimension=1, tiled=True).astype(f32)
    sum_down = lax.psum_scatter(down_low, "ctx", scatter_dimension=0, tiled=True).astype(f32)

    def attention(upstream, begin, count, buffers, at, starts, last):
        return attention_backward(flags, core, projected, kv_far, mixed_low, upstream, lse, act_t, far_t, w_qkv, plen, begin, count, buffers, at, starts, last)

    dense = n_ctx == 4 and n_exp == 8
    left, right = cut * 384, (pairs - cut) * 384
    z = me_e >> 1
    at_ctx, at_z = me_c.reshape(1), z.reshape(1)
    along_ctx, along_z = ("ctx", 4, 1), ("exp", 8, 2)
    across = lambda value: lax.ppermute(value, "exp", xor_pairs(n_exp, 1))
    mine_1, theirs_1, grads_1, *starts = attention(d_mixed, 0, cut, buffers, 0, None, False)
    if dense:
        got_1 = across(theirs_1)
    mine_2, theirs_2, grads_2, *starts = attention(d_mixed, cut, 1, right, 0, starts, False)
    if dense:
        mine_2, theirs_2, starts, got_1 = lax.optimization_barrier((mine_2, theirs_2, starts, got_1))
        sums_1 = sum_pieces(at_z, [[quarters(mine_1), quarters(got_1)]])
        parts_1 = swap(sums_1, along_z)
        mine_2 = after(mine_2, sums_1[0])
    mine_2, theirs_2, grads_3, *d_far = attention(d_mixed, cut + 1, pairs - cut - 1, (mine_2, theirs_2), 1, starts, True)
    if dense:
        mine_2, theirs_2, grads_3, d_far, parts_1 = lax.optimization_barrier((mine_2, theirs_2, grads_3, d_far, parts_1))
    send_far = lambda k: lax.ppermute(d_far[k - 1], "ctx", xor_pairs(n_ctx, k))
    far_back = [send_far(k) for k in range(1, n_ctx - 1)]
    if dense:
        sums_2 = sum_pieces(at_z, [[quarters(mine_2), quarters(across(theirs_2))]])
        parts_2 = swap(sums_2, along_z)
        mixed_out, d_logits = finish(chosen, out_got, groups, after(local_out, sums_2[0]), probs, d_probs)
        mixed_out, d_logits, far_back, d_far = lax.optimization_barrier((mixed_out, d_logits, far_back, d_far))
        far_back = far_back + [send_far(n_ctx - 1)]
        mixed_out, parts_2 = lax.optimization_barrier((mixed_out, parts_2))
        parts_1, parts_2 = ([quarters(p) for p in parts] for parts in (parts_1, parts_2))
        parts = swap(sum_pieces(at_ctx, [parts_1, parts_2]), along_ctx)
        [piece] = sum_pieces(at_ctx, [parts])
        spread_z = spread(piece, along_z)
    else:
        mixed_out, d_logits = finish(chosen, out_got, groups, local_out, probs, d_probs)
        far_back = far_back + [send_far(n_ctx - 1)]
    d_inputs = input_gradient([grads_1, grads_2, grads_3], x_low, attn_gain[None], d_hidden, w_qkv, far_back)

    d_prev = d_logits.transpose(1, 2, 0)
    total_gate, total_up, total_down = sum_gate_up[0][None], sum_gate_up[1][None], sum_down[None]
    if dense:
        d_inputs, spread_z = lax.optimization_barrier((d_inputs, spread_z))
        column = stack_pieces(spread_z)
        places = [jnp.stack([half, me_c, z]) for half in (core[0], 1 - core[0])]
        own, places = after((spread(column, along_ctx), places), total_gate, total_up, total_down)
        other = [across(piece) for piece in own]
        first = unpack_half(places[0], own, w_qkv, left, None, None)
        first, other = lax.optimization_barrier((first, other))
        out_sum, qkv_sum, d_router, d_mixing, d_const_vec, d_moe_gain, d_attn_gain = unpack_half(places[1], other, w_qkv, left, attn_gain[None], first)
    else:
        whole = lambda mine, theirs: jnp.where(core == 0, jnp.concatenate([mine, theirs], axis=0), jnp.concatenate([theirs, mine], axis=0))
        total_1, total_2 = [v.astype(f32) for v in lax.psum((whole(mine_1, theirs_1), whole(mine_2, theirs_2)), ("ctx", "exp"))]
        columns = jnp.concatenate([total_1[:, :left], total_2], axis=1).reshape(width, pairs, 3, 128)
        qkv_sum = columns.transpose(0, 2, 1, 3).reshape(width, 3 * width)
        out_sum, small = total_1[:, left : left + width], total_1[:, left + width :].T
        d_attn_gain = (jnp.sum(qkv_sum * w_qkv.astype(f32), axis=1) / attn_gain)
        d_router, d_mixing, d_const_vec, d_moe_gain = small[:ALL_EXPERTS], small[16:20].reshape(2, 2, width), small[20:22], small[24]
    return (
        mixed_out[None],
        d_inputs[None],
        d_prev,
        d_attn_gain,
        qkv_sum,
        out_sum,
        d_moe_gain,
        d_router.T,
        d_mixing.transpose(0, 2, 1),
        d_const_vec,
        total_gate,
        total_up,
        total_down,
    )


def solution(mesh):
    rows = P("ctx", "exp", None)
    expert = P("exp", None, None)
    summed = P("exp", "ctx", None)
    return jax.shard_map(
        body,
        mesh=mesh,
        in_specs=(rows, rows, rows, P(), P(), P(), P(), P(), P(), P(), expert, expert, expert, rows),
        out_specs=(rows, rows, rows, P(), P(), P(), P(), P(), P(), P(), summed, summed, summed),
        check_vma=False,
    )
```
